32 devices in a mesh: ctx: 8 (over y, x, core), fsdp: 4 (over z).
Axes of the slice: x: 2, y: 2, z: 4, core: 2. Of those that a mesh axis runs over, the one named last changes fastest.
Arguments:
- tokens: bfloat16 [4, 1152, 768], P('fsdp', 'ctx'), may hold values from -6 to 6
- segment_ids: int32 [4, 1152], P('fsdp', 'ctx'), may hold values from 0 to 1151, as said below
- valid_rows: int32 [4, 1152], P('fsdp', 'ctx'), may hold values from 0 to 1, as said below
- teacher: bfloat16 [4, 1152, 768], P('fsdp', 'ctx'), may hold values from -16 to 16
- cotangent: bfloat16 [4, 1152, 768], P('fsdp', 'ctx'), may hold values from -6 to 6
- first_gain: bfloat16 [768], P('fsdp'), may hold values from 0.5 to 1.5
- first_shift: bfloat16 [768], P('fsdp'), may hold values from -3 to 3
- query_weight: bfloat16 [768, 768], P('fsdp'), may hold values from -0.3125 to 0.3125
- query_bias: bfloat16 [768], P('fsdp'), may hold values from -3 to 3
- key_weight: bfloat16 [768, 768], P('fsdp'), may hold values from -0.3125 to 0.3125
- value_weight: bfloat16 [768, 768], P('fsdp'), may hold values from -0.21875 to 0.21875
- value_bias: bfloat16 [768], P('fsdp'), may hold values from -3 to 3
- output_weight: bfloat16 [768, 768], P('fsdp'), may hold values from -0.875 to 0.875
- output_bias: bfloat16 [768], P('fsdp'), may hold values from -3 to 3
- second_gain: bfloat16 [768], P('fsdp'), may hold values from 0.5 to 1.5
- second_shift: bfloat16 [768], P('fsdp'), may hold values from -3 to 3
- up_weight: bfloat16 [768, 3072], P('fsdp'), may hold values from -0.21875 to 0.21875
- up_bias: bfloat16 [3072], P('fsdp'), may hold values from -3 to 3
- down_weight: bfloat16 [3072, 768], P('fsdp'), may hold values from -0.109375 to 0.109375
- down_bias: bfloat16 [768], P('fsdp'), may hold values from -3 to 3
Outputs:
- layer_output: bfloat16 [4, 1152, 768], P('fsdp', 'ctx')
- loss_value: float32 [], replicated
- grad_tokens: bfloat16 [4, 1152, 768], P('fsdp', 'ctx')
- grad_first_gain: float32 [768], P('fsdp')
- grad_first_shift: float32 [768], P('fsdp')
- grad_query_weight: float32 [768, 768], P('fsdp')
- grad_query_bias: float32 [768], P('fsdp')
- grad_key_weight: float32 [768, 768], P('fsdp')
- grad_value_weight: float32 [768, 768], P('fsdp')
- grad_value_bias: float32 [768], P('fsdp')
- grad_output_weight: float32 [768, 768], P('fsdp')
- grad_output_bias: float32 [768], P('fsdp')
- grad_second_gain: float32 [768], P('fsdp')
- grad_second_shift: float32 [768], P('fsdp')
- grad_up_weight: float32 [768, 3072], P('fsdp')
- grad_up_bias: float32 [3072], P('fsdp')
- grad_down_weight: float32 [3072, 768], P('fsdp')
- grad_down_bias: float32 [768], P('fsdp')
The draws below stay inside these ranges and needn't reach their ends.
Inputs may be any that keep to these rules, and one draw needn't show every extreme that they name: `segment_ids`: within a sequence the ids never fall, and each is the position within the sequence of its document's first row; in every sequence one document has rows on every index of ctx. `valid_rows`: 1 where a row holds a token, 0 where it is padding.
All inputs are finite; a program needn't handle non-finite values.
Results may differ from the reference program's by a relative error of at most 0.023.
Values may be sent and summed in bfloat16 or wider, within the bound.
No kernel may reach another device: no remote copies, remote signals or barrier semaphores. Data moves between devices by JAX's collectives and lax.ppermute only.
A program may use at most 256 MiB of HBM per device.

```python
import jax
import jax.numpy as jnp
from jax import lax

D = 768
HEADS = 12
HEAD_DIM = 64
FF = 3072
TOK_DEV = 144
LENGTH = 1152
SEQS = 4
N_CTX = 8


def draw_segment_ids(key, part):
    head_key, tail_key, cut_key = jax.random.split(key, 3)
    heads = jax.random.randint(head_key, (SEQS, 1), 0, TOK_DEV)
    tails = jax.random.randint(tail_key, (SEQS, 1), LENGTH - TOK_DEV + 1, LENGTH + 1)
    position = jnp.arange(LENGTH, dtype=jnp.int32)[None, :]
    cuts = jax.random.randint(cut_key, (SEQS, LENGTH), 0, 6) == 0
    edges = (position < heads) | (position >= tails)
    starts = (position == 0) | (position == heads) | (position == tails) | (position == LENGTH - 1) | cuts & edges
    marks = jnp.where(starts, position, 0)
    return lax.cummax(marks, axis=1).astype(jnp.int32)


def draw_valid_rows(key, part):
    position = jnp.arange(LENGTH, dtype=jnp.int32)[None, :]
    ticket = jax.random.randint(key, (SEQS, LENGTH), 0, 10 * LENGTH)
    return (ticket < 2 * LENGTH + 7 * position).astype(jnp.int32)


def draw_teacher(key, part):
    noise_key = jax.random.fold_in(key, 7331)
    along = (jnp.arange(LENGTH, dtype=jnp.float32) / LENGTH)[None, :, None]
    spread = 0.5 + 2.5 * along
    values = jnp.clip(jax.random.normal(noise_key, (SEQS, LENGTH, D), jnp.float32), -5.0, 5.0) * spread
    return values.astype(jnp.bfloat16)


def level_of(stream_key, dims, cuts, smallest, largest):
    level, own = 1.0, jax.random.fold_in(stream_key, 6)
    for dim, parts in cuts:
        heights = jnp.exp(jax.random.uniform(jax.random.fold_in(own, dim), (parts,), jnp.float32, smallest / len(cuts), largest / len(cuts)))
        level = level * jnp.repeat(heights, dims[dim] // parts).reshape([-1 if axis == dim else 1 for axis in range(len(dims))])
    return level


def normal_values(rng, dims, deviation, bound, shards=(), held_as=jnp.bfloat16):
    loudness = level_of(rng, dims, shards, -0.22, 0.18) if shards else 1.0
    entries = jax.random.normal(rng, dims, jnp.float32) * deviation * loudness
    return jnp.minimum(jnp.maximum(entries, -bound), bound).astype(held_as)


def setup_inputs(seed: int = 0) -> dict:
    streams_of = jax.random.split(jax.random.key(seed), 21)
    tokens = normal_values(streams_of[0], (SEQS, LENGTH, D), 1.0, 6.0, ((0, 4), (1, 8)))
    segment_ids = draw_segment_ids(jax.random.fold_in(streams_of[20], 71), 0)
    valid_rows = draw_valid_rows(jax.random.fold_in(streams_of[20], 71), 0)
    teacher = draw_teacher(jax.random.fold_in(streams_of[20], 71), 0)
    cotangent = normal_values(streams_of[4], (SEQS, LENGTH, D), 1.0, 6.0, ((0, 4), (1, 8)))
    first_gain = jnp.clip(1.0 + 0.1 * jax.random.normal(streams_of[5], (D,), jnp.float32), 0.5, 1.5).astype(jnp.bfloat16)
    first_shift = normal_values(streams_of[6], (D,), 0.3, 3.0, ((0, 4),))
    query_weight = normal_values(streams_of[7], (D, D), (D // 2) ** -0.5, 0.3125, ((0, 4),))
    query_bias = normal_values(streams_of[8], (D,), 0.5, 3.0, ((0, 4),))
    key_weight = normal_values(streams_of[9], (D, D), (D // 2) ** -0.5, 0.3125, ((0, 4),))
    value_weight = normal_values(streams_of[10], (D, D), D ** -0.5, 0.21875, ((0, 4),))
    value_bias = normal_values(streams_of[11], (D,), 0.5, 3.0, ((0, 4),))
    output_weight = normal_values(streams_of[12], (D, D), (D // 16) ** -0.5, 0.875, ((0, 4),))
    output_bias = normal_values(streams_of[13], (D,), 0.5, 3.0, ((0, 4),))
    second_gain = jnp.clip(1.0 + 0.1 * jax.random.normal(streams_of[14], (D,), jnp.float32), 0.5, 1.5).astype(jnp.bfloat16)
    second_shift = normal_values(streams_of[15], (D,), 0.3, 3.0, ((0, 4),))
    up_weight = normal_values(streams_of[16], (D, FF), D ** -0.5, 0.21875, ((0, 4),))
    up_bias = normal_values(streams_of[17], (FF,), 0.5, 3.0, ((0, 4),))
    down_weight = normal_values(streams_of[18], (FF, D), FF ** -0.5, 0.109375, ((0, 4),))
    down_bias = normal_values(streams_of[19], (D,), 0.5, 3.0, ((0, 4),))
    return dict(tokens=tokens, segment_ids=segment_ids, valid_rows=valid_rows, teacher=teacher, cotangent=cotangent, first_gain=first_gain, first_shift=first_shift, query_weight=query_weight, query_bias=query_bias, key_weight=key_weight, value_weight=value_weight, value_bias=value_bias, output_weight=output_weight, output_bias=output_bias, second_gain=second_gain, second_shift=second_shift, up_weight=up_weight, up_bias=up_bias, down_weight=down_weight, down_bias=down_bias)


@jax.custom_vjp
def low(v):
    return lax.optimization_barrier(v.astype(jnp.bfloat16)).astype(jnp.float32)

@jax.custom_vjp
def low_back(v):
    return v

def low_keep(v):
    return (low(v), None)

def low_pass(kept, grad):
    return (grad,)

def back_keep(v):
    return (v, None)

def back_low(kept, grad):
    return (low(grad),)
low.defvjp(low_keep, low_pass)
low_back.defvjp(back_keep, back_low)
EPSILON = 1e-06
MASKED = -1e+30

def norm_rows(values, gain, shift):
    centre = lax.optimization_barrier(jnp.mean(values, axis=-1, keepdims=True))
    centred = values - centre
    spread = lax.optimization_barrier(jnp.mean(centred * centred, axis=-1, keepdims=True))
    return centred * lax.rsqrt(spread + EPSILON) * gain + shift

def product(left, right):
    return jnp.dot(left, right, precision=lax.Precision.HIGHEST)

def attend_sequence(queries, key_rows, value_rows, segment_row, valid_row):
    key_heads = key_rows.reshape(LENGTH, HEADS, HEAD_DIM)
    value_heads = value_rows.reshape(LENGTH, HEADS, HEAD_DIM)
    key_place = jnp.arange(LENGTH, dtype=jnp.int32)
    usable_key = valid_row == 1

    @jax.checkpoint
    def one_block(block_index):
        start = (block_index * TOK_DEV).astype(jnp.int32)
        query_heads = lax.dynamic_slice_in_dim(queries, start, TOK_DEV, 0).reshape(TOK_DEV, HEADS, HEAD_DIM)
        query_segment = lax.dynamic_slice_in_dim(segment_row, start, TOK_DEV, 0)
        query_place = start + jnp.arange(TOK_DEV, dtype=jnp.int32)
        allowed = (query_segment[:, None] == segment_row[None, :]) & (usable_key[None, :] | (query_place[:, None] == key_place[None, :]))
        scores = low_back(jnp.einsum('qhd,khd->hqk', query_heads, key_heads, precision=lax.Precision.HIGHEST) * HEAD_DIM ** (-0.5))
        probs = jax.nn.softmax(jnp.where(allowed[None], scores, MASKED), axis=-1)
        mixed = jnp.einsum('hqk,khd->qhd', low(probs), value_heads, precision=lax.Precision.HIGHEST)
        return mixed.reshape(TOK_DEV, D)
    pieces = lax.map(one_block, jnp.arange(N_CTX, dtype=jnp.int32))
    return pieces.reshape(LENGTH, D)

def attend_item(item):
    return attend_sequence(item[0], item[1], item[2], item[3], item[4])

def reference(tokens, segment_ids, valid_rows, teacher, cotangent, first_gain, first_shift, query_weight, query_bias, key_weight, value_weight, value_bias, output_weight, output_bias, second_gain, second_shift, up_weight, up_bias, down_weight, down_bias):
    valid_float = valid_rows.astype(jnp.float32)
    teach = teacher.astype(jnp.float32)
    valid_count = jnp.sum(valid_float)

    def forward(inputs, gain_one, shift_one, w_query, b_query, w_key, w_value, b_value, w_output, b_output, gain_two, shift_two, w_up, b_up, w_down, b_down):
        h_one = low(norm_rows(inputs, gain_one, shift_one))
        queries = low(low_back(product(h_one, w_query) + b_query))
        key_rows = low(low_back(product(h_one, w_key)))
        value_rows = low(low_back(product(h_one, w_value) + b_value))
        mixed = lax.map(attend_item, (queries, key_rows, value_rows, segment_ids, valid_rows))
        mixed = low(low_back(mixed))
        second = inputs + low_back(product(mixed, w_output) + b_output)
        h_two = low(norm_rows(second, gain_two, shift_two))
        hidden = low(jax.nn.gelu(low_back(product(h_two, w_up) + b_up), approximate=True))
        result = second + low_back(product(hidden, w_down) + b_down)
        mismatch = result - teach
        loss_value = jnp.sum(valid_float[:, :, None] * mismatch * mismatch) / (D * valid_count)
        return (result, loss_value)
    params = tuple((a.astype(jnp.float32) for a in (first_gain, first_shift, query_weight, query_bias, key_weight, value_weight, value_bias, output_weight, output_bias, second_gain, second_shift, up_weight, up_bias, down_weight, down_bias)))
    (result, loss_value), pull = jax.vjp(forward, tokens.astype(jnp.float32), *params)
    grads = pull((cotangent.astype(jnp.float32), jnp.ones((), jnp.float32)))
    return (result.astype(jnp.bfloat16), loss_value, grads[0].astype(jnp.bfloat16), grads[1], grads[2], grads[3], grads[4], grads[5], grads[6], grads[7], grads[8], grads[9], grads[10], grads[11], grads[12], grads[13], grads[14], grads[15])
```

```python
import jax
import jax.numpy as jnp
from jax import lax
from jax.experimental import pallas as pl
from jax.experimental.pallas import tpu as pltpu
from jax.sharding import PartitionSpec as P

HEADS = 12
HEAD_DIM = 64


EPSILON = 1e-06
MASKED = -1e30


def norm_rows(values, gain, shift):
    centre = jnp.mean(values, axis=-1, keepdims=True)
    centred = values - centre
    spread = jnp.mean(centred * centred, axis=-1, keepdims=True)
    return centred * lax.rsqrt(spread + EPSILON) * gain + shift


def tanh_gelu(values):
    return jax.nn.gelu(values, approximate=True)


def key_allowed(query_segment, query_place, key_codes, key_place):
    same_doc = query_segment[:, None] == (key_codes // 2)[None, :]
    usable = (key_codes % 2 == 1)[None, :] | (query_place[:, None] == key_place[None, :])
    return (same_doc & usable)[None, :, :]


def split_heads(values):
    return values.reshape(values.shape[0], HEADS, HEAD_DIM)


def head_scores(query_heads, key_heads, scale):
    return (
        jnp.einsum("qhd,khd->hqk", query_heads, key_heads, preferred_element_type=jnp.float32)
        * scale
    )


def row_sum(values):
    return jnp.sum(values, axis=0, dtype=jnp.float32)


def left_product(left, right):
    return jnp.einsum("rd,rf->df", left, right, preferred_element_type=jnp.float32)


def right_product(left, right):
    return jnp.einsum("rf,df->rd", left, right, preferred_element_type=jnp.float32)


def shards(
    tokens,
    segment_ids,
    valid_rows,
    teacher,
    cotangent,
    first_gain,
    first_shift,
    query_weight,
    query_bias,
    key_weight,
    value_weight,
    value_bias,
    output_weight,
    output_bias,
    second_gain,
    second_shift,
    up_weight,
    up_bias,
    down_weight,
    down_bias,
):
    tok_rows = tokens.shape[1]
    feature_width = tokens.shape[2]
    shard_count = lax.axis_size("ctx")
    key_block = 4 * tok_rows
    block_count = shard_count // 4
    scale = HEAD_DIM ** (-0.5)
    gain_one, shift_one, w_query, b_query, w_key, w_value, b_value, w_output, b_output = (
        lax.all_gather(first_gain, "fsdp", axis=0, tiled=True),
        lax.all_gather(first_shift, "fsdp", axis=0, tiled=True),
        lax.all_gather(query_weight, "fsdp", axis=0, tiled=True),
        lax.all_gather(query_bias, "fsdp", axis=0, tiled=True),
        lax.all_gather(key_weight, "fsdp", axis=0, tiled=True),
        lax.all_gather(value_weight, "fsdp", axis=0, tiled=True),
        lax.all_gather(value_bias, "fsdp", axis=0, tiled=True),
        lax.all_gather(output_weight, "fsdp", axis=0, tiled=True),
        lax.all_gather(output_bias, "fsdp", axis=0, tiled=True),
    )
    gain_two, shift_two, w_up, b_up, w_down, b_down = (
        lax.all_gather(second_gain, "fsdp", axis=0, tiled=True),
        lax.all_gather(second_shift, "fsdp", axis=0, tiled=True),
        lax.all_gather(up_weight, "fsdp", axis=0, tiled=True),
        lax.all_gather(up_bias, "fsdp", axis=0, tiled=True),
        lax.all_gather(down_weight, "fsdp", axis=0, tiled=True),
        lax.all_gather(down_bias, "fsdp", axis=0, tiled=True),
    )
    local_segment = segment_ids[0]
    local_valid = valid_rows[0]
    local_codes = local_segment * 2 + local_valid
    all_codes = lax.all_gather(local_codes, "ctx", axis=0, tiled=True)
    query_place = lax.axis_index("ctx") * tok_rows + jnp.arange(tok_rows, dtype=jnp.int32)
    inputs = tokens[0].astype(jnp.float32)
    gain_first = gain_one.astype(jnp.float32)
    shift_first = shift_one.astype(jnp.float32)
    gain_second = gain_two.astype(jnp.float32)
    shift_second = shift_two.astype(jnp.float32)
    h_one = norm_rows(inputs, gain_first, shift_first)
    h_one_low = h_one.astype(jnp.bfloat16)
    query_low = (
        jnp.dot(h_one_low, w_query, preferred_element_type=jnp.float32)
        + b_query.astype(jnp.float32)
    ).astype(jnp.bfloat16)
    key_low = jnp.dot(h_one_low, w_key, preferred_element_type=jnp.float32).astype(jnp.bfloat16)
    value_low = (
        jnp.dot(h_one_low, w_value, preferred_element_type=jnp.float32)
        + b_value.astype(jnp.float32)
    ).astype(jnp.bfloat16)
    key_all, value_all = (
        lax.all_gather(key_low, "ctx", axis=0, tiled=True),
        lax.all_gather(value_low, "ctx", axis=0, tiled=True),
    )
    query_heads = split_heads(query_low)

    def block_rows(source, block_index):
        return split_heads(lax.dynamic_slice_in_dim(source, block_index * key_block, key_block, 0))

    def block_allowed(block_index):
        start = block_index * key_block
        codes = lax.dynamic_slice_in_dim(all_codes, start, key_block, 0)
        return key_allowed(
            local_segment, query_place, codes, start + jnp.arange(key_block, dtype=jnp.int32)
        )

    def stats_step(block_index, state_pair):
        running_max, running_sum = state_pair
        allowed = block_allowed(block_index)
        scores = jnp.where(
            allowed, head_scores(query_heads, block_rows(key_all, block_index), scale), MASKED
        )
        new_max = jnp.maximum(running_max, jnp.max(scores, axis=2))
        weights = jnp.where(allowed, jnp.exp(scores - new_max[:, :, None]), 0.0)
        return (new_max, running_sum * jnp.exp(running_max - new_max) + jnp.sum(weights, axis=2))

    start_max = jnp.full((HEADS, tok_rows), MASKED, jnp.float32)
    start_sum = jnp.zeros((HEADS, tok_rows), jnp.float32)
    running_max, running_sum = lax.fori_loop(0, block_count, stats_step, (start_max, start_sum))
    log_total = running_max + jnp.log(running_sum)

    def mix_step(block_index, mixed_sum):
        allowed = block_allowed(block_index)
        scores = head_scores(query_heads, block_rows(key_all, block_index), scale)
        probs = jnp.where(allowed, jnp.exp(scores - log_total[:, :, None]), 0.0).astype(
            jnp.bfloat16
        )
        return mixed_sum + jnp.einsum(
            "hqk,khd->qhd",
            probs,
            block_rows(value_all, block_index),
            preferred_element_type=jnp.float32,
        )

    mixed_heads = lax.fori_loop(
        0, block_count, mix_step, jnp.zeros((tok_rows, HEADS, HEAD_DIM), jnp.float32)
    )
    mixed = mixed_heads.reshape(tok_rows, feature_width)
    mixed_low = mixed.astype(jnp.bfloat16)
    second = (
        inputs
        + jnp.dot(mixed_low, w_output, preferred_element_type=jnp.float32)
        + b_output.astype(jnp.float32)
    )
    h_two = norm_rows(second, gain_second, shift_second)
    h_two_low = h_two.astype(jnp.bfloat16)
    up_value = jnp.dot(h_two_low, w_up, preferred_element_type=jnp.float32) + b_up.astype(
        jnp.float32
    )
    act_low = tanh_gelu(up_value).astype(jnp.bfloat16)
    result = (
        second
        + jnp.dot(act_low, w_down, preferred_element_type=jnp.float32)
        + b_down.astype(jnp.float32)
    )
    layer_output = result.astype(jnp.bfloat16)[None]
    valid_float = local_valid.astype(jnp.float32)
    mismatch = result - teacher[0].astype(jnp.float32)
    error_sum, valid_count = lax.psum(
        (jnp.sum(valid_float[:, None] * mismatch * mismatch), jnp.sum(valid_float)), ("ctx", "fsdp")
    )
    loss_value = error_sum / (feature_width * valid_count)
    d_result = (
        cotangent[0].astype(jnp.float32)
        + 2.0 / (feature_width * valid_count) * valid_float[:, None] * mismatch
    )
    d_down = d_result.astype(jnp.bfloat16)
    grad_down_bias = row_sum(d_down)
    grad_down_weight = left_product(act_low, d_down)
    d_act = right_product(d_down, w_down)
    gelu_value, gelu_pull = jax.vjp(tanh_gelu, up_value)
    d_up = gelu_pull(d_act)[0].astype(jnp.bfloat16)
    grad_up_bias = row_sum(d_up)
    grad_up_weight = left_product(h_two_low, d_up)
    d_h_two = right_product(d_up, w_up)
    norm_two_value, norm_two_pull = jax.vjp(norm_rows, second, gain_second, shift_second)
    d_second_norm, grad_second_gain, grad_second_shift = norm_two_pull(d_h_two)
    d_second = d_result + d_second_norm
    d_attn = d_second.astype(jnp.bfloat16)
    grad_output_bias = row_sum(d_attn)
    grad_output_weight = left_product(mixed_low, d_attn)
    d_mixed = right_product(d_attn, w_output).astype(jnp.bfloat16)
    d_heads = split_heads(d_mixed)
    delta = jnp.einsum("qhd,qhd->hq", d_heads.astype(jnp.float32), mixed_heads)
    key_back, value_back = (key_all, value_all)

    def score_grads(block_index):
        allowed = block_allowed(block_index)
        key_piece = block_rows(key_back, block_index)
        value_piece = block_rows(value_back, block_index)
        scores = head_scores(query_heads, key_piece, scale)
        probs = jnp.where(allowed, jnp.exp(scores - log_total[:, :, None]), 0.0)
        d_probs = jnp.einsum(
            "qhd,khd->hqk", d_heads, value_piece, preferred_element_type=jnp.float32
        )
        d_scores = (probs * (d_probs - delta[:, :, None])).astype(jnp.bfloat16)
        return (key_piece, probs, d_scores)

    zero_query = jnp.zeros((tok_rows, HEADS, HEAD_DIM), jnp.float32)

    def reduce_step(block_index, state_triple):
        d_query_sum, d_key_rows, d_value_rows = state_triple
        key_piece, probs, d_scores = score_grads(block_index)
        d_query_sum = d_query_sum + jnp.einsum(
            "hqk,khd->qhd", d_scores, key_piece, preferred_element_type=jnp.float32
        )
        d_key_piece = jnp.einsum(
            "hqk,qhd->khd", d_scores, query_heads, preferred_element_type=jnp.float32
        ).reshape(key_block, feature_width)
        d_value_piece = jnp.einsum(
            "hqk,qhd->khd", probs.astype(jnp.bfloat16), d_heads, preferred_element_type=jnp.float32
        ).reshape(key_block, feature_width)
        d_key_rows = lax.dynamic_update_slice_in_dim(
            d_key_rows, d_key_piece, block_index * key_block, 0
        )
        d_value_rows = lax.dynamic_update_slice_in_dim(
            d_value_rows, d_value_piece, block_index * key_block, 0
        )
        return (d_query_sum, d_key_rows, d_value_rows)

    zero_rows = jnp.zeros((key_block * block_count, feature_width), jnp.float32)
    d_query_sum, d_key_rows, d_value_rows = lax.fori_loop(
        0, block_count, reduce_step, (zero_query, zero_rows, zero_rows)
    )
    d_key_local, d_value_local = (
        lax.psum_scatter(d_key_rows, "ctx", scatter_dimension=0, tiled=True),
        lax.psum_scatter(d_value_rows, "ctx", scatter_dimension=0, tiled=True),
    )
    d_query = (d_query_sum.reshape(tok_rows, feature_width) * scale).astype(jnp.bfloat16)
    d_key = (d_key_local * scale).astype(jnp.bfloat16)
    d_value = d_value_local.astype(jnp.bfloat16)
    grad_query_bias = row_sum(d_query)
    grad_query_weight = left_product(h_one_low, d_query)
    grad_key_weight = left_product(h_one_low, d_key)
    grad_value_bias = row_sum(d_value)
    grad_value_weight = left_product(h_one_low, d_value)
    d_h_one = (
        right_product(d_query, w_query)
        + right_product(d_key, w_key)
        + right_product(d_value, w_value)
    )
    norm_one_value, norm_one_pull = jax.vjp(norm_rows, inputs, gain_first, shift_first)
    d_inputs_norm, grad_first_gain, grad_first_shift = norm_one_pull(d_h_one)
    grad_tokens = (d_second + d_inputs_norm).astype(jnp.bfloat16)[None]
    shares = (
        lax.psum_scatter(
            grad_first_gain.astype(jnp.bfloat16), "fsdp", scatter_dimension=0, tiled=True
        ).astype(jnp.float32),
        lax.psum_scatter(
            grad_first_shift.astype(jnp.bfloat16), "fsdp", scatter_dimension=0, tiled=True
        ).astype(jnp.float32),
        lax.psum_scatter(
            grad_query_weight.astype(jnp.bfloat16), "fsdp", scatter_dimension=0, tiled=True
        ).astype(jnp.float32),
        lax.psum_scatter(
            grad_query_bias.astype(jnp.bfloat16), "fsdp", scatter_dimension=0, tiled=True
        ).astype(jnp.float32),
        lax.psum_scatter(
            grad_key_weight.astype(jnp.bfloat16), "fsdp", scatter_dimension=0, tiled=True
        ).astype(jnp.float32),
        lax.psum_scatter(
            grad_value_weight.astype(jnp.bfloat16), "fsdp", scatter_dimension=0, tiled=True
        ).astype(jnp.float32),
        lax.psum_scatter(
            grad_value_bias.astype(jnp.bfloat16), "fsdp", scatter_dimension=0, tiled=True
        ).astype(jnp.float32),
        lax.psum_scatter(
            grad_output_weight.astype(jnp.bfloat16), "fsdp", scatter_dimension=0, tiled=True
        ).astype(jnp.float32),
        lax.psum_scatter(
            grad_output_bias.astype(jnp.bfloat16), "fsdp", scatter_dimension=0, tiled=True
        ).astype(jnp.float32),
        lax.psum_scatter(
            grad_second_gain.astype(jnp.bfloat16), "fsdp", scatter_dimension=0, tiled=True
        ).astype(jnp.float32),
        lax.psum_scatter(
            grad_second_shift.astype(jnp.bfloat16), "fsdp", scatter_dimension=0, tiled=True
        ).astype(jnp.float32),
        lax.psum_scatter(
            grad_up_weight.astype(jnp.bfloat16), "fsdp", scatter_dimension=0, tiled=True
        ).astype(jnp.float32),
        lax.psum_scatter(
            grad_up_bias.astype(jnp.bfloat16), "fsdp", scatter_dimension=0, tiled=True
        ).astype(jnp.float32),
        lax.psum_scatter(
            grad_down_weight.astype(jnp.bfloat16), "fsdp", scatter_dimension=0, tiled=True
        ).astype(jnp.float32),
        lax.psum_scatter(
            grad_down_bias.astype(jnp.bfloat16), "fsdp", scatter_dimension=0, tiled=True
        ).astype(jnp.float32),
    )
    totals = lax.psum(
        (
            shares[0],
            shares[1],
            shares[2],
            shares[3],
            shares[4],
            shares[5],
            shares[6],
            shares[7],
            shares[8],
            shares[9],
            shares[10],
            shares[11],
            shares[12],
            shares[13],
            shares[14],
        ),
        "ctx",
    )
    return (
        layer_output,
        loss_value,
        grad_tokens,
        totals[0],
        totals[1],
        totals[2],
        totals[3],
        totals[4],
        totals[5],
        totals[6],
        totals[7],
        totals[8],
        totals[9],
        totals[10],
        totals[11],
        totals[12],
        totals[13],
        totals[14],
    )


def swap_cores(value):
    size = lax.axis_size("ctx")
    return lax.ppermute(value, "ctx", [(i, i ^ 1) for i in range(size)])


def swap_chips(value, step):
    size = lax.axis_size("ctx")
    return lax.ppermute(value, "ctx", [(i, i ^ (2 * step)) for i in range(size)])


def swap_planes(value, step):
    size = lax.axis_size("fsdp")
    return lax.ppermute(value, "fsdp", [(i, i ^ step) for i in range(size)])


def to_natural(pieces, index):
    odd, high = (index & 1) == 1, (index & 2) == 2
    a, b, c, d = pieces
    a, b = jnp.where(odd, b, a), jnp.where(odd, a, b)
    c, d = jnp.where(odd, d, c), jnp.where(odd, c, d)
    return [
        jnp.where(high, c, a),
        jnp.where(high, d, b),
        jnp.where(high, a, c),
        jnp.where(high, b, d),
    ]


def kernel_call_scratch(body, outs, where, args, scratch):
    return kernel_call(body, outs, where, args, scratch=scratch)


def kernel_call(body, outs, where, args, blocks=None, scratch=(), vmem=32):
    blocks = blocks or {}

    def spec(i, array):
        if i in blocks:
            shape, index = blocks[i]
            return pl.BlockSpec(shape, index)
        return pl.BlockSpec(memory_space=pltpu.VMEM)

    grid = pltpu.PrefetchScalarGridSpec(
        num_scalar_prefetch=1,
        grid=(1,),
        in_specs=[spec(i, a) for i, a in enumerate(args)],
        out_specs=jax.tree.map(lambda o: pl.BlockSpec(memory_space=pltpu.VMEM), outs),
        scratch_shapes=scratch,
    )
    moved = sum(a.size * a.dtype.itemsize for a in jax.tree.leaves((list(args), list(jax.tree.leaves(outs)))))
    return pl.pallas_call(
        body,
        out_shape=outs,
        grid_spec=grid,
        compiler_params=pltpu.CompilerParams(vmem_limit_bytes=vmem << 20),
        cost_estimate=pl.CostEstimate(flops=0, transcendentals=0, bytes_accessed=moved),
    )(where, *args)


def shaped(*shape, dtype=jnp.bfloat16):
    return jax.ShapeDtypeStruct(shape, dtype)


def rows_at(start, count, align):
    return pl.ds(pl.multiple_of(start, align), count)


def pack_tokens(where, tokens, segment, valid, out):
    rows, width = tokens.shape
    out[:rows, :] = tokens[...]
    out[rows:, :] = jnp.zeros((16, width), out.dtype)
    ids = segment[...]
    line = lax.broadcasted_iota(jnp.int32, (16, rows), 0)
    high, low = ids >> 7, ids & 127
    codes = jnp.where(
        line == 0, high, jnp.where(line == 1, low, jnp.where(line == 2, valid[...], 0))
    )
    out[rows:, :rows] = codes.astype(jnp.float32).astype(out.dtype)


def pack_projections(where, *refs):
    query, key, value = refs[:3]
    vectors, wide, out = refs[3:11], refs[11], refs[12]
    half, feat = query.shape[0], out.shape[1]
    for chip in range(4):

        @pl.when(where[0] == chip)
        def _():
            for i, weight in enumerate((query, key, value)):
                out[half * i : half * (i + 1), :] = weight[:, feat * chip : feat * (chip + 1)]

    row = [v[...].astype(jnp.float32).reshape(1, feat) for v in vectors]
    long = wide[...].astype(jnp.float32).reshape(1, 4 * feat)
    row += [long[:, feat * i : feat * (i + 1)] for i in range(4)]
    row += [jnp.zeros((4, feat), jnp.float32)]
    out[3 * half :, :] = jnp.concatenate(row, axis=0).astype(out.dtype)


def pack_up(where, up, output, out):
    units = up.shape[1] // 8
    for i in range(4):
        at = rows_at(2 * units * i + units * where[1], units, 128)
        out[:, units * i : units * (i + 1)] = up[:, at]
    out[:, 4 * units :] = output[:, rows_at(units * where[1], units, 128)]


def pack_down(where, down, near0, near1, near2, near3, other, out):
    count = jnp.zeros((1, 1), jnp.float32)
    for piece in (near0, near1, near2, near3):
        count += jnp.sum(piece[2:3, :].astype(jnp.float32), axis=1, keepdims=True)
    for k in range(4):
        count += jnp.sum(other[k, 2:3, :].astype(jnp.float32), axis=1, keepdims=True)
    rows, width = down.shape
    out[:rows, :] = down[...]
    high = jnp.floor(count / 128.0)
    low = count - high * 128.0
    line = lax.broadcasted_iota(jnp.int32, (16, width), 0)
    out[rows:, :] = jnp.where(line == 0, high, jnp.where(line == 1, low, 0.0)).astype(out.dtype)


def build_projections(where, n0, n1, n2, n3, far, query, key, value, vectors, short, long, held):
    chip, core, plane = where[0], where[1], where[2]
    rows, feat = n0.shape
    half = (rows - 16) // 3
    outs = (query, key, value)
    for s, piece in enumerate((n0, n1, n2, n3)):
        base = 2 * half * (plane ^ s)
        for i, out in enumerate(outs):
            out[rows_at(base + half * core, half, 32), :] = piece[half * i : half * (i + 1), :]
            out[rows_at(base + half * (1 - core), half, 32), :] = far[
                rows * s + half * i : rows * s + half * (i + 1), :
            ]
        held[plane ^ s] = piece[3 * half :, :].astype(jnp.float32)
    vectors[...] = jnp.zeros(vectors.shape, jnp.float32)
    for p in range(4):
        small = held[p]
        for i, r in enumerate((0, 1, 4, 5, 6, 7)):
            vectors[i : i + 1, feat * p : feat * (p + 1)] = small[r : r + 1, :]
        pair = jnp.where(core == 0, small[8:10, :], small[10:12, :])
        long[:, 2 * feat * p : 2 * feat * p + feat] = pair[:1, :]
        long[:, 2 * feat * p + feat : 2 * feat * (p + 1)] = pair[1:, :]
    short[...] = held[chip]


def build_up(where, up, output, p0, p1, p2, p3, out, out_half):
    chip, core, plane = where[0], where[1], where[2]
    units = up.shape[1] // 8
    shard = up.shape[0]
    part = shard // 4
    own = rows_at(shard * plane, shard, 64)
    for i in range(4):
        at = rows_at(2 * units * i + units * core, units, 128)
        out[own, units * i : units * (i + 1)] = up[:, at]
    out_half[own, :] = output[:, rows_at(units * core, units, 128)]
    for k, piece in enumerate((p0, p1, p2, p3)):
        for s in (1, 2, 3):
            at = rows_at(shard * (plane ^ s) + part * (chip ^ k), part, 16)
            block = slice(part * (s - 1), part * s)
            out[at, :] = piece[block, : 4 * units]
            out_half[at, :] = piece[block, 4 * units :]


def build_down(where, down, p0, p1, p2, p3, out):
    chip, plane = where[0], where[2]
    mine = down.shape[0]
    part = mine // 4
    out[rows_at(mine * plane, mine, 128), :] = down[...]
    for k, piece in enumerate((p0, p1, p2, p3)):
        for s in (1, 2, 3):
            at = rows_at(mine * (plane ^ s) + part * (chip ^ k), part, 32)
            out[at, :] = piece[part * (s - 1) : part * s, :]


def build_output(where, near, far, out):
    units = near.shape[1]
    out[:, rows_at(units * where[1], units, 128)] = near[...]
    out[:, rows_at(units * (1 - where[1]), units, 128)] = far[...]


def pack_gradients(where, kept, *refs):
    vectors, outs = refs[:10], refs[10:]
    chip, plane = where[0], where[2]
    rows, feat = outs[0].shape
    whole = [v[...].reshape(1, v.shape[0]) for v in vectors]
    for p in range(4):
        lines = [w[:, feat * p : feat * (p + 1)] for w in whole[:6]]
        up = whole[6][:, 2 * feat * p : 2 * feat * (p + 1)]
        owner = jnp.where(chip == p, 1.0, 0.0)
        lines += [up[:, :feat], up[:, feat:], whole[7] * owner, whole[8] * owner, whole[9]]
        lines += [jnp.zeros((5, feat), jnp.float32)]
        small = jnp.concatenate(lines, axis=0).astype(outs[0].dtype)
        for s in range(4):

            @pl.when(plane ^ s == p)
            def _():
                outs[s][: rows - 16, :] = kept[p].astype(outs[s].dtype)
                outs[s][rows - 16 :, :] = small


def sum_planes(where, n0, n1, n2, n3, out, held):
    plane = where[2]
    rows = out.shape[0]
    pieces = (n0, n1, n2, n3)
    body = pieces[0][: rows - 16, :].astype(jnp.float32)
    for piece in pieces[1:]:
        body = body + piece[: rows - 16, :].astype(jnp.float32)
    out[: rows - 16, :] = body.astype(out.dtype)
    for s, piece in enumerate(pieces):
        held[plane ^ s] = piece[rows - 16 :, :].astype(jnp.float32)
    small = held[0] + held[1] + held[2] + held[3]
    total = jnp.sum(small[10:11, :3], axis=1, keepdims=True)
    high = total.astype(out.dtype).astype(jnp.float32)
    middle = (total - high).astype(out.dtype).astype(jnp.float32)
    low = total - high - middle
    line = lax.broadcasted_iota(jnp.int32, small.shape, 0)
    column = lax.broadcasted_iota(jnp.int32, small.shape, 1)
    parts = jnp.where(column == 0, high, jnp.where(column == 1, middle, low))
    small = jnp.where((line == 10) & (column < 3), parts, small)
    out[rows - 16 :, :] = small.astype(out.dtype)


def finish_down(where, n0, n1, n2, n3, far, out):
    chip, core = where[0], where[1]
    part = n0.shape[0]
    for k, piece in enumerate((n0, n1, n2, n3)):
        at = part * (chip ^ k)
        out[rows_at(4 * part * core + at, part, 32), :] = piece[...].astype(jnp.float32)
        out[rows_at(4 * part * (1 - core) + at, part, 32), :] = far[
            part * k : part * (k + 1), :
        ].astype(jnp.float32)


def finish_up(where, n0, n1, n2, n3, far, out, out_half):
    chip, core = where[0], where[1]
    part = n0.shape[0]
    units = n0.shape[1] // 5
    for k, near in enumerate((n0, n1, n2, n3)):
        rows = rows_at(part * (chip ^ k), part, 16)
        for piece, side in ((near[...], core), (far[part * k : part * (k + 1), :], 1 - core)):
            wide = piece.astype(jnp.float32)
            for i in range(4):
                at = rows_at(2 * units * i + units * side, units, 128)
                out[rows, at] = wide[:, units * i : units * (i + 1)]
            out_half[rows, rows_at(units * side, units, 128)] = wide[:, 4 * units :]


def finish_projections(where, n0, n1, n2, n3, far, *outs):
    query, key, value, loss = outs[:4]
    flat, wide, held = outs[4:12], outs[12], outs[13]
    chip, core = where[0], where[1]
    rows, feat = n0.shape
    half = (rows - 16) // 3
    near = (n0, n1, n2, n3)
    for k, piece in enumerate(near):
        held[2 * (chip ^ k) + core] = piece[3 * half :, :].astype(jnp.float32)
        held[2 * (chip ^ k) + 1 - core] = far[rows * k + 3 * half : rows * (k + 1), :].astype(
            jnp.float32
        )
    for j in range(4):

        @pl.when(chip == j)
        def _():
            for k, piece in enumerate(near):
                columns = slice(feat * (j ^ k), feat * ((j ^ k) + 1))
                for i, out in enumerate((query, key, value)):
                    out[rows_at(half * core, half, 32), columns] = piece[
                        half * i : half * (i + 1), :
                    ].astype(jnp.float32)
                    out[rows_at(half * (1 - core), half, 32), columns] = far[
                        rows * k + half * i : rows * k + half * (i + 1), :
                    ].astype(jnp.float32)

    total = held[0]
    for i in range(1, 8):
        total = total + held[i]
    for i, line in enumerate((0, 1, 2, 3, 4, 5, 8, 9)):
        flat[i][...] = total[line]
    even = held[0] + held[2] + held[4] + held[6]
    odd = held[1] + held[3] + held[5] + held[7]
    for side, part in enumerate((even, odd)):
        for i in range(2):
            wide[0:1, 2 * feat * side + feat * i : 2 * feat * side + feat * (i + 1)] = part[
                6 + i : 7 + i, :
            ]
    loss[...] = jnp.broadcast_to(jnp.sum(total[10:11, :3], axis=1, keepdims=True), loss.shape)


def norm_parts(values):
    centre = jnp.mean(values, axis=-1, keepdims=True)
    centred = values - centre
    spread = jnp.mean(centred * centred, axis=-1, keepdims=True)
    inverse = lax.rsqrt(spread + EPSILON)
    return centred * inverse, inverse


def norm_back(grad, gain, unit, inverse):
    scaled = grad * gain
    return inverse * (
        scaled
        - jnp.mean(scaled, axis=-1, keepdims=True)
        - unit * jnp.mean(scaled * unit, axis=-1, keepdims=True)
    )


F32 = jnp.float32
BF16 = jnp.bfloat16


def dot_f32(left, right, dims):
    return lax.dot_general(left, right, (dims, ((), ())), preferred_element_type=F32)


def layer(
    tokens,
    segment_ids,
    valid_rows,
    teacher,
    cotangent,
    first_gain,
    first_shift,
    query_weight,
    query_bias,
    key_weight,
    value_weight,
    value_bias,
    output_weight,
    output_bias,
    second_gain,
    second_shift,
    up_weight,
    up_bias,
    down_weight,
    down_bias,
):
    rows = tokens.shape[1]
    width = tokens.shape[2]
    shard = query_weight.shape[0]
    half = shard // 2
    quarter = shard // 4
    hidden = up_weight.shape[1]
    unit_rows = down_weight.shape[0]
    core_units = unit_rows // 2
    part_units = core_units // 4
    feat = width // 4
    own_heads = feat // HEAD_DIM
    group = 4 * rows
    every = 2 * group
    scale = HEAD_DIM ** (-0.5)

    place = lax.axis_index("ctx")
    plane = lax.axis_index("fsdp")
    chip, core = place // 2, place % 2

    where = jnp.stack([chip, core, plane]).astype(jnp.int32)

    own_low = tokens[0]
    valid = valid_rows[0]
    bundle = kernel_call(
        pack_tokens, shaped(rows + 16, width), where, (own_low, segment_ids, valid_rows)
    )
    mine = [bundle] + [swap_chips(bundle, k) for k in (1, 2, 3)]
    other = swap_cores(jnp.stack(mine))

    core_rows = ((half, width), lambda i, w: (w[1], 0))
    sent = kernel_call(
        pack_projections,
        shaped(3 * half + 16, feat),
        where,
        (
            query_weight,
            key_weight,
            value_weight,
            first_gain,
            first_shift,
            query_bias,
            value_bias,
            output_bias,
            second_gain,
            second_shift,
            down_bias,
            up_bias,
        ),
        {0: core_rows, 1: core_rows, 2: core_rows},
    )
    sent = [sent] + [swap_planes(sent, s) for s in (1, 2, 3)]
    far = swap_cores(jnp.concatenate(sent, axis=0))
    w_query, w_key, w_value, vectors, short, b_up = kernel_call_scratch(
        build_projections,
        (
            shaped(width, feat),
            shaped(width, feat),
            shaped(width, feat),
            shaped(8, width, dtype=F32),
            shaped(16, feat, dtype=F32),
            shaped(1, hidden // 2, dtype=F32),
        ),
        where,
        (*sent, far),
        [pltpu.VMEM((4, 16, feat), F32)],
    )
    gain_one, shift_one, b_output, gain_two, shift_two, b_down = (vectors[i] for i in range(6))
    query_shift, value_shift = short[2], short[3]

    up_piece = kernel_call(
        pack_up,
        shaped(quarter, 5 * core_units),
        where,
        (up_weight, output_weight),
        {
            0: ((quarter, hidden), lambda i, w: (w[0], 0)),
            1: ((quarter, width), lambda i, w: (w[0], 0)),
        },
    )
    code_rows = ((16, width), lambda i, w: (rows // 16, 0))
    down_piece = kernel_call(
        pack_down,
        shaped(part_units + 16, width),
        where,
        (down_weight, *mine, other),
        {
            0: ((part_units, width), lambda i, w: (4 * w[1] + w[0], 0)),
            1: code_rows,
            2: code_rows,
            3: code_rows,
            4: code_rows,
            5: ((4, 16, width), lambda i, w: (0, rows // 16, 0)),
        },
    )
    up_far = jnp.concatenate([swap_planes(up_piece, s) for s in (1, 2, 3)], axis=0)
    down_far = [swap_planes(down_piece, s) for s in (1, 2, 3)]
    tail = slice(part_units, part_units + 2)
    counts = sum(a[tail, 0].astype(F32) for a in [down_piece] + down_far)
    valid_count = counts[0] * 128.0 + counts[1]
    down_far = jnp.concatenate([a[:part_units] for a in down_far], axis=0)
    up_all = [up_far] + [swap_chips(up_far, k) for k in (1, 2, 3)]
    down_all = [down_far] + [swap_chips(down_far, k) for k in (1, 2, 3)]
    w_up, out_near = kernel_call(
        build_up,
        (shaped(width, hidden // 2), shaped(width, core_units)),
        where,
        (up_weight, output_weight, *up_all),
    )
    w_down = kernel_call(
        build_down,
        shaped(hidden // 2, width),
        where,
        (down_weight, *down_all),
        {0: ((core_units, width), lambda i, w: (w[1], 0))},
    )
    w_output = kernel_call(
        build_output, shaped(width, width), where, (out_near, swap_cores(out_near))
    )

    inputs = jnp.concatenate(
        [a[:rows] for a in mine] + [other[:, :rows].reshape(group, width)], 0
    ).astype(F32)
    codes = jnp.concatenate([jnp.stack([a[rows:] for a in mine]), other[:, rows:]], 0)
    codes = codes[:, :3, :rows].astype(F32)
    key_ids = (codes[:, 0] * 128.0 + codes[:, 1]).reshape(every)
    key_valid = codes[:, 2].reshape(every)
    unit_one, inverse_one = norm_parts(inputs)
    h_one = (unit_one * gain_one + shift_one).astype(BF16)
    query = (dot_f32(h_one[:group], w_query, ((1,), (0,))) + query_shift).astype(BF16)
    key = dot_f32(h_one, w_key, ((1,), (0,))).astype(BF16)
    value = (dot_f32(h_one, w_value, ((1,), (0,))) + value_shift).astype(BF16)
    same = key_ids[:group, None] == key_ids[None, :]
    diagonal = jnp.arange(group)[:, None] == jnp.arange(every)[None, :]
    allowed = (same & ((key_valid == 1.0)[None, :] | diagonal))[None]
    query_heads = query.reshape(group, own_heads, HEAD_DIM)
    key_heads = key.reshape(every, own_heads, HEAD_DIM)
    value_heads = value.reshape(every, own_heads, HEAD_DIM)
    scores = jnp.where(allowed, head_scores(query_heads, key_heads, scale), MASKED)
    top = jnp.max(scores, axis=2, keepdims=True)
    weights = jnp.exp(scores - top)
    probs = weights / jnp.sum(weights, axis=2, keepdims=True)
    probs_low = probs.astype(BF16)
    mixed = jnp.einsum("hqk,khd->qhd", probs_low, value_heads, preferred_element_type=F32)
    mixed = mixed.reshape(group, feat)
    mixed_rows = mixed.astype(BF16).reshape(4, rows, feat)
    mixed_pieces = [mixed_rows[0]] + [swap_chips(mixed_rows[k], k) for k in (1, 2, 3)]
    mixed_low = jnp.concatenate(to_natural(mixed_pieces, chip), axis=1)

    second = own_low.astype(F32) + dot_f32(mixed_low, w_output, ((1,), (0,))) + b_output
    unit_two, inverse_two = norm_parts(second)
    h_two = (unit_two * gain_two + shift_two).astype(BF16)
    h_pair = jnp.concatenate([h_two, swap_cores(h_two)], axis=0)
    up_value = dot_f32(h_pair, w_up, ((1,), (0,))) + b_up
    act_low = tanh_gelu(up_value).astype(BF16)
    down_part = dot_f32(act_low, w_down, ((1,), (0,)))
    result = second + down_part[:rows] + swap_cores(down_part[rows:].astype(BF16)) + b_down
    layer_output = result.astype(BF16)[None]
    valid_float = valid.astype(F32)[:, None]
    mismatch = result - teacher[0].astype(F32)
    error_sum = jnp.sum(valid_float * mismatch * mismatch)
    d_result = (
        cotangent[0].astype(F32) + 2.0 / (width * valid_count) * valid_float * mismatch
    )
    d_down = d_result.astype(BF16)
    down_pair = jnp.concatenate([d_down, swap_cores(d_down)], axis=0)
    grad_down = dot_f32(act_low, down_pair, ((0,), (0,))).astype(BF16)
    d_act = dot_f32(down_pair, w_down, ((1,), (1,)))
    gelu_value, gelu_pull = jax.vjp(tanh_gelu, up_value)
    d_up = gelu_pull(d_act)[0].astype(BF16)
    grad_up = dot_f32(h_pair, d_up, ((0,), (0,))).astype(BF16)
    d_two_part = dot_f32(d_up, w_up, ((1,), (1,)))
    d_two = d_two_part[:rows] + swap_cores(d_two_part[rows:].astype(BF16))
    d_second = d_result + norm_back(d_two, gain_two, unit_two, inverse_two)
    d_attn = d_second.astype(BF16)
    grad_output = dot_f32(mixed_low, d_attn, ((0,), (0,)))
    d_mixed = dot_f32(d_attn, w_output, ((1,), (1,))).astype(BF16)

    def reduce_pieces(pieces):
        kept = lax.dynamic_index_in_dim(pieces, chip, 1, keepdims=False).astype(F32)
        for k in (1, 2, 3):
            kept = kept + swap_chips(
                lax.dynamic_index_in_dim(pieces, chip ^ k, 1, keepdims=False), k
            ).astype(F32)
        low = kept.astype(BF16)
        total = lax.dynamic_index_in_dim(kept, plane, 0, keepdims=False)
        for s in (1, 2, 3):
            total = total + swap_planes(
                lax.dynamic_index_in_dim(low, plane ^ s, 0, keepdims=False), s
            ).astype(F32)
        return total.astype(BF16)

    def collect(piece):
        near = [piece] + [swap_chips(piece, k) for k in (1, 2, 3)]
        return (*near, swap_cores(jnp.concatenate(near, axis=0)))

    pieces_down = grad_down.reshape(4, 4, part_units, width)
    grad_down_weight = kernel_call(
        finish_down,
        shaped(unit_rows, width, dtype=F32),
        where,
        collect(reduce_pieces(pieces_down)),
    )
    kept_out = lax.dynamic_slice_in_dim(grad_output, core_units * core, core_units, 1)
    kept_out = kept_out + swap_cores(
        lax.dynamic_slice_in_dim(grad_output, core_units * (1 - core), core_units, 1).astype(BF16)
    )
    pieces_up = jnp.concatenate([grad_up, kept_out.astype(BF16)], axis=1)
    pieces_up = pieces_up.reshape(4, 4, quarter, 5 * core_units)
    grad_up_weight, grad_output_weight = kernel_call(
        finish_up,
        (shaped(shard, hidden, dtype=F32), shaped(shard, width, dtype=F32)),
        where,
        collect(reduce_pieces(pieces_up)),
    )

    def to_chip(k):
        return swap_chips(lax.dynamic_slice(d_mixed, (0, feat * (chip ^ k)), (rows, feat)), k)

    own_part = lax.dynamic_slice(d_mixed, (0, feat * chip), (rows, feat))
    d_mix = jnp.concatenate([own_part] + [to_chip(k) for k in (1, 2, 3)], axis=0)
    d_heads = d_mix.reshape(group, own_heads, HEAD_DIM)
    delta = jnp.sum(d_heads.astype(F32) * mixed.reshape(group, own_heads, HEAD_DIM), axis=2)
    d_probs = jnp.einsum("qhd,khd->hqk", d_heads, value_heads, preferred_element_type=F32)
    d_scores = (probs * (d_probs - delta.T[:, :, None])).astype(BF16)
    d_query = jnp.einsum("hqk,khd->qhd", d_scores, key_heads, preferred_element_type=F32)
    d_key = jnp.einsum("hqk,qhd->khd", d_scores, query_heads, preferred_element_type=F32)
    d_value = jnp.einsum("hqk,qhd->khd", probs_low, d_heads, preferred_element_type=F32)
    d_query = (d_query.reshape(group, feat) * scale).astype(BF16)
    d_key = (d_key.reshape(every, feat) * scale).astype(BF16)
    d_value = d_value.reshape(every, feat).astype(BF16)
    grad_three = [
        dot_f32(h_one[:group], d_query, ((0,), (0,))),
        dot_f32(h_one, d_key, ((0,), (0,))),
        dot_f32(h_one, d_value, ((0,), (0,))),
    ]
    d_one = dot_f32(d_key, w_key, ((1,), (1,))) + dot_f32(
        d_value, w_value, ((1,), (1,))
    )
    d_one = jnp.concatenate(
        [d_one[:group] + dot_f32(d_query, w_query, ((1,), (1,))), d_one[group:]], axis=0
    )

    def core_half(value, side):
        return lax.dynamic_index_in_dim(value.reshape(4, 2, half, feat), side, 1, keepdims=False)

    kept = jnp.concatenate([core_half(a, core) for a in grad_three], axis=1)
    kept = kept + swap_cores(
        jnp.concatenate([core_half(a, 1 - core).astype(BF16) for a in grad_three], axis=1)
    ).astype(F32)
    high = error_sum.astype(BF16).astype(F32)
    middle = (error_sum - high).astype(BF16).astype(F32)
    low = error_sum - high - middle
    line = jnp.arange(feat)
    loss_row = jnp.where(line == 0, high, jnp.where(line == 1, middle, jnp.where(line == 2, low, 0.0)))
    whole_vectors = (
        jnp.sum(d_one * unit_one, axis=0),
        jnp.sum(d_one, axis=0),
        jnp.sum(d_attn, axis=0, dtype=F32),
        jnp.sum(d_two * unit_two, axis=0),
        jnp.sum(d_two, axis=0),
        jnp.sum(d_down, axis=0, dtype=F32),
        jnp.sum(d_up, axis=0, dtype=F32),
        jnp.sum(d_query, axis=0, dtype=F32),
        jnp.sum(d_value, axis=0, dtype=F32),
        loss_row,
    )
    arriving = kernel_call(
        pack_gradients, (shaped(3 * half + 16, feat),) * 4, where, (kept, *whole_vectors)
    )
    arriving = [arriving[0]] + [swap_planes(arriving[s], s) for s in (1, 2, 3)]
    piece = kernel_call_scratch(
        sum_planes,
        shaped(3 * half + 16, feat),
        where,
        arriving,
        [pltpu.VMEM((4, 16, feat), F32)],
    )
    finished = kernel_call_scratch(
        finish_projections,
        (shaped(shard, width, dtype=F32),) * 3
        + (shaped(8, 128, dtype=F32),)
        + (shaped(shard, dtype=F32),) * 8
        + (shaped(1, unit_rows, dtype=F32),),
        where,
        collect(piece),
        [pltpu.VMEM((8, 16, feat), F32)],
    )
    grad_all, loss_sum = finished[:3], finished[3]
    sums, two, grad_up_bias = finished[4:10], finished[10:12], finished[12].reshape(unit_rows)
    loss_value = loss_sum[0, 0] / (width * valid_count)

    d_half = d_one[:group] + swap_cores(d_one[group:].astype(BF16))
    d_low = d_half.astype(BF16).reshape(4, rows, width)
    d_own = d_half[:rows]
    for k in (1, 2, 3):
        d_own = d_own + swap_chips(d_low[k], k)
    d_inputs = norm_back(d_own, gain_one, unit_one[:rows], inverse_one[:rows])
    grad_tokens = (d_second + d_inputs).astype(BF16)[None]
    return (
        layer_output,
        loss_value,
        grad_tokens,
        sums[0],
        sums[1],
        grad_all[0],
        two[0],
        grad_all[1],
        grad_all[2],
        two[1],
        grad_output_weight,
        sums[2],
        sums[3],
        sums[4],
        grad_up_weight,
        grad_up_bias,
        grad_down_weight,
        sums[5],
    )


def solution(mesh):
    body = layer if (mesh.shape["ctx"], mesh.shape["fsdp"]) == (8, 4) else shards
    placed = (
        P("fsdp", "ctx", None),
        P("fsdp", "ctx"),
        P("fsdp", "ctx"),
        P("fsdp", "ctx", None),
        P("fsdp", "ctx", None),
        P("fsdp"),
        P("fsdp"),
        P("fsdp", None),
        P("fsdp"),
        P("fsdp", None),
        P("fsdp", None),
        P("fsdp"),
        P("fsdp", None),
        P("fsdp"),
        P("fsdp"),
        P("fsdp"),
        P("fsdp", None),
        P("fsdp"),
        P("fsdp", None),
        P("fsdp"),
    )
    return jax.shard_map(
        body,
        mesh=mesh,
        in_specs=placed,
        out_specs=(
            P("fsdp", "ctx", None),
            P(),
            P("fsdp", "ctx", None),
            P("fsdp"),
            P("fsdp"),
            P("fsdp", None),
            P("fsdp"),
            P("fsdp", None),
            P("fsdp", None),
            P("fsdp"),
            P("fsdp", None),
            P("fsdp"),
            P("fsdp"),
            P("fsdp"),
            P("fsdp", None),
            P("fsdp"),
            P("fsdp", None),
            P("fsdp"),
        ),
        check_vma=False,
    )
```

```python
import jax
import jax.numpy as jnp
from jax import lax
from jax.experimental import pallas as pl
from jax.experimental.pallas import tpu as pltpu
from jax.sharding import PartitionSpec as P

HEADS = 12
HEAD_DIM = 64


EPSILON = 1e-06
MASKED = -1e30


def norm_rows(values, gain, shift):
    centre = jnp.mean(values, axis=-1, keepdims=True)
    centred = values - centre
    spread = jnp.mean(centred * centred, axis=-1, keepdims=True)
    return centred * lax.rsqrt(spread + EPSILON) * gain + shift


def tanh_gelu(values):
    return jax.nn.gelu(values, approximate=True)


def key_allowed(query_segment, query_place, key_codes, key_place):
    same_doc = query_segment[:, None] == (key_codes // 2)[None, :]
    usable = (key_codes % 2 == 1)[None, :] | (query_place[:, None] == key_place[None, :])
    return (same_doc & usable)[None, :, :]


def split_heads(values):
    return values.reshape(values.shape[0], HEADS, HEAD_DIM)


def head_scores(query_heads, key_heads, scale):
    return (
        jnp.einsum("qhd,khd->hqk", query_heads, key_heads, preferred_element_type=jnp.float32)
        * scale
    )


def row_sum(values):
    return jnp.sum(values, axis=0, dtype=jnp.float32)


def left_product(left, right):
    return jnp.einsum("rd,rf->df", left, right, preferred_element_type=jnp.float32)


def right_product(left, right):
    return jnp.einsum("rf,df->rd", left, right, preferred_element_type=jnp.float32)


def shards(
    tokens,
    segment_ids,
    valid_rows,
    teacher,
    cotangent,
    first_gain,
    first_shift,
    query_weight,
    query_bias,
    key_weight,
    value_weight,
    value_bias,
    output_weight,
    output_bias,
    second_gain,
    second_shift,
    up_weight,
    up_bias,
    down_weight,
    down_bias,
):
    tok_rows = tokens.shape[1]
    feature_width = tokens.shape[2]
    shard_count = lax.axis_size("ctx")
    key_block = 4 * tok_rows
    block_count = shard_count // 4
    scale = HEAD_DIM ** (-0.5)
    gain_one, shift_one, w_query, b_query, w_key, w_value, b_value, w_output, b_output = (
        lax.all_gather(first_gain, "fsdp", axis=0, tiled=True),
        lax.all_gather(first_shift, "fsdp", axis=0, tiled=True),
        lax.all_gather(query_weight, "fsdp", axis=0, tiled=True),
        lax.all_gather(query_bias, "fsdp", axis=0, tiled=True),
        lax.all_gather(key_weight, "fsdp", axis=0, tiled=True),
        lax.all_gather(value_weight, "fsdp", axis=0, tiled=True),
        lax.all_gather(value_bias, "fsdp", axis=0, tiled=True),
        lax.all_gather(output_weight, "fsdp", axis=0, tiled=True),
        lax.all_gather(output_bias, "fsdp", axis=0, tiled=True),
    )
    gain_two, shift_two, w_up, b_up, w_down, b_down = (
        lax.all_gather(second_gain, "fsdp", axis=0, tiled=True),
        lax.all_gather(second_shift, "fsdp", axis=0, tiled=True),
        lax.all_gather(up_weight, "fsdp", axis=0, tiled=True),
        lax.all_gather(up_bias, "fsdp", axis=0, tiled=True),
        lax.all_gather(down_weight, "fsdp", axis=0, tiled=True),
        lax.all_gather(down_bias, "fsdp", axis=0, tiled=True),
    )
    local_segment = segment_ids[0]
    local_valid = valid_rows[0]
    local_codes = local_segment * 2 + local_valid
    all_codes = lax.all_gather(local_codes, "ctx", axis=0, tiled=True)
    query_place = lax.axis_index("ctx") * tok_rows + jnp.arange(tok_rows, dtype=jnp.int32)
    inputs = tokens[0].astype(jnp.float32)
    gain_first = gain_one.astype(jnp.float32)
    shift_first = shift_one.astype(jnp.float32)
    gain_second = gain_two.astype(jnp.float32)
    shift_second = shift_two.astype(jnp.float32)
    h_one = norm_rows(inputs, gain_first, shift_first)
    h_one_low = h_one.astype(jnp.bfloat16)
    query_low = (
        jnp.dot(h_one_low, w_query, preferred_element_type=jnp.float32)
        + b_query.astype(jnp.float32)
    ).astype(jnp.bfloat16)
    key_low = jnp.dot(h_one_low, w_key, preferred_element_type=jnp.float32).astype(jnp.bfloat16)
    value_low = (
        jnp.dot(h_one_low, w_value, preferred_element_type=jnp.float32)
        + b_value.astype(jnp.float32)
    ).astype(jnp.bfloat16)
    key_all, value_all = (
        lax.all_gather(key_low, "ctx", axis=0, tiled=True),
        lax.all_gather(value_low, "ctx", axis=0, tiled=True),
    )
    query_heads = split_heads(query_low)

    def block_rows(source, block_index):
        return split_heads(lax.dynamic_slice_in_dim(source, block_index * key_block, key_block, 0))

    def block_allowed(block_index):
        start = block_index * key_block
        codes = lax.dynamic_slice_in_dim(all_codes, start, key_block, 0)
        return key_allowed(
            local_segment, query_place, codes, start + jnp.arange(key_block, dtype=jnp.int32)
        )

    def stats_step(block_index, state_pair):
        running_max, running_sum = state_pair
        allowed = block_allowed(block_index)
        scores = jnp.where(
            allowed, head_scores(query_heads, block_rows(key_all, block_index), scale), MASKED
        )
        new_max = jnp.maximum(running_max, jnp.max(scores, axis=2))
        weights = jnp.where(allowed, jnp.exp(scores - new_max[:, :, None]), 0.0)
        return (new_max, running_sum * jnp.exp(running_max - new_max) + jnp.sum(weights, axis=2))

    start_max = jnp.full((HEADS, tok_rows), MASKED, jnp.float32)
    start_sum = jnp.zeros((HEADS, tok_rows), jnp.float32)
    running_max, running_sum = lax.fori_loop(0, block_count, stats_step, (start_max, start_sum))
    log_total = running_max + jnp.log(running_sum)

    def mix_step(block_index, mixed_sum):
        allowed = block_allowed(block_index)
        scores = head_scores(query_heads, block_rows(key_all, block_index), scale)
        probs = jnp.where(allowed, jnp.exp(scores - log_total[:, :, None]), 0.0).astype(
            jnp.bfloat16
        )
        return mixed_sum + jnp.einsum(
            "hqk,khd->qhd",
            probs,
            block_rows(value_all, block_index),
            preferred_element_type=jnp.float32,
        )

    mixed_heads = lax.fori_loop(
        0, block_count, mix_step, jnp.zeros((tok_rows, HEADS, HEAD_DIM), jnp.float32)
    )
    mixed = mixed_heads.reshape(tok_rows, feature_width)
    mixed_low = mixed.astype(jnp.bfloat16)
    second = (
        inputs
        + jnp.dot(mixed_low, w_output, preferred_element_type=jnp.float32)
        + b_output.astype(jnp.float32)
    )
    h_two = norm_rows(second, gain_second, shift_second)
    h_two_low = h_two.astype(jnp.bfloat16)
    up_value = jnp.dot(h_two_low, w_up, preferred_element_type=jnp.float32) + b_up.astype(
        jnp.float32
    )
    act_low = tanh_gelu(up_value).astype(jnp.bfloat16)
    result = (
        second
        + jnp.dot(act_low, w_down, preferred_element_type=jnp.float32)
        + b_down.astype(jnp.float32)
    )
    layer_output = result.astype(jnp.bfloat16)[None]
    valid_float = local_valid.astype(jnp.float32)
    mismatch = result - teacher[0].astype(jnp.float32)
    error_sum, valid_count = lax.psum(
        (jnp.sum(valid_float[:, None] * mismatch * mismatch), jnp.sum(valid_float)), ("ctx", "fsdp")
    )
    loss_value = error_sum / (feature_width * valid_count)
    d_result = (
        cotangent[0].astype(jnp.float32)
        + 2.0 / (feature_width * valid_count) * valid_float[:, None] * mismatch
    )
    d_down = d_result.astype(jnp.bfloat16)
    grad_down_bias = row_sum(d_down)
    grad_down_weight = left_product(act_low, d_down)
    d_act = right_product(d_down, w_down)
    gelu_value, gelu_pull = jax.vjp(tanh_gelu, up_value)
    d_up = gelu_pull(d_act)[0].astype(jnp.bfloat16)
    grad_up_bias = row_sum(d_up)
    grad_up_weight = left_product(h_two_low, d_up)
    d_h_two = right_product(d_up, w_up)
    norm_two_value, norm_two_pull = jax.vjp(norm_rows, second, gain_second, shift_second)
    d_second_norm, grad_second_gain, grad_second_shift = norm_two_pull(d_h_two)
    d_second = d_result + d_second_norm
    d_attn = d_second.astype(jnp.bfloat16)
    grad_output_bias = row_sum(d_attn)
    grad_output_weight = left_product(mixed_low, d_attn)
    d_mixed = right_product(d_attn, w_output).astype(jnp.bfloat16)
    d_heads = split_heads(d_mixed)
    delta = jnp.einsum("qhd,qhd->hq", d_heads.astype(jnp.float32), mixed_heads)
    key_back, value_back = (key_all, value_all)

    def score_grads(block_index):
        allowed = block_allowed(block_index)
        key_piece = block_rows(key_back, block_index)
        value_piece = block_rows(value_back, block_index)
        scores = head_scores(query_heads, key_piece, scale)
        probs = jnp.where(allowed, jnp.exp(scores - log_total[:, :, None]), 0.0)
        d_probs = jnp.einsum(
            "qhd,khd->hqk", d_heads, value_piece, preferred_element_type=jnp.float32
        )
        d_scores = (probs * (d_probs - delta[:, :, None])).astype(jnp.bfloat16)
        return (key_piece, probs, d_scores)

    zero_query = jnp.zeros((tok_rows, HEADS, HEAD_DIM), jnp.float32)

    def reduce_step(block_index, state_triple):
        d_query_sum, d_key_rows, d_value_rows = state_triple
        key_piece, probs, d_scores = score_grads(block_index)
        d_query_sum = d_query_sum + jnp.einsum(
            "hqk,khd->qhd", d_scores, key_piece, preferred_element_type=jnp.float32
        )
        d_key_piece = jnp.einsum(
            "hqk,qhd->khd", d_scores, query_heads, preferred_element_type=jnp.float32
        ).reshape(key_block, feature_width)
        d_value_piece = jnp.einsum(
            "hqk,qhd->khd", probs.astype(jnp.bfloat16), d_heads, preferred_element_type=jnp.float32
        ).reshape(key_block, feature_width)
        d_key_rows = lax.dynamic_update_slice_in_dim(
            d_key_rows, d_key_piece, block_index * key_block, 0
        )
        d_value_rows = lax.dynamic_update_slice_in_dim(
            d_value_rows, d_value_piece, block_index * key_block, 0
        )
        return (d_query_sum, d_key_rows, d_value_rows)

    zero_rows = jnp.zeros((key_block * block_count, feature_width), jnp.float32)
    d_query_sum, d_key_rows, d_value_rows = lax.fori_loop(
        0, block_count, reduce_step, (zero_query, zero_rows, zero_rows)
    )
    d_key_local, d_value_local = (
        lax.psum_scatter(d_key_rows, "ctx", scatter_dimension=0, tiled=True),
        lax.psum_scatter(d_value_rows, "ctx", scatter_dimension=0, tiled=True),
    )
    d_query = (d_query_sum.reshape(tok_rows, feature_width) * scale).astype(jnp.bfloat16)
    d_key = (d_key_local * scale).astype(jnp.bfloat16)
    d_value = d_value_local.astype(jnp.bfloat16)
    grad_query_bias = row_sum(d_query)
    grad_query_weight = left_product(h_one_low, d_query)
    grad_key_weight = left_product(h_one_low, d_key)
    grad_value_bias = row_sum(d_value)
    grad_value_weight = left_product(h_one_low, d_value)
    d_h_one = (
        right_product(d_query, w_query)
        + right_product(d_key, w_key)
        + right_product(d_value, w_value)
    )
    norm_one_value, norm_one_pull = jax.vjp(norm_rows, inputs, gain_first, shift_first)
    d_inputs_norm, grad_first_gain, grad_first_shift = norm_one_pull(d_h_one)
    grad_tokens = (d_second + d_inputs_norm).astype(jnp.bfloat16)[None]
    shares = (
        lax.psum_scatter(
            grad_first_gain.astype(jnp.bfloat16), "fsdp", scatter_dimension=0, tiled=True
        ).astype(jnp.float32),
        lax.psum_scatter(
            grad_first_shift.astype(jnp.bfloat16), "fsdp", scatter_dimension=0, tiled=True
        ).astype(jnp.float32),
        lax.psum_scatter(
            grad_query_weight.astype(jnp.bfloat16), "fsdp", scatter_dimension=0, tiled=True
        ).astype(jnp.float32),
        lax.psum_scatter(
            grad_query_bias.astype(jnp.bfloat16), "fsdp", scatter_dimension=0, tiled=True
        ).astype(jnp.float32),
        lax.psum_scatter(
            grad_key_weight.astype(jnp.bfloat16), "fsdp", scatter_dimension=0, tiled=True
        ).astype(jnp.float32),
        lax.psum_scatter(
            grad_value_weight.astype(jnp.bfloat16), "fsdp", scatter_dimension=0, tiled=True
        ).astype(jnp.float32),
        lax.psum_scatter(
            grad_value_bias.astype(jnp.bfloat16), "fsdp", scatter_dimension=0, tiled=True
        ).astype(jnp.float32),
        lax.psum_scatter(
            grad_output_weight.astype(jnp.bfloat16), "fsdp", scatter_dimension=0, tiled=True
        ).astype(jnp.float32),
        lax.psum_scatter(
            grad_output_bias.astype(jnp.bfloat16), "fsdp", scatter_dimension=0, tiled=True
        ).astype(jnp.float32),
        lax.psum_scatter(
            grad_second_gain.astype(jnp.bfloat16), "fsdp", scatter_dimension=0, tiled=True
        ).astype(jnp.float32),
        lax.psum_scatter(
            grad_second_shift.astype(jnp.bfloat16), "fsdp", scatter_dimension=0, tiled=True
        ).astype(jnp.float32),
        lax.psum_scatter(
            grad_up_weight.astype(jnp.bfloat16), "fsdp", scatter_dimension=0, tiled=True
        ).astype(jnp.float32),
        lax.psum_scatter(
            grad_up_bias.astype(jnp.bfloat16), "fsdp", scatter_dimension=0, tiled=True
        ).astype(jnp.float32),
        lax.psum_scatter(
            grad_down_weight.astype(jnp.bfloat16), "fsdp", scatter_dimension=0, tiled=True
        ).astype(jnp.float32),
        lax.psum_scatter(
            grad_down_bias.astype(jnp.bfloat16), "fsdp", scatter_dimension=0, tiled=True
        ).astype(jnp.float32),
    )
    totals = lax.psum(
        (
            shares[0],
            shares[1],
            shares[2],
            shares[3],
            shares[4],
            shares[5],
            shares[6],
            shares[7],
            shares[8],
            shares[9],
            shares[10],
            shares[11],
            shares[12],
            shares[13],
            shares[14],
        ),
        "ctx",
    )
    return (
        layer_output,
        loss_value,
        grad_tokens,
        totals[0],
        totals[1],
        totals[2],
        totals[3],
        totals[4],
        totals[5],
        totals[6],
        totals[7],
        totals[8],
        totals[9],
        totals[10],
        totals[11],
        totals[12],
        totals[13],
        totals[14],
    )


F32 = jnp.float32
BF16 = jnp.bfloat16
ANY = pl.BlockSpec(memory_space=pl.ANY)
VMEM = pl.BlockSpec(memory_space=pltpu.VMEM)
SMEM = pl.BlockSpec(memory_space=pltpu.SMEM)
NT = (((1,), (1,)), ((), ()))
TN = (((0,), (0,)), ((), ()))
NN = (((1,), (0,)), ((), ()))


def swap_cores(value):
    size = lax.axis_size("ctx")
    return lax.ppermute(value, "ctx", [(i, i ^ 1) for i in range(size)])


def both_cores(value):
    pairs = [[i, i + 1] for i in range(0, lax.axis_size("ctx"), 2)]
    return lax.all_gather(value, "ctx", axis=0, tiled=True, axis_index_groups=pairs)


def swap_chips(value, step):
    size = lax.axis_size("ctx")
    return lax.ppermute(value, "ctx", [(i, i ^ (2 * step)) for i in range(size)])


def swap_planes(value, step):
    size = lax.axis_size("fsdp")
    return lax.ppermute(value, "fsdp", [(i, i ^ step) for i in range(size)])


def trade_chips(value):
    size = lax.axis_size("ctx")
    groups = [[i for i in range(size) if i % 2 == c] for c in (0, 1)]
    return lax.all_to_all(value, "ctx", 0, 0, axis_index_groups=groups, tiled=True)


def trade_planes(value):
    return lax.all_to_all(value, "fsdp", 0, 0, tiled=True)


def shaped(*shape, dtype=BF16):
    return jax.ShapeDtypeStruct(shape, dtype)


def wide(*shape):
    return jax.ShapeDtypeStruct(shape, F32)


def local_call(body, outs, where, args, far=(), scratch=(), after=(), scalar=None, vmem=12, cost=0):
    args, after, many = list(args), list(after), isinstance(outs, tuple)
    count = len(args)

    def kernel(where_ref, *refs):
        body(where_ref, *refs[:count], *refs[count + len(after) :])

    return pl.pallas_call(
        kernel,
        out_shape=outs,
        in_specs=[pl.BlockSpec(memory_space=pltpu.SMEM)]
        + [ANY if i in far else VMEM for i in range(count)]
        + [ANY] * len(after),
        out_specs=tuple(SMEM if i == scalar else VMEM for i in range(len(outs))) if many else VMEM,
        scratch_shapes=scratch,
        compiler_params=pltpu.CompilerParams(vmem_limit_bytes=vmem << 20),
        cost_estimate=pl.CostEstimate(
            flops=cost * 10**9, transcendentals=0, bytes_accessed=cost * 10**6
        ),
    )(where, *args, *after)


def core_rows(core, count):
    return pl.ds(pl.multiple_of(count * core, 16), count)


def rows_at(start, count, align):
    return pl.ds(pl.multiple_of(start, align), count)


def dot(left, right, dims):
    return lax.dot_general(left, right, dims, preferred_element_type=F32)


def run_copies(copies, sems):
    started = [
        pltpu.make_async_copy(source, target, sems.at[i])
        for i, (source, target) in enumerate(copies)
    ]
    for copy in started:
        copy.start()
    for copy in started:
        copy.wait()


def unit_rows(values):
    centred = values - jnp.mean(values, axis=-1, keepdims=True)
    spread = jnp.mean(centred * centred, axis=-1, keepdims=True)
    inverse = lax.rsqrt(spread + EPSILON)
    return centred * inverse, inverse


def unit_back(grad, gain, unit, inverse):
    scaled = grad * gain
    return inverse * (
        scaled
        - jnp.mean(scaled, axis=-1, keepdims=True)
        - unit * jnp.mean(scaled * unit, axis=-1, keepdims=True)
    )


def pack_tokens(where, tokens, segment, valid, out):
    rows, width = tokens.shape
    ids = segment[...]
    line = lax.broadcasted_iota(jnp.int32, (16, rows), 0)
    codes = jnp.where(
        line == 0,
        ids >> 7,
        jnp.where(line == 1, ids & 127, jnp.where(line == 2, valid[...], 0)),
    )
    codes = codes.astype(F32).astype(out.dtype)
    for i in range(4):
        start = (rows + 16) * i
        out[start : start + rows, :] = tokens[...]
        out[start + rows : start + rows + 16, :] = jnp.zeros((16, width), out.dtype)
        out[start + rows : start + rows + 16, :rows] = codes


def pack_projections(where, *refs):
    weights, vectors, long, valid, out = refs[:3], refs[3:11], refs[11], refs[12], refs[13]
    held, small, held_long, sems = refs[14], refs[15:23], refs[23], refs[24]
    half, feat = held.shape[1], small[0].shape[0]
    own_rows = rows_at(half * where[1], half, 32)
    run_copies(
        [(w.at[own_rows], held.at[i]) for i, w in enumerate(weights)]
        + list(zip(vectors, small))
        + [(long, held_long)],
        sems,
    )
    for chip in range(4):

        @pl.when(where[0] == chip)
        def _():
            for i in range(3):
                out[:, feat * i : feat * (i + 1)] = held[i, :, feat * chip : feat * (chip + 1)]

    spread = held_long[...].astype(F32).reshape(1, 4 * feat)
    count = jnp.sum(valid[...].astype(F32), axis=1, keepdims=True)
    lines = [v[...].astype(F32).reshape(1, feat) for v in small]
    lines += [spread[:, feat * i : feat * (i + 1)] for i in range(4)]
    lines += [jnp.broadcast_to(count, (1, feat)), jnp.zeros((half - 13, feat), F32)]
    out[:, 3 * feat :] = jnp.concatenate(lines, axis=0).astype(out.dtype)


def pack_blocks(where, up, output, down, out_up, out_down, sems):
    chip, core = where[0], where[1]
    part, units = out_up.shape[0], out_up.shape[1] // 5
    rows = rows_at(part * chip, part, 16)
    down_part = out_down.shape[0]
    copies = [
        (
            up.at[rows, rows_at(2 * units * i + units * core, units, 128)],
            out_up.at[:, units * i : units * (i + 1)],
        )
        for i in range(4)
    ]
    copies += [
        (output.at[rows, rows_at(units * core, units, 128)], out_up.at[:, 4 * units :]),
        (down.at[rows_at(4 * down_part * core + down_part * chip, down_part, 32)], out_down),
    ]
    run_copies(copies, sems)


def stack_rows(where, *refs):
    pieces, out = refs[:-1], refs[-1]
    rows = pieces[0].shape[0]
    for i, piece in enumerate(pieces):
        out[rows * i : rows * (i + 1), :] = piece[...]


def three_blocks(pieces, part):
    p0, p1, p2, low, high = pieces
    parts = [(k, [(p, 0)]) for k, p in enumerate((p0, p1, p2))] + [(3, [(low, 0), (high, low.shape[0])])]
    found = []
    for k, refs in parts:
        for s in (1, 2, 3):
            for ref, base in refs:
                start, end = max(part * (s - 1), base), min(part * s, base + ref.shape[0])
                if start < end:
                    found.append((k, s, start - part * (s - 1), end - start, ref, start - base))
    return found


def cross_halves(where, from_x, from_y, to_x, to_y):
    cut = to_x.shape[0]
    to_x[...] = from_y[:cut, :]
    to_y[...] = from_x[cut:, :]


def build_up(where, up, p0, p1, p2, p3, p4, out, sems):
    chip, core, plane = where[0], where[1], where[2]
    units, shard = up.shape[1] // 8, up.shape[0]
    part = shard // 4
    own = rows_at(shard * plane, shard, 64)
    copies = [
        pltpu.make_async_copy(
            up.at[:, rows_at(2 * units * i + units * core, units, 128)],
            out.at[own, units * i : units * (i + 1)],
            sems.at[i],
        )
        for i in range(4)
    ]
    for copy in copies:
        copy.start()
    for k, s, offset, count, piece, start in three_blocks((p0, p1, p2, p3, p4), part):
        at = rows_at(shard * (plane ^ s) + part * (chip ^ k) + offset, count, 16)
        out[at, :] = piece[start : start + count, : 4 * units]
    for copy in copies:
        copy.wait()


def build_half(where, output, p0, p1, p2, p3, p4, out):
    chip, core, plane = where[0], where[1], where[2]
    shard, units = output.shape[0], out.shape[1]
    part = shard // 4
    out[rows_at(shard * plane, shard, 64), :] = output[:, rows_at(units * core, units, 128)]
    for k, s, offset, count, piece, start in three_blocks((p0, p1, p2, p3, p4), part):
        at = rows_at(shard * (plane ^ s) + part * (chip ^ k) + offset, count, 16)
        out[at, :] = piece[start : start + count, 4 * units :]


def build_down(where, down, p0, p1, p2, p3, p4, out, sem):
    chip, core, plane = where[0], where[1], where[2]
    mine = down.shape[0] // 2
    part = mine // 4
    own = pltpu.make_async_copy(
        down.at[rows_at(mine * core, mine, 128)], out.at[rows_at(mine * plane, mine, 128)], sem
    )
    own.start()
    for k, s, offset, count, piece, start in three_blocks((p0, p1, p2, p3, p4), part):
        at = rows_at(mine * (plane ^ s) + part * (chip ^ k) + offset, count, 16)
        out[at, :] = piece[start : start + count, :]
    own.wait()


def build_output(where, near, far, out):
    units = near.shape[1]
    out[:, rows_at(units * where[1], units, 128)] = near[...]
    out[:, rows_at(units * (1 - where[1]), units, 128)] = far[...]


def normalize_tokens(where, near, far, unit_low, key_row, query_column):
    rows = query_column.shape[0] // 4
    for i in range(8):
        block = (near if i < 4 else far).at[(rows + 16) * (i % 4) : (rows + 16) * (i % 4 + 1), :]
        unit, _ = unit_rows(block[:rows, :].astype(F32))
        unit_low[rows * i : rows * (i + 1), :] = unit
        codes = block[rows:, :].astype(F32)
        ids = codes[0:1, :rows] * 128.0 + codes[1:2, :rows]
        key_row[0:1, rows * i : rows * (i + 1)] = jnp.where(codes[2:3, :rows] == 1.0, ids, -1.0)
        if i < 4:
            query_column[rows * i : rows * (i + 1), :] = jnp.broadcast_to(
                ids.reshape(rows, 1), (rows, 128)
            )


def attend(where, *refs):
    units, key_row, query_column, weights, far_weights = refs[:3] + (refs[3:7], refs[7])
    h_one, w_three, projected, probs, mixed, sent, vectors, long = refs[8:16]
    small, bias = refs[16:]
    core, plane = where[1], where[2]
    half, width = weights[0].shape
    feat = width // 4
    group = query_column.shape[0]
    rows = group // 4

    count = jnp.zeros((1, 1), F32)
    for s, piece in enumerate(weights):
        base = 2 * half * (plane ^ s)
        w_three[rows_at(base + half * core, half, 32), :] = piece[:, : 3 * feat]
        other = far_weights[half * s : half * (s + 1), :]
        w_three[rows_at(base + half * (1 - core), half, 32), :] = other[:, : 3 * feat]
        near = piece[:16, 3 * feat :].astype(F32)
        small[plane ^ s] = near
        count += near[12:13, :1] + other[12:13, 3 * feat : 3 * feat + 1].astype(F32)
    vectors[...] = jnp.zeros(vectors.shape, F32)
    for p in range(4):
        lines = small[p]
        for i, r in enumerate((0, 1, 4, 5, 6, 7)):
            vectors[i : i + 1, feat * p : feat * (p + 1)] = lines[r : r + 1, :]
        pair = jnp.where(core == 0, lines[8:10, :], lines[10:12, :])
        long[:, 2 * feat * p : 2 * feat * p + feat] = pair[:1, :]
        long[:, 2 * feat * p + feat : 2 * feat * (p + 1)] = pair[1:, :]
    gain, shift = vectors[0:1, :], vectors[1:2, :]
    short = small[where[0]]
    h_one[...] = (units[...] * gain + shift).astype(BF16)
    values = dot(h_one[...], w_three[...], NN)
    query = (values[:group, :feat] + short[2:3, :]).astype(BF16) * jnp.asarray(
        HEAD_DIM**-0.5, BF16
    )
    projected[:group, :feat] = query
    projected[group:, :feat] = jnp.zeros((group, feat), BF16)
    projected[:, feat : 2 * feat] = values[:, feat : 2 * feat].astype(BF16)
    projected[:, 2 * feat :] = (values[:, 2 * feat :] + short[3:4, :]).astype(BF16)
    column = lax.broadcasted_iota(jnp.int32, (rows, 2 * group), 1)
    line = lax.broadcasted_iota(jnp.int32, (rows, 2 * group), 0)
    for k in range(4):
        ids = query_column[rows * k : rows * (k + 1), :1]
        allowed = (ids == key_row[0:1, :]) | (column == line + rows * k)
        bias[rows * k : rows * (k + 1), :] = jnp.where(allowed, 0.0, MASKED)
    for h in range(feat // HEAD_DIM):
        at = slice(HEAD_DIM * h, HEAD_DIM * (h + 1))
        keys = projected[:, feat + HEAD_DIM * h : feat + HEAD_DIM * (h + 1)]
        held = projected[:, 2 * feat + HEAD_DIM * h : 2 * feat + HEAD_DIM * (h + 1)]
        for k in range(4):
            block = slice(rows * k, rows * (k + 1))
            scores = dot(projected[block, at], keys, NT) + bias[block, :]
            weight = jnp.exp(scores - jnp.max(scores, axis=1, keepdims=True))
            weight = weight * (1.0 / jnp.sum(weight, axis=1, keepdims=True))
            low = weight.astype(BF16)
            probs[h, block, :] = low
            result = dot(low, held, NN)
            mixed[block, at] = result
            sent[(rows + 16) * k : (rows + 16) * k + rows, at] = result.astype(BF16)
    high = jnp.floor(count / 128.0)
    side = lax.broadcasted_iota(jnp.int32, (16, feat), 1)
    digits = jnp.where(side == 0, high, jnp.where(side == 1, count - 128.0 * high, 0.0))
    for k in range(4):
        sent[(rows + 16) * k + rows : (rows + 16) * (k + 1), :] = digits.astype(BF16)


def attend_back(where, d_all, probs, projected, mixed, h_one, w_three, vectors, *outs):
    d_three, kept, given, lines, d_scores, grads = outs
    core = where[1]
    group, feat = d_all.shape
    rows, width = group // 4, h_one.shape[1]
    scale = HEAD_DIM**-0.5
    d_three[group:, :feat] = jnp.zeros((group, feat), BF16)
    for h in range(feat // HEAD_DIM):
        at = slice(HEAD_DIM * h, HEAD_DIM * (h + 1))
        key_at = slice(feat + HEAD_DIM * h, feat + HEAD_DIM * (h + 1))
        value_at = slice(2 * feat + HEAD_DIM * h, 2 * feat + HEAD_DIM * (h + 1))
        keys, held = projected[:, key_at], projected[:, value_at]
        for k in range(4):
            block = slice(rows * k, rows * (k + 1))
            d_mixed = d_all[block, at]
            delta = jnp.sum(d_mixed.astype(F32) * mixed[block, at], axis=1, keepdims=True)
            d_probs = dot(d_mixed, held, NT)
            low = (probs[h, block, :].astype(F32) * (d_probs - delta)).astype(BF16)
            d_scores[block, :] = low
            d_three[block, at] = (dot(low, keys, NN) * scale).astype(BF16)
        d_three[:, key_at] = dot(d_scores[...], projected[:group, at], TN).astype(BF16)
        d_three[:, value_at] = dot(probs[h], d_all[:, at], TN).astype(BF16)
    grads[...] = dot(h_one[...], d_three[...], TN)
    half = kept.shape[0] // 4
    for p in range(4):
        block = slice(half * p, half * (p + 1))
        kept[block, :] = grads[rows_at(2 * half * p + half * core, half, 32), :]
        given[block, :] = grads[rows_at(2 * half * p + half * (1 - core), half, 32), :].astype(BF16)
    sums = jnp.sum(d_three[...].astype(F32), axis=0, keepdims=True)
    weight = w_three[...].astype(F32)
    with_gain = jnp.sum(grads[...] * weight, axis=1, keepdims=True)
    with_shift = jnp.sum(weight * sums, axis=1, keepdims=True)
    side = lax.broadcasted_iota(jnp.int32, (width, 128), 1)
    both = jnp.where(side == 0, with_gain, jnp.where(side == 1, with_shift, 0.0)).T
    d_shift = both[1:2, :]
    lines[0:1, :] = (both[0:1, :] - vectors[1:2, :] * d_shift) / vectors[0:1, :]
    lines[1:2, :] = d_shift
    lines[2:3, :] = jnp.zeros((1, width), F32)
    lines[2:3, :feat] = sums[:, :feat]
    lines[3:4, :] = jnp.zeros((1, width), F32)
    lines[3:4, :feat] = sums[:, 2 * feat :]
    lines[4:, :] = jnp.zeros((4, width), F32)


def inputs_back(where, d_three, w_three, near, far):
    group = near.shape[0]
    near[...] = dot(d_three[:group, :], w_three[...], NT)
    far[...] = dot(d_three[group:, :], w_three[...], NT).astype(BF16)


def share_inputs(where, near, far, *outs):
    rows = outs[0].shape[0]
    for k, out in enumerate(outs):
        at = rows_at(rows * (where[0] ^ k), rows, 16)
        out[...] = (near[at, :] + far[at, :].astype(F32)).astype(out.dtype)


def finish_inputs(where, d0, d1, d2, d3, tokens, d_second, vectors, out):
    total = d0[...]
    for piece in (d1, d2, d3):
        total = total + piece[...].astype(F32)
    unit, inverse = unit_rows(tokens[...].astype(F32))
    d_inputs = unit_back(total, vectors[0:1, :], unit, inverse)
    out[...] = (d_second[...] + d_inputs).astype(BF16)


def project_output(where, mixed, w_output, tokens, vectors, second, h_two, count):
    rows, width = tokens.shape
    feat = mixed.shape[1]
    total = tokens[...].astype(F32) + vectors[2:3, :]
    valid = jnp.zeros((1, 1), F32)
    for k in range(4):
        start = (rows + 16) * k
        total += dot(mixed[start : start + rows, :], w_output[feat * k : feat * (k + 1), :], NN)
        digits = mixed[start + rows : start + rows + 16, :].astype(F32)
        valid += digits[0:1, 0:1] * 128.0 + digits[0:1, 1:2]
    second[...] = total
    unit, _ = unit_rows(total)
    h_two[...] = (unit * vectors[3:4, :] + vectors[4:5, :]).astype(BF16)
    count[...] = jnp.broadcast_to(valid, count.shape)


def activate(where, h_pair, w_up, b_up, act, slope):
    rows = h_pair.shape[0] // 2
    root = 0.7978845608028654
    for i in range(2):
        block = slice(rows * i, rows * (i + 1))
        value = dot(h_pair[block, :], w_up[...], NN) + b_up[...]
        square = value * value
        bent = jnp.tanh(root * value * (1.0 + 0.044715 * square))
        act[block, :] = (0.5 * value * (1.0 + bent)).astype(BF16)
        slope[block, :] = 0.5 * (1.0 + bent) + 0.5 * value * (1.0 - bent * bent) * root * (
            1.0 + 3.0 * 0.044715 * square
        )


def project_down(where, act, w_down, near, far):
    rows, core = near.shape[0], where[1]
    near[...] = dot(act[core_rows(core, rows), :], w_down[...], NN)
    far[...] = dot(act[core_rows(1 - core, rows), :], w_down[...], NN).astype(BF16)


def compare(where, second, near, far, vectors, teacher, cotangent, valid, count, *outs):
    layer_output, d_result, d_down, lines = outs
    rows, width = second.shape
    other = far[core_rows(1 - where[1], rows), :].astype(F32)
    result = second[...] + near[...] + other + vectors[5:6, :]
    layer_output[...] = result.astype(BF16)
    kept = valid[...].astype(F32).reshape(rows, 1)
    mismatch = result - teacher[...].astype(F32)
    weighted = kept * mismatch
    error = jnp.sum(jnp.sum(weighted * mismatch, axis=1, keepdims=True), axis=0, keepdims=True)
    total = cotangent[...].astype(F32) + 2.0 / (width * count[0:1, 0:1]) * weighted
    d_result[...] = total
    low = total.astype(BF16)
    d_down[...] = low
    high = error.astype(BF16).astype(F32)
    middle = (error - high).astype(BF16).astype(F32)
    side = lax.broadcasted_iota(jnp.int32, (1, width), 1)
    parts = jnp.where(
        side == 0, high, jnp.where(side == 1, middle, jnp.where(side == 2, error - high - middle, 0.0))
    )
    lines[0:1, :] = jnp.sum(low.astype(F32), axis=0, keepdims=True)
    lines[1:2, :] = parts
    lines[2:, :] = jnp.zeros((6, width), F32)


def activate_back(where, d_down, w_down, slope, w_up, d_up, near, far, line):
    rows, core = near.shape[0], where[1]
    total = jnp.zeros(line.shape, F32)
    for i in range(2):
        block = slice(rows * i, rows * (i + 1))
        low = (dot(d_down[block, :], w_down[...], NT) * slope[block, :]).astype(BF16)
        d_up[block, :] = low
        total += jnp.sum(low.astype(F32), axis=0, keepdims=True)
    line[...] = total
    near[...] = dot(d_up[core_rows(core, rows), :], w_up[...], NT)
    far[...] = dot(d_up[core_rows(1 - core, rows), :], w_up[...], NT).astype(BF16)


def second_back(where, near, far, d_result, second, vectors, w_output, *outs):
    d_second, d_attn, lines, sent = outs
    rows = near.shape[0]
    d_two = near[...] + far[core_rows(1 - where[1], rows), :].astype(F32)
    unit, inverse = unit_rows(second[...])
    total = d_result[...] + unit_back(d_two, vectors[3:4, :], unit, inverse)
    d_second[...] = total
    low = total.astype(BF16)
    d_attn[...] = low
    lines[0:1, :] = jnp.sum(low.astype(F32), axis=0, keepdims=True)
    lines[1:2, :] = jnp.sum(d_two * unit, axis=0, keepdims=True)
    lines[2:3, :] = jnp.sum(d_two, axis=0, keepdims=True)
    lines[3:, :] = jnp.zeros((5, lines.shape[1]), F32)
    feat = sent.shape[1]
    for k in range(4):
        part = w_output[feat * k : feat * (k + 1), :]
        sent[rows * k : rows * (k + 1), :] = dot(low, part, NT).astype(BF16)


def output_grads(where, mixed, d_attn, kept, given):
    core = where[1]
    rows, width = d_attn.shape
    feat, units = mixed.shape[1], width // 2
    mine = d_attn[:, rows_at(units * core, units, 128)]
    others = d_attn[:, rows_at(units * (1 - core), units, 128)]
    for k in range(4):
        at = slice(feat * k, feat * (k + 1))
        piece = mixed[(rows + 16) * k : (rows + 16) * k + rows, :]
        kept[at, :] = dot(piece, mine, TN)
        given[at, :] = dot(piece, others, TN).astype(BF16)


def split_chips(chip, block, outs, count):
    own, to_x, to_y, then_x, then_y = outs
    for p in range(4):
        own[count * p : count * (p + 1), :] = block(chip, p)
    for p in (0, 1):
        low, high = slice(count * p, count * (p + 1)), slice(count * (p + 2), count * (p + 3))
        to_x[low, :] = block(chip ^ 1, p).astype(BF16)
        to_x[high, :] = block(chip ^ 3, p).astype(BF16)
        to_y[low, :] = block(chip ^ 2, p + 2).astype(BF16)
        to_y[high, :] = block(chip ^ 3, p + 2).astype(BF16)
        then_x[low, :] = block(chip ^ 1, p + 2)
        then_y[low, :] = block(chip ^ 2, p)


def pass_on(where, from_x, from_y, then_x, then_y, to_x, to_y):
    half = to_x.shape[0]
    to_x[...] = (then_x[...] + from_y[half:, :].astype(F32)).astype(BF16)
    to_y[...] = (then_y[...] + from_x[half:, :].astype(F32)).astype(BF16)


def add_chips(own, from_x, from_y, last_x, last_y):
    half = last_x.shape[0]
    low = own[:half, :] + from_x[:half, :].astype(F32) + last_y[...].astype(F32)
    high = own[half:, :] + from_y[:half, :].astype(F32) + last_x[...].astype(F32)
    return low, high


def down_grads(where, act, d_down, *refs):
    outs, total = refs[:5], refs[5]
    count = outs[0].shape[0] // 4
    total[...] = dot(act[...], d_down[...], TN)

    def block(j, p):
        return total[rows_at(4 * count * p + count * j, count, 32), :]

    split_chips(where[0], block, outs, count)


def up_grads(where, h_pair, d_up, kept, given, *refs):
    outs, total = refs[:5], refs[5]
    count, units = outs[0].shape[0] // 4, d_up.shape[1]
    total[:, :units] = dot(h_pair[...], d_up[...], TN)
    total[:, units:] = kept[...] + given[...].astype(F32)

    def block(j, p):
        return total[rows_at(4 * count * p + count * j, count, 16), :]

    split_chips(where[0], block, outs, count)


def send_planes(where, own, from_x, from_y, last_x, last_y, *refs):
    outs, total = refs[:4], refs[4]
    part, half = outs[0].shape[0], last_x.shape[0]
    total[:half, :], total[half:, :] = add_chips(own, from_x, from_y, last_x, last_y)
    for s, out in enumerate(outs):
        out[...] = total[rows_at(part * (where[2] ^ s), part, 16), :].astype(out.dtype)


def sum_pieces(where, own, p1, p2, p3, out):
    total = own[...].astype(F32)
    for piece in (p1, p2, p3):
        total = total + piece[...].astype(F32)
    out[...] = total.astype(out.dtype)


def finish_down(where, n0, n1, n2, n3, far, out):
    chip, core = where[0], where[1]
    both = n0.shape[0]
    part = both // 2
    for k, piece in enumerate((n0, n1, n2, n3)):
        at = part * (chip ^ k)
        out[rows_at(4 * part * core + at, part, 32), :] = piece[part:, :].astype(F32)
        out[rows_at(4 * part * (1 - core) + at, part, 32), :] = far[
            both * k + part : both * (k + 1), :
        ].astype(F32)


def finish_up(where, n0, n1, n2, n3, far, out, out_half):
    chip, core = where[0], where[1]
    part, units = n0.shape[0], n0.shape[1] // 5
    for k, near in enumerate((n0, n1, n2, n3)):
        rows = rows_at(part * (chip ^ k), part, 16)
        for piece, side in ((near[...], core), (far[part * k : part * (k + 1), :], 1 - core)):
            full = piece.astype(F32)
            for i in range(4):
                at = rows_at(2 * units * i + units * side, units, 128)
                out[rows, at] = full[:, units * i : units * (i + 1)]
            out_half[rows, rows_at(units * side, units, 128)] = full[:, 4 * units :]


def pack_gradients(
    where, kept, given, from_attention, from_second, from_result, up_line, own, *refs
):
    out = refs[4]
    chip = where[0]
    half, width = out.shape[0] // 8, out.shape[1]
    feat = width // 4
    down = add_chips(own, *refs[:4])
    for p in range(4):
        cut = slice(feat * p, feat * (p + 1))
        owner = jnp.where(chip == p, 1.0, 0.0)
        lines = [
            from_attention[0:1, cut],
            from_attention[1:2, cut],
            from_second[0:1, cut],
            from_second[1:2, cut],
            from_second[2:3, cut],
            from_result[0:1, cut],
            up_line[:, 2 * feat * p : 2 * feat * p + feat],
            up_line[:, 2 * feat * p + feat : 2 * feat * (p + 1)],
            from_attention[2:3, :feat] * owner,
            from_attention[3:4, :feat] * owner,
            from_result[1:2, :feat],
            jnp.zeros((half - 11, feat), F32),
        ]
        small = jnp.concatenate(lines, axis=0).astype(BF16)
        block = slice(half * p, half * (p + 1))
        arrived = given[rows_at(4 * half * (1 - where[1]) + half * p, half, 32), :]
        total = (kept[block, :] + arrived.astype(F32)).astype(BF16)
        start = 2 * half * p
        out[start : start + half, : 3 * feat] = total
        out[start : start + half, 3 * feat :] = small
        out[start + half : start + 2 * half, :] = down[p // 2][
            half * (p % 2) : half * (p % 2 + 1), :
        ].astype(BF16)


def sum_planes(where, arrived, out):
    both, width = out.shape
    half, feat = both // 2, width // 4
    total = arrived[:both, :].astype(F32)
    for p in (1, 2, 3):
        total = total + arrived[both * p : both * (p + 1), :].astype(F32)
    out[half:, :] = total[half:, :].astype(BF16)
    out[:half, : 3 * feat] = total[:half, : 3 * feat].astype(BF16)
    small = total[:16, 3 * feat :]
    total = jnp.sum(small[10:11, :3], axis=1, keepdims=True)
    high = total.astype(BF16).astype(F32)
    middle = (total - high).astype(BF16).astype(F32)
    line = lax.broadcasted_iota(jnp.int32, small.shape, 0)
    side = lax.broadcasted_iota(jnp.int32, small.shape, 1)
    parts = jnp.where(side == 0, high, jnp.where(side == 1, middle, total - high - middle))
    small = jnp.where((line == 10) & (side < 3), parts, small)
    out[:16, 3 * feat :] = small.astype(BF16)
    out[16:half, 3 * feat :] = jnp.zeros((half - 16, feat), BF16)


def finish_projections(where, n0, n1, n2, n3, far, count, *outs):
    query, key, value, loss = outs[:4]
    flat, up_line, held, whole_line = outs[4:12], outs[12], outs[13], outs[14]
    chip, core = where[0], where[1]
    both, width = n0.shape
    half, feat = both // 2, width // 4
    near = (n0, n1, n2, n3)
    for k, piece in enumerate(near):
        held[2 * (chip ^ k) + core] = piece[:16, 3 * feat :].astype(F32)
        held[2 * (chip ^ k) + 1 - core] = far[both * k : both * k + 16, 3 * feat :].astype(F32)
    for j in range(4):

        @pl.when(chip == j)
        def _():
            for k, piece in enumerate(near):
                columns = slice(feat * (j ^ k), feat * ((j ^ k) + 1))
                for i, out in enumerate((query, key, value)):
                    cut = slice(feat * i, feat * (i + 1))
                    out[rows_at(half * core, half, 32), columns] = piece[:half, cut].astype(F32)
                    out[rows_at(half * (1 - core), half, 32), columns] = far[
                        both * k : both * k + half, cut
                    ].astype(F32)

    total = held[0]
    for i in range(1, 8):
        total = total + held[i]
    for i, line in enumerate((0, 1, 2, 3, 4, 5, 8, 9)):
        flat[i][...] = total[line]
    even = held[0] + held[2] + held[4] + held[6]
    odd = held[1] + held[3] + held[5] + held[7]
    for side, part in enumerate((even, odd)):
        for i in range(2):
            at = 2 * feat * side + feat * i
            whole_line[0:1, at : at + feat] = part[6 + i : 7 + i, :]
    up_line[...] = whole_line[0]
    error = jnp.sum(total[10:11, :3], axis=1, keepdims=True)
    loss[0, 0] = jnp.sum(error / (width * count[0:1, 0:1]))


def layer(
    tokens,
    segment_ids,
    valid_rows,
    teacher,
    cotangent,
    first_gain,
    first_shift,
    query_weight,
    query_bias,
    key_weight,
    value_weight,
    value_bias,
    output_weight,
    output_bias,
    second_gain,
    second_shift,
    up_weight,
    up_bias,
    down_weight,
    down_bias,
):
    rows, width = tokens.shape[1], tokens.shape[2]
    shard = query_weight.shape[0]
    half, quarter = shard // 2, shard // 4
    hidden = up_weight.shape[1]
    units = hidden // 2
    own_units = down_weight.shape[0]
    core_units = own_units // 2
    part_units = core_units // 4
    feat = width // 4
    heads = feat // HEAD_DIM
    group = 4 * rows
    every = 2 * group
    steps = (1, 2, 3)

    place, plane = lax.axis_index("ctx"), lax.axis_index("fsdp")
    where = jnp.stack([place // 2, place % 2, plane]).astype(jnp.int32)
    dma = pltpu.SemaphoreType.DMA

    last = []

    def step(body, outs, args, **options):
        made = local_call(body, outs, where, args, after=tuple(last), **options)
        last[:] = [min(jax.tree.leaves(made), key=lambda a: a.size * a.dtype.itemsize)]
        return made

    def stack(pieces, cost=0):
        shape = len(pieces) * pieces[0].shape[0], pieces[0].shape[1]
        return step(stack_rows, shaped(*shape), pieces, cost=cost)

    own = tokens[0]
    smalls = (
        first_gain,
        first_shift,
        query_bias,
        value_bias,
        output_bias,
        second_gain,
        second_shift,
        down_bias,
    )
    up_piece, down_piece = step(
        pack_blocks,
        (shaped(quarter, 5 * core_units), shaped(part_units, width)),
        (up_weight, output_weight, down_weight),
        far=range(3),
        scratch=[dma((6,))],
    )
    up_far = [swap_planes(up_piece, s) for s in steps]
    near_tokens = trade_chips(
        step(pack_tokens, shaped(4 * (rows + 16), width), (own, segment_ids, valid_rows), cost=50)
    )
    projections = step(
        pack_projections,
        shaped(half, width),
        (query_weight, key_weight, value_weight, *smalls, up_bias, valid_rows),
        far=range(12),
        scratch=[
            pltpu.VMEM((3, half, width), BF16),
            *[pltpu.VMEM((feat,), BF16)] * 8,
            pltpu.VMEM((own_units,), BF16),
            dma((12,)),
        ],
    )
    near_weights = [projections] + [swap_planes(projections, s) for s in steps]
    far_tokens = swap_cores(near_tokens)
    up_far = stack(up_far, cost=50)
    unit_one, key_row, query_column = step(
        normalize_tokens,
        (wide(every, width), wide(8, every), wide(group, 128)),
        (near_tokens, far_tokens),
        cost=50,
    )
    far_weights = swap_cores(stack(near_weights))

    def all_chips(piece, cut):
        from_x, from_y = swap_chips(piece, 1), swap_chips(piece, 2)
        count, lanes = piece.shape
        to_x, to_y = step(
            cross_halves, (shaped(cut, lanes), shaped(count - cut, lanes)), (from_x, from_y), cost=50
        )
        return piece, from_x, from_y, swap_chips(to_x, 1), swap_chips(to_y, 2)

    up_all = all_chips(up_far, up_far.shape[0] // 32 * 16 + 16)
    down_far = [swap_planes(down_piece, s) for s in steps]

    h_one, w_three, projected, probs, mixed, sent, vectors, b_up = step(
        attend,
        (
            shaped(every, width),
            shaped(width, 3 * feat),
            shaped(every, 3 * feat),
            shaped(heads, group, every),
            wide(group, feat),
            shaped(4 * (rows + 16), feat),
            wide(8, width),
            wide(1, units),
        ),
        (unit_one, key_row, query_column, *near_weights, far_weights),
        scratch=[pltpu.VMEM((4, 16, feat), F32), pltpu.VMEM((group, every), F32)],
        vmem=24,
        cost=50,
    )
    mixed_low = trade_chips(sent)
    down_far = stack(down_far)
    out_near = step(build_half, shaped(width, core_units), (output_weight, *up_all))
    out_far = swap_cores(out_near)
    w_up = step(
        build_up, shaped(width, units), (up_weight, *up_all), far=(0,), scratch=[dma((4,))], cost=50
    )
    w_output = step(build_output, shaped(width, width), (out_near, out_far))

    second, h_two, count = step(
        project_output,
        (wide(rows, width), shaped(rows, width), wide(8, 128)),
        (mixed_low, w_output, own, vectors),
    )
    h_pair = both_cores(h_two)
    down_all = all_chips(down_far, down_far.shape[0] // 2)
    act, slope = step(
        activate,
        (shaped(2 * rows, units), wide(2 * rows, units)),
        (h_pair, w_up, b_up),
    )
    w_down = step(
        build_down, shaped(units, width), (down_weight, *down_all), far=(0,), scratch=[dma]
    )
    down_near, down_other = step(
        project_down, (wide(rows, width), shaped(rows, width)), (act, w_down)
    )
    layer_output, d_result, d_down, from_result = step(
        compare,
        (shaped(rows, width), wide(rows, width), shaped(rows, width), wide(8, width)),
        (
            second,
            down_near,
            both_cores(down_other),
            vectors,
            teacher[0],
            cotangent[0],
            valid_rows,
            count,
        ),
    )
    d_down = both_cores(d_down)

    def five(count, lanes):
        both = (shaped(4 * count, lanes),) * 2
        return (wide(4 * count, lanes),) + both + (wide(2 * count, lanes),) * 2

    def onward(parts, arrived):
        count, lanes = parts[3].shape
        to_x, to_y = step(pass_on, (shaped(count, lanes),) * 2, (*arrived, *parts[3:]), cost=50)
        return (parts[0], *arrived, swap_chips(to_x, 1), swap_chips(to_y, 2))

    down_parts = step(
        down_grads,
        five(part_units, width),
        (act, d_down),
        scratch=[pltpu.VMEM((units, width), F32)],
        vmem=24,
    )
    down_arrived = swap_chips(down_parts[1], 1), swap_chips(down_parts[2], 2)
    d_up, two_near, two_other, up_line = step(
        activate_back,
        (shaped(2 * rows, units), wide(rows, width), shaped(rows, width), wide(1, units)),
        (d_down, w_down, slope, w_up),
        cost=50,
    )
    d_second, d_attn, from_second, d_sent = step(
        second_back,
        (wide(rows, width), shaped(rows, width), wide(8, width), shaped(group, feat)),
        (two_near, both_cores(two_other), d_result, second, vectors, w_output),
    )
    d_mixed = trade_chips(d_sent)

    kept_out, given_out = step(
        output_grads,
        (wide(width, core_units), shaped(width, core_units)),
        (mixed_low, d_attn),
    )
    given_out = swap_cores(given_out)
    down_sums = onward(down_parts, down_arrived)
    up_parts = step(
        up_grads,
        five(quarter, 5 * core_units),
        (h_pair, d_up, kept_out, given_out),
        scratch=[pltpu.VMEM((width, 5 * core_units), F32)],
        vmem=24,
    )
    up_arrived = swap_chips(up_parts[1], 1), swap_chips(up_parts[2], 2)

    d_three, kept, given, from_attention = step(
        attend_back,
        (
            shaped(every, 3 * feat),
            wide(4 * half, 3 * feat),
            shaped(4 * half, 3 * feat),
            wide(8, width),
        ),
        (d_mixed, probs, projected, mixed, h_one, w_three, vectors),
        scratch=[pltpu.VMEM((group, every), BF16), pltpu.VMEM((width, 3 * feat), F32)],
        vmem=24,
        cost=50,
    )
    given = both_cores(given)
    d_near, d_far = step(
        inputs_back, (wide(group, width), shaped(group, width)), (d_three, w_three)
    )
    d_far = swap_cores(d_far)
    arrived = trade_planes(
        step(
            pack_gradients,
            shaped(8 * half, width),
            (kept, given, from_attention, from_second, from_result, up_line, *down_sums),
        )
    )
    up_sums = onward(up_parts, up_arrived)
    shares = step(
        share_inputs, (wide(rows, width),) + (shaped(rows, width),) * 3, (d_near, d_far)
    )
    shares = [shares[0]] + [swap_chips(shares[k], k) for k in steps]

    def spread(piece):
        return [piece] + [swap_chips(piece, k) for k in steps]

    def whole(near):
        return (*near, swap_cores(stack(near)))

    up_planes = step(
        send_planes,
        (wide(quarter, 5 * core_units),) + (shaped(quarter, 5 * core_units),) * 3,
        up_sums,
        scratch=[pltpu.VMEM((4 * quarter, 5 * core_units), F32)],
    )
    up_planes = [up_planes[0]] + [swap_planes(up_planes[s], s) for s in steps]
    grad_tokens = step(finish_inputs, shaped(rows, width), (*shares, own, d_second, vectors), cost=3)
    both = spread(step(sum_planes, shaped(2 * half, width), (arrived,)))
    up_near = spread(step(sum_pieces, shaped(quarter, 5 * core_units), up_planes))
    both = whole(both)
    finished = step(
        finish_projections,
        (wide(shard, width),) * 3
        + (wide(1, 1),)
        + (wide(shard),) * 8
        + (wide(own_units),),
        (*both, count),
        scratch=[pltpu.VMEM((8, 16, feat), F32), pltpu.VMEM((8, own_units), F32)],
        scalar=3,
    )
    grad_down_weight = step(finish_down, wide(own_units, width), both)
    grad_up_weight, grad_output_weight = step(
        finish_up, (wide(shard, hidden), wide(shard, width)), whole(up_near)
    )
    sums, two = finished[4:10], finished[10:12]
    return (
        layer_output[None],
        finished[3].reshape(()),
        grad_tokens[None],
        sums[0],
        sums[1],
        finished[0],
        two[0],
        finished[1],
        finished[2],
        two[1],
        grad_output_weight,
        sums[2],
        sums[3],
        sums[4],
        grad_up_weight,
        finished[12],
        grad_down_weight,
        sums[5],
    )


def solution(mesh):
    body = layer if (mesh.shape["ctx"], mesh.shape["fsdp"]) == (8, 4) else shards
    placed = (
        P("fsdp", "ctx", None),
        P("fsdp", "ctx"),
        P("fsdp", "ctx"),
        P("fsdp", "ctx", None),
        P("fsdp", "ctx", None),
        P("fsdp"),
        P("fsdp"),
        P("fsdp", None),
        P("fsdp"),
        P("fsdp", None),
        P("fsdp", None),
        P("fsdp"),
        P("fsdp", None),
        P("fsdp"),
        P("fsdp"),
        P("fsdp"),
        P("fsdp", None),
        P("fsdp"),
        P("fsdp", None),
        P("fsdp"),
    )
    return jax.shard_map(
        body,
        mesh=mesh,
        in_specs=placed,
        out_specs=(
            P("fsdp", "ctx", None),
            P(),
            P("fsdp", "ctx", None),
            P("fsdp"),
            P("fsdp"),
            P("fsdp", None),
            P("fsdp"),
            P("fsdp", None),
            P("fsdp", None),
            P("fsdp"),
            P("fsdp", None),
            P("fsdp"),
            P("fsdp"),
            P("fsdp"),
            P("fsdp", None),
            P("fsdp"),
            P("fsdp", None),
            P("fsdp"),
        ),
        check_vma=False,
    )
```

```python
import jax
import jax.numpy as jnp
from jax import lax
from jax.experimental import pallas as pl
from jax.experimental.pallas import tpu as pltpu
from jax.sharding import PartitionSpec as P

HEADS = 12
HEAD_DIM = 64


EPSILON = 1e-06
MASKED = -1e30


def norm_rows(values, gain, shift):
    centre = jnp.mean(values, axis=-1, keepdims=True)
    centred = values - centre
    spread = jnp.mean(centred * centred, axis=-1, keepdims=True)
    return centred * lax.rsqrt(spread + EPSILON) * gain + shift


def tanh_gelu(values):
    return jax.nn.gelu(values, approximate=True)


def key_allowed(query_segment, query_place, key_codes, key_place):
    same_doc = query_segment[:, None] == (key_codes // 2)[None, :]
    usable = (key_codes % 2 == 1)[None, :] | (query_place[:, None] == key_place[None, :])
    return (same_doc & usable)[None, :, :]


def split_heads(values):
    return values.reshape(values.shape[0], HEADS, HEAD_DIM)


def head_scores(query_heads, key_heads, scale):
    return (
        jnp.einsum("qhd,khd->hqk", query_heads, key_heads, preferred_element_type=jnp.float32)
        * scale
    )


def row_sum(values):
    return jnp.sum(values, axis=0, dtype=jnp.float32)


def left_product(left, right):
    return jnp.einsum("rd,rf->df", left, right, preferred_element_type=jnp.float32)


def right_product(left, right):
    return jnp.einsum("rf,df->rd", left, right, preferred_element_type=jnp.float32)


def shards(
    tokens,
    segment_ids,
    valid_rows,
    teacher,
    cotangent,
    first_gain,
    first_shift,
    query_weight,
    query_bias,
    key_weight,
    value_weight,
    value_bias,
    output_weight,
    output_bias,
    second_gain,
    second_shift,
    up_weight,
    up_bias,
    down_weight,
    down_bias,
):
    tok_rows = tokens.shape[1]
    feature_width = tokens.shape[2]
    shard_count = lax.axis_size("ctx")
    key_block = 4 * tok_rows
    block_count = shard_count // 4
    scale = HEAD_DIM ** (-0.5)
    gain_one, shift_one, w_query, b_query, w_key, w_value, b_value, w_output, b_output = (
        lax.all_gather(first_gain, "fsdp", axis=0, tiled=True),
        lax.all_gather(first_shift, "fsdp", axis=0, tiled=True),
        lax.all_gather(query_weight, "fsdp", axis=0, tiled=True),
        lax.all_gather(query_bias, "fsdp", axis=0, tiled=True),
        lax.all_gather(key_weight, "fsdp", axis=0, tiled=True),
        lax.all_gather(value_weight, "fsdp", axis=0, tiled=True),
        lax.all_gather(value_bias, "fsdp", axis=0, tiled=True),
        lax.all_gather(output_weight, "fsdp", axis=0, tiled=True),
        lax.all_gather(output_bias, "fsdp", axis=0, tiled=True),
    )
    gain_two, shift_two, w_up, b_up, w_down, b_down = (
        lax.all_gather(second_gain, "fsdp", axis=0, tiled=True),
        lax.all_gather(second_shift, "fsdp", axis=0, tiled=True),
        lax.all_gather(up_weight, "fsdp", axis=0, tiled=True),
        lax.all_gather(up_bias, "fsdp", axis=0, tiled=True),
        lax.all_gather(down_weight, "fsdp", axis=0, tiled=True),
        lax.all_gather(down_bias, "fsdp", axis=0, tiled=True),
    )
    local_segment = segment_ids[0]
    local_valid = valid_rows[0]
    local_codes = local_segment * 2 + local_valid
    all_codes = lax.all_gather(local_codes, "ctx", axis=0, tiled=True)
    query_place = lax.axis_index("ctx") * tok_rows + jnp.arange(tok_rows, dtype=jnp.int32)
    inputs = tokens[0].astype(jnp.float32)
    gain_first = gain_one.astype(jnp.float32)
    shift_first = shift_one.astype(jnp.float32)
    gain_second = gain_two.astype(jnp.float32)
    shift_second = shift_two.astype(jnp.float32)
    h_one = norm_rows(inputs, gain_first, shift_first)
    h_one_low = h_one.astype(jnp.bfloat16)
    query_low = (
        jnp.dot(h_one_low, w_query, preferred_element_type=jnp.float32)
        + b_query.astype(jnp.float32)
    ).astype(jnp.bfloat16)
    key_low = jnp.dot(h_one_low, w_key, preferred_element_type=jnp.float32).astype(jnp.bfloat16)
    value_low = (
        jnp.dot(h_one_low, w_value, preferred_element_type=jnp.float32)
        + b_value.astype(jnp.float32)
    ).astype(jnp.bfloat16)
    key_all, value_all = (
        lax.all_gather(key_low, "ctx", axis=0, tiled=True),
        lax.all_gather(value_low, "ctx", axis=0, tiled=True),
    )
    query_heads = split_heads(query_low)

    def block_rows(source, block_index):
        return split_heads(lax.dynamic_slice_in_dim(source, block_index * key_block, key_block, 0))

    def block_allowed(block_index):
        start = block_index * key_block
        codes = lax.dynamic_slice_in_dim(all_codes, start, key_block, 0)
        return key_allowed(
            local_segment, query_place, codes, start + jnp.arange(key_block, dtype=jnp.int32)
        )

    def stats_step(block_index, state_pair):
        running_max, running_sum = state_pair
        allowed = block_allowed(block_index)
        scores = jnp.where(
            allowed, head_scores(query_heads, block_rows(key_all, block_index), scale), MASKED
        )
        new_max = jnp.maximum(running_max, jnp.max(scores, axis=2))
        weights = jnp.where(allowed, jnp.exp(scores - new_max[:, :, None]), 0.0)
        return (new_max, running_sum * jnp.exp(running_max - new_max) + jnp.sum(weights, axis=2))

    start_max = jnp.full((HEADS, tok_rows), MASKED, jnp.float32)
    start_sum = jnp.zeros((HEADS, tok_rows), jnp.float32)
    running_max, running_sum = lax.fori_loop(0, block_count, stats_step, (start_max, start_sum))
    log_total = running_max + jnp.log(running_sum)

    def mix_step(block_index, mixed_sum):
        allowed = block_allowed(block_index)
        scores = head_scores(query_heads, block_rows(key_all, block_index), scale)
        probs = jnp.where(allowed, jnp.exp(scores - log_total[:, :, None]), 0.0).astype(
            jnp.bfloat16
        )
        return mixed_sum + jnp.einsum(
            "hqk,khd->qhd",
            probs,
            block_rows(value_all, block_index),
            preferred_element_type=jnp.float32,
        )

    mixed_heads = lax.fori_loop(
        0, block_count, mix_step, jnp.zeros((tok_rows, HEADS, HEAD_DIM), jnp.float32)
    )
    mixed = mixed_heads.reshape(tok_rows, feature_width)
    mixed_low = mixed.astype(jnp.bfloat16)
    second = (
        inputs
        + jnp.dot(mixed_low, w_output, preferred_element_type=jnp.float32)
        + b_output.astype(jnp.float32)
    )
    h_two = norm_rows(second, gain_second, shift_second)
    h_two_low = h_two.astype(jnp.bfloat16)
    up_value = jnp.dot(h_two_low, w_up, preferred_element_type=jnp.float32) + b_up.astype(
        jnp.float32
    )
    act_low = tanh_gelu(up_value).astype(jnp.bfloat16)
    result = (
        second
        + jnp.dot(act_low, w_down, preferred_element_type=jnp.float32)
        + b_down.astype(jnp.float32)
    )
    layer_output = result.astype(jnp.bfloat16)[None]
    valid_float = local_valid.astype(jnp.float32)
    mismatch = result - teacher[0].astype(jnp.float32)
    error_sum, valid_count = lax.psum(
        (jnp.sum(valid_float[:, None] * mismatch * mismatch), jnp.sum(valid_float)), ("ctx", "fsdp")
    )
    loss_value = error_sum / (feature_width * valid_count)
    d_result = (
        cotangent[0].astype(jnp.float32)
        + 2.0 / (feature_width * valid_count) * valid_float[:, None] * mismatch
    )
    d_down = d_result.astype(jnp.bfloat16)
    grad_down_bias = row_sum(d_down)
    grad_down_weight = left_product(act_low, d_down)
    d_act = right_product(d_down, w_down)
    gelu_value, gelu_pull = jax.vjp(tanh_gelu, up_value)
    d_up = gelu_pull(d_act)[0].astype(jnp.bfloat16)
    grad_up_bias = row_sum(d_up)
    grad_up_weight = left_product(h_two_low, d_up)
    d_h_two = right_product(d_up, w_up)
    norm_two_value, norm_two_pull = jax.vjp(norm_rows, second, gain_second, shift_second)
    d_second_norm, grad_second_gain, grad_second_shift = norm_two_pull(d_h_two)
    d_second = d_result + d_second_norm
    d_attn = d_second.astype(jnp.bfloat16)
    grad_output_bias = row_sum(d_attn)
    grad_output_weight = left_product(mixed_low, d_attn)
    d_mixed = right_product(d_attn, w_output).astype(jnp.bfloat16)
    d_heads = split_heads(d_mixed)
    delta = jnp.einsum("qhd,qhd->hq", d_heads.astype(jnp.float32), mixed_heads)
    key_back, value_back = (key_all, value_all)

    def score_grads(block_index):
        allowed = block_allowed(block_index)
        key_piece = block_rows(key_back, block_index)
        value_piece = block_rows(value_back, block_index)
        scores = head_scores(query_heads, key_piece, scale)
        probs = jnp.where(allowed, jnp.exp(scores - log_total[:, :, None]), 0.0)
        d_probs = jnp.einsum(
            "qhd,khd->hqk", d_heads, value_piece, preferred_element_type=jnp.float32
        )
        d_scores = (probs * (d_probs - delta[:, :, None])).astype(jnp.bfloat16)
        return (key_piece, probs, d_scores)

    zero_query = jnp.zeros((tok_rows, HEADS, HEAD_DIM), jnp.float32)

    def reduce_step(block_index, state_triple):
        d_query_sum, d_key_rows, d_value_rows = state_triple
        key_piece, probs, d_scores = score_grads(block_index)
        d_query_sum = d_query_sum + jnp.einsum(
            "hqk,khd->qhd", d_scores, key_piece, preferred_element_type=jnp.float32
        )
        d_key_piece = jnp.einsum(
            "hqk,qhd->khd", d_scores, query_heads, preferred_element_type=jnp.float32
        ).reshape(key_block, feature_width)
        d_value_piece = jnp.einsum(
            "hqk,qhd->khd", probs.astype(jnp.bfloat16), d_heads, preferred_element_type=jnp.float32
        ).reshape(key_block, feature_width)
        d_key_rows = lax.dynamic_update_slice_in_dim(
            d_key_rows, d_key_piece, block_index * key_block, 0
        )
        d_value_rows = lax.dynamic_update_slice_in_dim(
            d_value_rows, d_value_piece, block_index * key_block, 0
        )
        return (d_query_sum, d_key_rows, d_value_rows)

    zero_rows = jnp.zeros((key_block * block_count, feature_width), jnp.float32)
    d_query_sum, d_key_rows, d_value_rows = lax.fori_loop(
        0, block_count, reduce_step, (zero_query, zero_rows, zero_rows)
    )
    d_key_local, d_value_local = (
        lax.psum_scatter(d_key_rows, "ctx", scatter_dimension=0, tiled=True),
        lax.psum_scatter(d_value_rows, "ctx", scatter_dimension=0, tiled=True),
    )
    d_query = (d_query_sum.reshape(tok_rows, feature_width) * scale).astype(jnp.bfloat16)
    d_key = (d_key_local * scale).astype(jnp.bfloat16)
    d_value = d_value_local.astype(jnp.bfloat16)
    grad_query_bias = row_sum(d_query)
    grad_query_weight = left_product(h_one_low, d_query)
    grad_key_weight = left_product(h_one_low, d_key)
    grad_value_bias = row_sum(d_value)
    grad_value_weight = left_product(h_one_low, d_value)
    d_h_one = (
        right_product(d_query, w_query)
        + right_product(d_key, w_key)
        + right_product(d_value, w_value)
    )
    norm_one_value, norm_one_pull = jax.vjp(norm_rows, inputs, gain_first, shift_first)
    d_inputs_norm, grad_first_gain, grad_first_shift = norm_one_pull(d_h_one)
    grad_tokens = (d_second + d_inputs_norm).astype(jnp.bfloat16)[None]
    shares = (
        lax.psum_scatter(
            grad_first_gain.astype(jnp.bfloat16), "fsdp", scatter_dimension=0, tiled=True
        ).astype(jnp.float32),
        lax.psum_scatter(
            grad_first_shift.astype(jnp.bfloat16), "fsdp", scatter_dimension=0, tiled=True
        ).astype(jnp.float32),
        lax.psum_scatter(
            grad_query_weight.astype(jnp.bfloat16), "fsdp", scatter_dimension=0, tiled=True
        ).astype(jnp.float32),
        lax.psum_scatter(
            grad_query_bias.astype(jnp.bfloat16), "fsdp", scatter_dimension=0, tiled=True
        ).astype(jnp.float32),
        lax.psum_scatter(
            grad_key_weight.astype(jnp.bfloat16), "fsdp", scatter_dimension=0, tiled=True
        ).astype(jnp.float32),
        lax.psum_scatter(
            grad_value_weight.astype(jnp.bfloat16), "fsdp", scatter_dimension=0, tiled=True
        ).astype(jnp.float32),
        lax.psum_scatter(
            grad_value_bias.astype(jnp.bfloat16), "fsdp", scatter_dimension=0, tiled=True
        ).astype(jnp.float32),
        lax.psum_scatter(
            grad_output_weight.astype(jnp.bfloat16), "fsdp", scatter_dimension=0, tiled=True
        ).astype(jnp.float32),
        lax.psum_scatter(
            grad_output_bias.astype(jnp.bfloat16), "fsdp", scatter_dimension=0, tiled=True
        ).astype(jnp.float32),
        lax.psum_scatter(
            grad_second_gain.astype(jnp.bfloat16), "fsdp", scatter_dimension=0, tiled=True
        ).astype(jnp.float32),
        lax.psum_scatter(
            grad_second_shift.astype(jnp.bfloat16), "fsdp", scatter_dimension=0, tiled=True
        ).astype(jnp.float32),
        lax.psum_scatter(
            grad_up_weight.astype(jnp.bfloat16), "fsdp", scatter_dimension=0, tiled=True
        ).astype(jnp.float32),
        lax.psum_scatter(
            grad_up_bias.astype(jnp.bfloat16), "fsdp", scatter_dimension=0, tiled=True
        ).astype(jnp.float32),
        lax.psum_scatter(
            grad_down_weight.astype(jnp.bfloat16), "fsdp", scatter_dimension=0, tiled=True
        ).astype(jnp.float32),
        lax.psum_scatter(
            grad_down_bias.astype(jnp.bfloat16), "fsdp", scatter_dimension=0, tiled=True
        ).astype(jnp.float32),
    )
    totals = lax.psum(
        (
            shares[0],
            shares[1],
            shares[2],
            shares[3],
            shares[4],
            shares[5],
            shares[6],
            shares[7],
            shares[8],
            shares[9],
            shares[10],
            shares[11],
            shares[12],
            shares[13],
            shares[14],
        ),
        "ctx",
    )
    return (
        layer_output,
        loss_value,
        grad_tokens,
        totals[0],
        totals[1],
        totals[2],
        totals[3],
        totals[4],
        totals[5],
        totals[6],
        totals[7],
        totals[8],
        totals[9],
        totals[10],
        totals[11],
        totals[12],
        totals[13],
        totals[14],
    )


F32 = jnp.float32
BF16 = jnp.bfloat16
ANY = pl.BlockSpec(memory_space=pl.ANY)
HBM = pl.BlockSpec(memory_space=pltpu.HBM)
VMEM = pl.BlockSpec(memory_space=pltpu.VMEM)
SMEM = pl.BlockSpec(memory_space=pltpu.SMEM)
NT = (((1,), (1,)), ((), ()))
TN = (((0,), (0,)), ((), ()))
NN = (((1,), (0,)), ((), ()))


def swap_cores(value):
    size = lax.axis_size("ctx")
    return lax.ppermute(value, "ctx", [(i, i ^ 1) for i in range(size)])


def both_cores(value):
    pairs = [[i, i + 1] for i in range(0, lax.axis_size("ctx"), 2)]
    return lax.all_gather(value, "ctx", axis=0, tiled=True, axis_index_groups=pairs)


def swap_chips(value, step):
    size = lax.axis_size("ctx")
    return lax.ppermute(value, "ctx", [(i, i ^ (2 * step)) for i in range(size)])


def swap_planes(value, step):
    size = lax.axis_size("fsdp")
    return lax.ppermute(value, "fsdp", [(i, i ^ step) for i in range(size)])


def trade_chips(value):
    size = lax.axis_size("ctx")
    groups = [[i for i in range(size) if i % 2 == c] for c in (0, 1)]
    return lax.all_to_all(value, "ctx", 0, 0, axis_index_groups=groups, tiled=True)


def trade_planes(value):
    return lax.all_to_all(value, "fsdp", 0, 0, tiled=True)


def shaped(*shape, dtype=BF16):
    return jax.ShapeDtypeStruct(shape, dtype)


def wide(*shape):
    return jax.ShapeDtypeStruct(shape, F32)


def local_call(
    body, outs, where, args, far=(), far_outs=(), scalar=None, scratch=(), after=(), vmem=12, cost=0
):
    args = [
        pltpu.with_memory_space_constraint(a, pltpu.HBM) if i in far else a
        for i, a in enumerate(args)
    ]
    after = list(after)
    many = isinstance(outs, tuple)
    outs = outs if many else (outs,)
    count, made = len(args), len(outs)

    def kernel(where_ref, *refs):
        token = refs[count + len(after) + made]
        token[...] = jnp.zeros(token.shape, token.dtype)
        start = count + len(after)
        body(where_ref, *refs[:count], *refs[start : start + made], *refs[start + made + 1 :])

    def place(i):
        return HBM if i in far_outs else SMEM if i == scalar else VMEM

    results = pl.pallas_call(
        kernel,
        out_shape=(
            *(pltpu.HBM(o.shape, o.dtype) if i in far_outs else o for i, o in enumerate(outs)),
            wide(8, 128),
        ),
        in_specs=[SMEM] + [HBM if i in far else VMEM for i in range(count)] + [ANY] * len(after),
        out_specs=(*(place(i) for i in range(made)), VMEM),
        scratch_shapes=scratch,
        compiler_params=pltpu.CompilerParams(vmem_limit_bytes=vmem << 20),
        cost_estimate=pl.CostEstimate(
            flops=cost * 10**9, transcendentals=0, bytes_accessed=cost * 10**6
        ),
    )(where, *args, *after)
    return (results[:-1] if many else results[0]), results[-1]


def core_rows(core, count):
    return pl.ds(pl.multiple_of(count * core, 16), count)


def rows_at(start, count, align):
    return pl.ds(pl.multiple_of(start, align), count)


def dot(left, right, dims):
    return lax.dot_general(left, right, dims, preferred_element_type=F32)


def run_copies(copies, sems):
    started = [
        pltpu.make_async_copy(source, target, sems.at[i])
        for i, (source, target) in enumerate(copies)
    ]
    for copy in started:
        copy.start()
    for copy in started:
        copy.wait()


def unit_rows(values):
    centred = values - jnp.mean(values, axis=-1, keepdims=True)
    spread = jnp.mean(centred * centred, axis=-1, keepdims=True)
    inverse = lax.rsqrt(spread + EPSILON)
    return centred * inverse, inverse


def unit_back(grad, gain, unit, inverse):
    scaled = grad * gain
    return inverse * (
        scaled
        - jnp.mean(scaled, axis=-1, keepdims=True)
        - unit * jnp.mean(scaled * unit, axis=-1, keepdims=True)
    )


def pack_tokens(where, tokens, segment, valid, out):
    rows, width = tokens.shape
    ids = segment[...]
    line = lax.broadcasted_iota(jnp.int32, (16, rows), 0)
    codes = jnp.where(
        line == 0,
        ids >> 7,
        jnp.where(line == 1, ids & 127, jnp.where(line == 2, valid[...], 0)),
    )
    out[:rows, :] = tokens[...]
    out[rows:, :] = jnp.zeros((16, width), out.dtype)
    out[rows:, :rows] = codes.astype(F32).astype(out.dtype)


def order_chips(where, p0, p1, p2, p3, out):
    rows = p0.shape[0]
    for k, piece in enumerate((p0, p1, p2, p3)):
        out[rows_at(rows * (where[0] ^ k), rows, 16), :] = piece[...]


def far_planes(where, arrived, out):
    part = arrived.shape[0] // 4
    for s in (1, 2, 3):
        out[part * (s - 1) : part * s, :] = arrived[rows_at(part * (where[2] ^ s), part, 16), :]


def pack_projections(where, *refs):
    weights, vectors, long, valid, out = refs[:3], refs[3:11], refs[11], refs[12], refs[13]
    held, small, held_long, sems = refs[14], refs[15:23], refs[23], refs[24]
    half, feat = held.shape[1], small[0].shape[0]
    own_rows = rows_at(half * where[1], half, 32)
    run_copies(
        [(w.at[own_rows], held.at[i]) for i, w in enumerate(weights)]
        + list(zip(vectors, small))
        + [(long, held_long)],
        sems,
    )
    for chip in range(4):

        @pl.when(where[0] == chip)
        def _():
            for i in range(3):
                out[:, feat * i : feat * (i + 1)] = held[i, :, feat * chip : feat * (chip + 1)]

    spread = held_long[...].astype(F32).reshape(1, 4 * feat)
    count = jnp.sum(valid[...].astype(F32), axis=1, keepdims=True)
    lines = [v[...].astype(F32).reshape(1, feat) for v in small]
    lines += [spread[:, feat * i : feat * (i + 1)] for i in range(4)]
    lines += [jnp.broadcast_to(count, (1, feat)), jnp.zeros((half - 13, feat), F32)]
    out[:, 3 * feat :] = jnp.concatenate(lines, axis=0).astype(out.dtype)


def pack_blocks(where, up, output, down, out_up, out_down, sems):
    chip, core = where[0], where[1]
    part, units = out_up.shape[0] // 4, out_up.shape[1] // 5
    rows = rows_at(part * chip, part, 16)
    down_part = out_down.shape[0]
    copies = []
    for p in range(4):
        block = slice(part * p, part * (p + 1))
        copies += [
            (
                up.at[rows, rows_at(2 * units * i + units * core, units, 128)],
                out_up.at[block, units * i : units * (i + 1)],
            )
            for i in range(4)
        ]
        copies.append(
            (output.at[rows, rows_at(units * core, units, 128)], out_up.at[block, 4 * units :])
        )
    copies.append(
        (down.at[rows_at(4 * down_part * core + down_part * chip, down_part, 32)], out_down)
    )
    run_copies(copies, sems)


def stack_rows(where, *refs):
    pieces, out = refs[:-1], refs[-1]
    rows = pieces[0].shape[0]
    for i, piece in enumerate(pieces):
        out[rows * i : rows * (i + 1), :] = piece[...]


def three_blocks(pieces, part):
    p0, p1, p2, low, high = pieces
    parts = [(k, [(p, 0)]) for k, p in enumerate((p0, p1, p2))] + [(3, [(low, 0), (high, low.shape[0])])]
    found = []
    for k, refs in parts:
        for s in (1, 2, 3):
            for ref, base in refs:
                start, end = max(part * (s - 1), base), min(part * s, base + ref.shape[0])
                if start < end:
                    found.append((k, s, start - part * (s - 1), end - start, ref, start - base))
    return found


def cross_halves(where, from_x, from_y, to_x, to_y):
    cut = to_x.shape[0]
    to_x[...] = from_y[:cut, :]
    to_y[...] = from_x[cut:, :]


def build_up(where, up, p0, p1, p2, p3, p4, out, sems):
    chip, core, plane = where[0], where[1], where[2]
    units, shard = up.shape[1] // 8, up.shape[0]
    part = shard // 4
    own = rows_at(shard * plane, shard, 64)
    copies = [
        pltpu.make_async_copy(
            up.at[:, rows_at(2 * units * i + units * core, units, 128)],
            out.at[own, units * i : units * (i + 1)],
            sems.at[i],
        )
        for i in range(4)
    ]
    for copy in copies:
        copy.start()
    for k, s, offset, count, piece, start in three_blocks((p0, p1, p2, p3, p4), part):
        at = rows_at(shard * (plane ^ s) + part * (chip ^ k) + offset, count, 16)
        out[at, :] = piece[start : start + count, : 4 * units]
    for copy in copies:
        copy.wait()


def build_half(where, output, p0, p1, p2, p3, p4, out, sem):
    chip, core, plane = where[0], where[1], where[2]
    shard, units = output.shape[0], out.shape[1]
    part = shard // 4
    own = pltpu.make_async_copy(
        output.at[:, rows_at(units * core, units, 128)],
        out.at[rows_at(shard * plane, shard, 64)],
        sem,
    )
    own.start()
    for k, s, offset, count, piece, start in three_blocks((p0, p1, p2, p3, p4), part):
        at = rows_at(shard * (plane ^ s) + part * (chip ^ k) + offset, count, 16)
        out[at, :] = piece[start : start + count, 4 * units :]
    own.wait()


def build_down(where, down, p0, p1, p2, p3, p4, out, sem):
    chip, core, plane = where[0], where[1], where[2]
    mine = down.shape[0] // 2
    part = mine // 4
    own = pltpu.make_async_copy(
        down.at[rows_at(mine * core, mine, 128)], out.at[rows_at(mine * plane, mine, 128)], sem
    )
    own.start()
    for k, s, offset, count, piece, start in three_blocks((p0, p1, p2, p3, p4), part):
        at = rows_at(mine * (plane ^ s) + part * (chip ^ k) + offset, count, 16)
        out[at, :] = piece[start : start + count, :]
    own.wait()


def build_output(where, near, far, out):
    units = near.shape[1]
    out[:, rows_at(units * where[1], units, 128)] = near[...]
    out[:, rows_at(units * (1 - where[1]), units, 128)] = far[...]


def normalize_tokens(where, near, far, unit_low, key_row, query_column):
    rows = query_column.shape[0] // 4
    for i in range(8):
        block = (near if i < 4 else far).at[(rows + 16) * (i % 4) : (rows + 16) * (i % 4 + 1), :]
        unit, _ = unit_rows(block[:rows, :].astype(F32))
        unit_low[rows * i : rows * (i + 1), :] = unit
        codes = block[rows:, :].astype(F32)
        ids = codes[0:1, :rows] * 128.0 + codes[1:2, :rows]
        key_row[0:1, rows * i : rows * (i + 1)] = jnp.where(codes[2:3, :rows] == 1.0, ids, -1.0)
        if i < 4:
            query_column[rows * i : rows * (i + 1), :] = jnp.broadcast_to(
                ids.reshape(rows, 1), (rows, 128)
            )


def attend(where, *refs):
    units, key_row, query_column, weights, far_weights = refs[:3] + (refs[3:7], refs[7])
    saved, sent, vectors, long = refs[8:13], refs[13], refs[14], refs[15]
    small, bias, h_one, w_three, projected, probs, mixed, sems = refs[16:]
    kept = (h_one, w_three, projected, mixed)
    copies = [
        pltpu.make_async_copy(source, saved[i], sems.at[j])
        for j, (i, source) in enumerate(zip((0, 1, 2, 4), kept))
    ]
    core, plane = where[1], where[2]
    half, width = weights[0].shape
    feat = width // 4
    group = query_column.shape[0]
    rows = group // 4

    count = jnp.zeros((1, 1), F32)
    for s, piece in enumerate(weights):
        base = 2 * half * (plane ^ s)
        w_three[rows_at(base + half * core, half, 32), :] = piece[:, : 3 * feat]
        other = far_weights[half * s : half * (s + 1), :]
        w_three[rows_at(base + half * (1 - core), half, 32), :] = other[:, : 3 * feat]
        near = piece[:16, 3 * feat :].astype(F32)
        small[plane ^ s] = near
        count += near[12:13, :1] + other[12:13, 3 * feat : 3 * feat + 1].astype(F32)
    vectors[...] = jnp.zeros(vectors.shape, F32)
    for p in range(4):
        lines = small[p]
        for i, r in enumerate((0, 1, 4, 5, 6, 7)):
            vectors[i : i + 1, feat * p : feat * (p + 1)] = lines[r : r + 1, :]
        pair = jnp.where(core == 0, lines[8:10, :], lines[10:12, :])
        long[:, 2 * feat * p : 2 * feat * p + feat] = pair[:1, :]
        long[:, 2 * feat * p + feat : 2 * feat * (p + 1)] = pair[1:, :]
    gain, shift = vectors[0:1, :], vectors[1:2, :]
    short = small[where[0]]
    copies[1].start()
    h_one[...] = (units[...] * gain + shift).astype(BF16)
    copies[0].start()
    values = dot(h_one[...], w_three[...], NN)
    query = (values[:group, :feat] + short[2:3, :]).astype(BF16) * jnp.asarray(
        HEAD_DIM**-0.5, BF16
    )
    projected[:group, :feat] = query
    projected[group:, :feat] = jnp.zeros((group, feat), BF16)
    projected[:, feat : 2 * feat] = values[:, feat : 2 * feat].astype(BF16)
    projected[:, 2 * feat :] = (values[:, 2 * feat :] + short[3:4, :]).astype(BF16)
    copies[2].start()
    column = lax.broadcasted_iota(jnp.int32, (rows, 2 * group), 1)
    line = lax.broadcasted_iota(jnp.int32, (rows, 2 * group), 0)
    for k in range(4):
        ids = query_column[rows * k : rows * (k + 1), :1]
        allowed = (ids == key_row[0:1, :]) | (column == line + rows * k)
        bias[rows * k : rows * (k + 1), :] = jnp.where(allowed, 0.0, MASKED)
    for h in range(feat // HEAD_DIM):
        at = slice(HEAD_DIM * h, HEAD_DIM * (h + 1))
        keys = projected[:, feat + HEAD_DIM * h : feat + HEAD_DIM * (h + 1)]
        held = projected[:, 2 * feat + HEAD_DIM * h : 2 * feat + HEAD_DIM * (h + 1)]
        for k in range(4):
            block = slice(rows * k, rows * (k + 1))
            scores = dot(projected[block, at], keys, NT) + bias[block, :]
            weight = jnp.exp(scores - jnp.max(scores, axis=1, keepdims=True))
            weight = weight * (1.0 / jnp.sum(weight, axis=1, keepdims=True))
            low = weight.astype(BF16)
            probs[h, block, :] = low
            result = dot(low, held, NN)
            mixed[block, at] = result
            sent[(rows + 16) * k : (rows + 16) * k + rows, at] = result.astype(BF16)
        copies.append(pltpu.make_async_copy(probs.at[h], saved[3].at[h], sems.at[4 + h]))
        copies[-1].start()
    copies[3].start()
    high = jnp.floor(count / 128.0)
    side = lax.broadcasted_iota(jnp.int32, (16, feat), 1)
    digits = jnp.where(side == 0, high, jnp.where(side == 1, count - 128.0 * high, 0.0))
    for k in range(4):
        sent[(rows + 16) * k + rows : (rows + 16) * (k + 1), :] = digits.astype(BF16)
    for copy in copies:
        copy.wait()


def attend_back(where, d_all, vectors, *refs):
    saved, (near, far, kept, given, lines) = refs[:5], refs[5:10]
    d_three, d_scores, grads, h_one, w_three, projected, probs, mixed, sems = refs[10:]
    core = where[1]
    pairs = [(saved[2], projected), (saved[4], mixed)]
    pairs += [(saved[3].at[h], probs.at[h]) for h in range(probs.shape[0])]
    pairs += [(saved[0], h_one), (saved[1], w_three)]
    copies = [pltpu.make_async_copy(a, b, sems.at[i]) for i, (a, b) in enumerate(pairs)]
    for copy in copies:
        copy.start()
    copies[0].wait()
    copies[1].wait()
    group, feat = d_all.shape
    rows, width = group // 4, h_one.shape[1]
    scale = HEAD_DIM**-0.5
    d_three[group:, :feat] = jnp.zeros((group, feat), BF16)
    for h in range(feat // HEAD_DIM):
        at = slice(HEAD_DIM * h, HEAD_DIM * (h + 1))
        key_at = slice(feat + HEAD_DIM * h, feat + HEAD_DIM * (h + 1))
        value_at = slice(2 * feat + HEAD_DIM * h, 2 * feat + HEAD_DIM * (h + 1))
        keys, held = projected[:, key_at], projected[:, value_at]
        copies[2 + h].wait()
        for k in range(4):
            block = slice(rows * k, rows * (k + 1))
            d_mixed = d_all[block, at]
            delta = jnp.sum(d_mixed.astype(F32) * mixed[block, at], axis=1, keepdims=True)
            d_probs = dot(d_mixed, held, NT)
            low = (probs[h, block, :].astype(F32) * (d_probs - delta)).astype(BF16)
            d_scores[block, :] = low
            d_three[block, at] = (dot(low, keys, NN) * scale).astype(BF16)
        d_three[:, key_at] = dot(d_scores[...], projected[:group, at], TN).astype(BF16)
        d_three[:, value_at] = dot(probs[h], d_all[:, at], TN).astype(BF16)
    for copy in copies[2 + probs.shape[0] :]:
        copy.wait()
    grads[...] = dot(h_one[...], d_three[...], TN)
    near[...] = dot(d_three[:group, :], w_three[...], NT).astype(BF16)
    far[...] = dot(d_three[group:, :], w_three[...], NT).astype(BF16)
    half = kept.shape[0] // 4
    for p in range(4):
        block = slice(half * p, half * (p + 1))
        kept[block, :] = grads[rows_at(2 * half * p + half * core, half, 32), :].astype(BF16)
        given[block, :] = grads[rows_at(2 * half * p + half * (1 - core), half, 32), :].astype(BF16)
    sums = jnp.sum(d_three[...].astype(F32), axis=0, keepdims=True)
    weight = w_three[...].astype(F32)
    with_gain = jnp.sum(grads[...] * weight, axis=1, keepdims=True)
    with_shift = jnp.sum(weight * sums, axis=1, keepdims=True)
    side = lax.broadcasted_iota(jnp.int32, (width, 128), 1)
    both = jnp.where(side == 0, with_gain, jnp.where(side == 1, with_shift, 0.0)).T
    d_shift = both[1:2, :]
    lines[0:1, :] = (both[0:1, :] - vectors[1:2, :] * d_shift) / vectors[0:1, :]
    lines[1:2, :] = d_shift
    lines[2:3, :] = jnp.zeros((1, width), F32)
    lines[2:3, :feat] = sums[:, :feat]
    lines[3:4, :] = jnp.zeros((1, width), F32)
    lines[3:4, :feat] = sums[:, 2 * feat :]
    lines[4:, :] = jnp.zeros((4, width), F32)


def share_inputs(where, near, far, *outs):
    rows = outs[0].shape[0]
    for k, out in enumerate(outs):
        at = rows_at(rows * (where[0] ^ k), rows, 16)
        out[...] = (near[at, :].astype(F32) + far[at, :].astype(F32)).astype(out.dtype)


def finish_inputs(where, d0, d1, d2, d3, tokens, d_second, vectors, out):
    total = d0[...].astype(F32)
    for piece in (d1, d2, d3):
        total = total + piece[...].astype(F32)
    unit, inverse = unit_rows(tokens[...].astype(F32))
    d_inputs = unit_back(total, vectors[0:1, :], unit, inverse)
    out[...] = (d_second[...] + d_inputs).astype(BF16)


def project_output(where, mixed, w_output, tokens, vectors, second, h_two, count):
    rows, width = tokens.shape
    feat = mixed.shape[1]
    total = tokens[...].astype(F32) + vectors[2:3, :]
    valid = jnp.zeros((1, 1), F32)
    for k in range(4):
        start = (rows + 16) * k
        total += dot(mixed[start : start + rows, :], w_output[feat * k : feat * (k + 1), :], NN)
        digits = mixed[start + rows : start + rows + 16, :].astype(F32)
        valid += digits[0:1, 0:1] * 128.0 + digits[0:1, 1:2]
    second[...] = total
    unit, _ = unit_rows(total)
    h_two[...] = (unit * vectors[3:4, :] + vectors[4:5, :]).astype(BF16)
    count[...] = jnp.broadcast_to(valid, count.shape)


def activate(where, h_pair, w_up, b_up, act, slope):
    rows = h_pair.shape[0] // 2
    root = 0.7978845608028654
    for i in range(2):
        block = slice(rows * i, rows * (i + 1))
        value = dot(h_pair[block, :], w_up[...], NN) + b_up[...]
        square = value * value
        bent = jnp.tanh(root * value * (1.0 + 0.044715 * square))
        act[block, :] = (0.5 * value * (1.0 + bent)).astype(BF16)
        slope[block, :] = 0.5 * (1.0 + bent) + 0.5 * value * (1.0 - bent * bent) * root * (
            1.0 + 3.0 * 0.044715 * square
        )


def project_down(where, act, w_down, near, far):
    rows, core = near.shape[0], where[1]
    near[...] = dot(act[core_rows(core, rows), :], w_down[...], NN)
    far[...] = dot(act[core_rows(1 - core, rows), :], w_down[...], NN).astype(BF16)


def compare(where, second, near, far, vectors, teacher, cotangent, valid, count, *outs):
    layer_output, d_result, d_down, lines = outs
    rows, width = second.shape
    other = far[core_rows(1 - where[1], rows), :].astype(F32)
    result = second[...] + near[...] + other + vectors[5:6, :]
    layer_output[...] = result.astype(BF16)
    kept = valid[...].astype(F32).reshape(rows, 1)
    mismatch = result - teacher[...].astype(F32)
    weighted = kept * mismatch
    error = jnp.sum(jnp.sum(weighted * mismatch, axis=1, keepdims=True), axis=0, keepdims=True)
    total = cotangent[...].astype(F32) + 2.0 / (width * count[0:1, 0:1]) * weighted
    d_result[...] = total
    low = total.astype(BF16)
    d_down[...] = low
    high = error.astype(BF16).astype(F32)
    middle = (error - high).astype(BF16).astype(F32)
    side = lax.broadcasted_iota(jnp.int32, (1, width), 1)
    parts = jnp.where(
        side == 0, high, jnp.where(side == 1, middle, jnp.where(side == 2, error - high - middle, 0.0))
    )
    lines[0:1, :] = jnp.sum(low.astype(F32), axis=0, keepdims=True)
    lines[1:2, :] = parts
    lines[2:, :] = jnp.zeros((6, width), F32)


def activate_back(where, d_down, w_down, slope, w_up, d_up, near, far, line):
    rows, core = near.shape[0], where[1]
    total = jnp.zeros(line.shape, F32)
    for i in range(2):
        block = slice(rows * i, rows * (i + 1))
        low = (dot(d_down[block, :], w_down[...], NT) * slope[block, :]).astype(BF16)
        d_up[block, :] = low
        total += jnp.sum(low.astype(F32), axis=0, keepdims=True)
    line[...] = total
    near[...] = dot(d_up[core_rows(core, rows), :], w_up[...], NT)
    far[...] = dot(d_up[core_rows(1 - core, rows), :], w_up[...], NT).astype(BF16)


def second_back(where, near, far, d_result, second, vectors, w_output, *outs):
    d_second, d_attn, lines, sent = outs
    rows = near.shape[0]
    d_two = near[...] + far[core_rows(1 - where[1], rows), :].astype(F32)
    unit, inverse = unit_rows(second[...])
    total = d_result[...] + unit_back(d_two, vectors[3:4, :], unit, inverse)
    d_second[...] = total
    low = total.astype(BF16)
    d_attn[...] = low
    lines[0:1, :] = jnp.sum(low.astype(F32), axis=0, keepdims=True)
    lines[1:2, :] = jnp.sum(d_two * unit, axis=0, keepdims=True)
    lines[2:3, :] = jnp.sum(d_two, axis=0, keepdims=True)
    lines[3:, :] = jnp.zeros((5, lines.shape[1]), F32)
    feat = sent.shape[1]
    for k in range(4):
        part = w_output[feat * k : feat * (k + 1), :]
        sent[rows * k : rows * (k + 1), :] = dot(low, part, NT).astype(BF16)


def split_chips(chip, block, outs, count):
    own, to_x, to_y, then_x, then_y = outs
    for p in range(4):
        own[count * p : count * (p + 1), :] = block(chip, p).astype(BF16)
    for p in (0, 1):
        low, high = slice(count * p, count * (p + 1)), slice(count * (p + 2), count * (p + 3))
        to_x[low, :] = block(chip ^ 1, p).astype(BF16)
        to_x[high, :] = block(chip ^ 3, p).astype(BF16)
        to_y[low, :] = block(chip ^ 2, p + 2).astype(BF16)
        to_y[high, :] = block(chip ^ 3, p + 2).astype(BF16)
        then_x[low, :] = block(chip ^ 1, p + 2).astype(BF16)
        then_y[low, :] = block(chip ^ 2, p).astype(BF16)


def pass_on(where, from_x, from_y, then_x, then_y, to_x, to_y):
    half = to_x.shape[0]
    to_x[...] = (then_x[...].astype(F32) + from_y[half:, :].astype(F32)).astype(BF16)
    to_y[...] = (then_y[...].astype(F32) + from_x[half:, :].astype(F32)).astype(BF16)


def add_chips(own, from_x, from_y, last_x, last_y):
    half = last_x.shape[0]
    low = own[:half, :].astype(F32) + from_x[:half, :].astype(F32) + last_y[...].astype(F32)
    high = own[half:, :].astype(F32) + from_y[:half, :].astype(F32) + last_x[...].astype(F32)
    return low, high


def down_grads(where, act, d_down, *refs):
    outs, total = refs[:5], refs[5]
    count = outs[0].shape[0] // 4
    total[...] = dot(act[...], d_down[...], TN)

    def block(j, p):
        return total[rows_at(4 * count * p + count * j, count, 32), :]

    split_chips(where[0], block, outs, count)


def up_grads(where, h_pair, d_up, mixed, d_attn, *refs):
    outs, total = refs[:5], refs[5]
    count, units = outs[0].shape[0] // 4, d_up.shape[1]
    total[:, :units] = dot(h_pair[...], d_up[...], TN)
    rows, width = d_attn.shape[0] // 2, d_attn.shape[1]
    feat = mixed.shape[1]
    columns = d_attn[:, rows_at(width // 2 * where[1], width // 2, 128)]
    for j in range(4):
        product = 0.0
        for i in range(2):
            start = 4 * (rows + 16) * i + (rows + 16) * j
            product += dot(mixed[start : start + rows, :], columns[rows * i : rows * (i + 1), :], TN)
        total[feat * j : feat * (j + 1), units:] = product

    def block(j, p):
        return total[rows_at(4 * count * p + count * j, count, 16), :]

    split_chips(where[0], block, outs, count)


def send_planes(where, own, from_x, from_y, last_x, last_y, *refs):
    outs, total = refs[:4], refs[4]
    part, half = outs[0].shape[0], last_x.shape[0]
    total[:half, :], total[half:, :] = add_chips(own, from_x, from_y, last_x, last_y)
    for s, out in enumerate(outs):
        out[...] = total[rows_at(part * (where[2] ^ s), part, 16), :].astype(out.dtype)


def sum_pieces(where, own, p1, p2, p3, out):
    total = own[...].astype(F32)
    for piece in (p1, p2, p3):
        total = total + piece[...].astype(F32)
    out[...] = total.astype(out.dtype)


def finish_down(where, near, far, out, held, sems):
    core = where[1]
    both = near.shape[0] // 4
    part = both // 2
    copies = []
    for j in range(4):
        block = slice(both * j + part, both * (j + 1))
        for side, piece in ((core, near), (1 - core, far)):
            at = rows_at(4 * part * side + part * j, part, 32)
            held[at, :] = piece[block, :].astype(F32)
            copies.append(pltpu.make_async_copy(held.at[at], out.at[at], sems.at[len(copies)]))
            copies[-1].start()
    for copy in copies:
        copy.wait()


def finish_up(where, n0, n1, n2, n3, far, out, out_half, held, held_half, sems):
    chip, core = where[0], where[1]
    part, units = n0.shape[0], n0.shape[1] // 5
    copies = []
    for k, near in enumerate((n0, n1, n2, n3)):
        rows = rows_at(part * (chip ^ k), part, 16)
        for piece, side in ((near[...], core), (far[part * k : part * (k + 1), :], 1 - core)):
            full = piece.astype(F32)
            for i in range(4):
                at = rows_at(2 * units * i + units * side, units, 128)
                held[rows, at] = full[:, units * i : units * (i + 1)]
            held_half[rows, rows_at(units * side, units, 128)] = full[:, 4 * units :]
        for source, target in ((held, out), (held_half, out_half)):
            copies.append(
                pltpu.make_async_copy(source.at[rows], target.at[rows], sems.at[len(copies)])
            )
            copies[-1].start()
    for copy in copies:
        copy.wait()


def sum_chips(where, own, from_x, from_y, last_x, last_y, out):
    half = last_x.shape[0]
    low, high = add_chips(own, from_x, from_y, last_x, last_y)
    out[:half, :], out[half:, :] = low.astype(BF16), high.astype(BF16)


def pack_gradients(
    where, kept, given, from_attention, from_second, from_result, up_line, down, out, down_sum
):
    chip = where[0]
    part = down_sum.shape[0]
    arrived_down = down[:part, :].astype(F32)
    for p in (1, 2, 3):
        arrived_down = arrived_down + down[part * p : part * (p + 1), :].astype(F32)
    down_sum[...] = arrived_down.astype(BF16)
    half, width = out.shape[0] // 4, out.shape[1]
    feat = width // 4
    for p in range(4):
        cut = slice(feat * p, feat * (p + 1))
        owner = jnp.where(chip == p, 1.0, 0.0)
        lines = [
            from_attention[0:1, cut],
            from_attention[1:2, cut],
            from_second[0:1, cut],
            from_second[1:2, cut],
            from_second[2:3, cut],
            from_result[0:1, cut],
            up_line[:, 2 * feat * p : 2 * feat * p + feat],
            up_line[:, 2 * feat * p + feat : 2 * feat * (p + 1)],
            from_attention[2:3, :feat] * owner,
            from_attention[3:4, :feat] * owner,
            from_result[1:2, :feat],
            jnp.zeros((half - 11, feat), F32),
        ]
        small = jnp.concatenate(lines, axis=0).astype(BF16)
        block = slice(half * p, half * (p + 1))
        arrived = given[rows_at(4 * half * (1 - where[1]) + half * p, half, 32), :]
        total = (kept[block, :].astype(F32) + arrived.astype(F32)).astype(BF16)
        out[block, : 3 * feat] = total
        out[block, 3 * feat :] = small


def sum_planes(where, arrived, down, out):
    both, width = out.shape[0] // 4, out.shape[1]
    half, feat = both // 2, width // 4
    total = arrived[:half, :].astype(F32)
    for p in (1, 2, 3):
        total = total + arrived[half * p : half * (p + 1), :].astype(F32)
    small = total[:16, 3 * feat :]
    error = jnp.sum(small[10:11, :3], axis=1, keepdims=True)
    high = error.astype(BF16).astype(F32)
    middle = (error - high).astype(BF16).astype(F32)
    line = lax.broadcasted_iota(jnp.int32, small.shape, 0)
    side = lax.broadcasted_iota(jnp.int32, small.shape, 1)
    parts = jnp.where(side == 0, high, jnp.where(side == 1, middle, error - high - middle))
    small = jnp.where((line == 10) & (side < 3), parts, small)
    for j in range(4):
        start = both * j
        out[start : start + half, : 3 * feat] = total[:, : 3 * feat].astype(BF16)
        out[start : start + 16, 3 * feat :] = small.astype(BF16)
        out[start + 16 : start + half, 3 * feat :] = jnp.zeros((half - 16, feat), BF16)
        out[start + half : start + both, :] = down[...]


def finish_projections(where, near, far, count, *outs):
    query, key, value, loss = outs[:4]
    flat, up_line, held, whole_line = outs[4:12], outs[12], outs[13], outs[14]
    core = where[1]
    both, width = near.shape[0] // 4, near.shape[1]
    half, feat = both // 2, width // 4
    for j in range(4):
        start = both * j
        for side, piece in ((core, near), (1 - core, far)):
            held[2 * j + side] = piece[start : start + 16, 3 * feat :].astype(F32)
            rows = rows_at(half * side, half, 32)
            for i, out in enumerate((query, key, value)):
                out[rows, feat * j : feat * (j + 1)] = piece[
                    start : start + half, feat * i : feat * (i + 1)
                ].astype(F32)
    total = held[0]
    for i in range(1, 8):
        total = total + held[i]
    for i, line in enumerate((0, 1, 2, 3, 4, 5, 8, 9)):
        flat[i][...] = total[line]
    even = held[0] + held[2] + held[4] + held[6]
    odd = held[1] + held[3] + held[5] + held[7]
    for side, part in enumerate((even, odd)):
        for i in range(2):
            at = 2 * feat * side + feat * i
            whole_line[0:1, at : at + feat] = part[6 + i : 7 + i, :]
    up_line[...] = whole_line[0]
    error = jnp.sum(total[10:11, :3], axis=1, keepdims=True)
    loss[0, 0] = jnp.sum(error / (width * count[0:1, 0:1]))


def layer(
    tokens,
    segment_ids,
    valid_rows,
    teacher,
    cotangent,
    first_gain,
    first_shift,
    query_weight,
    query_bias,
    key_weight,
    value_weight,
    value_bias,
    output_weight,
    output_bias,
    second_gain,
    second_shift,
    up_weight,
    up_bias,
    down_weight,
    down_bias,
):
    rows, width = tokens.shape[1], tokens.shape[2]
    shard = query_weight.shape[0]
    half, quarter = shard // 2, shard // 4
    hidden = up_weight.shape[1]
    units = hidden // 2
    own_units = down_weight.shape[0]
    core_units = own_units // 2
    part_units = core_units // 4
    feat = width // 4
    heads = feat // HEAD_DIM
    group = 4 * rows
    every = 2 * group
    steps = (1, 2, 3)

    place, plane = lax.axis_index("ctx"), lax.axis_index("fsdp")
    where = jnp.stack([place // 2, place % 2, plane]).astype(jnp.int32)
    dma = pltpu.SemaphoreType.DMA

    last = []

    def step(body, outs, args, **options):
        made, token = local_call(body, outs, where, args, after=last, **options)
        last[:] = [token]
        return made

    def stack(pieces, cost=0):
        shape = len(pieces) * pieces[0].shape[0], pieces[0].shape[1]
        return step(stack_rows, shaped(*shape), pieces, cost=cost)

    own = tokens[0]
    smalls = (
        first_gain,
        first_shift,
        query_bias,
        value_bias,
        output_bias,
        second_gain,
        second_shift,
        down_bias,
    )
    up_piece, down_piece = step(
        pack_blocks,
        (shaped(4 * quarter, 5 * core_units), shaped(part_units, width)),
        (up_weight, output_weight, down_weight),
        far=range(3),
        scratch=[dma((21,))],
    )
    up_far = trade_planes(up_piece)
    bundle = step(pack_tokens, shaped(rows + 16, width), (own, segment_ids, valid_rows), cost=50)
    near_tokens = [bundle] + [swap_chips(bundle, k) for k in steps]
    projections = step(
        pack_projections,
        shaped(half, width),
        (query_weight, key_weight, value_weight, *smalls, up_bias, valid_rows),
        far=range(12),
        scratch=[
            pltpu.VMEM((3, half, width), BF16),
            *[pltpu.VMEM((feat,), BF16)] * 8,
            pltpu.VMEM((own_units,), BF16),
            dma((12,)),
        ],
        cost=0,
    )
    near_tokens = step(order_chips, shaped(4 * (rows + 16), width), near_tokens, cost=0)
    far_tokens = swap_cores(near_tokens)
    up_far = step(far_planes, shaped(3 * quarter, 5 * core_units), (up_far,), cost=0)
    up_three = up_far, swap_chips(up_far, 1), swap_chips(up_far, 2)
    near_weights = [projections] + [swap_planes(projections, s) for s in steps]
    unit_one, key_row, query_column = step(
        normalize_tokens,
        (wide(every, width), wide(8, every), wide(group, 128)),
        (near_tokens, far_tokens),
        cost=1,
    )
    far_weights = swap_cores(stack(near_weights))

    def first_chips(piece):
        return piece, swap_chips(piece, 1), swap_chips(piece, 2)

    def all_chips(three, cut):
        count, lanes = three[0].shape
        to_x, to_y = step(cross_halves, (shaped(cut, lanes), shaped(count - cut, lanes)), three[1:], cost=50)
        return (*three, swap_chips(to_x, 1), swap_chips(to_y, 2))

    up_all = all_chips(up_three, up_far.shape[0] // 32 * 16 + 16)
    down_far = [swap_planes(down_piece, s) for s in steps]

    h_one, w_three, projected, probs, mixed, sent, vectors, b_up = step(
        attend,
        (
            shaped(every, width),
            shaped(width, 3 * feat),
            shaped(every, 3 * feat),
            shaped(heads, group, every),
            wide(group, feat),
            shaped(4 * (rows + 16), feat),
            wide(8, width),
            wide(1, units),
        ),
        (unit_one, key_row, query_column, *near_weights, far_weights),
        far_outs=range(5),
        scratch=[
            pltpu.VMEM((4, 16, feat), F32),
            pltpu.VMEM((group, every), F32),
            pltpu.VMEM((every, width), BF16),
            pltpu.VMEM((width, 3 * feat), BF16),
            pltpu.VMEM((every, 3 * feat), BF16),
            pltpu.VMEM((heads, group, every), BF16),
            pltpu.VMEM((group, feat), F32),
            dma((4 + heads,)),
        ],
        vmem=28,
        cost=50,
    )
    mixed_low = trade_chips(sent)
    down_far = first_chips(stack(down_far))
    out_near = step(
        build_half,
        shaped(width, core_units),
        (output_weight, *up_all),
        far=(0,),
        scratch=[dma],
    )
    out_far = swap_cores(out_near)
    w_up = step(
        build_up, shaped(width, units), (up_weight, *up_all), far=(0,), scratch=[dma((4,))], cost=50
    )
    w_output = step(build_output, shaped(width, width), (out_near, out_far))

    second, h_two, count = step(
        project_output,
        (wide(rows, width), shaped(rows, width), wide(8, 128)),
        (mixed_low, w_output, own, vectors),
    )
    h_pair = both_cores(h_two)
    mixed_pair = both_cores(mixed_low)
    down_all = all_chips(down_far, down_far[0].shape[0] // 2)
    act, slope = step(
        activate,
        (shaped(2 * rows, units), wide(2 * rows, units)),
        (h_pair, w_up, b_up),
    )
    w_down = step(
        build_down, shaped(units, width), (down_weight, *down_all), far=(0,), scratch=[dma]
    )
    down_near, down_other = step(
        project_down, (wide(rows, width), shaped(rows, width)), (act, w_down)
    )
    layer_output, d_result, d_down, from_result = step(
        compare,
        (shaped(rows, width), wide(rows, width), shaped(rows, width), wide(8, width)),
        (
            second,
            down_near,
            both_cores(down_other),
            vectors,
            teacher[0],
            cotangent[0],
            valid_rows,
            count,
        ),
    )
    d_down = both_cores(d_down)

    def five(count, lanes):
        return (shaped(4 * count, lanes),) * 3 + (shaped(2 * count, lanes),) * 2

    def onward(parts, arrived):
        count, lanes = parts[3].shape
        to_x, to_y = step(pass_on, (shaped(count, lanes),) * 2, (*arrived, *parts[3:]), cost=50)
        return (parts[0], *arrived, swap_chips(to_x, 1), swap_chips(to_y, 2))

    down_parts = step(
        down_grads,
        five(part_units, width),
        (act, d_down),
        scratch=[pltpu.VMEM((units, width), F32)],
        vmem=24,
    )
    down_arrived = swap_chips(down_parts[1], 1), swap_chips(down_parts[2], 2)
    d_up, two_near, two_other, up_line = step(
        activate_back,
        (shaped(2 * rows, units), wide(rows, width), shaped(rows, width), wide(1, units)),
        (d_down, w_down, slope, w_up),
        cost=50,
    )
    d_second, d_attn, from_second, d_sent = step(
        second_back,
        (wide(rows, width), shaped(rows, width), wide(8, width), shaped(group, feat)),
        (two_near, both_cores(two_other), d_result, second, vectors, w_output),
    )
    d_mixed = trade_chips(d_sent)

    down_sums = onward(down_parts, down_arrived)
    attn_pair = both_cores(d_attn)
    up_parts = step(
        up_grads,
        five(quarter, 5 * core_units),
        (h_pair, d_up, mixed_pair, attn_pair),
        scratch=[pltpu.VMEM((width, 5 * core_units), F32)],
        vmem=24,
        cost=2,
    )
    up_arrived = swap_chips(up_parts[1], 1), swap_chips(up_parts[2], 2)
    down_planes = trade_planes(step(sum_chips, shaped(4 * part_units, width), down_sums))

    d_near, d_far, kept, given, from_attention = step(
        attend_back,
        (
            shaped(group, width),
            shaped(group, width),
            shaped(4 * half, 3 * feat),
            shaped(4 * half, 3 * feat),
            wide(8, width),
        ),
        (d_mixed, vectors, h_one, w_three, projected, probs, mixed),
        far=range(2, 7),
        scratch=[
            pltpu.VMEM((every, 3 * feat), BF16),
            pltpu.VMEM((group, every), BF16),
            pltpu.VMEM((width, 3 * feat), F32),
            pltpu.VMEM((every, width), BF16),
            pltpu.VMEM((width, 3 * feat), BF16),
            pltpu.VMEM((every, 3 * feat), BF16),
            pltpu.VMEM((heads, group, every), BF16),
            pltpu.VMEM((group, feat), F32),
            dma((4 + heads,)),
        ],
        vmem=28,
        cost=50,
    )
    d_far = swap_cores(d_far)
    up_sums = onward(up_parts, up_arrived)
    given = both_cores(given)
    arrived, down_planes = step(
        pack_gradients,
        (shaped(4 * half, width), shaped(part_units, width)),
        (kept, given, from_attention, from_second, from_result, up_line, down_planes),
        cost=1,
    )
    arrived = trade_planes(arrived)

    def spread(piece):
        return [piece] + [swap_chips(piece, k) for k in steps]

    def whole(near):
        return (*near, swap_cores(stack(near, cost=1)))

    up_planes = step(
        send_planes,
        (shaped(quarter, 5 * core_units),) * 4,
        up_sums,
        scratch=[pltpu.VMEM((4 * quarter, 5 * core_units), F32)],
        cost=50,
    )
    up_planes = [up_planes[0]] + [swap_planes(up_planes[s], s) for s in steps]
    shares = step(share_inputs, (shaped(rows, width),) * 4, (d_near, d_far), cost=50)
    shares = [shares[0]] + [swap_chips(shares[k], k) for k in steps]
    both = trade_chips(step(sum_planes, shaped(8 * half, width), (arrived, down_planes), cost=50))
    up_near = spread(step(sum_pieces, shaped(quarter, 5 * core_units), up_planes, cost=50))
    grad_tokens = step(finish_inputs, shaped(rows, width), (*shares, own, d_second, vectors), cost=50)
    both = (both, swap_cores(both))
    finished = step(
        finish_projections,
        (wide(shard, width),) * 3
        + (wide(1, 1),)
        + (wide(shard),) * 8
        + (wide(own_units),),
        (*both, count),
        scratch=[pltpu.VMEM((8, 16, feat), F32), pltpu.VMEM((8, own_units), F32)],
        scalar=3,
        cost=50,
    )
    grad_down_weight = step(
        finish_down,
        wide(own_units, width),
        both,
        far_outs=(0,),
        scratch=[pltpu.VMEM((own_units, width), F32), dma((8,))],
    )
    grad_up_weight, grad_output_weight = step(
        finish_up,
        (wide(shard, hidden), wide(shard, width)),
        whole(up_near),
        far_outs=(0, 1),
        scratch=[pltpu.VMEM((shard, hidden), F32), pltpu.VMEM((shard, width), F32), dma((8,))],
    )
    sums, two = finished[4:10], finished[10:12]
    return (
        layer_output[None],
        finished[3].reshape(()),
        grad_tokens[None],
        sums[0],
        sums[1],
        finished[0],
        two[0],
        finished[1],
        finished[2],
        two[1],
        grad_output_weight,
        sums[2],
        sums[3],
        sums[4],
        grad_up_weight,
        finished[12],
        grad_down_weight,
        sums[5],
    )


def solution(mesh):
    body = layer if (mesh.shape["ctx"], mesh.shape["fsdp"]) == (8, 4) else shards
    placed = (
        P("fsdp", "ctx", None),
        P("fsdp", "ctx"),
        P("fsdp", "ctx"),
        P("fsdp", "ctx", None),
        P("fsdp", "ctx", None),
        P("fsdp"),
        P("fsdp"),
        P("fsdp", None),
        P("fsdp"),
        P("fsdp", None),
        P("fsdp", None),
        P("fsdp"),
        P("fsdp", None),
        P("fsdp"),
        P("fsdp"),
        P("fsdp"),
        P("fsdp", None),
        P("fsdp"),
        P("fsdp", None),
        P("fsdp"),
    )
    return jax.shard_map(
        body,
        mesh=mesh,
        in_specs=placed,
        out_specs=(
            P("fsdp", "ctx", None),
            P(),
            P("fsdp", "ctx", None),
            P("fsdp"),
            P("fsdp"),
            P("fsdp", None),
            P("fsdp"),
            P("fsdp", None),
            P("fsdp", None),
            P("fsdp"),
            P("fsdp", None),
            P("fsdp"),
            P("fsdp"),
            P("fsdp"),
            P("fsdp", None),
            P("fsdp"),
            P("fsdp", None),
            P("fsdp"),
        ),
        check_vma=False,
    )
```

```python
import jax
import jax.numpy as jnp
from jax import lax
from jax.experimental import pallas as pl
from jax.experimental.pallas import tpu as pltpu
from jax.sharding import PartitionSpec as P

HEADS = 12
HEAD_DIM = 64


EPSILON = 1e-06
MASKED = -1e30


def norm_rows(values, gain, shift):
    centre = jnp.mean(values, axis=-1, keepdims=True)
    centred = values - centre
    spread = jnp.mean(centred * centred, axis=-1, keepdims=True)
    return centred * lax.rsqrt(spread + EPSILON) * gain + shift


def tanh_gelu(values):
    return jax.nn.gelu(values, approximate=True)


def key_allowed(query_segment, query_place, key_codes, key_place):
    same_doc = query_segment[:, None] == (key_codes // 2)[None, :]
    usable = (key_codes % 2 == 1)[None, :] | (query_place[:, None] == key_place[None, :])
    return (same_doc & usable)[None, :, :]


def split_heads(values):
    return values.reshape(values.shape[0], HEADS, HEAD_DIM)


def head_scores(query_heads, key_heads, scale):
    return (
        jnp.einsum("qhd,khd->hqk", query_heads, key_heads, preferred_element_type=jnp.float32)
        * scale
    )


def row_sum(values):
    return jnp.sum(values, axis=0, dtype=jnp.float32)


def left_product(left, right):
    return jnp.einsum("rd,rf->df", left, right, preferred_element_type=jnp.float32)


def right_product(left, right):
    return jnp.einsum("rf,df->rd", left, right, preferred_element_type=jnp.float32)


def shards(
    tokens,
    segment_ids,
    valid_rows,
    teacher,
    cotangent,
    first_gain,
    first_shift,
    query_weight,
    query_bias,
    key_weight,
    value_weight,
    value_bias,
    output_weight,
    output_bias,
    second_gain,
    second_shift,
    up_weight,
    up_bias,
    down_weight,
    down_bias,
):
    tok_rows = tokens.shape[1]
    feature_width = tokens.shape[2]
    shard_count = lax.axis_size("ctx")
    key_block = 4 * tok_rows
    block_count = shard_count // 4
    scale = HEAD_DIM ** (-0.5)
    gain_one, shift_one, w_query, b_query, w_key, w_value, b_value, w_output, b_output = (
        lax.all_gather(first_gain, "fsdp", axis=0, tiled=True),
        lax.all_gather(first_shift, "fsdp", axis=0, tiled=True),
        lax.all_gather(query_weight, "fsdp", axis=0, tiled=True),
        lax.all_gather(query_bias, "fsdp", axis=0, tiled=True),
        lax.all_gather(key_weight, "fsdp", axis=0, tiled=True),
        lax.all_gather(value_weight, "fsdp", axis=0, tiled=True),
        lax.all_gather(value_bias, "fsdp", axis=0, tiled=True),
        lax.all_gather(output_weight, "fsdp", axis=0, tiled=True),
        lax.all_gather(output_bias, "fsdp", axis=0, tiled=True),
    )
    gain_two, shift_two, w_up, b_up, w_down, b_down = (
        lax.all_gather(second_gain, "fsdp", axis=0, tiled=True),
        lax.all_gather(second_shift, "fsdp", axis=0, tiled=True),
        lax.all_gather(up_weight, "fsdp", axis=0, tiled=True),
        lax.all_gather(up_bias, "fsdp", axis=0, tiled=True),
        lax.all_gather(down_weight, "fsdp", axis=0, tiled=True),
        lax.all_gather(down_bias, "fsdp", axis=0, tiled=True),
    )
    local_segment = segment_ids[0]
    local_valid = valid_rows[0]
    local_codes = local_segment * 2 + local_valid
    all_codes = lax.all_gather(local_codes, "ctx", axis=0, tiled=True)
    query_place = lax.axis_index("ctx") * tok_rows + jnp.arange(tok_rows, dtype=jnp.int32)
    inputs = tokens[0].astype(jnp.float32)
    gain_first = gain_one.astype(jnp.float32)
    shift_first = shift_one.astype(jnp.float32)
    gain_second = gain_two.astype(jnp.float32)
    shift_second = shift_two.astype(jnp.float32)
    h_one = norm_rows(inputs, gain_first, shift_first)
    h_one_low = h_one.astype(jnp.bfloat16)
    query_low = (
        jnp.dot(h_one_low, w_query, preferred_element_type=jnp.float32)
        + b_query.astype(jnp.float32)
    ).astype(jnp.bfloat16)
    key_low = jnp.dot(h_one_low, w_key, preferred_element_type=jnp.float32).astype(jnp.bfloat16)
    value_low = (
        jnp.dot(h_one_low, w_value, preferred_element_type=jnp.float32)
        + b_value.astype(jnp.float32)
    ).astype(jnp.bfloat16)
    key_all, value_all = (
        lax.all_gather(key_low, "ctx", axis=0, tiled=True),
        lax.all_gather(value_low, "ctx", axis=0, tiled=True),
    )
    query_heads = split_heads(query_low)

    def block_rows(source, block_index):
        return split_heads(lax.dynamic_slice_in_dim(source, block_index * key_block, key_block, 0))

    def block_allowed(block_index):
        start = block_index * key_block
        codes = lax.dynamic_slice_in_dim(all_codes, start, key_block, 0)
        return key_allowed(
            local_segment, query_place, codes, start + jnp.arange(key_block, dtype=jnp.int32)
        )

    def stats_step(block_index, state_pair):
        running_max, running_sum = state_pair
        allowed = block_allowed(block_index)
        scores = jnp.where(
            allowed, head_scores(query_heads, block_rows(key_all, block_index), scale), MASKED
        )
        new_max = jnp.maximum(running_max, jnp.max(scores, axis=2))
        weights = jnp.where(allowed, jnp.exp(scores - new_max[:, :, None]), 0.0)
        return (new_max, running_sum * jnp.exp(running_max - new_max) + jnp.sum(weights, axis=2))

    start_max = jnp.full((HEADS, tok_rows), MASKED, jnp.float32)
    start_sum = jnp.zeros((HEADS, tok_rows), jnp.float32)
    running_max, running_sum = lax.fori_loop(0, block_count, stats_step, (start_max, start_sum))
    log_total = running_max + jnp.log(running_sum)

    def mix_step(block_index, mixed_sum):
        allowed = block_allowed(block_index)
        scores = head_scores(query_heads, block_rows(key_all, block_index), scale)
        probs = jnp.where(allowed, jnp.exp(scores - log_total[:, :, None]), 0.0).astype(
            jnp.bfloat16
        )
        return mixed_sum + jnp.einsum(
            "hqk,khd->qhd",
            probs,
            block_rows(value_all, block_index),
            preferred_element_type=jnp.float32,
        )

    mixed_heads = lax.fori_loop(
        0, block_count, mix_step, jnp.zeros((tok_rows, HEADS, HEAD_DIM), jnp.float32)
    )
    mixed = mixed_heads.reshape(tok_rows, feature_width)
    mixed_low = mixed.astype(jnp.bfloat16)
    second = (
        inputs
        + jnp.dot(mixed_low, w_output, preferred_element_type=jnp.float32)
        + b_output.astype(jnp.float32)
    )
    h_two = norm_rows(second, gain_second, shift_second)
    h_two_low = h_two.astype(jnp.bfloat16)
    up_value = jnp.dot(h_two_low, w_up, preferred_element_type=jnp.float32) + b_up.astype(
        jnp.float32
    )
    act_low = tanh_gelu(up_value).astype(jnp.bfloat16)
    result = (
        second
        + jnp.dot(act_low, w_down, preferred_element_type=jnp.float32)
        + b_down.astype(jnp.float32)
    )
    layer_output = result.astype(jnp.bfloat16)[None]
    valid_float = local_valid.astype(jnp.float32)
    mismatch = result - teacher[0].astype(jnp.float32)
    error_sum, valid_count = lax.psum(
        (jnp.sum(valid_float[:, None] * mismatch * mismatch), jnp.sum(valid_float)), ("ctx", "fsdp")
    )
    loss_value = error_sum / (feature_width * valid_count)
    d_result = (
        cotangent[0].astype(jnp.float32)
        + 2.0 / (feature_width * valid_count) * valid_float[:, None] * mismatch
    )
    d_down = d_result.astype(jnp.bfloat16)
    grad_down_bias = row_sum(d_down)
    grad_down_weight = left_product(act_low, d_down)
    d_act = right_product(d_down, w_down)
    gelu_value, gelu_pull = jax.vjp(tanh_gelu, up_value)
    d_up = gelu_pull(d_act)[0].astype(jnp.bfloat16)
    grad_up_bias = row_sum(d_up)
    grad_up_weight = left_product(h_two_low, d_up)
    d_h_two = right_product(d_up, w_up)
    norm_two_value, norm_two_pull = jax.vjp(norm_rows, second, gain_second, shift_second)
    d_second_norm, grad_second_gain, grad_second_shift = norm_two_pull(d_h_two)
    d_second = d_result + d_second_norm
    d_attn = d_second.astype(jnp.bfloat16)
    grad_output_bias = row_sum(d_attn)
    grad_output_weight = left_product(mixed_low, d_attn)
    d_mixed = right_product(d_attn, w_output).astype(jnp.bfloat16)
    d_heads = split_heads(d_mixed)
    delta = jnp.einsum("qhd,qhd->hq", d_heads.astype(jnp.float32), mixed_heads)
    key_back, value_back = (key_all, value_all)

    def score_grads(block_index):
        allowed = block_allowed(block_index)
        key_piece = block_rows(key_back, block_index)
        value_piece = block_rows(value_back, block_index)
        scores = head_scores(query_heads, key_piece, scale)
        probs = jnp.where(allowed, jnp.exp(scores - log_total[:, :, None]), 0.0)
        d_probs = jnp.einsum(
            "qhd,khd->hqk", d_heads, value_piece, preferred_element_type=jnp.float32
        )
        d_scores = (probs * (d_probs - delta[:, :, None])).astype(jnp.bfloat16)
        return (key_piece, probs, d_scores)

    zero_query = jnp.zeros((tok_rows, HEADS, HEAD_DIM), jnp.float32)

    def reduce_step(block_index, state_triple):
        d_query_sum, d_key_rows, d_value_rows = state_triple
        key_piece, probs, d_scores = score_grads(block_index)
        d_query_sum = d_query_sum + jnp.einsum(
            "hqk,khd->qhd", d_scores, key_piece, preferred_element_type=jnp.float32
        )
        d_key_piece = jnp.einsum(
            "hqk,qhd->khd", d_scores, query_heads, preferred_element_type=jnp.float32
        ).reshape(key_block, feature_width)
        d_value_piece = jnp.einsum(
            "hqk,qhd->khd", probs.astype(jnp.bfloat16), d_heads, preferred_element_type=jnp.float32
        ).reshape(key_block, feature_width)
        d_key_rows = lax.dynamic_update_slice_in_dim(
            d_key_rows, d_key_piece, block_index * key_block, 0
        )
        d_value_rows = lax.dynamic_update_slice_in_dim(
            d_value_rows, d_value_piece, block_index * key_block, 0
        )
        return (d_query_sum, d_key_rows, d_value_rows)

    zero_rows = jnp.zeros((key_block * block_count, feature_width), jnp.float32)
    d_query_sum, d_key_rows, d_value_rows = lax.fori_loop(
        0, block_count, reduce_step, (zero_query, zero_rows, zero_rows)
    )
    d_key_local, d_value_local = (
        lax.psum_scatter(d_key_rows, "ctx", scatter_dimension=0, tiled=True),
        lax.psum_scatter(d_value_rows, "ctx", scatter_dimension=0, tiled=True),
    )
    d_query = (d_query_sum.reshape(tok_rows, feature_width) * scale).astype(jnp.bfloat16)
    d_key = (d_key_local * scale).astype(jnp.bfloat16)
    d_value = d_value_local.astype(jnp.bfloat16)
    grad_query_bias = row_sum(d_query)
    grad_query_weight = left_product(h_one_low, d_query)
    grad_key_weight = left_product(h_one_low, d_key)
    grad_value_bias = row_sum(d_value)
    grad_value_weight = left_product(h_one_low, d_value)
    d_h_one = (
        right_product(d_query, w_query)
        + right_product(d_key, w_key)
        + right_product(d_value, w_value)
    )
    norm_one_value, norm_one_pull = jax.vjp(norm_rows, inputs, gain_first, shift_first)
    d_inputs_norm, grad_first_gain, grad_first_shift = norm_one_pull(d_h_one)
    grad_tokens = (d_second + d_inputs_norm).astype(jnp.bfloat16)[None]
    shares = (
        lax.psum_scatter(
            grad_first_gain.astype(jnp.bfloat16), "fsdp", scatter_dimension=0, tiled=True
        ).astype(jnp.float32),
        lax.psum_scatter(
            grad_first_shift.astype(jnp.bfloat16), "fsdp", scatter_dimension=0, tiled=True
        ).astype(jnp.float32),
        lax.psum_scatter(
            grad_query_weight.astype(jnp.bfloat16), "fsdp", scatter_dimension=0, tiled=True
        ).astype(jnp.float32),
        lax.psum_scatter(
            grad_query_bias.astype(jnp.bfloat16), "fsdp", scatter_dimension=0, tiled=True
        ).astype(jnp.float32),
        lax.psum_scatter(
            grad_key_weight.astype(jnp.bfloat16), "fsdp", scatter_dimension=0, tiled=True
        ).astype(jnp.float32),
        lax.psum_scatter(
            grad_value_weight.astype(jnp.bfloat16), "fsdp", scatter_dimension=0, tiled=True
        ).astype(jnp.float32),
        lax.psum_scatter(
            grad_value_bias.astype(jnp.bfloat16), "fsdp", scatter_dimension=0, tiled=True
        ).astype(jnp.float32),
        lax.psum_scatter(
            grad_output_weight.astype(jnp.bfloat16), "fsdp", scatter_dimension=0, tiled=True
        ).astype(jnp.float32),
        lax.psum_scatter(
            grad_output_bias.astype(jnp.bfloat16), "fsdp", scatter_dimension=0, tiled=True
        ).astype(jnp.float32),
        lax.psum_scatter(
            grad_second_gain.astype(jnp.bfloat16), "fsdp", scatter_dimension=0, tiled=True
        ).astype(jnp.float32),
        lax.psum_scatter(
            grad_second_shift.astype(jnp.bfloat16), "fsdp", scatter_dimension=0, tiled=True
        ).astype(jnp.float32),
        lax.psum_scatter(
            grad_up_weight.astype(jnp.bfloat16), "fsdp", scatter_dimension=0, tiled=True
        ).astype(jnp.float32),
        lax.psum_scatter(
            grad_up_bias.astype(jnp.bfloat16), "fsdp", scatter_dimension=0, tiled=True
        ).astype(jnp.float32),
        lax.psum_scatter(
            grad_down_weight.astype(jnp.bfloat16), "fsdp", scatter_dimension=0, tiled=True
        ).astype(jnp.float32),
        lax.psum_scatter(
            grad_down_bias.astype(jnp.bfloat16), "fsdp", scatter_dimension=0, tiled=True
        ).astype(jnp.float32),
    )
    totals = lax.psum(
        (
            shares[0],
            shares[1],
            shares[2],
            shares[3],
            shares[4],
            shares[5],
            shares[6],
            shares[7],
            shares[8],
            shares[9],
            shares[10],
            shares[11],
            shares[12],
            shares[13],
            shares[14],
        ),
        "ctx",
    )
    return (
        layer_output,
        loss_value,
        grad_tokens,
        totals[0],
        totals[1],
        totals[2],
        totals[3],
        totals[4],
        totals[5],
        totals[6],
        totals[7],
        totals[8],
        totals[9],
        totals[10],
        totals[11],
        totals[12],
        totals[13],
        totals[14],
    )


F32 = jnp.float32
BF16 = jnp.bfloat16
ANY = pl.BlockSpec(memory_space=pl.ANY)
HBM = pl.BlockSpec(memory_space=pltpu.HBM)
VMEM = pl.BlockSpec(memory_space=pltpu.VMEM)
SMEM = pl.BlockSpec(memory_space=pltpu.SMEM)
NT = (((1,), (1,)), ((), ()))
TN = (((0,), (0,)), ((), ()))
NN = (((1,), (0,)), ((), ()))


def swap_cores(value):
    size = lax.axis_size("ctx")
    return lax.ppermute(value, "ctx", [(i, i ^ 1) for i in range(size)])


def both_cores(value):
    pairs = [[i, i + 1] for i in range(0, lax.axis_size("ctx"), 2)]
    return lax.all_gather(value, "ctx", axis=0, tiled=True, axis_index_groups=pairs)


def swap_chips(value, step):
    size = lax.axis_size("ctx")
    return lax.ppermute(value, "ctx", [(i, i ^ (2 * step)) for i in range(size)])


def swap_planes(value, step):
    size = lax.axis_size("fsdp")
    return lax.ppermute(value, "fsdp", [(i, i ^ step) for i in range(size)])


def trade_chips(value):
    size = lax.axis_size("ctx")
    groups = [[i for i in range(size) if i % 2 == c] for c in (0, 1)]
    return lax.all_to_all(value, "ctx", 0, 0, axis_index_groups=groups, tiled=True)


def trade_planes(value):
    return lax.all_to_all(value, "fsdp", 0, 0, tiled=True)


def shaped(*shape, dtype=BF16):
    return jax.ShapeDtypeStruct(shape, dtype)


def wide(*shape):
    return jax.ShapeDtypeStruct(shape, F32)


def local_call(
    body,
    outs,
    where,
    args,
    far=(),
    far_outs=(),
    fetch=(),
    store=(),
    scalar=None,
    scratch=(),
    after=(),
    vmem=14,
    cost=0,
):
    fetch, store = list(fetch), list(store)
    args = [
        pltpu.with_memory_space_constraint(a, pltpu.HBM) if i in far or i in fetch else a
        for i, a in enumerate(args)
    ]
    after = list(after)
    many = isinstance(outs, tuple)
    outs = outs if many else (outs,)
    count, made, moved = len(args), len(outs), len(fetch) + len(store)
    held = [pltpu.VMEM(args[i].shape, args[i].dtype) for i in fetch]
    held += [pltpu.VMEM(outs[i].shape, outs[i].dtype) for i in store]
    if moved:
        held.append(pltpu.SemaphoreType.DMA((moved,)))

    def kernel(where_ref, *refs):
        start = count + len(after)
        given, results = list(refs[:count]), list(refs[start : start + made])
        token, extra = refs[start + made], refs[start + made + 1 :]
        extra, copied = extra[: len(extra) - len(held)], extra[len(extra) - len(held) :]
        token[...] = jnp.zeros(token.shape, token.dtype)
        into = [
            pltpu.make_async_copy(given[i], copied[n], copied[-1].at[n])
            for n, i in enumerate(fetch)
        ]
        out_of = [
            pltpu.make_async_copy(copied[n], results[i], copied[-1].at[n])
            for n, i in enumerate(store, len(fetch))
        ]
        for copy in into:
            copy.start()
        for n, i in enumerate(fetch):
            given[i] = copied[n]
        for n, i in enumerate(store, len(fetch)):
            results[i] = copied[n]
        for copy in into:
            copy.wait()
        body(where_ref, *given, *results, *extra)
        for copy in out_of:
            copy.start()
        for copy in out_of:
            copy.wait()

    def place(i):
        return HBM if i in far_outs or i in store else SMEM if i == scalar else VMEM

    results = pl.pallas_call(
        kernel,
        out_shape=(
            *(
                pltpu.HBM(o.shape, o.dtype) if i in far_outs or i in store else o
                for i, o in enumerate(outs)
            ),
            wide(8, 128),
        ),
        in_specs=[SMEM]
        + [HBM if i in far or i in fetch else VMEM for i in range(count)]
        + [ANY] * len(after),
        out_specs=(*(place(i) for i in range(made)), VMEM),
        scratch_shapes=[*scratch, *held],
        compiler_params=pltpu.CompilerParams(vmem_limit_bytes=vmem << 20),
        cost_estimate=pl.CostEstimate(
            flops=cost * 10**9, transcendentals=0, bytes_accessed=cost * 10**6
        ),
    )(where, *args, *after)
    return (results[:-1] if many else results[0]), results[-1]


def core_rows(core, count):
    return pl.ds(pl.multiple_of(count * core, 16), count)


def rows_at(start, count, align):
    return pl.ds(pl.multiple_of(start, align), count)


def dot(left, right, dims):
    return lax.dot_general(left, right, dims, preferred_element_type=F32)


def run_copies(copies, sems):
    started = [
        pltpu.make_async_copy(source, target, sems.at[i])
        for i, (source, target) in enumerate(copies)
    ]
    for copy in started:
        copy.start()
    for copy in started:
        copy.wait()


def unit_rows(values):
    centred = values - jnp.mean(values, axis=-1, keepdims=True)
    spread = jnp.mean(centred * centred, axis=-1, keepdims=True)
    inverse = lax.rsqrt(spread + EPSILON)
    return centred * inverse, inverse


def unit_back(grad, gain, unit, inverse):
    scaled = grad * gain
    return inverse * (
        scaled
        - jnp.mean(scaled, axis=-1, keepdims=True)
        - unit * jnp.mean(scaled * unit, axis=-1, keepdims=True)
    )


def pack_tokens(where, tokens, segment, valid, out):
    rows, width = tokens.shape
    ids = segment[...]
    line = lax.broadcasted_iota(jnp.int32, (16, rows), 0)
    codes = jnp.where(
        line == 0,
        ids >> 7,
        jnp.where(line == 1, ids & 127, jnp.where(line == 2, valid[...], 0)),
    )
    out[:rows, :] = tokens[...]
    out[rows:, :] = jnp.zeros((16, width), out.dtype)
    out[rows:, :rows] = codes.astype(F32).astype(out.dtype)


def order_chips(where, p0, p1, p2, p3, out):
    rows = p0.shape[0]
    for k, piece in enumerate((p0, p1, p2, p3)):
        out[rows_at(rows * (where[0] ^ k), rows, 16), :] = piece[...]


def far_planes(where, arrived, out):
    part = arrived.shape[0] // 4
    for s in (1, 2, 3):
        out[part * (s - 1) : part * s, :] = arrived[rows_at(part * (where[2] ^ s), part, 16), :]


def pack_projections(where, *refs):
    weights, vectors, long, valid, out = refs[:3], refs[3:11], refs[11], refs[12], refs[13]
    held, small, held_long, sems = refs[14], refs[15:23], refs[23], refs[24]
    half, feat = held.shape[1], small[0].shape[0]
    own_rows = rows_at(half * where[1], half, 32)
    run_copies(
        [(w.at[own_rows], held.at[i]) for i, w in enumerate(weights)]
        + list(zip(vectors, small))
        + [(long, held_long)],
        sems,
    )
    for chip in range(4):

        @pl.when(where[0] == chip)
        def _():
            for i in range(3):
                out[:, feat * i : feat * (i + 1)] = held[i, :, feat * chip : feat * (chip + 1)]

    spread = held_long[...].astype(F32).reshape(1, 4 * feat)
    count = jnp.sum(valid[...].astype(F32), axis=1, keepdims=True)
    lines = [v[...].astype(F32).reshape(1, feat) for v in small]
    lines += [spread[:, feat * i : feat * (i + 1)] for i in range(4)]
    lines += [jnp.broadcast_to(count, (1, feat)), jnp.zeros((half - 13, feat), F32)]
    out[:, 3 * feat :] = jnp.concatenate(lines, axis=0).astype(out.dtype)


def pack_down(where, down, out, sem):
    part = out.shape[0]
    rows = rows_at(4 * part * where[1] + part * where[0], part, 32)
    copy = pltpu.make_async_copy(down.at[rows], out, sem)
    copy.start()
    copy.wait()


def pack_blocks(where, up, output, out_up, sems):
    chip, core = where[0], where[1]
    part, units = out_up.shape[0] // 4, out_up.shape[1] // 5
    rows = rows_at(part * chip, part, 16)
    pairs = [
        (
            up.at[rows, rows_at(2 * units * i + units * core, units, 128)],
            out_up.at[:part, units * i : units * (i + 1)],
        )
        for i in range(4)
    ]
    pairs.append((output.at[rows, rows_at(units * core, units, 128)], out_up.at[:part, 4 * units :]))
    run_copies(pairs, sems)
    for p in (1, 2, 3):
        out_up[part * p : part * (p + 1), :] = out_up[:part, :]


def stack_rows(where, *refs):
    pieces, out = refs[:-1], refs[-1]
    rows = pieces[0].shape[0]
    for i, piece in enumerate(pieces):
        out[rows * i : rows * (i + 1), :] = piece[...]


def three_blocks(pieces, part):
    p0, p1, p2, low, high = pieces
    parts = [(k, [(p, 0)]) for k, p in enumerate((p0, p1, p2))] + [(3, [(low, 0), (high, low.shape[0])])]
    found = []
    for k, refs in parts:
        for s in (1, 2, 3):
            for ref, base in refs:
                start, end = max(part * (s - 1), base), min(part * s, base + ref.shape[0])
                if start < end:
                    found.append((k, s, start - part * (s - 1), end - start, ref, start - base))
    return found


def cross_halves(where, from_x, from_y, to_x, to_y):
    cut = to_x.shape[0]
    to_x[...] = from_y[:cut, :]
    to_y[...] = from_x[cut:, :]


def build_up(where, up, p0, p1, p2, p3, p4, out, sems):
    chip, core, plane = where[0], where[1], where[2]
    units, shard = up.shape[1] // 8, up.shape[0]
    part = shard // 4
    own = rows_at(shard * plane, shard, 64)
    pairs = [
        (
            up.at[:, rows_at(2 * units * i + units * core, units, 128)],
            out.at[own, units * i : units * (i + 1)],
        )
        for i in range(4)
    ]
    for k, s, offset, count, piece, start in three_blocks((p0, p1, p2, p3, p4), part):
        at = rows_at(shard * (plane ^ s) + part * (chip ^ k) + offset, count, 16)
        pairs.append((piece.at[start : start + count, : 4 * units], out.at[at]))
    run_copies(pairs, sems)


def build_half(where, output, p0, p1, p2, p3, p4, out, sems):
    chip, core, plane = where[0], where[1], where[2]
    shard, units = output.shape[0], out.shape[1]
    part = shard // 4
    pairs = [
        (
            output.at[:, rows_at(units * core, units, 128)],
            out.at[rows_at(shard * plane, shard, 64)],
        )
    ]
    for k, s, offset, count, piece, start in three_blocks((p0, p1, p2, p3, p4), part):
        at = rows_at(shard * (plane ^ s) + part * (chip ^ k) + offset, count, 16)
        pairs.append((piece.at[start : start + count, 4 * units :], out.at[at]))
    run_copies(pairs, sems)


def build_down(where, down, p0, p1, p2, p3, p4, out, sem):
    chip, core, plane = where[0], where[1], where[2]
    mine = down.shape[0] // 2
    part = mine // 4
    own = pltpu.make_async_copy(
        down.at[rows_at(mine * core, mine, 128)], out.at[rows_at(mine * plane, mine, 128)], sem
    )
    own.start()
    for k, s, offset, count, piece, start in three_blocks((p0, p1, p2, p3, p4), part):
        at = rows_at(mine * (plane ^ s) + part * (chip ^ k) + offset, count, 16)
        out[at, :] = piece[start : start + count, :]
    own.wait()


def build_output(where, near, far, out):
    units = near.shape[1]
    out[:, rows_at(units * where[1], units, 128)] = near[...]
    out[:, rows_at(units * (1 - where[1]), units, 128)] = far[...]


def normalize_tokens(where, near, far, unit_low, key_row, query_column):
    rows = query_column.shape[0] // 4
    for i in range(8):
        block = (near if i < 4 else far).at[(rows + 16) * (i % 4) : (rows + 16) * (i % 4 + 1), :]
        unit, _ = unit_rows(block[:rows, :].astype(F32))
        unit_low[rows * i : rows * (i + 1), :] = unit
        codes = block[rows:, :].astype(F32)
        ids = codes[0:1, :rows] * 128.0 + codes[1:2, :rows]
        key_row[0:1, rows * i : rows * (i + 1)] = jnp.where(codes[2:3, :rows] == 1.0, ids, -1.0)
        if i < 4:
            query_column[rows * i : rows * (i + 1), :] = jnp.broadcast_to(
                ids.reshape(rows, 1), (rows, 128)
            )


def attend(where, *refs):
    units, key_row, query_column, weights, far_weights = refs[:3] + (refs[3:7], refs[7])
    saved, sent, vectors, long = refs[8:13], refs[13], refs[14], refs[15]
    small, bias, h_one, w_three, projected, probs, mixed, sems = refs[16:]
    kept = (h_one, w_three, projected, mixed)
    copies = [
        pltpu.make_async_copy(source, saved[i], sems.at[j])
        for j, (i, source) in enumerate(zip((0, 1, 2, 4), kept))
    ]
    core, plane = where[1], where[2]
    half, width = weights[0].shape
    feat = width // 4
    group = query_column.shape[0]
    rows = group // 4

    count = jnp.zeros((1, 1), F32)
    for s, piece in enumerate(weights):
        base = 2 * half * (plane ^ s)
        w_three[rows_at(base + half * core, half, 32), :] = piece[:, : 3 * feat]
        other = far_weights[half * s : half * (s + 1), :]
        w_three[rows_at(base + half * (1 - core), half, 32), :] = other[:, : 3 * feat]
        near = piece[:16, 3 * feat :].astype(F32)
        small[plane ^ s] = near
        count += near[12:13, :1] + other[12:13, 3 * feat : 3 * feat + 1].astype(F32)
    vectors[...] = jnp.zeros(vectors.shape, F32)
    for p in range(4):
        lines = small[p]
        for i, r in enumerate((0, 1, 4, 5, 6, 7)):
            vectors[i : i + 1, feat * p : feat * (p + 1)] = lines[r : r + 1, :]
        pair = jnp.where(core == 0, lines[8:10, :], lines[10:12, :])
        long[:, 2 * feat * p : 2 * feat * p + feat] = pair[:1, :]
        long[:, 2 * feat * p + feat : 2 * feat * (p + 1)] = pair[1:, :]
    gain, shift = vectors[0:1, :], vectors[1:2, :]
    short = small[where[0]]
    copies[1].start()
    h_one[...] = (units[...] * gain + shift).astype(BF16)
    copies[0].start()
    values = dot(h_one[...], w_three[...], NN)
    query = (values[:group, :feat] + short[2:3, :]).astype(BF16) * jnp.asarray(
        HEAD_DIM**-0.5, BF16
    )
    projected[:group, :feat] = query
    projected[group:, :feat] = jnp.zeros((group, feat), BF16)
    projected[:, feat : 2 * feat] = values[:, feat : 2 * feat].astype(BF16)
    projected[:, 2 * feat :] = (values[:, 2 * feat :] + short[3:4, :]).astype(BF16)
    copies[2].start()
    column = lax.broadcasted_iota(jnp.int32, (rows, 2 * group), 1)
    line = lax.broadcasted_iota(jnp.int32, (rows, 2 * group), 0)
    for k in range(4):
        ids = query_column[rows * k : rows * (k + 1), :1]
        allowed = (ids == key_row[0:1, :]) | (column == line + rows * k)
        bias[rows * k : rows * (k + 1), :] = jnp.where(allowed, 0.0, MASKED)
    for h in range(feat // HEAD_DIM):
        at = slice(HEAD_DIM * h, HEAD_DIM * (h + 1))
        keys = projected[:, feat + HEAD_DIM * h : feat + HEAD_DIM * (h + 1)]
        held = projected[:, 2 * feat + HEAD_DIM * h : 2 * feat + HEAD_DIM * (h + 1)]
        for k in range(4):
            block = slice(rows * k, rows * (k + 1))
            scores = dot(projected[block, at], keys, NT) + bias[block, :]
            weight = jnp.exp(scores - jnp.max(scores, axis=1, keepdims=True))
            weight = weight * (1.0 / jnp.sum(weight, axis=1, keepdims=True))
            low = weight.astype(BF16)
            probs[h, block, :] = low
            result = dot(low, held, NN)
            mixed[block, at] = result
            sent[(rows + 16) * k : (rows + 16) * k + rows, at] = result.astype(BF16)
        copies.append(pltpu.make_async_copy(probs.at[h], saved[3].at[h], sems.at[4 + h]))
        copies[-1].start()
    copies[3].start()
    high = jnp.floor(count / 128.0)
    side = lax.broadcasted_iota(jnp.int32, (16, feat), 1)
    digits = jnp.where(side == 0, high, jnp.where(side == 1, count - 128.0 * high, 0.0))
    for k in range(4):
        sent[(rows + 16) * k + rows : (rows + 16) * (k + 1), :] = digits.astype(BF16)
    for copy in copies:
        copy.wait()


def attend_back(where, d_all, vectors, *refs):
    saved, (near, far, kept, given, lines) = refs[:5], refs[5:10]
    d_three, d_scores, grads, h_one, w_three, projected, probs, mixed, sems = refs[10:]
    core = where[1]
    pairs = [(saved[2], projected), (saved[4], mixed)]
    pairs += [(saved[3].at[h], probs.at[h]) for h in range(probs.shape[0])]
    pairs += [(saved[0], h_one), (saved[1], w_three)]
    copies = [pltpu.make_async_copy(a, b, sems.at[i]) for i, (a, b) in enumerate(pairs)]
    for copy in copies:
        copy.start()
    copies[0].wait()
    copies[1].wait()
    group, feat = d_all.shape
    rows, width = group // 4, h_one.shape[1]
    scale = HEAD_DIM**-0.5
    d_three[group:, :feat] = jnp.zeros((group, feat), BF16)
    for h in range(feat // HEAD_DIM):
        at = slice(HEAD_DIM * h, HEAD_DIM * (h + 1))
        key_at = slice(feat + HEAD_DIM * h, feat + HEAD_DIM * (h + 1))
        value_at = slice(2 * feat + HEAD_DIM * h, 2 * feat + HEAD_DIM * (h + 1))
        keys, held = projected[:, key_at], projected[:, value_at]
        copies[2 + h].wait()
        for k in range(4):
            block = slice(rows * k, rows * (k + 1))
            d_mixed = d_all[block, at]
            delta = jnp.sum(d_mixed.astype(F32) * mixed[block, at], axis=1, keepdims=True)
            d_probs = dot(d_mixed, held, NT)
            low = (probs[h, block, :].astype(F32) * (d_probs - delta)).astype(BF16)
            d_scores[block, :] = low
            d_three[block, at] = (dot(low, keys, NN) * scale).astype(BF16)
        d_three[:, key_at] = dot(d_scores[...], projected[:group, at], TN).astype(BF16)
        d_three[:, value_at] = dot(probs[h], d_all[:, at], TN).astype(BF16)
    for copy in copies[2 + probs.shape[0] :]:
        copy.wait()
    grads[...] = dot(h_one[...], d_three[...], TN)
    near[...] = dot(d_three[:group, :], w_three[...], NT).astype(BF16)
    far[...] = dot(d_three[group:, :], w_three[...], NT).astype(BF16)
    half = kept.shape[0] // 4
    for p in range(4):
        block = slice(half * p, half * (p + 1))
        kept[block, :] = grads[rows_at(2 * half * p + half * core, half, 32), :].astype(BF16)
        given[block, :] = grads[rows_at(2 * half * p + half * (1 - core), half, 32), :].astype(BF16)
    sums = jnp.sum(d_three[...].astype(F32), axis=0, keepdims=True)
    weight = w_three[...].astype(F32)
    with_gain = jnp.sum(grads[...] * weight, axis=1, keepdims=True)
    with_shift = jnp.sum(weight * sums, axis=1, keepdims=True)
    side = lax.broadcasted_iota(jnp.int32, (width, 128), 1)
    both = jnp.where(side == 0, with_gain, jnp.where(side == 1, with_shift, 0.0)).T
    d_shift = both[1:2, :]
    lines[0:1, :] = (both[0:1, :] - vectors[1:2, :] * d_shift) / vectors[0:1, :]
    lines[1:2, :] = d_shift
    lines[2:3, :] = jnp.zeros((1, width), F32)
    lines[2:3, :feat] = sums[:, :feat]
    lines[3:4, :] = jnp.zeros((1, width), F32)
    lines[3:4, :feat] = sums[:, 2 * feat :]
    lines[4:, :] = jnp.zeros((4, width), F32)


def share_inputs(where, near, far, *outs):
    rows = outs[0].shape[0]
    for k, out in enumerate(outs):
        at = rows_at(rows * (where[0] ^ k), rows, 16)
        out[...] = (near[at, :].astype(F32) + far[at, :].astype(F32)).astype(out.dtype)


def finish_inputs(where, d0, d1, d2, d3, tokens, d_second, vectors, out):
    total = d0[...].astype(F32)
    for piece in (d1, d2, d3):
        total = total + piece[...].astype(F32)
    unit, inverse = unit_rows(tokens[...].astype(F32))
    d_inputs = unit_back(total, vectors[0:1, :], unit, inverse)
    out[...] = (d_second[...] + d_inputs).astype(BF16)


def project_output(where, mixed, w_output, tokens, vectors, second, h_two, count):
    rows, width = tokens.shape
    feat = mixed.shape[1]
    total = tokens[...].astype(F32) + vectors[2:3, :]
    valid = jnp.zeros((1, 1), F32)
    for k in range(4):
        start = (rows + 16) * k
        total += dot(mixed[start : start + rows, :], w_output[feat * k : feat * (k + 1), :], NN)
        digits = mixed[start + rows : start + rows + 16, :].astype(F32)
        valid += digits[0:1, 0:1] * 128.0 + digits[0:1, 1:2]
    second[...] = total
    unit, _ = unit_rows(total)
    h_two[...] = (unit * vectors[3:4, :] + vectors[4:5, :]).astype(BF16)
    count[...] = jnp.broadcast_to(valid, count.shape)


def activate(where, h_pair, w_up, b_up, act, slope):
    rows = h_pair.shape[0] // 2
    root = 0.7978845608028654
    for i in range(2):
        block = slice(rows * i, rows * (i + 1))
        value = dot(h_pair[block, :], w_up[...], NN) + b_up[...]
        square = value * value
        bent = jnp.tanh(root * value * (1.0 + 0.044715 * square))
        act[block, :] = (0.5 * value * (1.0 + bent)).astype(BF16)
        slope[block, :] = 0.5 * (1.0 + bent) + 0.5 * value * (1.0 - bent * bent) * root * (
            1.0 + 3.0 * 0.044715 * square
        )


def project_down(where, act, w_down, near, far):
    rows, core = near.shape[0], where[1]
    near[...] = dot(act[core_rows(core, rows), :], w_down[...], NN)
    far[...] = dot(act[core_rows(1 - core, rows), :], w_down[...], NN).astype(BF16)


def compare(where, second, near, far, vectors, teacher, cotangent, valid, count, *outs):
    layer_output, d_result, d_down, lines = outs
    rows, width = second.shape
    other = far[core_rows(1 - where[1], rows), :].astype(F32)
    result = second[...] + near[...] + other + vectors[5:6, :]
    layer_output[...] = result.astype(BF16)
    kept = valid[...].astype(F32).reshape(rows, 1)
    mismatch = result - teacher[...].astype(F32)
    weighted = kept * mismatch
    error = jnp.sum(jnp.sum(weighted * mismatch, axis=1, keepdims=True), axis=0, keepdims=True)
    total = cotangent[...].astype(F32) + 2.0 / (width * count[0:1, 0:1]) * weighted
    d_result[...] = total
    low = total.astype(BF16)
    d_down[...] = low
    high = error.astype(BF16).astype(F32)
    middle = (error - high).astype(BF16).astype(F32)
    side = lax.broadcasted_iota(jnp.int32, (1, width), 1)
    parts = jnp.where(
        side == 0, high, jnp.where(side == 1, middle, jnp.where(side == 2, error - high - middle, 0.0))
    )
    lines[0:1, :] = jnp.sum(low.astype(F32), axis=0, keepdims=True)
    lines[1:2, :] = parts
    lines[2:, :] = jnp.zeros((6, width), F32)


def activate_back(where, d_down, w_down, slope, w_up, d_up, near, far, line):
    rows, core = near.shape[0], where[1]
    total = jnp.zeros(line.shape, F32)
    for i in range(2):
        block = slice(rows * i, rows * (i + 1))
        low = (dot(d_down[block, :], w_down[...], NT) * slope[block, :]).astype(BF16)
        d_up[block, :] = low
        total += jnp.sum(low.astype(F32), axis=0, keepdims=True)
    line[...] = total
    near[...] = dot(d_up[core_rows(core, rows), :], w_up[...], NT)
    far[...] = dot(d_up[core_rows(1 - core, rows), :], w_up[...], NT).astype(BF16)


def second_back(where, near, far, d_result, second, vectors, w_output, *outs):
    d_second, d_attn, lines, sent = outs
    rows = near.shape[0]
    d_two = near[...] + far[core_rows(1 - where[1], rows), :].astype(F32)
    unit, inverse = unit_rows(second[...])
    total = d_result[...] + unit_back(d_two, vectors[3:4, :], unit, inverse)
    d_second[...] = total
    low = total.astype(BF16)
    d_attn[...] = low
    lines[0:1, :] = jnp.sum(low.astype(F32), axis=0, keepdims=True)
    lines[1:2, :] = jnp.sum(d_two * unit, axis=0, keepdims=True)
    lines[2:3, :] = jnp.sum(d_two, axis=0, keepdims=True)
    lines[3:, :] = jnp.zeros((5, lines.shape[1]), F32)
    feat = sent.shape[1]
    for k in range(4):
        part = w_output[feat * k : feat * (k + 1), :]
        sent[rows * k : rows * (k + 1), :] = dot(low, part, NT).astype(BF16)


def split_chips(chip, block, outs, count):
    own, to_x, to_y, then_x, then_y = outs
    for p in range(4):
        own[count * p : count * (p + 1), :] = block(chip, p).astype(BF16)
    for p in (0, 1):
        low, high = slice(count * p, count * (p + 1)), slice(count * (p + 2), count * (p + 3))
        to_x[low, :] = block(chip ^ 1, p).astype(BF16)
        to_x[high, :] = block(chip ^ 3, p).astype(BF16)
        to_y[low, :] = block(chip ^ 2, p + 2).astype(BF16)
        to_y[high, :] = block(chip ^ 3, p + 2).astype(BF16)
        then_x[low, :] = block(chip ^ 1, p + 2).astype(BF16)
        then_y[low, :] = block(chip ^ 2, p).astype(BF16)


def pass_on(where, from_x, from_y, then_x, then_y, to_x, to_y):
    half = to_x.shape[0]
    to_x[...] = (then_x[...].astype(F32) + from_y[half:, :].astype(F32)).astype(BF16)
    to_y[...] = (then_y[...].astype(F32) + from_x[half:, :].astype(F32)).astype(BF16)


def add_chips(own, from_x, from_y, last_x, last_y):
    half = last_x.shape[0]
    low = own[:half, :].astype(F32) + from_x[:half, :].astype(F32) + last_y[...].astype(F32)
    high = own[half:, :].astype(F32) + from_y[:half, :].astype(F32) + last_x[...].astype(F32)
    return low, high


def down_grads(where, act, d_down, *refs):
    outs, total = refs[:5], refs[5]
    count = outs[0].shape[0] // 4
    total[...] = dot(act[...], d_down[...], TN).astype(BF16)

    def block(j, p):
        return total[rows_at(4 * count * p + count * j, count, 32), :]

    split_chips(where[0], block, outs, count)


def output_grads(where, mixed, d_attn, kept, given):
    core = where[1]
    rows, width = d_attn.shape
    feat, units = mixed.shape[1], width // 2
    mine = d_attn[:, rows_at(units * core, units, 128)]
    others = d_attn[:, rows_at(units * (1 - core), units, 128)]
    for j in range(4):
        at = slice(feat * j, feat * (j + 1))
        piece = mixed[(rows + 16) * j : (rows + 16) * j + rows, :]
        kept[at, :] = dot(piece, mine, TN).astype(BF16)
        given[at, :] = dot(piece, others, TN).astype(BF16)


def up_grads(where, h_pair, d_up, kept, given, *refs):
    outs, total = refs[:5], refs[5]
    count, units = outs[0].shape[0] // 4, d_up.shape[1]
    total[:, :units] = dot(h_pair[...], d_up[...], TN).astype(BF16)
    total[:, units:] = (kept[...].astype(F32) + given[...].astype(F32)).astype(BF16)

    def block(j, p):
        return total[rows_at(4 * count * p + count * j, count, 16), :]

    split_chips(where[0], block, outs, count)


def send_planes(where, own, from_x, from_y, last_x, last_y, *refs):
    outs, total = refs[:4], refs[4]
    part, half = outs[0].shape[0], last_x.shape[0]
    total[:half, :], total[half:, :] = add_chips(own, from_x, from_y, last_x, last_y)
    for s, out in enumerate(outs):
        out[...] = total[rows_at(part * (where[2] ^ s), part, 16), :].astype(out.dtype)


def sum_pieces(where, own, p1, p2, p3, out):
    total = own[...].astype(F32)
    for piece in (p1, p2, p3):
        total = total + piece[...].astype(F32)
    out[...] = total.astype(out.dtype)


def finish_down(where, near, far, out, held, sems):
    core = where[1]
    both = near.shape[0] // 4
    part = both // 2
    copies = []
    for j in range(4):
        block = slice(both * j + part, both * (j + 1))
        for side, piece in ((core, near), (1 - core, far)):
            at = rows_at(4 * part * side + part * j, part, 32)
            held[at, :] = piece[block, :].astype(F32)
            copies.append(pltpu.make_async_copy(held.at[at], out.at[at], sems.at[len(copies)]))
            copies[-1].start()
    for copy in copies:
        copy.wait()


def finish_up(where, n0, n1, n2, n3, far, out, out_half, held, held_half, sems):
    chip, core = where[0], where[1]
    part, units = n0.shape[0], n0.shape[1] // 5
    copies = []
    for k, near in enumerate((n0, n1, n2, n3)):
        rows = rows_at(part * (chip ^ k), part, 16)
        for piece, side in ((near[...], core), (far[part * k : part * (k + 1), :], 1 - core)):
            full = piece.astype(F32)
            for i in range(4):
                at = rows_at(2 * units * i + units * side, units, 128)
                held[rows, at] = full[:, units * i : units * (i + 1)]
            held_half[rows, rows_at(units * side, units, 128)] = full[:, 4 * units :]
        for source, target in ((held, out), (held_half, out_half)):
            copies.append(
                pltpu.make_async_copy(source.at[rows], target.at[rows], sems.at[len(copies)])
            )
            copies[-1].start()
    for copy in copies:
        copy.wait()


def sum_chips(where, own, from_x, from_y, last_x, last_y, out):
    half = last_x.shape[0]
    low, high = add_chips(own, from_x, from_y, last_x, last_y)
    out[:half, :], out[half:, :] = low.astype(BF16), high.astype(BF16)


def pack_gradients(
    where, kept, given, from_attention, from_second, from_result, up_line, down, out, down_sum
):
    chip = where[0]
    part = down_sum.shape[0]
    arrived_down = down[:part, :].astype(F32)
    for p in (1, 2, 3):
        arrived_down = arrived_down + down[part * p : part * (p + 1), :].astype(F32)
    down_sum[...] = arrived_down.astype(BF16)
    half, width = out.shape[0] // 4, out.shape[1]
    feat = width // 4
    for p in range(4):
        cut = slice(feat * p, feat * (p + 1))
        owner = jnp.where(chip == p, 1.0, 0.0)
        lines = [
            from_attention[0:1, cut],
            from_attention[1:2, cut],
            from_second[0:1, cut],
            from_second[1:2, cut],
            from_second[2:3, cut],
            from_result[0:1, cut],
            up_line[:, 2 * feat * p : 2 * feat * p + feat],
            up_line[:, 2 * feat * p + feat : 2 * feat * (p + 1)],
            from_attention[2:3, :feat] * owner,
            from_attention[3:4, :feat] * owner,
            from_result[1:2, :feat],
            jnp.zeros((half - 11, feat), F32),
        ]
        small = jnp.concatenate(lines, axis=0).astype(BF16)
        block = slice(half * p, half * (p + 1))
        total = (kept[block, :].astype(F32) + given[block, :].astype(F32)).astype(BF16)
        out[block, : 3 * feat] = total
        out[block, 3 * feat :] = small


def sum_planes(where, arrived, down, out):
    both, width = out.shape[0] // 4, out.shape[1]
    half, feat = both // 2, width // 4
    total = arrived[:half, :].astype(F32)
    for p in (1, 2, 3):
        total = total + arrived[half * p : half * (p + 1), :].astype(F32)
    small = total[:16, 3 * feat :]
    error = jnp.sum(small[10:11, :3], axis=1, keepdims=True)
    high = error.astype(BF16).astype(F32)
    middle = (error - high).astype(BF16).astype(F32)
    line = lax.broadcasted_iota(jnp.int32, small.shape, 0)
    side = lax.broadcasted_iota(jnp.int32, small.shape, 1)
    parts = jnp.where(side == 0, high, jnp.where(side == 1, middle, error - high - middle))
    small = jnp.where((line == 10) & (side < 3), parts, small)
    for j in range(4):
        start = both * j
        out[start : start + half, : 3 * feat] = total[:, : 3 * feat].astype(BF16)
        out[start : start + 16, 3 * feat :] = small.astype(BF16)
        out[start + 16 : start + half, 3 * feat :] = jnp.zeros((half - 16, feat), BF16)
        out[start + half : start + both, :] = down[...]


def finish_projections(where, near, far, count, *outs):
    query, key, value, loss = outs[:4]
    flat, up_line, held, whole_line = outs[4:12], outs[12], outs[13], outs[14]
    core = where[1]
    both, width = near.shape[0] // 4, near.shape[1]
    half, feat = both // 2, width // 4
    for j in range(4):
        start = both * j
        for side, piece in ((core, near), (1 - core, far)):
            held[2 * j + side] = piece[start : start + 16, 3 * feat :].astype(F32)
            rows = rows_at(half * side, half, 32)
            for i, out in enumerate((query, key, value)):
                out[rows, feat * j : feat * (j + 1)] = piece[
                    start : start + half, feat * i : feat * (i + 1)
                ].astype(F32)
    total = held[0]
    for i in range(1, 8):
        total = total + held[i]
    for i, line in enumerate((0, 1, 2, 3, 4, 5, 8, 9)):
        flat[i][...] = total[line]
    even = held[0] + held[2] + held[4] + held[6]
    odd = held[1] + held[3] + held[5] + held[7]
    for side, part in enumerate((even, odd)):
        for i in range(2):
            at = 2 * feat * side + feat * i
            whole_line[0:1, at : at + feat] = part[6 + i : 7 + i, :]
    up_line[...] = whole_line[0]
    error = jnp.sum(total[10:11, :3], axis=1, keepdims=True)
    loss[0, 0] = jnp.sum(error / (width * count[0:1, 0:1]))


def layer(
    tokens,
    segment_ids,
    valid_rows,
    teacher,
    cotangent,
    first_gain,
    first_shift,
    query_weight,
    query_bias,
    key_weight,
    value_weight,
    value_bias,
    output_weight,
    output_bias,
    second_gain,
    second_shift,
    up_weight,
    up_bias,
    down_weight,
    down_bias,
):
    rows, width = tokens.shape[1], tokens.shape[2]
    shard = query_weight.shape[0]
    half, quarter = shard // 2, shard // 4
    hidden = up_weight.shape[1]
    units = hidden // 2
    own_units = down_weight.shape[0]
    core_units = own_units // 2
    part_units = core_units // 4
    feat = width // 4
    heads = feat // HEAD_DIM
    group = 4 * rows
    every = 2 * group
    steps = (1, 2, 3)

    place, plane = lax.axis_index("ctx"), lax.axis_index("fsdp")
    where = jnp.stack([place // 2, place % 2, plane]).astype(jnp.int32)
    dma = pltpu.SemaphoreType.DMA

    last = []

    def step(body, outs, args, **options):
        made, token = local_call(body, outs, where, args, after=last, **options)
        last[:] = [token]
        return made

    def stack(pieces, cost=0):
        shape = len(pieces) * pieces[0].shape[0], pieces[0].shape[1]
        return step(stack_rows, shaped(*shape), pieces, cost=cost)

    own = tokens[0]
    smalls = (
        first_gain,
        first_shift,
        query_bias,
        value_bias,
        output_bias,
        second_gain,
        second_shift,
        down_bias,
    )
    up_piece = step(
        pack_blocks,
        shaped(4 * quarter, 5 * core_units),
        (up_weight, output_weight),
        far=range(2),
        scratch=[dma((5,))],
    )
    up_far = trade_planes(up_piece)
    bundle = step(pack_tokens, shaped(rows + 16, width), (own, segment_ids, valid_rows), cost=50)
    near_tokens = [bundle] + [swap_chips(bundle, k) for k in steps]
    projections = step(
        pack_projections,
        shaped(half, width),
        (query_weight, key_weight, value_weight, *smalls, up_bias, valid_rows),
        far=range(12),
        scratch=[
            pltpu.VMEM((3, half, width), BF16),
            *[pltpu.VMEM((feat,), BF16)] * 8,
            pltpu.VMEM((own_units,), BF16),
            dma((12,)),
        ],
        cost=0,
    )
    near_tokens = step(order_chips, shaped(4 * (rows + 16), width), near_tokens, cost=0)
    far_tokens = swap_cores(near_tokens)
    up_far = step(far_planes, shaped(3 * quarter, 5 * core_units), (up_far,), cost=0)
    up_three = up_far, swap_chips(up_far, 1), swap_chips(up_far, 2)
    near_weights = [projections] + [swap_planes(projections, s) for s in steps]
    unit_one, key_row, query_column = step(
        normalize_tokens,
        (wide(every, width), wide(8, every), wide(group, 128)),
        (near_tokens, far_tokens),
        cost=1,
    )
    far_weights = swap_cores(stack(near_weights))

    def first_chips(piece):
        return piece, swap_chips(piece, 1), swap_chips(piece, 2)

    def all_chips(three, cut):
        count, lanes = three[0].shape
        to_x, to_y = step(cross_halves, (shaped(cut, lanes), shaped(count - cut, lanes)), three[1:], cost=50)
        return (*three, swap_chips(to_x, 1), swap_chips(to_y, 2))

    up_all = all_chips(up_three, up_far.shape[0] // 32 * 16 + 16)
    down_piece = step(
        pack_down, shaped(part_units, width), (down_weight,), far=(0,), scratch=[dma]
    )
    down_far = [swap_planes(down_piece, s) for s in steps]

    h_one, w_three, projected, probs, mixed, sent, vectors, b_up = step(
        attend,
        (
            shaped(every, width),
            shaped(width, 3 * feat),
            shaped(every, 3 * feat),
            shaped(heads, group, every),
            wide(group, feat),
            shaped(4 * (rows + 16), feat),
            wide(8, width),
            wide(1, units),
        ),
        (unit_one, key_row, query_column, *near_weights, far_weights),
        far_outs=range(5),
        scratch=[
            pltpu.VMEM((4, 16, feat), F32),
            pltpu.VMEM((group, every), F32),
            pltpu.VMEM((every, width), BF16),
            pltpu.VMEM((width, 3 * feat), BF16),
            pltpu.VMEM((every, 3 * feat), BF16),
            pltpu.VMEM((heads, group, every), BF16),
            pltpu.VMEM((group, feat), F32),
            dma((4 + heads,)),
        ],
        vmem=28,
        cost=50,
    )
    mixed_low = trade_chips(sent)
    down_far = first_chips(stack(down_far))
    out_near = step(
        build_half,
        shaped(width, core_units),
        (output_weight, *up_all),
        far=range(6),
        scratch=[dma((20,))],
    )
    out_far = swap_cores(out_near)
    w_up = step(
        build_up, shaped(width, units), (up_weight, *up_all), far=range(6), scratch=[dma((20,))], cost=50
    )
    w_output = step(build_output, shaped(width, width), (out_near, out_far))

    second, h_two, count = step(
        project_output,
        (wide(rows, width), shaped(rows, width), wide(8, 128)),
        (mixed_low, w_output, own, vectors),
    )
    h_pair = both_cores(h_two)
    down_all = all_chips(down_far, down_far[0].shape[0] // 2)
    act, slope = step(
        activate,
        (shaped(2 * rows, units), wide(2 * rows, units)),
        (h_pair, w_up, b_up),
    )
    w_down = step(
        build_down, shaped(units, width), (down_weight, *down_all), far=(0,), scratch=[dma]
    )
    down_near, down_other = step(
        project_down, (wide(rows, width), shaped(rows, width)), (act, w_down)
    )
    layer_output, d_result, d_down, from_result = step(
        compare,
        (shaped(rows, width), wide(rows, width), shaped(rows, width), wide(8, width)),
        (
            second,
            down_near,
            both_cores(down_other),
            vectors,
            teacher[0],
            cotangent[0],
            valid_rows,
            count,
        ),
    )
    d_down = both_cores(d_down)

    def five(count, lanes):
        return (shaped(4 * count, lanes),) * 3 + (shaped(2 * count, lanes),) * 2

    def onward(parts, arrived, fetch):
        count, lanes = parts[3].shape
        to_x, to_y = step(
            pass_on, (shaped(count, lanes),) * 2, (*arrived, *parts[3:]), fetch=fetch, cost=50
        )
        return (parts[0], *arrived, swap_chips(to_x, 1), swap_chips(to_y, 2))

    down_parts = step(
        down_grads,
        five(part_units, width),
        (act, d_down),
        scratch=[pltpu.VMEM((units, width), BF16)],
        vmem=24,
    )
    down_arrived = swap_chips(down_parts[1], 1), swap_chips(down_parts[2], 2)
    d_up, two_near, two_other, up_line = step(
        activate_back,
        (shaped(2 * rows, units), wide(rows, width), shaped(rows, width), wide(1, units)),
        (d_down, w_down, slope, w_up),
        cost=50,
    )
    d_second, d_attn, from_second, d_sent = step(
        second_back,
        (wide(rows, width), shaped(rows, width), wide(8, width), shaped(group, feat)),
        (two_near, both_cores(two_other), d_result, second, vectors, w_output),
    )
    d_mixed = trade_chips(d_sent)

    kept_out, given_out = step(
        output_grads,
        (shaped(width, core_units), shaped(width, core_units)),
        (mixed_low, d_attn),
        cost=1,
    )
    given_out = swap_cores(given_out)
    down_sums = onward(down_parts, down_arrived, ())
    up_parts = step(
        up_grads,
        five(quarter, 5 * core_units),
        (h_pair, d_up, kept_out, given_out),
        store=(0, 3, 4),
        scratch=[pltpu.VMEM((width, 5 * core_units), BF16)],
        vmem=24,
        cost=5,
    )
    up_arrived = swap_chips(up_parts[1], 1), swap_chips(up_parts[2], 2)
    down_planes = trade_planes(step(sum_chips, shaped(4 * part_units, width), down_sums))

    d_near, d_far, kept, given, from_attention = step(
        attend_back,
        (
            shaped(group, width),
            shaped(group, width),
            shaped(4 * half, 3 * feat),
            shaped(4 * half, 3 * feat),
            wide(8, width),
        ),
        (d_mixed, vectors, h_one, w_three, projected, probs, mixed),
        far=range(2, 7),
        store=(2, 3),
        scratch=[
            pltpu.VMEM((every, 3 * feat), BF16),
            pltpu.VMEM((group, every), BF16),
            pltpu.VMEM((width, 3 * feat), F32),
            pltpu.VMEM((every, width), BF16),
            pltpu.VMEM((width, 3 * feat), BF16),
            pltpu.VMEM((every, 3 * feat), BF16),
            pltpu.VMEM((heads, group, every), BF16),
            pltpu.VMEM((group, feat), F32),
            dma((4 + heads,)),
        ],
        vmem=28,
        cost=50,
    )
    given, d_far = swap_cores(given), swap_cores(d_far)
    up_sums = onward(up_parts, up_arrived, (2, 3))
    arrived, down_planes = step(
        pack_gradients,
        (shaped(4 * half, width), shaped(part_units, width)),
        (kept, given, from_attention, from_second, from_result, up_line, down_planes),
        fetch=(0, 1),
        cost=1,
    )
    arrived = trade_planes(arrived)

    def spread(piece):
        return [piece] + [swap_chips(piece, k) for k in steps]

    def whole(near):
        return (*near, swap_cores(stack(near, cost=1)))

    up_planes = step(
        send_planes,
        (shaped(quarter, 5 * core_units),) * 4,
        up_sums,
        fetch=(0,),
        scratch=[pltpu.VMEM((4 * quarter, 5 * core_units), F32)],
        cost=50,
    )
    up_planes = [up_planes[0]] + [swap_planes(up_planes[s], s) for s in steps]
    shares = step(share_inputs, (shaped(rows, width),) * 4, (d_near, d_far), store=(0,), cost=50)
    shares = [shares[0]] + [swap_chips(shares[k], k) for k in steps]
    both = trade_chips(step(sum_planes, shaped(8 * half, width), (arrived, down_planes), cost=50))
    up_near = spread(step(sum_pieces, shaped(quarter, 5 * core_units), up_planes, cost=50))
    grad_tokens = step(
        finish_inputs, shaped(rows, width), (*shares, own, d_second, vectors), fetch=(0, 4), cost=50
    )
    both = (both, swap_cores(both))
    finished = step(
        finish_projections,
        (wide(shard, width),) * 3
        + (wide(1, 1),)
        + (wide(shard),) * 8
        + (wide(own_units),),
        (*both, count),
        scratch=[pltpu.VMEM((8, 16, feat), F32), pltpu.VMEM((8, own_units), F32)],
        scalar=3,
    )
    grad_down_weight = step(
        finish_down,
        wide(own_units, width),
        both,
        far_outs=(0,),
        scratch=[pltpu.VMEM((own_units, width), F32), dma((8,))],
    )
    grad_up_weight, grad_output_weight = step(
        finish_up,
        (wide(shard, hidden), wide(shard, width)),
        whole(up_near),
        far_outs=(0, 1),
        scratch=[pltpu.VMEM((shard, hidden), F32), pltpu.VMEM((shard, width), F32), dma((8,))],
    )
    sums, two = finished[4:10], finished[10:12]
    return (
        layer_output[None],
        finished[3].reshape(()),
        grad_tokens[None],
        sums[0],
        sums[1],
        finished[0],
        two[0],
        finished[1],
        finished[2],
        two[1],
        grad_output_weight,
        sums[2],
        sums[3],
        sums[4],
        grad_up_weight,
        finished[12],
        grad_down_weight,
        sums[5],
    )


def solution(mesh):
    body = layer if (mesh.shape["ctx"], mesh.shape["fsdp"]) == (8, 4) else shards
    placed = (
        P("fsdp", "ctx", None),
        P("fsdp", "ctx"),
        P("fsdp", "ctx"),
        P("fsdp", "ctx", None),
        P("fsdp", "ctx", None),
        P("fsdp"),
        P("fsdp"),
        P("fsdp", None),
        P("fsdp"),
        P("fsdp", None),
        P("fsdp", None),
        P("fsdp"),
        P("fsdp", None),
        P("fsdp"),
        P("fsdp"),
        P("fsdp"),
        P("fsdp", None),
        P("fsdp"),
        P("fsdp", None),
        P("fsdp"),
    )
    return jax.shard_map(
        body,
        mesh=mesh,
        in_specs=placed,
        out_specs=(
            P("fsdp", "ctx", None),
            P(),
            P("fsdp", "ctx", None),
            P("fsdp"),
            P("fsdp"),
            P("fsdp", None),
            P("fsdp"),
            P("fsdp", None),
            P("fsdp", None),
            P("fsdp"),
            P("fsdp", None),
            P("fsdp"),
            P("fsdp"),
            P("fsdp"),
            P("fsdp", None),
            P("fsdp"),
            P("fsdp", None),
            P("fsdp"),
        ),
        check_vma=False,
    )
```

```python
import jax
import jax.numpy as jnp
from jax import lax
from jax.experimental import pallas as pl
from jax.experimental.pallas import tpu as pltpu
from jax.sharding import PartitionSpec as P

HEADS = 12
HEAD_DIM = 64


EPSILON = 1e-06
MASKED = -1e30


def norm_rows(values, gain, shift):
    centre = jnp.mean(values, axis=-1, keepdims=True)
    centred = values - centre
    spread = jnp.mean(centred * centred, axis=-1, keepdims=True)
    return centred * lax.rsqrt(spread + EPSILON) * gain + shift


def tanh_gelu(values):
    return jax.nn.gelu(values, approximate=True)


def key_allowed(query_segment, query_place, key_codes, key_place):
    same_doc = query_segment[:, None] == (key_codes // 2)[None, :]
    usable = (key_codes % 2 == 1)[None, :] | (query_place[:, None] == key_place[None, :])
    return (same_doc & usable)[None, :, :]


def split_heads(values):
    return values.reshape(values.shape[0], HEADS, HEAD_DIM)


def head_scores(query_heads, key_heads, scale):
    return (
        jnp.einsum("qhd,khd->hqk", query_heads, key_heads, preferred_element_type=jnp.float32)
        * scale
    )


def row_sum(values):
    return jnp.sum(values, axis=0, dtype=jnp.float32)


def left_product(left, right):
    return jnp.einsum("rd,rf->df", left, right, preferred_element_type=jnp.float32)


def right_product(left, right):
    return jnp.einsum("rf,df->rd", left, right, preferred_element_type=jnp.float32)


def shards(
    tokens,
    segment_ids,
    valid_rows,
    teacher,
    cotangent,
    first_gain,
    first_shift,
    query_weight,
    query_bias,
    key_weight,
    value_weight,
    value_bias,
    output_weight,
    output_bias,
    second_gain,
    second_shift,
    up_weight,
    up_bias,
    down_weight,
    down_bias,
):
    tok_rows = tokens.shape[1]
    feature_width = tokens.shape[2]
    shard_count = lax.axis_size("ctx")
    key_block = 4 * tok_rows
    block_count = shard_count // 4
    scale = HEAD_DIM ** (-0.5)
    gain_one, shift_one, w_query, b_query, w_key, w_value, b_value, w_output, b_output = (
        lax.all_gather(first_gain, "fsdp", axis=0, tiled=True),
        lax.all_gather(first_shift, "fsdp", axis=0, tiled=True),
        lax.all_gather(query_weight, "fsdp", axis=0, tiled=True),
        lax.all_gather(query_bias, "fsdp", axis=0, tiled=True),
        lax.all_gather(key_weight, "fsdp", axis=0, tiled=True),
        lax.all_gather(value_weight, "fsdp", axis=0, tiled=True),
        lax.all_gather(value_bias, "fsdp", axis=0, tiled=True),
        lax.all_gather(output_weight, "fsdp", axis=0, tiled=True),
        lax.all_gather(output_bias, "fsdp", axis=0, tiled=True),
    )
    gain_two, shift_two, w_up, b_up, w_down, b_down = (
        lax.all_gather(second_gain, "fsdp", axis=0, tiled=True),
        lax.all_gather(second_shift, "fsdp", axis=0, tiled=True),
        lax.all_gather(up_weight, "fsdp", axis=0, tiled=True),
        lax.all_gather(up_bias, "fsdp", axis=0, tiled=True),
        lax.all_gather(down_weight, "fsdp", axis=0, tiled=True),
        lax.all_gather(down_bias, "fsdp", axis=0, tiled=True),
    )
    local_segment = segment_ids[0]
    local_valid = valid_rows[0]
    local_codes = local_segment * 2 + local_valid
    all_codes = lax.all_gather(local_codes, "ctx", axis=0, tiled=True)
    query_place = lax.axis_index("ctx") * tok_rows + jnp.arange(tok_rows, dtype=jnp.int32)
    inputs = tokens[0].astype(jnp.float32)
    gain_first = gain_one.astype(jnp.float32)
    shift_first = shift_one.astype(jnp.float32)
    gain_second = gain_two.astype(jnp.float32)
    shift_second = shift_two.astype(jnp.float32)
    h_one = norm_rows(inputs, gain_first, shift_first)
    h_one_low = h_one.astype(jnp.bfloat16)
    query_low = (
        jnp.dot(h_one_low, w_query, preferred_element_type=jnp.float32)
        + b_query.astype(jnp.float32)
    ).astype(jnp.bfloat16)
    key_low = jnp.dot(h_one_low, w_key, preferred_element_type=jnp.float32).astype(jnp.bfloat16)
    value_low = (
        jnp.dot(h_one_low, w_value, preferred_element_type=jnp.float32)
        + b_value.astype(jnp.float32)
    ).astype(jnp.bfloat16)
    key_all, value_all = (
        lax.all_gather(key_low, "ctx", axis=0, tiled=True),
        lax.all_gather(value_low, "ctx", axis=0, tiled=True),
    )
    query_heads = split_heads(query_low)

    def block_rows(source, block_index):
        return split_heads(lax.dynamic_slice_in_dim(source, block_index * key_block, key_block, 0))

    def block_allowed(block_index):
        start = block_index * key_block
        codes = lax.dynamic_slice_in_dim(all_codes, start, key_block, 0)
        return key_allowed(
            local_segment, query_place, codes, start + jnp.arange(key_block, dtype=jnp.int32)
        )

    def stats_step(block_index, state_pair):
        running_max, running_sum = state_pair
        allowed = block_allowed(block_index)
        scores = jnp.where(
            allowed, head_scores(query_heads, block_rows(key_all, block_index), scale), MASKED
        )
        new_max = jnp.maximum(running_max, jnp.max(scores, axis=2))
        weights = jnp.where(allowed, jnp.exp(scores - new_max[:, :, None]), 0.0)
        return (new_max, running_sum * jnp.exp(running_max - new_max) + jnp.sum(weights, axis=2))

    start_max = jnp.full((HEADS, tok_rows), MASKED, jnp.float32)
    start_sum = jnp.zeros((HEADS, tok_rows), jnp.float32)
    running_max, running_sum = lax.fori_loop(0, block_count, stats_step, (start_max, start_sum))
    log_total = running_max + jnp.log(running_sum)

    def mix_step(block_index, mixed_sum):
        allowed = block_allowed(block_index)
        scores = head_scores(query_heads, block_rows(key_all, block_index), scale)
        probs = jnp.where(allowed, jnp.exp(scores - log_total[:, :, None]), 0.0).astype(
            jnp.bfloat16
        )
        return mixed_sum + jnp.einsum(
            "hqk,khd->qhd",
            probs,
            block_rows(value_all, block_index),
            preferred_element_type=jnp.float32,
        )

    mixed_heads = lax.fori_loop(
        0, block_count, mix_step, jnp.zeros((tok_rows, HEADS, HEAD_DIM), jnp.float32)
    )
    mixed = mixed_heads.reshape(tok_rows, feature_width)
    mixed_low = mixed.astype(jnp.bfloat16)
    second = (
        inputs
        + jnp.dot(mixed_low, w_output, preferred_element_type=jnp.float32)
        + b_output.astype(jnp.float32)
    )
    h_two = norm_rows(second, gain_second, shift_second)
    h_two_low = h_two.astype(jnp.bfloat16)
    up_value = jnp.dot(h_two_low, w_up, preferred_element_type=jnp.float32) + b_up.astype(
        jnp.float32
    )
    act_low = tanh_gelu(up_value).astype(jnp.bfloat16)
    result = (
        second
        + jnp.dot(act_low, w_down, preferred_element_type=jnp.float32)
        + b_down.astype(jnp.float32)
    )
    layer_output = result.astype(jnp.bfloat16)[None]
    valid_float = local_valid.astype(jnp.float32)
    mismatch = result - teacher[0].astype(jnp.float32)
    error_sum, valid_count = lax.psum(
        (jnp.sum(valid_float[:, None] * mismatch * mismatch), jnp.sum(valid_float)), ("ctx", "fsdp")
    )
    loss_value = error_sum / (feature_width * valid_count)
    d_result = (
        cotangent[0].astype(jnp.float32)
        + 2.0 / (feature_width * valid_count) * valid_float[:, None] * mismatch
    )
    d_down = d_result.astype(jnp.bfloat16)
    grad_down_bias = row_sum(d_down)
    grad_down_weight = left_product(act_low, d_down)
    d_act = right_product(d_down, w_down)
    gelu_value, gelu_pull = jax.vjp(tanh_gelu, up_value)
    d_up = gelu_pull(d_act)[0].astype(jnp.bfloat16)
    grad_up_bias = row_sum(d_up)
    grad_up_weight = left_product(h_two_low, d_up)
    d_h_two = right_product(d_up, w_up)
    norm_two_value, norm_two_pull = jax.vjp(norm_rows, second, gain_second, shift_second)
    d_second_norm, grad_second_gain, grad_second_shift = norm_two_pull(d_h_two)
    d_second = d_result + d_second_norm
    d_attn = d_second.astype(jnp.bfloat16)
    grad_output_bias = row_sum(d_attn)
    grad_output_weight = left_product(mixed_low, d_attn)
    d_mixed = right_product(d_attn, w_output).astype(jnp.bfloat16)
    d_heads = split_heads(d_mixed)
    delta = jnp.einsum("qhd,qhd->hq", d_heads.astype(jnp.float32), mixed_heads)
    key_back, value_back = (key_all, value_all)

    def score_grads(block_index):
        allowed = block_allowed(block_index)
        key_piece = block_rows(key_back, block_index)
        value_piece = block_rows(value_back, block_index)
        scores = head_scores(query_heads, key_piece, scale)
        probs = jnp.where(allowed, jnp.exp(scores - log_total[:, :, None]), 0.0)
        d_probs = jnp.einsum(
            "qhd,khd->hqk", d_heads, value_piece, preferred_element_type=jnp.float32
        )
        d_scores = (probs * (d_probs - delta[:, :, None])).astype(jnp.bfloat16)
        return (key_piece, probs, d_scores)

    zero_query = jnp.zeros((tok_rows, HEADS, HEAD_DIM), jnp.float32)

    def reduce_step(block_index, state_triple):
        d_query_sum, d_key_rows, d_value_rows = state_triple
        key_piece, probs, d_scores = score_grads(block_index)
        d_query_sum = d_query_sum + jnp.einsum(
            "hqk,khd->qhd", d_scores, key_piece, preferred_element_type=jnp.float32
        )
        d_key_piece = jnp.einsum(
            "hqk,qhd->khd", d_scores, query_heads, preferred_element_type=jnp.float32
        ).reshape(key_block, feature_width)
        d_value_piece = jnp.einsum(
            "hqk,qhd->khd", probs.astype(jnp.bfloat16), d_heads, preferred_element_type=jnp.float32
        ).reshape(key_block, feature_width)
        d_key_rows = lax.dynamic_update_slice_in_dim(
            d_key_rows, d_key_piece, block_index * key_block, 0
        )
        d_value_rows = lax.dynamic_update_slice_in_dim(
            d_value_rows, d_value_piece, block_index * key_block, 0
        )
        return (d_query_sum, d_key_rows, d_value_rows)

    zero_rows = jnp.zeros((key_block * block_count, feature_width), jnp.float32)
    d_query_sum, d_key_rows, d_value_rows = lax.fori_loop(
        0, block_count, reduce_step, (zero_query, zero_rows, zero_rows)
    )
    d_key_local, d_value_local = (
        lax.psum_scatter(d_key_rows, "ctx", scatter_dimension=0, tiled=True),
        lax.psum_scatter(d_value_rows, "ctx", scatter_dimension=0, tiled=True),
    )
    d_query = (d_query_sum.reshape(tok_rows, feature_width) * scale).astype(jnp.bfloat16)
    d_key = (d_key_local * scale).astype(jnp.bfloat16)
    d_value = d_value_local.astype(jnp.bfloat16)
    grad_query_bias = row_sum(d_query)
    grad_query_weight = left_product(h_one_low, d_query)
    grad_key_weight = left_product(h_one_low, d_key)
    grad_value_bias = row_sum(d_value)
    grad_value_weight = left_product(h_one_low, d_value)
    d_h_one = (
        right_product(d_query, w_query)
        + right_product(d_key, w_key)
        + right_product(d_value, w_value)
    )
    norm_one_value, norm_one_pull = jax.vjp(norm_rows, inputs, gain_first, shift_first)
    d_inputs_norm, grad_first_gain, grad_first_shift = norm_one_pull(d_h_one)
    grad_tokens = (d_second + d_inputs_norm).astype(jnp.bfloat16)[None]
    shares = (
        lax.psum_scatter(
            grad_first_gain.astype(jnp.bfloat16), "fsdp", scatter_dimension=0, tiled=True
        ).astype(jnp.float32),
        lax.psum_scatter(
            grad_first_shift.astype(jnp.bfloat16), "fsdp", scatter_dimension=0, tiled=True
        ).astype(jnp.float32),
        lax.psum_scatter(
            grad_query_weight.astype(jnp.bfloat16), "fsdp", scatter_dimension=0, tiled=True
        ).astype(jnp.float32),
        lax.psum_scatter(
            grad_query_bias.astype(jnp.bfloat16), "fsdp", scatter_dimension=0, tiled=True
        ).astype(jnp.float32),
        lax.psum_scatter(
            grad_key_weight.astype(jnp.bfloat16), "fsdp", scatter_dimension=0, tiled=True
        ).astype(jnp.float32),
        lax.psum_scatter(
            grad_value_weight.astype(jnp.bfloat16), "fsdp", scatter_dimension=0, tiled=True
        ).astype(jnp.float32),
        lax.psum_scatter(
            grad_value_bias.astype(jnp.bfloat16), "fsdp", scatter_dimension=0, tiled=True
        ).astype(jnp.float32),
        lax.psum_scatter(
            grad_output_weight.astype(jnp.bfloat16), "fsdp", scatter_dimension=0, tiled=True
        ).astype(jnp.float32),
        lax.psum_scatter(
            grad_output_bias.astype(jnp.bfloat16), "fsdp", scatter_dimension=0, tiled=True
        ).astype(jnp.float32),
        lax.psum_scatter(
            grad_second_gain.astype(jnp.bfloat16), "fsdp", scatter_dimension=0, tiled=True
        ).astype(jnp.float32),
        lax.psum_scatter(
            grad_second_shift.astype(jnp.bfloat16), "fsdp", scatter_dimension=0, tiled=True
        ).astype(jnp.float32),
        lax.psum_scatter(
            grad_up_weight.astype(jnp.bfloat16), "fsdp", scatter_dimension=0, tiled=True
        ).astype(jnp.float32),
        lax.psum_scatter(
            grad_up_bias.astype(jnp.bfloat16), "fsdp", scatter_dimension=0, tiled=True
        ).astype(jnp.float32),
        lax.psum_scatter(
            grad_down_weight.astype(jnp.bfloat16), "fsdp", scatter_dimension=0, tiled=True
        ).astype(jnp.float32),
        lax.psum_scatter(
            grad_down_bias.astype(jnp.bfloat16), "fsdp", scatter_dimension=0, tiled=True
        ).astype(jnp.float32),
    )
    totals = lax.psum(
        (
            shares[0],
            shares[1],
            shares[2],
            shares[3],
            shares[4],
            shares[5],
            shares[6],
            shares[7],
            shares[8],
            shares[9],
            shares[10],
            shares[11],
            shares[12],
            shares[13],
            shares[14],
        ),
        "ctx",
    )
    return (
        layer_output,
        loss_value,
        grad_tokens,
        totals[0],
        totals[1],
        totals[2],
        totals[3],
        totals[4],
        totals[5],
        totals[6],
        totals[7],
        totals[8],
        totals[9],
        totals[10],
        totals[11],
        totals[12],
        totals[13],
        totals[14],
    )


F32 = jnp.float32
BF16 = jnp.bfloat16
ANY = pl.BlockSpec(memory_space=pl.ANY)
HBM = pl.BlockSpec(memory_space=pltpu.HBM)
VMEM = pl.BlockSpec(memory_space=pltpu.VMEM)
SMEM = pl.BlockSpec(memory_space=pltpu.SMEM)
NT = (((1,), (1,)), ((), ()))
TN = (((0,), (0,)), ((), ()))
NN = (((1,), (0,)), ((), ()))


def swap_cores(value):
    size = lax.axis_size("ctx")
    return lax.ppermute(value, "ctx", [(i, i ^ 1) for i in range(size)])


def both_cores(value):
    pairs = [[i, i + 1] for i in range(0, lax.axis_size("ctx"), 2)]
    return lax.all_gather(value, "ctx", axis=0, tiled=True, axis_index_groups=pairs)


def swap_chips(value, step):
    size = lax.axis_size("ctx")
    return lax.ppermute(value, "ctx", [(i, i ^ (2 * step)) for i in range(size)])


def swap_planes(value, step):
    size = lax.axis_size("fsdp")
    return lax.ppermute(value, "fsdp", [(i, i ^ step) for i in range(size)])


def trade_chips(value):
    size = lax.axis_size("ctx")
    groups = [[i for i in range(size) if i % 2 == c] for c in (0, 1)]
    return lax.all_to_all(value, "ctx", 0, 0, axis_index_groups=groups, tiled=True)


def trade_planes(value):
    return lax.all_to_all(value, "fsdp", 0, 0, tiled=True)


def shaped(*shape, dtype=BF16):
    return jax.ShapeDtypeStruct(shape, dtype)


def wide(*shape):
    return jax.ShapeDtypeStruct(shape, F32)


def local_call(
    body,
    outs,
    where,
    args,
    far=(),
    far_outs=(),
    fetch=(),
    store=(),
    scalar=None,
    scratch=(),
    after=(),
    vmem=14,
    cost=0,
):
    fetch, store = list(fetch), list(store)
    args = [
        pltpu.with_memory_space_constraint(a, pltpu.HBM) if i in far or i in fetch else a
        for i, a in enumerate(args)
    ]
    after = list(after)
    many = isinstance(outs, tuple)
    outs = outs if many else (outs,)
    count, made, moved = len(args), len(outs), len(fetch) + len(store)
    held = [pltpu.VMEM(args[i].shape, args[i].dtype) for i in fetch]
    held += [pltpu.VMEM(outs[i].shape, outs[i].dtype) for i in store]
    if moved:
        held.append(pltpu.SemaphoreType.DMA((moved,)))

    def kernel(where_ref, *refs):
        start = count + len(after)
        given, results = list(refs[:count]), list(refs[start : start + made])
        token, extra = refs[start + made], refs[start + made + 1 :]
        extra, copied = extra[: len(extra) - len(held)], extra[len(extra) - len(held) :]
        token[...] = jnp.zeros(token.shape, token.dtype)
        into = [
            pltpu.make_async_copy(given[i], copied[n], copied[-1].at[n])
            for n, i in enumerate(fetch)
        ]
        out_of = [
            pltpu.make_async_copy(copied[n], results[i], copied[-1].at[n])
            for n, i in enumerate(store, len(fetch))
        ]
        for copy in into:
            copy.start()
        for n, i in enumerate(fetch):
            given[i] = copied[n]
        for n, i in enumerate(store, len(fetch)):
            results[i] = copied[n]
        for copy in into:
            copy.wait()
        body(where_ref, *given, *results, *extra)
        for copy in out_of:
            copy.start()
        for copy in out_of:
            copy.wait()

    def place(i):
        return HBM if i in far_outs or i in store else SMEM if i == scalar else VMEM

    results = pl.pallas_call(
        kernel,
        out_shape=(
            *(
                pltpu.HBM(o.shape, o.dtype) if i in far_outs or i in store else o
                for i, o in enumerate(outs)
            ),
            wide(8, 128),
        ),
        in_specs=[SMEM]
        + [HBM if i in far or i in fetch else VMEM for i in range(count)]
        + [ANY] * len(after),
        out_specs=(*(place(i) for i in range(made)), VMEM),
        scratch_shapes=[*scratch, *held],
        compiler_params=pltpu.CompilerParams(vmem_limit_bytes=vmem << 20),
        cost_estimate=pl.CostEstimate(
            flops=cost * 10**9, transcendentals=0, bytes_accessed=cost * 10**6
        ),
    )(where, *args, *after)
    return (results[:-1] if many else results[0]), results[-1]


def core_rows(core, count):
    return pl.ds(pl.multiple_of(count * core, 16), count)


def rows_at(start, count, align):
    return pl.ds(pl.multiple_of(start, align), count)


def dot(left, right, dims):
    return lax.dot_general(left, right, dims, preferred_element_type=F32)


def run_copies(copies, sems):
    started = [
        pltpu.make_async_copy(source, target, sems.at[i])
        for i, (source, target) in enumerate(copies)
    ]
    for copy in started:
        copy.start()
    for copy in started:
        copy.wait()


def unit_rows(values):
    centred = values - jnp.mean(values, axis=-1, keepdims=True)
    spread = jnp.mean(centred * centred, axis=-1, keepdims=True)
    inverse = lax.rsqrt(spread + EPSILON)
    return centred * inverse, inverse


def unit_back(grad, gain, unit, inverse):
    scaled = grad * gain
    return inverse * (
        scaled
        - jnp.mean(scaled, axis=-1, keepdims=True)
        - unit * jnp.mean(scaled * unit, axis=-1, keepdims=True)
    )


def put_small(out, start, small):
    third = small.shape[1] // 3
    lanes = slice(9 * third, 10 * third)
    for q in range(3):
        block = slice(start + 16 * q, start + 16 * (q + 1))
        out[block, lanes] = small[:, third * q : third * (q + 1)].astype(out.dtype)


def get_small(piece, start, feat):
    third = feat // 3
    lanes = slice(9 * third, 10 * third)
    parts = [piece[start + 16 * q : start + 16 * (q + 1), lanes].astype(F32) for q in range(3)]
    return jnp.concatenate(parts, axis=1)


def pack_tokens(where, tokens, segment, valid, out):
    rows, width = tokens.shape
    ids = segment[...]
    line = lax.broadcasted_iota(jnp.int32, (16, rows), 0)
    codes = jnp.where(
        line == 0,
        ids >> 7,
        jnp.where(line == 1, ids & 127, jnp.where(line == 2, valid[...], 0)),
    )
    out[:rows, :] = tokens[...]
    out[rows:, :] = jnp.zeros((16, width), out.dtype)
    out[rows:, :rows] = codes.astype(F32).astype(out.dtype)


def order_chips(where, p0, p1, p2, p3, out):
    rows = p0.shape[0]
    for k, piece in enumerate((p0, p1, p2, p3)):
        out[rows_at(rows * (where[0] ^ k), rows, 16), :] = piece[...]


def far_planes(where, arrived, out):
    part = arrived.shape[0] // 4
    for s in (1, 2, 3):
        out[part * (s - 1) : part * s, :] = arrived[rows_at(part * (where[2] ^ s), part, 16), :]


def pack_projections(where, *refs):
    weights, vectors, long, valid, out = refs[:3], refs[3:11], refs[11], refs[12], refs[13]
    held, small, held_long, sems = refs[14], refs[15:23], refs[23], refs[24]
    half, feat = held.shape[1], small[0].shape[0]
    out[48:, 3 * feat :] = jnp.zeros((half - 48, feat // 3), out.dtype)
    own_rows = rows_at(half * where[1], half, 32)
    run_copies(
        [(w.at[own_rows], held.at[i]) for i, w in enumerate(weights)]
        + list(zip(vectors, small))
        + [(long, held_long)],
        sems,
    )
    for chip in range(4):

        @pl.when(where[0] == chip)
        def _():
            for i in range(3):
                out[:, feat * i : feat * (i + 1)] = held[i, :, feat * chip : feat * (chip + 1)]

    spread = held_long[...].astype(F32).reshape(1, 4 * feat)
    count = jnp.sum(valid[...].astype(F32), axis=1, keepdims=True)
    lines = [v[...].astype(F32).reshape(1, feat) for v in small]
    lines += [spread[:, feat * i : feat * (i + 1)] for i in range(4)]
    lines += [jnp.broadcast_to(count, (1, feat)), jnp.zeros((3, feat), F32)]
    put_small(out, 0, jnp.concatenate(lines, axis=0))


def pack_down(where, down, out, sem):
    part = out.shape[0]
    rows = rows_at(4 * part * where[1] + part * where[0], part, 32)
    copy = pltpu.make_async_copy(down.at[rows], out, sem)
    copy.start()
    copy.wait()


def pack_blocks(where, up, output, out_up, sems):
    chip, core = where[0], where[1]
    part, units = out_up.shape[0] // 4, out_up.shape[1] // 5
    rows = rows_at(part * chip, part, 16)
    pairs = [
        (
            up.at[rows, rows_at(2 * units * i + units * core, units, 128)],
            out_up.at[:part, units * i : units * (i + 1)],
        )
        for i in range(4)
    ]
    pairs.append((output.at[rows, rows_at(units * core, units, 128)], out_up.at[:part, 4 * units :]))
    run_copies(pairs, sems)
    for p in (1, 2, 3):
        out_up[part * p : part * (p + 1), :] = out_up[:part, :]


def stack_rows(where, *refs):
    pieces, out = refs[:-1], refs[-1]
    rows = pieces[0].shape[0]
    for i, piece in enumerate(pieces):
        out[rows * i : rows * (i + 1), :] = piece[...]


def three_blocks(pieces, part):
    p0, p1, p2, low, high = pieces
    parts = [(k, [(p, 0)]) for k, p in enumerate((p0, p1, p2))] + [(3, [(low, 0), (high, low.shape[0])])]
    found = []
    for k, refs in parts:
        for s in (1, 2, 3):
            for ref, base in refs:
                start, end = max(part * (s - 1), base), min(part * s, base + ref.shape[0])
                if start < end:
                    found.append((k, s, start - part * (s - 1), end - start, ref, start - base))
    return found


def cross_halves(where, from_x, from_y, to_x, to_y):
    cut = to_x.shape[0]
    to_x[...] = from_y[:cut, :]
    to_y[...] = from_x[cut:, :]


def build_up(where, up, p0, p1, p2, p3, p4, out, sems):
    chip, core, plane = where[0], where[1], where[2]
    units, shard = up.shape[1] // 8, up.shape[0]
    part = shard // 4
    own = rows_at(shard * plane, shard, 64)
    pairs = [
        (
            up.at[:, rows_at(2 * units * i + units * core, units, 128)],
            out.at[own, units * i : units * (i + 1)],
        )
        for i in range(4)
    ]
    for k, s, offset, count, piece, start in three_blocks((p0, p1, p2, p3, p4), part):
        at = rows_at(shard * (plane ^ s) + part * (chip ^ k) + offset, count, 16)
        pairs.append((piece.at[start : start + count, : 4 * units], out.at[at]))
    run_copies(pairs, sems)


def build_half(where, output, p0, p1, p2, p3, p4, out, sems):
    chip, core, plane = where[0], where[1], where[2]
    shard, units = output.shape[0], out.shape[1]
    part = shard // 4
    pairs = [
        (
            output.at[:, rows_at(units * core, units, 128)],
            out.at[rows_at(shard * plane, shard, 64)],
        )
    ]
    for k, s, offset, count, piece, start in three_blocks((p0, p1, p2, p3, p4), part):
        at = rows_at(shard * (plane ^ s) + part * (chip ^ k) + offset, count, 16)
        pairs.append((piece.at[start : start + count, 4 * units :], out.at[at]))
    run_copies(pairs, sems)


def build_down(where, down, p0, p1, p2, p3, p4, out, sem):
    chip, core, plane = where[0], where[1], where[2]
    mine = down.shape[0] // 2
    part = mine // 4
    own = pltpu.make_async_copy(
        down.at[rows_at(mine * core, mine, 128)], out.at[rows_at(mine * plane, mine, 128)], sem
    )
    own.start()
    for k, s, offset, count, piece, start in three_blocks((p0, p1, p2, p3, p4), part):
        at = rows_at(mine * (plane ^ s) + part * (chip ^ k) + offset, count, 16)
        out[at, :] = piece[start : start + count, :]
    own.wait()


def build_output(where, near, far, out):
    units = near.shape[1]
    out[:, rows_at(units * where[1], units, 128)] = near[...]
    out[:, rows_at(units * (1 - where[1]), units, 128)] = far[...]


def normalize_tokens(where, near, far, unit_low, key_row, query_column):
    rows = query_column.shape[0] // 4
    for i in range(8):
        block = (near if i < 4 else far).at[(rows + 16) * (i % 4) : (rows + 16) * (i % 4 + 1), :]
        unit, _ = unit_rows(block[:rows, :].astype(F32))
        unit_low[rows * i : rows * (i + 1), :] = unit
        codes = block[rows:, :].astype(F32)
        ids = codes[0:1, :rows] * 128.0 + codes[1:2, :rows]
        key_row[0:1, rows * i : rows * (i + 1)] = jnp.where(codes[2:3, :rows] == 1.0, ids, -1.0)
        if i < 4:
            query_column[rows * i : rows * (i + 1), :] = jnp.broadcast_to(
                ids.reshape(rows, 1), (rows, 128)
            )


def attend(where, *refs):
    units, key_row, query_column, weights, far_weights = refs[:3] + (refs[3:7], refs[7])
    saved, sent, vectors, long = refs[8:13], refs[13], refs[14], refs[15]
    small, bias, h_one, w_three, projected, probs, mixed, sems = refs[16:]
    kept = (h_one, w_three, projected, mixed)
    copies = [
        pltpu.make_async_copy(source, saved[i], sems.at[j])
        for j, (i, source) in enumerate(zip((0, 1, 2, 4), kept))
    ]
    core, plane = where[1], where[2]
    half, feat = weights[0].shape[0], small.shape[2]
    group = query_column.shape[0]
    rows = group // 4

    count = jnp.zeros((1, 1), F32)
    for s, piece in enumerate(weights):
        base = 2 * half * (plane ^ s)
        w_three[rows_at(base + half * core, half, 32), :] = piece[:, : 3 * feat]
        other = far_weights[half * s : half * (s + 1), :]
        w_three[rows_at(base + half * (1 - core), half, 32), :] = other[:, : 3 * feat]
        near = get_small(piece, 0, feat)
        small[plane ^ s] = near
        count += near[12:13, :1] + other[12:13, 3 * feat : 3 * feat + 1].astype(F32)
    vectors[...] = jnp.zeros(vectors.shape, F32)
    for p in range(4):
        lines = small[p]
        for i, r in enumerate((0, 1, 4, 5, 6, 7)):
            vectors[i : i + 1, feat * p : feat * (p + 1)] = lines[r : r + 1, :]
        pair = jnp.where(core == 0, lines[8:10, :], lines[10:12, :])
        long[:, 2 * feat * p : 2 * feat * p + feat] = pair[:1, :]
        long[:, 2 * feat * p + feat : 2 * feat * (p + 1)] = pair[1:, :]
    gain, shift = vectors[0:1, :], vectors[1:2, :]
    short = small[where[0]]
    copies[1].start()
    h_one[...] = (units[...] * gain + shift).astype(BF16)
    copies[0].start()
    values = dot(h_one[...], w_three[...], NN)
    query = (values[:group, :feat] + short[2:3, :]).astype(BF16) * jnp.asarray(
        HEAD_DIM**-0.5, BF16
    )
    projected[:group, :feat] = query
    projected[group:, :feat] = jnp.zeros((group, feat), BF16)
    projected[:, feat : 2 * feat] = values[:, feat : 2 * feat].astype(BF16)
    projected[:, 2 * feat :] = (values[:, 2 * feat :] + short[3:4, :]).astype(BF16)
    copies[2].start()
    column = lax.broadcasted_iota(jnp.int32, (rows, 2 * group), 1)
    line = lax.broadcasted_iota(jnp.int32, (rows, 2 * group), 0)
    for k in range(4):
        ids = query_column[rows * k : rows * (k + 1), :1]
        allowed = (ids == key_row[0:1, :]) | (column == line + rows * k)
        bias[rows * k : rows * (k + 1), :] = jnp.where(allowed, 0.0, MASKED)
    for h in range(feat // HEAD_DIM):
        at = slice(HEAD_DIM * h, HEAD_DIM * (h + 1))
        keys = projected[:, feat + HEAD_DIM * h : feat + HEAD_DIM * (h + 1)]
        held = projected[:, 2 * feat + HEAD_DIM * h : 2 * feat + HEAD_DIM * (h + 1)]
        for k in range(4):
            block = slice(rows * k, rows * (k + 1))
            scores = dot(projected[block, at], keys, NT) + bias[block, :]
            weight = jnp.exp(scores - jnp.max(scores, axis=1, keepdims=True))
            weight = weight * (1.0 / jnp.sum(weight, axis=1, keepdims=True))
            low = weight.astype(BF16)
            probs[h, block, :] = low
            result = dot(low, held, NN)
            mixed[block, at] = result
            sent[(rows + 16) * k : (rows + 16) * k + rows, at] = result.astype(BF16)
        copies.append(pltpu.make_async_copy(probs.at[h], saved[3].at[h], sems.at[4 + h]))
        copies[-1].start()
    copies[3].start()
    high = jnp.floor(count / 128.0)
    side = lax.broadcasted_iota(jnp.int32, (16, feat), 1)
    digits = jnp.where(side == 0, high, jnp.where(side == 1, count - 128.0 * high, 0.0))
    for k in range(4):
        sent[(rows + 16) * k + rows : (rows + 16) * (k + 1), :] = digits.astype(BF16)
    for copy in copies:
        copy.wait()


def attend_back(where, d_all, vectors, *refs):
    saved, (near, far, kept, given, lines) = refs[:5], refs[5:10]
    d_three, d_scores, grads, h_one, w_three, projected, probs, mixed, sems = refs[10:]
    core = where[1]
    pairs = [(saved[2], projected), (saved[4], mixed)]
    pairs += [(saved[3].at[h], probs.at[h]) for h in range(probs.shape[0])]
    pairs += [(saved[0], h_one), (saved[1], w_three)]
    copies = [pltpu.make_async_copy(a, b, sems.at[i]) for i, (a, b) in enumerate(pairs)]
    for copy in copies:
        copy.start()
    copies[0].wait()
    copies[1].wait()
    group, feat = d_all.shape
    rows, width = group // 4, h_one.shape[1]
    scale = HEAD_DIM**-0.5
    d_three[group:, :feat] = jnp.zeros((group, feat), BF16)
    for h in range(feat // HEAD_DIM):
        at = slice(HEAD_DIM * h, HEAD_DIM * (h + 1))
        key_at = slice(feat + HEAD_DIM * h, feat + HEAD_DIM * (h + 1))
        value_at = slice(2 * feat + HEAD_DIM * h, 2 * feat + HEAD_DIM * (h + 1))
        keys, held = projected[:, key_at], projected[:, value_at]
        copies[2 + h].wait()
        for k in range(4):
            block = slice(rows * k, rows * (k + 1))
            d_mixed = d_all[block, at]
            delta = jnp.sum(d_mixed.astype(F32) * mixed[block, at], axis=1, keepdims=True)
            d_probs = dot(d_mixed, held, NT)
            low = (probs[h, block, :].astype(F32) * (d_probs - delta)).astype(BF16)
            d_scores[block, :] = low
            d_three[block, at] = (dot(low, keys, NN) * scale).astype(BF16)
        d_three[:, key_at] = dot(d_scores[...], projected[:group, at], TN).astype(BF16)
        d_three[:, value_at] = dot(probs[h], d_all[:, at], TN).astype(BF16)
    for copy in copies[2 + probs.shape[0] :]:
        copy.wait()
    grads[...] = dot(h_one[...], d_three[...], TN)
    near[...] = dot(d_three[:group, :], w_three[...], NT).astype(BF16)
    far[...] = dot(d_three[group:, :], w_three[...], NT).astype(BF16)
    half = kept.shape[0] // 4
    for p in range(4):
        block = slice(half * p, half * (p + 1))
        kept[block, :] = grads[rows_at(2 * half * p + half * core, half, 32), :].astype(BF16)
        given[block, :] = grads[rows_at(2 * half * p + half * (1 - core), half, 32), :].astype(BF16)
    sums = jnp.sum(d_three[...].astype(F32), axis=0, keepdims=True)
    weight = w_three[...].astype(F32)
    with_gain = jnp.sum(grads[...] * weight, axis=1, keepdims=True)
    with_shift = jnp.sum(weight * sums, axis=1, keepdims=True)
    side = lax.broadcasted_iota(jnp.int32, (width, 128), 1)
    both = jnp.where(side == 0, with_gain, jnp.where(side == 1, with_shift, 0.0)).T
    d_shift = both[1:2, :]
    lines[0:1, :] = (both[0:1, :] - vectors[1:2, :] * d_shift) / vectors[0:1, :]
    lines[1:2, :] = d_shift
    lines[2:3, :] = jnp.zeros((1, width), F32)
    lines[2:3, :feat] = sums[:, :feat]
    lines[3:4, :] = jnp.zeros((1, width), F32)
    lines[3:4, :feat] = sums[:, 2 * feat :]
    lines[4:, :] = jnp.zeros((4, width), F32)


def share_inputs(where, near, far, *outs):
    rows = outs[0].shape[0]
    for k, out in enumerate(outs):
        at = rows_at(rows * (where[0] ^ k), rows, 16)
        out[...] = (near[at, :].astype(F32) + far[at, :].astype(F32)).astype(out.dtype)


def finish_inputs(where, d0, d1, d2, d3, tokens, d_second, vectors, out):
    total = d0[...].astype(F32)
    for piece in (d1, d2, d3):
        total = total + piece[...].astype(F32)
    unit, inverse = unit_rows(tokens[...].astype(F32))
    d_inputs = unit_back(total, vectors[0:1, :], unit, inverse)
    out[...] = (d_second[...] + d_inputs).astype(BF16)


def project_output(where, mixed, w_output, tokens, vectors, second, h_two, count):
    rows, width = tokens.shape
    feat = mixed.shape[1]
    total = tokens[...].astype(F32) + vectors[2:3, :]
    valid = jnp.zeros((1, 1), F32)
    for k in range(4):
        start = (rows + 16) * k
        total += dot(mixed[start : start + rows, :], w_output[feat * k : feat * (k + 1), :], NN)
        digits = mixed[start + rows : start + rows + 16, :].astype(F32)
        valid += digits[0:1, 0:1] * 128.0 + digits[0:1, 1:2]
    second[...] = total
    unit, _ = unit_rows(total)
    h_two[...] = (unit * vectors[3:4, :] + vectors[4:5, :]).astype(BF16)
    count[...] = jnp.broadcast_to(valid, count.shape)


def activate(where, h_pair, w_up, b_up, act, slope):
    rows = h_pair.shape[0] // 2
    root = 0.7978845608028654
    for i in range(2):
        block = slice(rows * i, rows * (i + 1))
        value = dot(h_pair[block, :], w_up[...], NN) + b_up[...]
        square = value * value
        bent = jnp.tanh(root * value * (1.0 + 0.044715 * square))
        act[block, :] = (0.5 * value * (1.0 + bent)).astype(BF16)
        slope[block, :] = 0.5 * (1.0 + bent) + 0.5 * value * (1.0 - bent * bent) * root * (
            1.0 + 3.0 * 0.044715 * square
        )


def project_down(where, act, w_down, near, far):
    rows, core = near.shape[0], where[1]
    near[...] = dot(act[core_rows(core, rows), :], w_down[...], NN)
    far[...] = dot(act[core_rows(1 - core, rows), :], w_down[...], NN).astype(BF16)


def compare(where, second, near, far, vectors, teacher, cotangent, valid, count, *outs):
    layer_output, d_result, d_down, lines = outs
    rows, width = second.shape
    other = far[core_rows(1 - where[1], rows), :].astype(F32)
    result = second[...] + near[...] + other + vectors[5:6, :]
    layer_output[...] = result.astype(BF16)
    kept = valid[...].astype(F32).reshape(rows, 1)
    mismatch = result - teacher[...].astype(F32)
    weighted = kept * mismatch
    error = jnp.sum(jnp.sum(weighted * mismatch, axis=1, keepdims=True), axis=0, keepdims=True)
    total = cotangent[...].astype(F32) + 2.0 / (width * count[0:1, 0:1]) * weighted
    d_result[...] = total
    low = total.astype(BF16)
    d_down[...] = low
    high = error.astype(BF16).astype(F32)
    middle = (error - high).astype(BF16).astype(F32)
    side = lax.broadcasted_iota(jnp.int32, (1, width), 1)
    parts = jnp.where(
        side == 0, high, jnp.where(side == 1, middle, jnp.where(side == 2, error - high - middle, 0.0))
    )
    lines[0:1, :] = jnp.sum(low.astype(F32), axis=0, keepdims=True)
    lines[1:2, :] = parts
    lines[2:, :] = jnp.zeros((6, width), F32)


def activate_back(where, d_down, w_down, slope, w_up, d_up, near, far, line):
    rows, core = near.shape[0], where[1]
    total = jnp.zeros(line.shape, F32)
    for i in range(2):
        block = slice(rows * i, rows * (i + 1))
        low = (dot(d_down[block, :], w_down[...], NT) * slope[block, :]).astype(BF16)
        d_up[block, :] = low
        total += jnp.sum(low.astype(F32), axis=0, keepdims=True)
    line[...] = total
    near[...] = dot(d_up[core_rows(core, rows), :], w_up[...], NT)
    far[...] = dot(d_up[core_rows(1 - core, rows), :], w_up[...], NT).astype(BF16)


def second_back(where, near, far, d_result, second, vectors, w_output, *outs):
    d_second, d_attn, lines, sent = outs
    rows = near.shape[0]
    d_two = near[...] + far[core_rows(1 - where[1], rows), :].astype(F32)
    unit, inverse = unit_rows(second[...])
    total = d_result[...] + unit_back(d_two, vectors[3:4, :], unit, inverse)
    d_second[...] = total
    low = total.astype(BF16)
    d_attn[...] = low
    lines[0:1, :] = jnp.sum(low.astype(F32), axis=0, keepdims=True)
    lines[1:2, :] = jnp.sum(d_two * unit, axis=0, keepdims=True)
    lines[2:3, :] = jnp.sum(d_two, axis=0, keepdims=True)
    lines[3:, :] = jnp.zeros((5, lines.shape[1]), F32)
    feat = sent.shape[1]
    for k in range(4):
        part = w_output[feat * k : feat * (k + 1), :]
        sent[rows * k : rows * (k + 1), :] = dot(low, part, NT).astype(BF16)


def split_chips(chip, block, outs, count):
    own, to_x, to_y, then_x, then_y = outs
    for p in range(4):
        own[count * p : count * (p + 1), :] = block(chip, p).astype(BF16)
    for p in (0, 1):
        low, high = slice(count * p, count * (p + 1)), slice(count * (p + 2), count * (p + 3))
        to_x[low, :] = block(chip ^ 1, p).astype(BF16)
        to_x[high, :] = block(chip ^ 3, p).astype(BF16)
        to_y[low, :] = block(chip ^ 2, p + 2).astype(BF16)
        to_y[high, :] = block(chip ^ 3, p + 2).astype(BF16)
        then_x[low, :] = block(chip ^ 1, p + 2).astype(BF16)
        then_y[low, :] = block(chip ^ 2, p).astype(BF16)


def pass_on(where, from_x, from_y, then_x, then_y, to_x, to_y):
    half = to_x.shape[0]
    to_x[...] = (then_x[...].astype(F32) + from_y[half:, :].astype(F32)).astype(BF16)
    to_y[...] = (then_y[...].astype(F32) + from_x[half:, :].astype(F32)).astype(BF16)


def add_chips(own, from_x, from_y, last_x, last_y):
    half = last_x.shape[0]
    low = own[:half, :].astype(F32) + from_x[:half, :].astype(F32) + last_y[...].astype(F32)
    high = own[half:, :].astype(F32) + from_y[:half, :].astype(F32) + last_x[...].astype(F32)
    return low, high


def down_grads(where, act, d_down, *refs):
    outs, total = refs[:5], refs[5]
    count = outs[0].shape[0] // 4
    total[...] = dot(act[...], d_down[...], TN).astype(BF16)

    def block(j, p):
        return total[rows_at(4 * count * p + count * j, count, 32), :]

    split_chips(where[0], block, outs, count)


def output_grads(where, mixed, d_attn, kept, given):
    core = where[1]
    rows, width = d_attn.shape
    feat, units = mixed.shape[1], width // 2
    mine = d_attn[:, rows_at(units * core, units, 128)]
    others = d_attn[:, rows_at(units * (1 - core), units, 128)]
    for j in range(4):
        at = slice(feat * j, feat * (j + 1))
        piece = mixed[(rows + 16) * j : (rows + 16) * j + rows, :]
        kept[at, :] = dot(piece, mine, TN).astype(BF16)
        given[at, :] = dot(piece, others, TN).astype(BF16)


def up_grads(where, h_pair, d_up, kept, given, *refs):
    outs, total = refs[:4], refs[4]
    count, units = outs[0].shape[0] // 4, d_up.shape[1]
    total[:, :units] = dot(h_pair[...], d_up[...], TN).astype(BF16)
    total[:, units:] = (kept[...].astype(F32) + given[...].astype(F32)).astype(BF16)
    for k, out in enumerate(outs):
        for p in range(4):
            at = rows_at(4 * count * p + count * (where[0] ^ k), count, 16)
            out[count * p : count * (p + 1), :] = total[at, :]


def send_planes(where, own, p1, p2, p3, *refs):
    outs, total = refs[:4], refs[4]
    part = outs[0].shape[0]
    added = own[...].astype(F32)
    for piece in (p1, p2, p3):
        added = added + piece[...].astype(F32)
    total[...] = added
    for s, out in enumerate(outs):
        out[...] = total[rows_at(part * (where[2] ^ s), part, 16), :].astype(out.dtype)


def sum_pieces(where, own, p1, p2, p3, out):
    total = own[...].astype(F32)
    for piece in (p1, p2, p3):
        total = total + piece[...].astype(F32)
    out[...] = total.astype(out.dtype)


def finish_down(where, near, far, out, held, sems):
    core = where[1]
    both = near.shape[0] // 4
    part = both // 2
    copies = []
    for j in range(4):
        block = slice(both * j + part, both * (j + 1))
        for side, piece in ((core, near), (1 - core, far)):
            at = rows_at(4 * part * side + part * j, part, 32)
            held[at, :] = piece[block, :].astype(F32)
            copies.append(pltpu.make_async_copy(held.at[at], out.at[at], sems.at[len(copies)]))
            copies[-1].start()
    for copy in copies:
        copy.wait()


def finish_up(where, n0, n1, n2, n3, far, out, out_half, held, held_half, sems):
    chip, core = where[0], where[1]
    part, units = n0.shape[0], n0.shape[1] // 5
    copies = []
    for k, near in enumerate((n0, n1, n2, n3)):
        rows = rows_at(part * (chip ^ k), part, 16)
        for piece, side in ((near[...], core), (far[part * k : part * (k + 1), :], 1 - core)):
            full = piece.astype(F32)
            for i in range(4):
                at = rows_at(2 * units * i + units * side, units, 128)
                held[rows, at] = full[:, units * i : units * (i + 1)]
            held_half[rows, rows_at(units * side, units, 128)] = full[:, 4 * units :]
        for source, target in ((held, out), (held_half, out_half)):
            copies.append(
                pltpu.make_async_copy(source.at[rows], target.at[rows], sems.at[len(copies)])
            )
            copies[-1].start()
    for copy in copies:
        copy.wait()


def sum_chips(where, own, from_x, from_y, last_x, last_y, out):
    half = last_x.shape[0]
    low, high = add_chips(own, from_x, from_y, last_x, last_y)
    out[:half, :], out[half:, :] = low.astype(BF16), high.astype(BF16)


def pack_gradients(
    where, kept, given, from_attention, from_second, from_result, up_line, down, out, down_sum
):
    chip = where[0]
    part = down_sum.shape[0]
    arrived_down = down[:part, :].astype(F32)
    for p in (1, 2, 3):
        arrived_down = arrived_down + down[part * p : part * (p + 1), :].astype(F32)
    down_sum[...] = arrived_down.astype(BF16)
    half, feat = out.shape[0] // 4, kept.shape[1] // 3
    for p in range(4):
        cut = slice(feat * p, feat * (p + 1))
        owner = jnp.where(chip == p, 1.0, 0.0)
        lines = [
            from_attention[0:1, cut],
            from_attention[1:2, cut],
            from_second[0:1, cut],
            from_second[1:2, cut],
            from_second[2:3, cut],
            from_result[0:1, cut],
            up_line[:, 2 * feat * p : 2 * feat * p + feat],
            up_line[:, 2 * feat * p + feat : 2 * feat * (p + 1)],
            from_attention[2:3, :feat] * owner,
            from_attention[3:4, :feat] * owner,
            from_result[1:2, :feat],
            jnp.zeros((5, feat), F32),
        ]
        small = jnp.concatenate(lines, axis=0)
        block = slice(half * p, half * (p + 1))
        total = (kept[block, :].astype(F32) + given[block, :].astype(F32)).astype(BF16)
        out[block, : 3 * feat] = total
        out[half * p + 48 : half * (p + 1), 3 * feat :] = jnp.zeros((half - 48, feat // 3), BF16)
        put_small(out, half * p, small)


def sum_planes(where, arrived, down, out):
    both, width = out.shape[0] // 4, out.shape[1]
    half, feat = both // 2, width // 4
    total = arrived[:half, :].astype(F32)
    for p in (1, 2, 3):
        total = total + arrived[half * p : half * (p + 1), :].astype(F32)
    small = get_small(total, 0, feat)
    error = jnp.sum(small[10:11, :3], axis=1, keepdims=True)
    high = error.astype(BF16).astype(F32)
    middle = (error - high).astype(BF16).astype(F32)
    line = lax.broadcasted_iota(jnp.int32, small.shape, 0)
    side = lax.broadcasted_iota(jnp.int32, small.shape, 1)
    parts = jnp.where(side == 0, high, jnp.where(side == 1, middle, error - high - middle))
    small = jnp.where((line == 10) & (side < 3), parts, small)
    for j in range(4):
        start = both * j
        out[start : start + half, : 3 * feat] = total[:, : 3 * feat].astype(BF16)
        out[start : start + 16, 3 * feat :] = small.astype(BF16)
        out[start + 16 : start + half, 3 * feat :] = jnp.zeros((half - 16, feat), BF16)
        out[start + half : start + both, :] = down[...]


def finish_projections(where, near, far, count, *outs):
    query, key, value, loss = outs[:4]
    flat, up_line, held, whole_line = outs[4:12], outs[12], outs[13], outs[14]
    core = where[1]
    both, width = near.shape[0] // 4, near.shape[1]
    half, feat = both // 2, width // 4
    for j in range(4):
        start = both * j
        for side, piece in ((core, near), (1 - core, far)):
            held[2 * j + side] = piece[start : start + 16, 3 * feat :].astype(F32)
            rows = rows_at(half * side, half, 32)
            for i, out in enumerate((query, key, value)):
                out[rows, feat * j : feat * (j + 1)] = piece[
                    start : start + half, feat * i : feat * (i + 1)
                ].astype(F32)
    total = held[0]
    for i in range(1, 8):
        total = total + held[i]
    for i, line in enumerate((0, 1, 2, 3, 4, 5, 8, 9)):
        flat[i][...] = total[line]
    even = held[0] + held[2] + held[4] + held[6]
    odd = held[1] + held[3] + held[5] + held[7]
    for side, part in enumerate((even, odd)):
        for i in range(2):
            at = 2 * feat * side + feat * i
            whole_line[0:1, at : at + feat] = part[6 + i : 7 + i, :]
    up_line[...] = whole_line[0]
    error = jnp.sum(total[10:11, :3], axis=1, keepdims=True)
    loss[0, 0] = jnp.sum(error / (width * count[0:1, 0:1]))


def layer(
    tokens,
    segment_ids,
    valid_rows,
    teacher,
    cotangent,
    first_gain,
    first_shift,
    query_weight,
    query_bias,
    key_weight,
    value_weight,
    value_bias,
    output_weight,
    output_bias,
    second_gain,
    second_shift,
    up_weight,
    up_bias,
    down_weight,
    down_bias,
):
    rows, width = tokens.shape[1], tokens.shape[2]
    shard = query_weight.shape[0]
    half, quarter = shard // 2, shard // 4
    hidden = up_weight.shape[1]
    units = hidden // 2
    own_units = down_weight.shape[0]
    core_units = own_units // 2
    part_units = core_units // 4
    feat = width // 4
    heads = feat // HEAD_DIM
    group = 4 * rows
    every = 2 * group
    steps = (1, 2, 3)

    place, plane = lax.axis_index("ctx"), lax.axis_index("fsdp")
    where = jnp.stack([place // 2, place % 2, plane]).astype(jnp.int32)
    dma = pltpu.SemaphoreType.DMA

    last = []

    def step(body, outs, args, **options):
        made, token = local_call(body, outs, where, args, after=last, **options)
        last[:] = [token]
        return made

    def stack(pieces, cost=0):
        shape = len(pieces) * pieces[0].shape[0], pieces[0].shape[1]
        return step(stack_rows, shaped(*shape), pieces, cost=cost)

    own = tokens[0]
    smalls = (
        first_gain,
        first_shift,
        query_bias,
        value_bias,
        output_bias,
        second_gain,
        second_shift,
        down_bias,
    )
    up_piece = step(
        pack_blocks,
        shaped(4 * quarter, 5 * core_units),
        (up_weight, output_weight),
        far=range(2),
        scratch=[dma((5,))],
    )
    up_far = trade_planes(up_piece)
    bundle = step(pack_tokens, shaped(rows + 16, width), (own, segment_ids, valid_rows), cost=50)
    near_tokens = [bundle] + [swap_chips(bundle, k) for k in steps]
    lanes = 3 * feat + feat // 3
    projections = step(
        pack_projections,
        shaped(half, lanes),
        (query_weight, key_weight, value_weight, *smalls, up_bias, valid_rows),
        far=range(12),
        scratch=[
            pltpu.VMEM((3, half, width), BF16),
            *[pltpu.VMEM((feat,), BF16)] * 8,
            pltpu.VMEM((own_units,), BF16),
            dma((12,)),
        ],
        cost=0,
    )
    near_tokens = step(order_chips, shaped(4 * (rows + 16), width), near_tokens, cost=0)
    far_tokens = swap_cores(near_tokens)
    up_far = step(far_planes, shaped(3 * quarter, 5 * core_units), (up_far,), cost=0)
    up_three = up_far, swap_chips(up_far, 1), swap_chips(up_far, 2)
    near_weights = [projections] + [swap_planes(projections, s) for s in steps]
    unit_one, key_row, query_column = step(
        normalize_tokens,
        (wide(every, width), wide(8, every), wide(group, 128)),
        (near_tokens, far_tokens),
        cost=1,
    )
    far_weights = swap_cores(stack(near_weights))

    def first_chips(piece):
        return piece, swap_chips(piece, 1), swap_chips(piece, 2)

    def all_chips(three, cut):
        count, lanes = three[0].shape
        to_x, to_y = step(cross_halves, (shaped(cut, lanes), shaped(count - cut, lanes)), three[1:], cost=50)
        return (*three, swap_chips(to_x, 1), swap_chips(to_y, 2))

    up_all = all_chips(up_three, up_far.shape[0] // 32 * 16 + 16)
    down_piece = step(
        pack_down, shaped(part_units, width), (down_weight,), far=(0,), scratch=[dma]
    )
    down_far = [swap_planes(down_piece, s) for s in steps]

    h_one, w_three, projected, probs, mixed, sent, vectors, b_up = step(
        attend,
        (
            shaped(every, width),
            shaped(width, 3 * feat),
            shaped(every, 3 * feat),
            shaped(heads, group, every),
            wide(group, feat),
            shaped(4 * (rows + 16), feat),
            wide(8, width),
            wide(1, units),
        ),
        (unit_one, key_row, query_column, *near_weights, far_weights),
        far_outs=range(5),
        scratch=[
            pltpu.VMEM((4, 16, feat), F32),
            pltpu.VMEM((group, every), F32),
            pltpu.VMEM((every, width), BF16),
            pltpu.VMEM((width, 3 * feat), BF16),
            pltpu.VMEM((every, 3 * feat), BF16),
            pltpu.VMEM((heads, group, every), BF16),
            pltpu.VMEM((group, feat), F32),
            dma((4 + heads,)),
        ],
        vmem=28,
        cost=50,
    )
    mixed_low = trade_chips(sent)
    down_far = first_chips(stack(down_far))
    out_near = step(
        build_half,
        shaped(width, core_units),
        (output_weight, *up_all),
        far=range(6),
        scratch=[dma((20,))],
    )
    out_far = swap_cores(out_near)
    w_up = step(
        build_up, shaped(width, units), (up_weight, *up_all), far=range(6), scratch=[dma((20,))], cost=50
    )
    w_output = step(build_output, shaped(width, width), (out_near, out_far))

    down_all = all_chips(down_far, down_far[0].shape[0] // 2)
    second, h_two, count = step(
        project_output,
        (wide(rows, width), shaped(rows, width), wide(8, 128)),
        (mixed_low, w_output, own, vectors),
    )
    h_pair = both_cores(h_two)
    act, slope = step(
        activate,
        (shaped(2 * rows, units), wide(2 * rows, units)),
        (h_pair, w_up, b_up),
    )
    w_down = step(
        build_down, shaped(units, width), (down_weight, *down_all), far=(0,), scratch=[dma]
    )
    down_near, down_other = step(
        project_down, (wide(rows, width), shaped(rows, width)), (act, w_down)
    )
    layer_output, d_result, d_down, from_result = step(
        compare,
        (shaped(rows, width), wide(rows, width), shaped(rows, width), wide(8, width)),
        (
            second,
            down_near,
            both_cores(down_other),
            vectors,
            teacher[0],
            cotangent[0],
            valid_rows,
            count,
        ),
    )
    d_down = both_cores(d_down)

    def five(count, lanes):
        return (shaped(4 * count, lanes),) * 3 + (shaped(2 * count, lanes),) * 2

    def onward(parts, arrived):
        count, lanes = parts[3].shape
        to_x, to_y = step(
            pass_on, (shaped(count, lanes),) * 2, (*arrived, *parts[3:]),
            cost=50,
        )
        return (parts[0], *arrived, swap_chips(to_x, 1), swap_chips(to_y, 2))

    down_parts = step(
        down_grads,
        five(part_units, width),
        (act, d_down),
        scratch=[pltpu.VMEM((units, width), BF16)],
        vmem=24,
    )
    down_arrived = swap_chips(down_parts[1], 1), swap_chips(down_parts[2], 2)
    d_up, two_near, two_other, up_line = step(
        activate_back,
        (shaped(2 * rows, units), wide(rows, width), shaped(rows, width), wide(1, units)),
        (d_down, w_down, slope, w_up),
        cost=50,
    )
    d_second, d_attn, from_second, d_sent = step(
        second_back,
        (wide(rows, width), shaped(rows, width), wide(8, width), shaped(group, feat)),
        (two_near, both_cores(two_other), d_result, second, vectors, w_output),
    )
    d_mixed = trade_chips(d_sent)

    kept_out, given_out = step(
        output_grads,
        (shaped(width, core_units), shaped(width, core_units)),
        (mixed_low, d_attn),
        cost=1,
    )
    given_out = swap_cores(given_out)
    down_sums = onward(down_parts, down_arrived)
    up_parts = step(
        up_grads,
        (shaped(4 * quarter, 5 * core_units),) * 4,
        (h_pair, d_up, kept_out, given_out),
        store=(0,),
        scratch=[pltpu.VMEM((width, 5 * core_units), BF16)],
        vmem=24,
        cost=5,
    )
    up_sums = [up_parts[0]] + [swap_chips(up_parts[k], k) for k in steps]
    down_planes = trade_planes(step(sum_chips, shaped(4 * part_units, width), down_sums))

    d_near, d_far, kept, given, from_attention = step(
        attend_back,
        (
            shaped(group, width),
            shaped(group, width),
            shaped(4 * half, 3 * feat),
            shaped(4 * half, 3 * feat),
            wide(8, width),
        ),
        (d_mixed, vectors, h_one, w_three, projected, probs, mixed),
        far=range(2, 7),
        store=(2, 3),
        scratch=[
            pltpu.VMEM((every, 3 * feat), BF16),
            pltpu.VMEM((group, every), BF16),
            pltpu.VMEM((width, 3 * feat), F32),
            pltpu.VMEM((every, width), BF16),
            pltpu.VMEM((width, 3 * feat), BF16),
            pltpu.VMEM((every, 3 * feat), BF16),
            pltpu.VMEM((heads, group, every), BF16),
            pltpu.VMEM((group, feat), F32),
            dma((4 + heads,)),
        ],
        vmem=28,
        cost=50,
    )
    given, d_far = swap_cores(given), swap_cores(d_far)
    arrived, down_planes = step(
        pack_gradients,
        (shaped(4 * half, lanes), shaped(part_units, width)),
        (kept, given, from_attention, from_second, from_result, up_line, down_planes),
        fetch=(0, 1),
        cost=1,
    )
    arrived = trade_planes(arrived)

    def spread(piece):
        return [piece] + [swap_chips(piece, k) for k in steps]

    def whole(near):
        return (*near, swap_cores(stack(near, cost=1)))

    up_planes = step(
        send_planes,
        (shaped(quarter, 5 * core_units),) * 4,
        up_sums,
        fetch=(0,),
        scratch=[pltpu.VMEM((4 * quarter, 5 * core_units), F32)],
        cost=50,
    )
    up_planes = [up_planes[0]] + [swap_planes(up_planes[s], s) for s in steps]
    shares = step(share_inputs, (shaped(rows, width),) * 4, (d_near, d_far), store=(0,), cost=50)
    shares = [shares[0]] + [swap_chips(shares[k], k) for k in steps]
    both = trade_chips(step(sum_planes, shaped(8 * half, width), (arrived, down_planes), cost=50))
    up_near = spread(step(sum_pieces, shaped(quarter, 5 * core_units), up_planes, cost=50))
    grad_tokens = step(
        finish_inputs, shaped(rows, width), (*shares, own, d_second, vectors), fetch=(0, 4), cost=50
    )
    both = (both, swap_cores(both))
    up_whole = whole(up_near)
    finished = step(
        finish_projections,
        (wide(shard, width),) * 3
        + (wide(1, 1),)
        + (wide(shard),) * 8
        + (wide(own_units),),
        (*both, count),
        scratch=[pltpu.VMEM((8, 16, feat), F32), pltpu.VMEM((8, own_units), F32)],
        scalar=3,
    )
    grad_down_weight = step(
        finish_down,
        wide(own_units, width),
        both,
        far_outs=(0,),
        scratch=[pltpu.VMEM((own_units, width), F32), dma((8,))],
    )
    grad_up_weight, grad_output_weight = step(
        finish_up,
        (wide(shard, hidden), wide(shard, width)),
        up_whole,
        far_outs=(0, 1),
        scratch=[pltpu.VMEM((shard, hidden), F32), pltpu.VMEM((shard, width), F32), dma((8,))],
    )
    sums, two = finished[4:10], finished[10:12]
    return (
        layer_output[None],
        finished[3].reshape(()),
        grad_tokens[None],
        sums[0],
        sums[1],
        finished[0],
        two[0],
        finished[1],
        finished[2],
        two[1],
        grad_output_weight,
        sums[2],
        sums[3],
        sums[4],
        grad_up_weight,
        finished[12],
        grad_down_weight,
        sums[5],
    )


def solution(mesh):
    body = layer if (mesh.shape["ctx"], mesh.shape["fsdp"]) == (8, 4) else shards
    placed = (
        P("fsdp", "ctx", None),
        P("fsdp", "ctx"),
        P("fsdp", "ctx"),
        P("fsdp", "ctx", None),
        P("fsdp", "ctx", None),
        P("fsdp"),
        P("fsdp"),
        P("fsdp", None),
        P("fsdp"),
        P("fsdp", None),
        P("fsdp", None),
        P("fsdp"),
        P("fsdp", None),
        P("fsdp"),
        P("fsdp"),
        P("fsdp"),
        P("fsdp", None),
        P("fsdp"),
        P("fsdp", None),
        P("fsdp"),
    )
    return jax.shard_map(
        body,
        mesh=mesh,
        in_specs=placed,
        out_specs=(
            P("fsdp", "ctx", None),
            P(),
            P("fsdp", "ctx", None),
            P("fsdp"),
            P("fsdp"),
            P("fsdp", None),
            P("fsdp"),
            P("fsdp", None),
            P("fsdp", None),
            P("fsdp"),
            P("fsdp", None),
            P("fsdp"),
            P("fsdp"),
            P("fsdp"),
            P("fsdp", None),
            P("fsdp"),
            P("fsdp", None),
            P("fsdp"),
        ),
        check_vma=False,
    )
```

```python
import jax
import jax.numpy as jnp
from jax import lax
from jax.experimental import pallas as pl
from jax.experimental.pallas import tpu as pltpu
from jax.sharding import PartitionSpec as P

HEADS = 12
HEAD_DIM = 64


EPSILON = 1e-06
MASKED = -1e30


def norm_rows(values, gain, shift):
    centre = jnp.mean(values, axis=-1, keepdims=True)
    centred = values - centre
    spread = jnp.mean(centred * centred, axis=-1, keepdims=True)
    return centred * lax.rsqrt(spread + EPSILON) * gain + shift


def tanh_gelu(values):
    return jax.nn.gelu(values, approximate=True)


def key_allowed(query_segment, query_place, key_codes, key_place):
    same_doc = query_segment[:, None] == (key_codes // 2)[None, :]
    usable = (key_codes % 2 == 1)[None, :] | (query_place[:, None] == key_place[None, :])
    return (same_doc & usable)[None, :, :]


def split_heads(values):
    return values.reshape(values.shape[0], HEADS, HEAD_DIM)


def head_scores(query_heads, key_heads, scale):
    return (
        jnp.einsum("qhd,khd->hqk", query_heads, key_heads, preferred_element_type=jnp.float32)
        * scale
    )


def row_sum(values):
    return jnp.sum(values, axis=0, dtype=jnp.float32)


def left_product(left, right):
    return jnp.einsum("rd,rf->df", left, right, preferred_element_type=jnp.float32)


def right_product(left, right):
    return jnp.einsum("rf,df->rd", left, right, preferred_element_type=jnp.float32)


def shards(
    tokens,
    segment_ids,
    valid_rows,
    teacher,
    cotangent,
    first_gain,
    first_shift,
    query_weight,
    query_bias,
    key_weight,
    value_weight,
    value_bias,
    output_weight,
    output_bias,
    second_gain,
    second_shift,
    up_weight,
    up_bias,
    down_weight,
    down_bias,
):
    tok_rows = tokens.shape[1]
    feature_width = tokens.shape[2]
    shard_count = lax.axis_size("ctx")
    key_block = 4 * tok_rows
    block_count = shard_count // 4
    scale = HEAD_DIM ** (-0.5)
    gain_one, shift_one, w_query, b_query, w_key, w_value, b_value, w_output, b_output = (
        lax.all_gather(first_gain, "fsdp", axis=0, tiled=True),
        lax.all_gather(first_shift, "fsdp", axis=0, tiled=True),
        lax.all_gather(query_weight, "fsdp", axis=0, tiled=True),
        lax.all_gather(query_bias, "fsdp", axis=0, tiled=True),
        lax.all_gather(key_weight, "fsdp", axis=0, tiled=True),
        lax.all_gather(value_weight, "fsdp", axis=0, tiled=True),
        lax.all_gather(value_bias, "fsdp", axis=0, tiled=True),
        lax.all_gather(output_weight, "fsdp", axis=0, tiled=True),
        lax.all_gather(output_bias, "fsdp", axis=0, tiled=True),
    )
    gain_two, shift_two, w_up, b_up, w_down, b_down = (
        lax.all_gather(second_gain, "fsdp", axis=0, tiled=True),
        lax.all_gather(second_shift, "fsdp", axis=0, tiled=True),
        lax.all_gather(up_weight, "fsdp", axis=0, tiled=True),
        lax.all_gather(up_bias, "fsdp", axis=0, tiled=True),
        lax.all_gather(down_weight, "fsdp", axis=0, tiled=True),
        lax.all_gather(down_bias, "fsdp", axis=0, tiled=True),
    )
    local_segment = segment_ids[0]
    local_valid = valid_rows[0]
    local_codes = local_segment * 2 + local_valid
    all_codes = lax.all_gather(local_codes, "ctx", axis=0, tiled=True)
    query_place = lax.axis_index("ctx") * tok_rows + jnp.arange(tok_rows, dtype=jnp.int32)
    inputs = tokens[0].astype(jnp.float32)
    gain_first = gain_one.astype(jnp.float32)
    shift_first = shift_one.astype(jnp.float32)
    gain_second = gain_two.astype(jnp.float32)
    shift_second = shift_two.astype(jnp.float32)
    h_one = norm_rows(inputs, gain_first, shift_first)
    h_one_low = h_one.astype(jnp.bfloat16)
    query_low = (
        jnp.dot(h_one_low, w_query, preferred_element_type=jnp.float32)
        + b_query.astype(jnp.float32)
    ).astype(jnp.bfloat16)
    key_low = jnp.dot(h_one_low, w_key, preferred_element_type=jnp.float32).astype(jnp.bfloat16)
    value_low = (
        jnp.dot(h_one_low, w_value, preferred_element_type=jnp.float32)
        + b_value.astype(jnp.float32)
    ).astype(jnp.bfloat16)
    key_all, value_all = (
        lax.all_gather(key_low, "ctx", axis=0, tiled=True),
        lax.all_gather(value_low, "ctx", axis=0, tiled=True),
    )
    query_heads = split_heads(query_low)

    def block_rows(source, block_index):
        return split_heads(lax.dynamic_slice_in_dim(source, block_index * key_block, key_block, 0))

    def block_allowed(block_index):
        start = block_index * key_block
        codes = lax.dynamic_slice_in_dim(all_codes, start, key_block, 0)
        return key_allowed(
            local_segment, query_place, codes, start + jnp.arange(key_block, dtype=jnp.int32)
        )

    def stats_step(block_index, state_pair):
        running_max, running_sum = state_pair
        allowed = block_allowed(block_index)
        scores = jnp.where(
            allowed, head_scores(query_heads, block_rows(key_all, block_index), scale), MASKED
        )
        new_max = jnp.maximum(running_max, jnp.max(scores, axis=2))
        weights = jnp.where(allowed, jnp.exp(scores - new_max[:, :, None]), 0.0)
        return (new_max, running_sum * jnp.exp(running_max - new_max) + jnp.sum(weights, axis=2))

    start_max = jnp.full((HEADS, tok_rows), MASKED, jnp.float32)
    start_sum = jnp.zeros((HEADS, tok_rows), jnp.float32)
    running_max, running_sum = lax.fori_loop(0, block_count, stats_step, (start_max, start_sum))
    log_total = running_max + jnp.log(running_sum)

    def mix_step(block_index, mixed_sum):
        allowed = block_allowed(block_index)
        scores = head_scores(query_heads, block_rows(key_all, block_index), scale)
        probs = jnp.where(allowed, jnp.exp(scores - log_total[:, :, None]), 0.0).astype(
            jnp.bfloat16
        )
        return mixed_sum + jnp.einsum(
            "hqk,khd->qhd",
            probs,
            block_rows(value_all, block_index),
            preferred_element_type=jnp.float32,
        )

    mixed_heads = lax.fori_loop(
        0, block_count, mix_step, jnp.zeros((tok_rows, HEADS, HEAD_DIM), jnp.float32)
    )
    mixed = mixed_heads.reshape(tok_rows, feature_width)
    mixed_low = mixed.astype(jnp.bfloat16)
    second = (
        inputs
        + jnp.dot(mixed_low, w_output, preferred_element_type=jnp.float32)
        + b_output.astype(jnp.float32)
    )
    h_two = norm_rows(second, gain_second, shift_second)
    h_two_low = h_two.astype(jnp.bfloat16)
    up_value = jnp.dot(h_two_low, w_up, preferred_element_type=jnp.float32) + b_up.astype(
        jnp.float32
    )
    act_low = tanh_gelu(up_value).astype(jnp.bfloat16)
    result = (
        second
        + jnp.dot(act_low, w_down, preferred_element_type=jnp.float32)
        + b_down.astype(jnp.float32)
    )
    layer_output = result.astype(jnp.bfloat16)[None]
    valid_float = local_valid.astype(jnp.float32)
    mismatch = result - teacher[0].astype(jnp.float32)
    error_sum, valid_count = lax.psum(
        (jnp.sum(valid_float[:, None] * mismatch * mismatch), jnp.sum(valid_float)), ("ctx", "fsdp")
    )
    loss_value = error_sum / (feature_width * valid_count)
    d_result = (
        cotangent[0].astype(jnp.float32)
        + 2.0 / (feature_width * valid_count) * valid_float[:, None] * mismatch
    )
    d_down = d_result.astype(jnp.bfloat16)
    grad_down_bias = row_sum(d_down)
    grad_down_weight = left_product(act_low, d_down)
    d_act = right_product(d_down, w_down)
    gelu_value, gelu_pull = jax.vjp(tanh_gelu, up_value)
    d_up = gelu_pull(d_act)[0].astype(jnp.bfloat16)
    grad_up_bias = row_sum(d_up)
    grad_up_weight = left_product(h_two_low, d_up)
    d_h_two = right_product(d_up, w_up)
    norm_two_value, norm_two_pull = jax.vjp(norm_rows, second, gain_second, shift_second)
    d_second_norm, grad_second_gain, grad_second_shift = norm_two_pull(d_h_two)
    d_second = d_result + d_second_norm
    d_attn = d_second.astype(jnp.bfloat16)
    grad_output_bias = row_sum(d_attn)
    grad_output_weight = left_product(mixed_low, d_attn)
    d_mixed = right_product(d_attn, w_output).astype(jnp.bfloat16)
    d_heads = split_heads(d_mixed)
    delta = jnp.einsum("qhd,qhd->hq", d_heads.astype(jnp.float32), mixed_heads)
    key_back, value_back = (key_all, value_all)

    def score_grads(block_index):
        allowed = block_allowed(block_index)
        key_piece = block_rows(key_back, block_index)
        value_piece = block_rows(value_back, block_index)
        scores = head_scores(query_heads, key_piece, scale)
        probs = jnp.where(allowed, jnp.exp(scores - log_total[:, :, None]), 0.0)
        d_probs = jnp.einsum(
            "qhd,khd->hqk", d_heads, value_piece, preferred_element_type=jnp.float32
        )
        d_scores = (probs * (d_probs - delta[:, :, None])).astype(jnp.bfloat16)
        return (key_piece, probs, d_scores)

    zero_query = jnp.zeros((tok_rows, HEADS, HEAD_DIM), jnp.float32)

    def reduce_step(block_index, state_triple):
        d_query_sum, d_key_rows, d_value_rows = state_triple
        key_piece, probs, d_scores = score_grads(block_index)
        d_query_sum = d_query_sum + jnp.einsum(
            "hqk,khd->qhd", d_scores, key_piece, preferred_element_type=jnp.float32
        )
        d_key_piece = jnp.einsum(
            "hqk,qhd->khd", d_scores, query_heads, preferred_element_type=jnp.float32
        ).reshape(key_block, feature_width)
        d_value_piece = jnp.einsum(
            "hqk,qhd->khd", probs.astype(jnp.bfloat16), d_heads, preferred_element_type=jnp.float32
        ).reshape(key_block, feature_width)
        d_key_rows = lax.dynamic_update_slice_in_dim(
            d_key_rows, d_key_piece, block_index * key_block, 0
        )
        d_value_rows = lax.dynamic_update_slice_in_dim(
            d_value_rows, d_value_piece, block_index * key_block, 0
        )
        return (d_query_sum, d_key_rows, d_value_rows)

    zero_rows = jnp.zeros((key_block * block_count, feature_width), jnp.float32)
    d_query_sum, d_key_rows, d_value_rows = lax.fori_loop(
        0, block_count, reduce_step, (zero_query, zero_rows, zero_rows)
    )
    d_key_local, d_value_local = (
        lax.psum_scatter(d_key_rows, "ctx", scatter_dimension=0, tiled=True),
        lax.psum_scatter(d_value_rows, "ctx", scatter_dimension=0, tiled=True),
    )
    d_query = (d_query_sum.reshape(tok_rows, feature_width) * scale).astype(jnp.bfloat16)
    d_key = (d_key_local * scale).astype(jnp.bfloat16)
    d_value = d_value_local.astype(jnp.bfloat16)
    grad_query_bias = row_sum(d_query)
    grad_query_weight = left_product(h_one_low, d_query)
    grad_key_weight = left_product(h_one_low, d_key)
    grad_value_bias = row_sum(d_value)
    grad_value_weight = left_product(h_one_low, d_value)
    d_h_one = (
        right_product(d_query, w_query)
        + right_product(d_key, w_key)
        + right_product(d_value, w_value)
    )
    norm_one_value, norm_one_pull = jax.vjp(norm_rows, inputs, gain_first, shift_first)
    d_inputs_norm, grad_first_gain, grad_first_shift = norm_one_pull(d_h_one)
    grad_tokens = (d_second + d_inputs_norm).astype(jnp.bfloat16)[None]
    shares = (
        lax.psum_scatter(
            grad_first_gain.astype(jnp.bfloat16), "fsdp", scatter_dimension=0, tiled=True
        ).astype(jnp.float32),
        lax.psum_scatter(
            grad_first_shift.astype(jnp.bfloat16), "fsdp", scatter_dimension=0, tiled=True
        ).astype(jnp.float32),
        lax.psum_scatter(
            grad_query_weight.astype(jnp.bfloat16), "fsdp", scatter_dimension=0, tiled=True
        ).astype(jnp.float32),
        lax.psum_scatter(
            grad_query_bias.astype(jnp.bfloat16), "fsdp", scatter_dimension=0, tiled=True
        ).astype(jnp.float32),
        lax.psum_scatter(
            grad_key_weight.astype(jnp.bfloat16), "fsdp", scatter_dimension=0, tiled=True
        ).astype(jnp.float32),
        lax.psum_scatter(
            grad_value_weight.astype(jnp.bfloat16), "fsdp", scatter_dimension=0, tiled=True
        ).astype(jnp.float32),
        lax.psum_scatter(
            grad_value_bias.astype(jnp.bfloat16), "fsdp", scatter_dimension=0, tiled=True
        ).astype(jnp.float32),
        lax.psum_scatter(
            grad_output_weight.astype(jnp.bfloat16), "fsdp", scatter_dimension=0, tiled=True
        ).astype(jnp.float32),
        lax.psum_scatter(
            grad_output_bias.astype(jnp.bfloat16), "fsdp", scatter_dimension=0, tiled=True
        ).astype(jnp.float32),
        lax.psum_scatter(
            grad_second_gain.astype(jnp.bfloat16), "fsdp", scatter_dimension=0, tiled=True
        ).astype(jnp.float32),
        lax.psum_scatter(
            grad_second_shift.astype(jnp.bfloat16), "fsdp", scatter_dimension=0, tiled=True
        ).astype(jnp.float32),
        lax.psum_scatter(
            grad_up_weight.astype(jnp.bfloat16), "fsdp", scatter_dimension=0, tiled=True
        ).astype(jnp.float32),
        lax.psum_scatter(
            grad_up_bias.astype(jnp.bfloat16), "fsdp", scatter_dimension=0, tiled=True
        ).astype(jnp.float32),
        lax.psum_scatter(
            grad_down_weight.astype(jnp.bfloat16), "fsdp", scatter_dimension=0, tiled=True
        ).astype(jnp.float32),
        lax.psum_scatter(
            grad_down_bias.astype(jnp.bfloat16), "fsdp", scatter_dimension=0, tiled=True
        ).astype(jnp.float32),
    )
    totals = lax.psum(
        (
            shares[0],
            shares[1],
            shares[2],
            shares[3],
            shares[4],
            shares[5],
            shares[6],
            shares[7],
            shares[8],
            shares[9],
            shares[10],
            shares[11],
            shares[12],
            shares[13],
            shares[14],
        ),
        "ctx",
    )
    return (
        layer_output,
        loss_value,
        grad_tokens,
        totals[0],
        totals[1],
        totals[2],
        totals[3],
        totals[4],
        totals[5],
        totals[6],
        totals[7],
        totals[8],
        totals[9],
        totals[10],
        totals[11],
        totals[12],
        totals[13],
        totals[14],
    )


F32 = jnp.float32
BF16 = jnp.bfloat16
ANY = pl.BlockSpec(memory_space=pl.ANY)
HBM = pl.BlockSpec(memory_space=pltpu.HBM)
VMEM = pl.BlockSpec(memory_space=pltpu.VMEM)
SMEM = pl.BlockSpec(memory_space=pltpu.SMEM)
NT = (((1,), (1,)), ((), ()))
TN = (((0,), (0,)), ((), ()))
NN = (((1,), (0,)), ((), ()))


def swap_cores(value):
    size = lax.axis_size("ctx")
    return lax.ppermute(value, "ctx", [(i, i ^ 1) for i in range(size)])


def both_cores(value):
    pairs = [[i, i + 1] for i in range(0, lax.axis_size("ctx"), 2)]
    return lax.all_gather(value, "ctx", axis=0, tiled=True, axis_index_groups=pairs)


def swap_chips(value, step):
    size = lax.axis_size("ctx")
    return lax.ppermute(value, "ctx", [(i, i ^ (2 * step)) for i in range(size)])


def swap_planes(value, step):
    size = lax.axis_size("fsdp")
    return lax.ppermute(value, "fsdp", [(i, i ^ step) for i in range(size)])


def trade_chips(value):
    size = lax.axis_size("ctx")
    groups = [[i for i in range(size) if i % 2 == c] for c in (0, 1)]
    return lax.all_to_all(value, "ctx", 0, 0, axis_index_groups=groups, tiled=True)


def trade_planes(value):
    return lax.all_to_all(value, "fsdp", 0, 0, tiled=True)


def shaped(*shape, dtype=BF16):
    return jax.ShapeDtypeStruct(shape, dtype)


def wide(*shape):
    return jax.ShapeDtypeStruct(shape, F32)


def local_call(
    body,
    outs,
    where,
    args,
    far=(),
    far_outs=(),
    fetch=(),
    store=(),
    scalar=None,
    scratch=(),
    after=(),
    vmem=14,
    cost=0,
):
    fetch, store = list(fetch), list(store)
    args = [
        pltpu.with_memory_space_constraint(a, pltpu.HBM) if i in far or i in fetch else a
        for i, a in enumerate(args)
    ]
    after = list(after)
    many = isinstance(outs, tuple)
    outs = outs if many else (outs,)
    count, made, moved = len(args), len(outs), len(fetch) + len(store)
    held = [pltpu.VMEM(args[i].shape, args[i].dtype) for i in fetch]
    held += [pltpu.VMEM(outs[i].shape, outs[i].dtype) for i in store]
    if moved:
        held.append(pltpu.SemaphoreType.DMA((moved,)))

    def kernel(where_ref, *refs):
        start = count + len(after)
        given, results = list(refs[:count]), list(refs[start : start + made])
        token, extra = refs[start + made], refs[start + made + 1 :]
        extra, copied = extra[: len(extra) - len(held)], extra[len(extra) - len(held) :]
        token[...] = jnp.zeros(token.shape, token.dtype)
        into = [
            pltpu.make_async_copy(given[i], copied[n], copied[-1].at[n])
            for n, i in enumerate(fetch)
        ]
        out_of = [
            pltpu.make_async_copy(copied[n], results[i], copied[-1].at[n])
            for n, i in enumerate(store, len(fetch))
        ]
        for copy in into:
            copy.start()
        for n, i in enumerate(fetch):
            given[i] = copied[n]
        for n, i in enumerate(store, len(fetch)):
            results[i] = copied[n]
        for copy in into:
            copy.wait()
        body(where_ref, *given, *results, *extra)
        for copy in out_of:
            copy.start()
        for copy in out_of:
            copy.wait()

    def place(i):
        return HBM if i in far_outs or i in store else SMEM if i == scalar else VMEM

    results = pl.pallas_call(
        kernel,
        out_shape=(
            *(
                pltpu.HBM(o.shape, o.dtype) if i in far_outs or i in store else o
                for i, o in enumerate(outs)
            ),
            wide(8, 128),
        ),
        in_specs=[SMEM]
        + [HBM if i in far or i in fetch else VMEM for i in range(count)]
        + [ANY] * len(after),
        out_specs=(*(place(i) for i in range(made)), VMEM),
        scratch_shapes=[*scratch, *held],
        compiler_params=pltpu.CompilerParams(vmem_limit_bytes=vmem << 20),
        cost_estimate=pl.CostEstimate(
            flops=cost * 10**9, transcendentals=0, bytes_accessed=cost * 10**6
        ),
    )(where, *args, *after)
    return (results[:-1] if many else results[0]), results[-1]


def core_rows(core, count):
    return pl.ds(pl.multiple_of(count * core, 16), count)


def rows_at(start, count, align):
    return pl.ds(pl.multiple_of(start, align), count)


def dot(left, right, dims):
    return lax.dot_general(left, right, dims, preferred_element_type=F32)


def run_copies(copies, sems):
    started = [
        pltpu.make_async_copy(source, target, sems.at[i])
        for i, (source, target) in enumerate(copies)
    ]
    for copy in started:
        copy.start()
    for copy in started:
        copy.wait()


def unit_rows(values):
    centred = values - jnp.mean(values, axis=-1, keepdims=True)
    spread = jnp.mean(centred * centred, axis=-1, keepdims=True)
    inverse = lax.rsqrt(spread + EPSILON)
    return centred * inverse, inverse


def unit_back(grad, gain, unit, inverse):
    scaled = grad * gain
    return inverse * (
        scaled
        - jnp.mean(scaled, axis=-1, keepdims=True)
        - unit * jnp.mean(scaled * unit, axis=-1, keepdims=True)
    )


def put_small(out, start, small):
    third = small.shape[1] // 3
    lanes = slice(9 * third, 10 * third)
    for q in range(3):
        block = slice(start + 16 * q, start + 16 * (q + 1))
        out[block, lanes] = small[:, third * q : third * (q + 1)].astype(out.dtype)


def get_small(piece, start, feat):
    third = feat // 3
    lanes = slice(9 * third, 10 * third)
    parts = [piece[start + 16 * q : start + 16 * (q + 1), lanes].astype(F32) for q in range(3)]
    return jnp.concatenate(parts, axis=1)


def pack_tokens(where, tokens, segment, valid, out):
    rows, width = tokens.shape
    ids = segment[...]
    line = lax.broadcasted_iota(jnp.int32, (16, rows), 0)
    codes = jnp.where(
        line == 0,
        ids >> 7,
        jnp.where(line == 1, ids & 127, jnp.where(line == 2, valid[...], 0)),
    )
    out[:rows, :] = tokens[...]
    out[rows:, :] = jnp.zeros((16, width), out.dtype)
    out[rows:, :rows] = codes.astype(F32).astype(out.dtype)


def order_chips(where, p0, p1, p2, p3, out):
    rows = p0.shape[0]
    for k, piece in enumerate((p0, p1, p2, p3)):
        out[rows_at(rows * (where[0] ^ k), rows, 16), :] = piece[...]


def far_planes(where, arrived, out):
    part = arrived.shape[0] // 4
    for s in (1, 2, 3):
        out[part * (s - 1) : part * s, :] = arrived[rows_at(part * (where[2] ^ s), part, 16), :]


def pack_projections(where, *refs):
    weights, vectors, long, valid, out = refs[:3], refs[3:11], refs[11], refs[12], refs[13]
    held, small, held_long, sems = refs[14], refs[15:23], refs[23], refs[24]
    half, feat = held.shape[1], small[0].shape[0]
    out[48:, 3 * feat :] = jnp.zeros((half - 48, feat // 3), out.dtype)
    own_rows = rows_at(half * where[1], half, 32)
    run_copies(
        [(w.at[own_rows], held.at[i]) for i, w in enumerate(weights)]
        + list(zip(vectors, small))
        + [(long, held_long)],
        sems,
    )
    for chip in range(4):

        @pl.when(where[0] == chip)
        def _():
            for i in range(3):
                out[:, feat * i : feat * (i + 1)] = held[i, :, feat * chip : feat * (chip + 1)]

    spread = held_long[...].astype(F32).reshape(1, 4 * feat)
    count = jnp.sum(valid[...].astype(F32), axis=1, keepdims=True)
    lines = [v[...].astype(F32).reshape(1, feat) for v in small]
    lines += [spread[:, feat * i : feat * (i + 1)] for i in range(4)]
    lines += [jnp.broadcast_to(count, (1, feat)), jnp.zeros((3, feat), F32)]
    put_small(out, 0, jnp.concatenate(lines, axis=0))


def pack_down(where, down, out, sem):
    part = out.shape[0]
    rows = rows_at(4 * part * where[1] + part * where[0], part, 32)
    copy = pltpu.make_async_copy(down.at[rows], out, sem)
    copy.start()
    copy.wait()


def pack_blocks(where, up, output, out_up, sems):
    chip, core = where[0], where[1]
    part, units = out_up.shape[0] // 4, out_up.shape[1] // 5
    rows = rows_at(part * chip, part, 16)
    pairs = [
        (
            up.at[rows, rows_at(2 * units * i + units * core, units, 128)],
            out_up.at[:part, units * i : units * (i + 1)],
        )
        for i in range(4)
    ]
    pairs.append((output.at[rows, rows_at(units * core, units, 128)], out_up.at[:part, 4 * units :]))
    run_copies(pairs, sems)
    for p in (1, 2, 3):
        out_up[part * p : part * (p + 1), :] = out_up[:part, :]


def stack_rows(where, *refs):
    pieces, out = refs[:-1], refs[-1]
    rows = pieces[0].shape[0]
    for i, piece in enumerate(pieces):
        out[rows * i : rows * (i + 1), :] = piece[...]


def three_blocks(pieces, part):
    p0, p1, p2, low, high = pieces
    parts = [(k, [(p, 0)]) for k, p in enumerate((p0, p1, p2))] + [(3, [(low, 0), (high, low.shape[0])])]
    found = []
    for k, refs in parts:
        for s in (1, 2, 3):
            for ref, base in refs:
                start, end = max(part * (s - 1), base), min(part * s, base + ref.shape[0])
                if start < end:
                    found.append((k, s, start - part * (s - 1), end - start, ref, start - base))
    return found


def cross_halves(where, from_x, from_y, to_x, to_y):
    cut = to_x.shape[0]
    to_x[...] = from_y[:cut, :]
    to_y[...] = from_x[cut:, :]


def build_up(where, up, p0, p1, p2, p3, p4, out, sems):
    chip, core, plane = where[0], where[1], where[2]
    units, shard = up.shape[1] // 8, up.shape[0]
    part = shard // 4
    own = rows_at(shard * plane, shard, 64)
    pairs = [
        (
            up.at[:, rows_at(2 * units * i + units * core, units, 128)],
            out.at[own, units * i : units * (i + 1)],
        )
        for i in range(4)
    ]
    for k, s, offset, count, piece, start in three_blocks((p0, p1, p2, p3, p4), part):
        at = rows_at(shard * (plane ^ s) + part * (chip ^ k) + offset, count, 16)
        pairs.append((piece.at[start : start + count, : 4 * units], out.at[at]))
    run_copies(pairs, sems)


def build_half(where, output, p0, p1, p2, p3, p4, out, sems):
    chip, core, plane = where[0], where[1], where[2]
    shard, units = output.shape[0], out.shape[1]
    part = shard // 4
    pairs = [
        (
            output.at[:, rows_at(units * core, units, 128)],
            out.at[rows_at(shard * plane, shard, 64)],
        )
    ]
    for k, s, offset, count, piece, start in three_blocks((p0, p1, p2, p3, p4), part):
        at = rows_at(shard * (plane ^ s) + part * (chip ^ k) + offset, count, 16)
        pairs.append((piece.at[start : start + count, 4 * units :], out.at[at]))
    run_copies(pairs, sems)


def build_down(where, down, p0, p1, p2, p3, p4, out, sem):
    chip, core, plane = where[0], where[1], where[2]
    mine = down.shape[0] // 2
    part = mine // 4
    own = pltpu.make_async_copy(
        down.at[rows_at(mine * core, mine, 128)], out.at[rows_at(mine * plane, mine, 128)], sem
    )
    own.start()
    for k, s, offset, count, piece, start in three_blocks((p0, p1, p2, p3, p4), part):
        at = rows_at(mine * (plane ^ s) + part * (chip ^ k) + offset, count, 16)
        out[at, :] = piece[start : start + count, :]
    own.wait()


def build_output(where, near, far, out):
    units = near.shape[1]
    out[:, rows_at(units * where[1], units, 128)] = near[...]
    out[:, rows_at(units * (1 - where[1]), units, 128)] = far[...]


def normalize_tokens(where, near, far, unit_low, key_row, query_column):
    rows = query_column.shape[0] // 4
    for i in range(8):
        block = (near if i < 4 else far).at[(rows + 16) * (i % 4) : (rows + 16) * (i % 4 + 1), :]
        unit, _ = unit_rows(block[:rows, :].astype(F32))
        unit_low[rows * i : rows * (i + 1), :] = unit
        codes = block[rows:, :].astype(F32)
        ids = codes[0:1, :rows] * 128.0 + codes[1:2, :rows]
        key_row[0:1, rows * i : rows * (i + 1)] = jnp.where(codes[2:3, :rows] == 1.0, ids, -1.0)
        if i < 4:
            query_column[rows * i : rows * (i + 1), :] = jnp.broadcast_to(
                ids.reshape(rows, 1), (rows, 128)
            )


def attend(where, *refs):
    units, key_row, query_column, weights, far_weights = refs[:3] + (refs[3:7], refs[7])
    saved, sent, vectors, long = refs[8:13], refs[13], refs[14], refs[15]
    small, bias, h_one, w_three, projected, probs, mixed, sems = refs[16:]
    kept = (h_one, w_three, projected, mixed)
    copies = [
        pltpu.make_async_copy(source, saved[i], sems.at[j])
        for j, (i, source) in enumerate(zip((0, 1, 2, 4), kept))
    ]
    core, plane = where[1], where[2]
    half, feat = weights[0].shape[0], small.shape[2]
    group = query_column.shape[0]
    rows = group // 4

    count = jnp.zeros((1, 1), F32)
    for s, piece in enumerate(weights):
        base = 2 * half * (plane ^ s)
        w_three[rows_at(base + half * core, half, 32), :] = piece[:, : 3 * feat]
        other = far_weights[half * s : half * (s + 1), :]
        w_three[rows_at(base + half * (1 - core), half, 32), :] = other[:, : 3 * feat]
        near = get_small(piece, 0, feat)
        small[plane ^ s] = near
        count += near[12:13, :1] + other[12:13, 3 * feat : 3 * feat + 1].astype(F32)
    vectors[...] = jnp.zeros(vectors.shape, F32)
    for p in range(4):
        lines = small[p]
        for i, r in enumerate((0, 1, 4, 5, 6, 7)):
            vectors[i : i + 1, feat * p : feat * (p + 1)] = lines[r : r + 1, :]
        pair = jnp.where(core == 0, lines[8:10, :], lines[10:12, :])
        long[:, 2 * feat * p : 2 * feat * p + feat] = pair[:1, :]
        long[:, 2 * feat * p + feat : 2 * feat * (p + 1)] = pair[1:, :]
    gain, shift = vectors[0:1, :], vectors[1:2, :]
    short = small[where[0]]
    copies[1].start()
    h_one[...] = (units[...] * gain + shift).astype(BF16)
    copies[0].start()
    values = dot(h_one[...], w_three[...], NN)
    query = (values[:group, :feat] + short[2:3, :]).astype(BF16) * jnp.asarray(
        HEAD_DIM**-0.5, BF16
    )
    projected[:group, :feat] = query
    projected[group:, :feat] = jnp.zeros((group, feat), BF16)
    projected[:, feat : 2 * feat] = values[:, feat : 2 * feat].astype(BF16)
    projected[:, 2 * feat :] = (values[:, 2 * feat :] + short[3:4, :]).astype(BF16)
    copies[2].start()
    column = lax.broadcasted_iota(jnp.int32, (rows, 2 * group), 1)
    line = lax.broadcasted_iota(jnp.int32, (rows, 2 * group), 0)
    for k in range(4):
        ids = query_column[rows * k : rows * (k + 1), :1]
        allowed = (ids == key_row[0:1, :]) | (column == line + rows * k)
        bias[rows * k : rows * (k + 1), :] = jnp.where(allowed, 0.0, MASKED)
    for h in range(feat // HEAD_DIM):
        at = slice(HEAD_DIM * h, HEAD_DIM * (h + 1))
        keys = projected[:, feat + HEAD_DIM * h : feat + HEAD_DIM * (h + 1)]
        held = projected[:, 2 * feat + HEAD_DIM * h : 2 * feat + HEAD_DIM * (h + 1)]
        for k in range(4):
            block = slice(rows * k, rows * (k + 1))
            scores = dot(projected[block, at], keys, NT) + bias[block, :]
            weight = jnp.exp(scores - jnp.max(scores, axis=1, keepdims=True))
            weight = weight * (1.0 / jnp.sum(weight, axis=1, keepdims=True))
            low = weight.astype(BF16)
            probs[h, block, :] = low
            result = dot(low, held, NN)
            mixed[block, at] = result
            sent[(rows + 16) * k : (rows + 16) * k + rows, at] = result.astype(BF16)
        copies.append(pltpu.make_async_copy(probs.at[h], saved[3].at[h], sems.at[4 + h]))
        copies[-1].start()
    copies[3].start()
    high = jnp.floor(count / 128.0)
    side = lax.broadcasted_iota(jnp.int32, (16, feat), 1)
    digits = jnp.where(side == 0, high, jnp.where(side == 1, count - 128.0 * high, 0.0))
    for k in range(4):
        sent[(rows + 16) * k + rows : (rows + 16) * (k + 1), :] = digits.astype(BF16)
    for copy in copies:
        copy.wait()


def attend_back(where, d_all, vectors, *refs):
    saved, (near, far, kept, given, lines) = refs[:5], refs[5:10]
    d_three, d_scores, grads, h_one, w_three, projected, probs, mixed, sems = refs[10:]
    core = where[1]
    pairs = [(saved[2], projected), (saved[4], mixed)]
    pairs += [(saved[3].at[h], probs.at[h]) for h in range(probs.shape[0])]
    pairs += [(saved[0], h_one), (saved[1], w_three)]
    copies = [pltpu.make_async_copy(a, b, sems.at[i]) for i, (a, b) in enumerate(pairs)]
    for copy in copies:
        copy.start()
    copies[0].wait()
    copies[1].wait()
    group, feat = d_all.shape
    rows, width = group // 4, h_one.shape[1]
    scale = HEAD_DIM**-0.5
    d_three[group:, :feat] = jnp.zeros((group, feat), BF16)
    for h in range(feat // HEAD_DIM):
        at = slice(HEAD_DIM * h, HEAD_DIM * (h + 1))
        key_at = slice(feat + HEAD_DIM * h, feat + HEAD_DIM * (h + 1))
        value_at = slice(2 * feat + HEAD_DIM * h, 2 * feat + HEAD_DIM * (h + 1))
        keys, held = projected[:, key_at], projected[:, value_at]
        copies[2 + h].wait()
        for k in range(4):
            block = slice(rows * k, rows * (k + 1))
            d_mixed = d_all[block, at]
            delta = jnp.sum(d_mixed.astype(F32) * mixed[block, at], axis=1, keepdims=True)
            d_probs = dot(d_mixed, held, NT)
            low = (probs[h, block, :].astype(F32) * (d_probs - delta)).astype(BF16)
            d_scores[block, :] = low
            d_three[block, at] = (dot(low, keys, NN) * scale).astype(BF16)
        d_three[:, key_at] = dot(d_scores[...], projected[:group, at], TN).astype(BF16)
        d_three[:, value_at] = dot(probs[h], d_all[:, at], TN).astype(BF16)
    for copy in copies[2 + probs.shape[0] :]:
        copy.wait()
    grads[...] = dot(h_one[...], d_three[...], TN)
    near[...] = dot(d_three[:group, :], w_three[...], NT).astype(BF16)
    far[...] = dot(d_three[group:, :], w_three[...], NT).astype(BF16)
    half = kept.shape[0] // 4
    for p in range(4):
        block = slice(half * p, half * (p + 1))
        kept[block, :] = grads[rows_at(2 * half * p + half * core, half, 32), :].astype(BF16)
        given[block, :] = grads[rows_at(2 * half * p + half * (1 - core), half, 32), :].astype(BF16)
    sums = jnp.sum(d_three[...].astype(F32), axis=0, keepdims=True)
    weight = w_three[...].astype(F32)
    with_gain = jnp.sum(grads[...] * weight, axis=1, keepdims=True)
    with_shift = jnp.sum(weight * sums, axis=1, keepdims=True)
    side = lax.broadcasted_iota(jnp.int32, (width, 128), 1)
    both = jnp.where(side == 0, with_gain, jnp.where(side == 1, with_shift, 0.0)).T
    d_shift = both[1:2, :]
    lines[0:1, :] = (both[0:1, :] - vectors[1:2, :] * d_shift) / vectors[0:1, :]
    lines[1:2, :] = d_shift
    lines[2:3, :] = jnp.zeros((1, width), F32)
    lines[2:3, :feat] = sums[:, :feat]
    lines[3:4, :] = jnp.zeros((1, width), F32)
    lines[3:4, :feat] = sums[:, 2 * feat :]
    lines[4:, :] = jnp.zeros((4, width), F32)


def share_inputs(where, near, far, *outs):
    rows = outs[0].shape[0]
    for k, out in enumerate(outs):
        at = rows_at(rows * (where[0] ^ k), rows, 16)
        out[...] = (near[at, :].astype(F32) + far[at, :].astype(F32)).astype(out.dtype)


def finish_inputs(where, d0, d1, d2, d3, tokens, d_second, vectors, out):
    total = d0[...].astype(F32)
    for piece in (d1, d2, d3):
        total = total + piece[...].astype(F32)
    unit, inverse = unit_rows(tokens[...].astype(F32))
    d_inputs = unit_back(total, vectors[0:1, :], unit, inverse)
    out[...] = (d_second[...] + d_inputs).astype(BF16)


def project_output(where, mixed, w_output, tokens, vectors, second, h_two, count):
    rows, width = tokens.shape
    feat = mixed.shape[1]
    total = tokens[...].astype(F32) + vectors[2:3, :]
    valid = jnp.zeros((1, 1), F32)
    for k in range(4):
        start = (rows + 16) * k
        total += dot(mixed[start : start + rows, :], w_output[feat * k : feat * (k + 1), :], NN)
        digits = mixed[start + rows : start + rows + 16, :].astype(F32)
        valid += digits[0:1, 0:1] * 128.0 + digits[0:1, 1:2]
    second[...] = total
    unit, _ = unit_rows(total)
    h_two[...] = (unit * vectors[3:4, :] + vectors[4:5, :]).astype(BF16)
    count[...] = jnp.broadcast_to(valid, count.shape)


def activate(where, h_pair, w_up, b_up, act, slope):
    root = 0.7978845608028654
    value = dot(h_pair[...], w_up[...], NN) + b_up[...]
    square = value * value
    bent = jnp.tanh(root * value * (1.0 + 0.044715 * square))
    act[...] = (0.5 * value * (1.0 + bent)).astype(BF16)
    slope[...] = 0.5 * (1.0 + bent) + 0.5 * value * (1.0 - bent * bent) * root * (
        1.0 + 3.0 * 0.044715 * square
    )


def project_down(where, act, w_down, near, far, both):
    rows, core = near.shape[0], where[1]
    both[...] = dot(act[...], w_down[...], NN)
    near[...] = both[core_rows(core, rows), :]
    far[...] = both[core_rows(1 - core, rows), :].astype(BF16)


def compare(where, second, near, far, vectors, teacher, cotangent, valid, count, *outs):
    layer_output, d_result, d_down, lines = outs
    rows, width = second.shape
    other = far[core_rows(1 - where[1], rows), :].astype(F32)
    result = second[...] + near[...] + other + vectors[5:6, :]
    layer_output[...] = result.astype(BF16)
    kept = valid[...].astype(F32).reshape(rows, 1)
    mismatch = result - teacher[...].astype(F32)
    weighted = kept * mismatch
    error = jnp.sum(jnp.sum(weighted * mismatch, axis=1, keepdims=True), axis=0, keepdims=True)
    total = cotangent[...].astype(F32) + 2.0 / (width * count[0:1, 0:1]) * weighted
    d_result[...] = total
    low = total.astype(BF16)
    d_down[...] = low
    high = error.astype(BF16).astype(F32)
    middle = (error - high).astype(BF16).astype(F32)
    side = lax.broadcasted_iota(jnp.int32, (1, width), 1)
    parts = jnp.where(
        side == 0, high, jnp.where(side == 1, middle, jnp.where(side == 2, error - high - middle, 0.0))
    )
    lines[0:1, :] = jnp.sum(low.astype(F32), axis=0, keepdims=True)
    lines[1:2, :] = parts
    lines[2:, :] = jnp.zeros((6, width), F32)


def activate_back(where, d_down, w_down, slope, w_up, d_up, near, far, line, both):
    rows, core = near.shape[0], where[1]
    low = (dot(d_down[...], w_down[...], NT) * slope[...]).astype(BF16)
    d_up[...] = low
    line[...] = jnp.sum(low.astype(F32), axis=0, keepdims=True)
    both[...] = dot(low, w_up[...], NT)
    near[...] = both[core_rows(core, rows), :]
    far[...] = both[core_rows(1 - core, rows), :].astype(BF16)


def second_back(where, near, far, d_result, second, vectors, w_output, *outs):
    d_second, d_attn, lines, sent = outs
    rows = near.shape[0]
    d_two = near[...] + far[core_rows(1 - where[1], rows), :].astype(F32)
    unit, inverse = unit_rows(second[...])
    total = d_result[...] + unit_back(d_two, vectors[3:4, :], unit, inverse)
    d_second[...] = total
    low = total.astype(BF16)
    d_attn[...] = low
    lines[0:1, :] = jnp.sum(low.astype(F32), axis=0, keepdims=True)
    lines[1:2, :] = jnp.sum(d_two * unit, axis=0, keepdims=True)
    lines[2:3, :] = jnp.sum(d_two, axis=0, keepdims=True)
    lines[3:, :] = jnp.zeros((5, lines.shape[1]), F32)
    feat = sent.shape[1]
    for k in range(4):
        part = w_output[feat * k : feat * (k + 1), :]
        sent[rows * k : rows * (k + 1), :] = dot(low, part, NT).astype(BF16)


def split_chips(chip, block, outs, count):
    own, to_x, to_y, then_x, then_y = outs
    for p in range(4):
        own[count * p : count * (p + 1), :] = block(chip, p).astype(BF16)
    for p in (0, 1):
        low, high = slice(count * p, count * (p + 1)), slice(count * (p + 2), count * (p + 3))
        to_x[low, :] = block(chip ^ 1, p).astype(BF16)
        to_x[high, :] = block(chip ^ 3, p).astype(BF16)
        to_y[low, :] = block(chip ^ 2, p + 2).astype(BF16)
        to_y[high, :] = block(chip ^ 3, p + 2).astype(BF16)
        then_x[low, :] = block(chip ^ 1, p + 2).astype(BF16)
        then_y[low, :] = block(chip ^ 2, p).astype(BF16)


def pass_on(where, from_x, from_y, then_x, then_y, to_x, to_y):
    half = to_x.shape[0]
    to_x[...] = (then_x[...].astype(F32) + from_y[half:, :].astype(F32)).astype(BF16)
    to_y[...] = (then_y[...].astype(F32) + from_x[half:, :].astype(F32)).astype(BF16)


def add_chips(own, from_x, from_y, last_x, last_y):
    half = last_x.shape[0]
    low = own[:half, :].astype(F32) + from_x[:half, :].astype(F32) + last_y[...].astype(F32)
    high = own[half:, :].astype(F32) + from_y[:half, :].astype(F32) + last_x[...].astype(F32)
    return low, high


def down_grads(where, act, d_down, *refs):
    outs, total = refs[:5], refs[5]
    count = outs[0].shape[0] // 4
    total[...] = dot(act[...], d_down[...], TN).astype(BF16)

    def block(j, p):
        return total[rows_at(4 * count * p + count * j, count, 32), :]

    split_chips(where[0], block, outs, count)


def output_grads(where, mixed, d_attn, kept, given):
    core = where[1]
    rows, width = d_attn.shape
    feat, units = mixed.shape[1], width // 2
    mine = d_attn[:, rows_at(units * core, units, 128)]
    others = d_attn[:, rows_at(units * (1 - core), units, 128)]
    for j in range(4):
        at = slice(feat * j, feat * (j + 1))
        piece = mixed[(rows + 16) * j : (rows + 16) * j + rows, :]
        kept[at, :] = dot(piece, mine, TN).astype(BF16)
        given[at, :] = dot(piece, others, TN).astype(BF16)


def up_grads(where, h_pair, d_up, kept, given, *refs):
    outs, total = refs[:4], refs[4]
    count, units = outs[0].shape[0] // 4, d_up.shape[1]
    total[:, :units] = dot(h_pair[...], d_up[...], TN).astype(BF16)
    total[:, units:] = (kept[...].astype(F32) + given[...].astype(F32)).astype(BF16)
    for k, out in enumerate(outs):
        for p in range(4):
            at = rows_at(4 * count * p + count * (where[0] ^ k), count, 16)
            out[count * p : count * (p + 1), :] = total[at, :]


def send_planes(where, own, p1, p2, p3, *refs):
    outs, total = refs[:4], refs[4]
    part = outs[0].shape[0]
    added = own[...].astype(F32)
    for piece in (p1, p2, p3):
        added = added + piece[...].astype(F32)
    total[...] = added
    for s, out in enumerate(outs):
        out[...] = total[rows_at(part * (where[2] ^ s), part, 16), :].astype(out.dtype)


def sum_pieces(where, own, p1, p2, p3, out):
    total = own[...].astype(F32)
    for piece in (p1, p2, p3):
        total = total + piece[...].astype(F32)
    out[...] = total.astype(out.dtype)


def start_down(where, near, far, out, held, sems):
    core = where[1]
    both = near.shape[0] // 4
    part = both // 2
    copies = []
    for j in range(4):
        block = slice(both * j + part, both * (j + 1))
        for side, piece in ((core, near), (1 - core, far)):
            at = rows_at(4 * part * side + part * j, part, 32)
            held[at, :] = piece[block, :].astype(F32)
            copies.append(pltpu.make_async_copy(held.at[at], out.at[at], sems.at[len(copies)]))
            copies[-1].start()
    return copies


def finish_up(where, n0, n1, n2, n3, far, out, out_half, held, held_half, sems):
    chip, core = where[0], where[1]
    part, units = n0.shape[0], n0.shape[1] // 5
    copies = []
    for k, near in enumerate((n0, n1, n2, n3)):
        rows = rows_at(part * (chip ^ k), part, 16)
        for piece, side in ((near[...], core), (far[part * k : part * (k + 1), :], 1 - core)):
            full = piece.astype(F32)
            for i in range(4):
                at = rows_at(2 * units * i + units * side, units, 128)
                held[rows, at] = full[:, units * i : units * (i + 1)]
            held_half[rows, rows_at(units * side, units, 128)] = full[:, 4 * units :]
        for source, target in ((held, out), (held_half, out_half)):
            copies.append(
                pltpu.make_async_copy(source.at[rows], target.at[rows], sems.at[len(copies)])
            )
            copies[-1].start()
    for copy in copies:
        copy.wait()


def sum_chips(where, own, from_x, from_y, last_x, last_y, out):
    half = last_x.shape[0]
    low, high = add_chips(own, from_x, from_y, last_x, last_y)
    out[:half, :], out[half:, :] = low.astype(BF16), high.astype(BF16)


def pack_gradients(
    where, kept, given, from_attention, from_second, from_result, up_line, down, out, down_sum
):
    chip = where[0]
    part = down_sum.shape[0]
    arrived_down = down[:part, :].astype(F32)
    for p in (1, 2, 3):
        arrived_down = arrived_down + down[part * p : part * (p + 1), :].astype(F32)
    down_sum[...] = arrived_down.astype(BF16)
    half, feat = out.shape[0] // 4, kept.shape[1] // 3
    for p in range(4):
        cut = slice(feat * p, feat * (p + 1))
        owner = jnp.where(chip == p, 1.0, 0.0)
        lines = [
            from_attention[0:1, cut],
            from_attention[1:2, cut],
            from_second[0:1, cut],
            from_second[1:2, cut],
            from_second[2:3, cut],
            from_result[0:1, cut],
            up_line[:, 2 * feat * p : 2 * feat * p + feat],
            up_line[:, 2 * feat * p + feat : 2 * feat * (p + 1)],
            from_attention[2:3, :feat] * owner,
            from_attention[3:4, :feat] * owner,
            from_result[1:2, :feat],
            jnp.zeros((5, feat), F32),
        ]
        small = jnp.concatenate(lines, axis=0)
        block = slice(half * p, half * (p + 1))
        total = (kept[block, :].astype(F32) + given[block, :].astype(F32)).astype(BF16)
        out[block, : 3 * feat] = total
        out[half * p + 48 : half * (p + 1), 3 * feat :] = jnp.zeros((half - 48, feat // 3), BF16)
        put_small(out, half * p, small)


def sum_planes(where, arrived, down, out):
    both, width = out.shape[0] // 4, out.shape[1]
    half, feat = both // 2, width // 4
    total = arrived[:half, :].astype(F32)
    for p in (1, 2, 3):
        total = total + arrived[half * p : half * (p + 1), :].astype(F32)
    small = get_small(total, 0, feat)
    error = jnp.sum(small[10:11, :3], axis=1, keepdims=True)
    high = error.astype(BF16).astype(F32)
    middle = (error - high).astype(BF16).astype(F32)
    line = lax.broadcasted_iota(jnp.int32, small.shape, 0)
    side = lax.broadcasted_iota(jnp.int32, small.shape, 1)
    parts = jnp.where(side == 0, high, jnp.where(side == 1, middle, error - high - middle))
    small = jnp.where((line == 10) & (side < 3), parts, small)
    for j in range(4):
        start = both * j
        out[start : start + half, : 3 * feat] = total[:, : 3 * feat].astype(BF16)
        out[start : start + 16, 3 * feat :] = small.astype(BF16)
        out[start + 16 : start + half, 3 * feat :] = jnp.zeros((half - 16, feat), BF16)
        out[start + half : start + both, :] = down[...]


def finish_projections(where, near, far, count, *outs):
    query, key, value, loss = outs[:4]
    flat, up_line, held, whole_line = outs[4:12], outs[12], outs[13], outs[14]
    core = where[1]
    both, width = near.shape[0] // 4, near.shape[1]
    half, feat = both // 2, width // 4
    for j in range(4):
        start = both * j
        for side, piece in ((core, near), (1 - core, far)):
            held[2 * j + side] = piece[start : start + 16, 3 * feat :].astype(F32)
            rows = rows_at(half * side, half, 32)
            for i, out in enumerate((query, key, value)):
                out[rows, feat * j : feat * (j + 1)] = piece[
                    start : start + half, feat * i : feat * (i + 1)
                ].astype(F32)
    total = held[0]
    for i in range(1, 8):
        total = total + held[i]
    for i, line in enumerate((0, 1, 2, 3, 4, 5, 8, 9)):
        flat[i][...] = total[line]
    even = held[0] + held[2] + held[4] + held[6]
    odd = held[1] + held[3] + held[5] + held[7]
    for side, part in enumerate((even, odd)):
        for i in range(2):
            at = 2 * feat * side + feat * i
            whole_line[0:1, at : at + feat] = part[6 + i : 7 + i, :]
    up_line[...] = whole_line[0]
    error = jnp.sum(total[10:11, :3], axis=1, keepdims=True)
    loss[0, 0] = jnp.sum(error / (width * count[0:1, 0:1]))


def finish_gathered(where, near, far, count, *refs):
    outs, down, scratch = refs[:13], refs[13], refs[14:]
    copies = start_down(where, near, far, down, scratch[2], scratch[3])
    finish_projections(where, near, far, count, *outs, *scratch[:2])
    for copy in copies:
        copy.wait()


def layer(
    tokens,
    segment_ids,
    valid_rows,
    teacher,
    cotangent,
    first_gain,
    first_shift,
    query_weight,
    query_bias,
    key_weight,
    value_weight,
    value_bias,
    output_weight,
    output_bias,
    second_gain,
    second_shift,
    up_weight,
    up_bias,
    down_weight,
    down_bias,
):
    rows, width = tokens.shape[1], tokens.shape[2]
    shard = query_weight.shape[0]
    half, quarter = shard // 2, shard // 4
    hidden = up_weight.shape[1]
    units = hidden // 2
    own_units = down_weight.shape[0]
    core_units = own_units // 2
    part_units = core_units // 4
    feat = width // 4
    heads = feat // HEAD_DIM
    group = 4 * rows
    every = 2 * group
    steps = (1, 2, 3)

    place, plane = lax.axis_index("ctx"), lax.axis_index("fsdp")
    where = jnp.stack([place // 2, place % 2, plane]).astype(jnp.int32)
    dma = pltpu.SemaphoreType.DMA

    last = []

    def step(body, outs, args, **options):
        made, token = local_call(body, outs, where, args, after=last, **options)
        last[:] = [token]
        return made

    def stack(pieces, cost=0):
        shape = len(pieces) * pieces[0].shape[0], pieces[0].shape[1]
        return step(stack_rows, shaped(*shape), pieces, cost=cost)

    own = tokens[0]
    smalls = (
        first_gain,
        first_shift,
        query_bias,
        value_bias,
        output_bias,
        second_gain,
        second_shift,
        down_bias,
    )
    up_piece = step(
        pack_blocks,
        shaped(4 * quarter, 5 * core_units),
        (up_weight, output_weight),
        far=range(2),
        scratch=[dma((5,))],
    )
    up_far = trade_planes(up_piece)
    bundle = step(pack_tokens, shaped(rows + 16, width), (own, segment_ids, valid_rows), cost=50)
    near_tokens = [bundle] + [swap_chips(bundle, k) for k in steps]
    lanes = 3 * feat + feat // 3
    projections = step(
        pack_projections,
        shaped(half, lanes),
        (query_weight, key_weight, value_weight, *smalls, up_bias, valid_rows),
        far=range(12),
        scratch=[
            pltpu.VMEM((3, half, width), BF16),
            *[pltpu.VMEM((feat,), BF16)] * 8,
            pltpu.VMEM((own_units,), BF16),
            dma((12,)),
        ],
        cost=0,
    )
    near_tokens = step(order_chips, shaped(4 * (rows + 16), width), near_tokens, cost=0)
    far_tokens = swap_cores(near_tokens)
    up_far = step(far_planes, shaped(3 * quarter, 5 * core_units), (up_far,), cost=0)
    up_three = up_far, swap_chips(up_far, 1), swap_chips(up_far, 2)
    near_weights = [projections] + [swap_planes(projections, s) for s in steps]
    unit_one, key_row, query_column = step(
        normalize_tokens,
        (wide(every, width), wide(8, every), wide(group, 128)),
        (near_tokens, far_tokens),
        cost=1,
    )
    far_weights = swap_cores(stack(near_weights))

    def first_chips(piece):
        return piece, swap_chips(piece, 1), swap_chips(piece, 2)

    def all_chips(three, cut):
        count, lanes = three[0].shape
        to_x, to_y = step(cross_halves, (shaped(cut, lanes), shaped(count - cut, lanes)), three[1:], cost=50)
        return (*three, swap_chips(to_x, 1), swap_chips(to_y, 2))

    up_all = all_chips(up_three, up_far.shape[0] // 32 * 16 + 16)
    down_piece = step(
        pack_down, shaped(part_units, width), (down_weight,), far=(0,), scratch=[dma]
    )
    down_far = [swap_planes(down_piece, s) for s in steps]

    h_one, w_three, projected, probs, mixed, sent, vectors, b_up = step(
        attend,
        (
            shaped(every, width),
            shaped(width, 3 * feat),
            shaped(every, 3 * feat),
            shaped(heads, group, every),
            wide(group, feat),
            shaped(4 * (rows + 16), feat),
            wide(8, width),
            wide(1, units),
        ),
        (unit_one, key_row, query_column, *near_weights, far_weights),
        far_outs=range(5),
        scratch=[
            pltpu.VMEM((4, 16, feat), F32),
            pltpu.VMEM((group, every), F32),
            pltpu.VMEM((every, width), BF16),
            pltpu.VMEM((width, 3 * feat), BF16),
            pltpu.VMEM((every, 3 * feat), BF16),
            pltpu.VMEM((heads, group, every), BF16),
            pltpu.VMEM((group, feat), F32),
            dma((4 + heads,)),
        ],
        vmem=28,
        cost=50,
    )
    mixed_low = trade_chips(sent)
    down_far = first_chips(stack(down_far))
    out_near = step(
        build_half,
        shaped(width, core_units),
        (output_weight, *up_all),
        far=range(6),
        scratch=[dma((20,))],
    )
    out_far = swap_cores(out_near)
    w_up = step(
        build_up, shaped(width, units), (up_weight, *up_all), far=range(6), scratch=[dma((20,))], cost=50
    )
    w_output = step(build_output, shaped(width, width), (out_near, out_far))

    down_all = all_chips(down_far, down_far[0].shape[0] // 2)
    second, h_two, count = step(
        project_output,
        (wide(rows, width), shaped(rows, width), wide(8, 128)),
        (mixed_low, w_output, own, vectors),
    )
    h_pair = both_cores(h_two)
    act, slope = step(
        activate,
        (shaped(2 * rows, units), wide(2 * rows, units)),
        (h_pair, w_up, b_up),
    )
    w_down = step(
        build_down, shaped(units, width), (down_weight, *down_all), far=(0,), scratch=[dma]
    )
    down_near, down_other = step(
        project_down,
        (wide(rows, width), shaped(rows, width)),
        (act, w_down),
        scratch=[pltpu.VMEM((2 * rows, width), F32)],
    )
    layer_output, d_result, d_down, from_result = step(
        compare,
        (shaped(rows, width), wide(rows, width), shaped(rows, width), wide(8, width)),
        (
            second,
            down_near,
            both_cores(down_other),
            vectors,
            teacher[0],
            cotangent[0],
            valid_rows,
            count,
        ),
    )
    d_down = both_cores(d_down)

    def five(count, lanes):
        return (shaped(4 * count, lanes),) * 3 + (shaped(2 * count, lanes),) * 2

    def onward(parts, arrived):
        count, lanes = parts[3].shape
        to_x, to_y = step(
            pass_on, (shaped(count, lanes),) * 2, (*arrived, *parts[3:]),
            cost=50,
        )
        return (parts[0], *arrived, swap_chips(to_x, 1), swap_chips(to_y, 2))

    down_parts = step(
        down_grads,
        five(part_units, width),
        (act, d_down),
        scratch=[pltpu.VMEM((units, width), BF16)],
        vmem=24,
    )
    down_arrived = swap_chips(down_parts[1], 1), swap_chips(down_parts[2], 2)
    d_up, two_near, two_other, up_line = step(
        activate_back,
        (shaped(2 * rows, units), wide(rows, width), shaped(rows, width), wide(1, units)),
        (d_down, w_down, slope, w_up),
        scratch=[pltpu.VMEM((2 * rows, width), F32)],
        cost=50,
    )
    d_second, d_attn, from_second, d_sent = step(
        second_back,
        (wide(rows, width), shaped(rows, width), wide(8, width), shaped(group, feat)),
        (two_near, both_cores(two_other), d_result, second, vectors, w_output),
    )
    d_mixed = trade_chips(d_sent)

    kept_out, given_out = step(
        output_grads,
        (shaped(width, core_units), shaped(width, core_units)),
        (mixed_low, d_attn),
        cost=1,
    )
    given_out = swap_cores(given_out)
    down_sums = onward(down_parts, down_arrived)
    up_parts = step(
        up_grads,
        (shaped(4 * quarter, 5 * core_units),) * 4,
        (h_pair, d_up, kept_out, given_out),
        store=(0,),
        scratch=[pltpu.VMEM((width, 5 * core_units), BF16)],
        vmem=24,
        cost=5,
    )
    up_sums = [up_parts[0]] + [swap_chips(up_parts[k], k) for k in steps]
    down_planes = trade_planes(step(sum_chips, shaped(4 * part_units, width), down_sums))

    d_near, d_far, kept, given, from_attention = step(
        attend_back,
        (
            shaped(group, width),
            shaped(group, width),
            shaped(4 * half, 3 * feat),
            shaped(4 * half, 3 * feat),
            wide(8, width),
        ),
        (d_mixed, vectors, h_one, w_three, projected, probs, mixed),
        far=range(2, 7),
        store=(2, 3),
        scratch=[
            pltpu.VMEM((every, 3 * feat), BF16),
            pltpu.VMEM((group, every), BF16),
            pltpu.VMEM((width, 3 * feat), F32),
            pltpu.VMEM((every, width), BF16),
            pltpu.VMEM((width, 3 * feat), BF16),
            pltpu.VMEM((every, 3 * feat), BF16),
            pltpu.VMEM((heads, group, every), BF16),
            pltpu.VMEM((group, feat), F32),
            dma((4 + heads,)),
        ],
        vmem=28,
        cost=50,
    )
    given, d_far = swap_cores(given), swap_cores(d_far)
    arrived, down_planes = step(
        pack_gradients,
        (shaped(4 * half, lanes), shaped(part_units, width)),
        (kept, given, from_attention, from_second, from_result, up_line, down_planes),
        fetch=(0, 1),
        cost=1,
    )
    arrived = trade_planes(arrived)

    def spread(piece):
        return [piece] + [swap_chips(piece, k) for k in steps]

    def whole(near):
        return (*near, swap_cores(stack(near, cost=1)))

    up_planes = step(
        send_planes,
        (shaped(quarter, 5 * core_units),) * 4,
        up_sums,
        fetch=(0,),
        scratch=[pltpu.VMEM((4 * quarter, 5 * core_units), F32)],
        cost=50,
    )
    up_planes = [up_planes[0]] + [swap_planes(up_planes[s], s) for s in steps]
    shares = step(share_inputs, (shaped(rows, width),) * 4, (d_near, d_far), store=(0,), cost=50)
    shares = [shares[0]] + [swap_chips(shares[k], k) for k in steps]
    both = trade_chips(step(sum_planes, shaped(8 * half, width), (arrived, down_planes), cost=50))
    up_near = spread(step(sum_pieces, shaped(quarter, 5 * core_units), up_planes, cost=50))
    grad_tokens = step(
        finish_inputs, shaped(rows, width), (*shares, own, d_second, vectors), fetch=(0, 4), cost=50
    )
    both = (both, swap_cores(both))
    up_whole = whole(up_near)
    finished = step(
        finish_gathered,
        (wide(shard, width),) * 3
        + (wide(1, 1),)
        + (wide(shard),) * 8
        + (wide(own_units), wide(own_units, width)),
        (*both, count),
        far_outs=(13,),
        scratch=[
            pltpu.VMEM((8, 16, feat), F32),
            pltpu.VMEM((8, own_units), F32),
            pltpu.VMEM((own_units, width), F32),
            dma((8,)),
        ],
        scalar=3,
    )
    grad_down_weight = finished[13]
    grad_up_weight, grad_output_weight = step(
        finish_up,
        (wide(shard, hidden), wide(shard, width)),
        up_whole,
        far_outs=(0, 1),
        scratch=[pltpu.VMEM((shard, hidden), F32), pltpu.VMEM((shard, width), F32), dma((8,))],
    )
    sums, two = finished[4:10], finished[10:12]
    return (
        layer_output[None],
        finished[3].reshape(()),
        grad_tokens[None],
        sums[0],
        sums[1],
        finished[0],
        two[0],
        finished[1],
        finished[2],
        two[1],
        grad_output_weight,
        sums[2],
        sums[3],
        sums[4],
        grad_up_weight,
        finished[12],
        grad_down_weight,
        sums[5],
    )


def solution(mesh):
    body = layer if (mesh.shape["ctx"], mesh.shape["fsdp"]) == (8, 4) else shards
    placed = (
        P("fsdp", "ctx", None),
        P("fsdp", "ctx"),
        P("fsdp", "ctx"),
        P("fsdp", "ctx", None),
        P("fsdp", "ctx", None),
        P("fsdp"),
        P("fsdp"),
        P("fsdp", None),
        P("fsdp"),
        P("fsdp", None),
        P("fsdp", None),
        P("fsdp"),
        P("fsdp", None),
        P("fsdp"),
        P("fsdp"),
        P("fsdp"),
        P("fsdp", None),
        P("fsdp"),
        P("fsdp", None),
        P("fsdp"),
    )
    return jax.shard_map(
        body,
        mesh=mesh,
        in_specs=placed,
        out_specs=(
            P("fsdp", "ctx", None),
            P(),
            P("fsdp", "ctx", None),
            P("fsdp"),
            P("fsdp"),
            P("fsdp", None),
            P("fsdp"),
            P("fsdp", None),
            P("fsdp", None),
            P("fsdp"),
            P("fsdp", None),
            P("fsdp"),
            P("fsdp"),
            P("fsdp"),
            P("fsdp", None),
            P("fsdp"),
            P("fsdp", None),
            P("fsdp"),
        ),
        check_vma=False,
    )
```

```python
import jax
import jax.numpy as jnp
from jax import lax
from jax.experimental import pallas as pl
from jax.experimental.pallas import tpu as pltpu
from jax.sharding import PartitionSpec as P

HEADS = 12
HEAD_DIM = 64


EPSILON = 1e-06
MASKED = -1e30


def norm_rows(values, gain, shift):
    centre = jnp.mean(values, axis=-1, keepdims=True)
    centred = values - centre
    spread = jnp.mean(centred * centred, axis=-1, keepdims=True)
    return centred * lax.rsqrt(spread + EPSILON) * gain + shift


def tanh_gelu(values):
    return jax.nn.gelu(values, approximate=True)


def key_allowed(query_segment, query_place, key_codes, key_place):
    same_doc = query_segment[:, None] == (key_codes // 2)[None, :]
    usable = (key_codes % 2 == 1)[None, :] | (query_place[:, None] == key_place[None, :])
    return (same_doc & usable)[None, :, :]


def split_heads(values):
    return values.reshape(values.shape[0], HEADS, HEAD_DIM)


def head_scores(query_heads, key_heads, scale):
    return (
        jnp.einsum("qhd,khd->hqk", query_heads, key_heads, preferred_element_type=jnp.float32)
        * scale
    )


def row_sum(values):
    return jnp.sum(values, axis=0, dtype=jnp.float32)


def left_product(left, right):
    return jnp.einsum("rd,rf->df", left, right, preferred_element_type=jnp.float32)


def right_product(left, right):
    return jnp.einsum("rf,df->rd", left, right, preferred_element_type=jnp.float32)


def shards(
    tokens,
    segment_ids,
    valid_rows,
    teacher,
    cotangent,
    first_gain,
    first_shift,
    query_weight,
    query_bias,
    key_weight,
    value_weight,
    value_bias,
    output_weight,
    output_bias,
    second_gain,
    second_shift,
    up_weight,
    up_bias,
    down_weight,
    down_bias,
):
    tok_rows = tokens.shape[1]
    feature_width = tokens.shape[2]
    shard_count = lax.axis_size("ctx")
    key_block = 4 * tok_rows
    block_count = shard_count // 4
    scale = HEAD_DIM ** (-0.5)
    gain_one, shift_one, w_query, b_query, w_key, w_value, b_value, w_output, b_output = (
        lax.all_gather(first_gain, "fsdp", axis=0, tiled=True),
        lax.all_gather(first_shift, "fsdp", axis=0, tiled=True),
        lax.all_gather(query_weight, "fsdp", axis=0, tiled=True),
        lax.all_gather(query_bias, "fsdp", axis=0, tiled=True),
        lax.all_gather(key_weight, "fsdp", axis=0, tiled=True),
        lax.all_gather(value_weight, "fsdp", axis=0, tiled=True),
        lax.all_gather(value_bias, "fsdp", axis=0, tiled=True),
        lax.all_gather(output_weight, "fsdp", axis=0, tiled=True),
        lax.all_gather(output_bias, "fsdp", axis=0, tiled=True),
    )
    gain_two, shift_two, w_up, b_up, w_down, b_down = (
        lax.all_gather(second_gain, "fsdp", axis=0, tiled=True),
        lax.all_gather(second_shift, "fsdp", axis=0, tiled=True),
        lax.all_gather(up_weight, "fsdp", axis=0, tiled=True),
        lax.all_gather(up_bias, "fsdp", axis=0, tiled=True),
        lax.all_gather(down_weight, "fsdp", axis=0, tiled=True),
        lax.all_gather(down_bias, "fsdp", axis=0, tiled=True),
    )
    local_segment = segment_ids[0]
    local_valid = valid_rows[0]
    local_codes = local_segment * 2 + local_valid
    all_codes = lax.all_gather(local_codes, "ctx", axis=0, tiled=True)
    query_place = lax.axis_index("ctx") * tok_rows + jnp.arange(tok_rows, dtype=jnp.int32)
    inputs = tokens[0].astype(jnp.float32)
    gain_first = gain_one.astype(jnp.float32)
    shift_first = shift_one.astype(jnp.float32)
    gain_second = gain_two.astype(jnp.float32)
    shift_second = shift_two.astype(jnp.float32)
    h_one = norm_rows(inputs, gain_first, shift_first)
    h_one_low = h_one.astype(jnp.bfloat16)
    query_low = (
        jnp.dot(h_one_low, w_query, preferred_element_type=jnp.float32)
        + b_query.astype(jnp.float32)
    ).astype(jnp.bfloat16)
    key_low = jnp.dot(h_one_low, w_key, preferred_element_type=jnp.float32).astype(jnp.bfloat16)
    value_low = (
        jnp.dot(h_one_low, w_value, preferred_element_type=jnp.float32)
        + b_value.astype(jnp.float32)
    ).astype(jnp.bfloat16)
    key_all, value_all = (
        lax.all_gather(key_low, "ctx", axis=0, tiled=True),
        lax.all_gather(value_low, "ctx", axis=0, tiled=True),
    )
    query_heads = split_heads(query_low)

    def block_rows(source, block_index):
        return split_heads(lax.dynamic_slice_in_dim(source, block_index * key_block, key_block, 0))

    def block_allowed(block_index):
        start = block_index * key_block
        codes = lax.dynamic_slice_in_dim(all_codes, start, key_block, 0)
        return key_allowed(
            local_segment, query_place, codes, start + jnp.arange(key_block, dtype=jnp.int32)
        )

    def stats_step(block_index, state_pair):
        running_max, running_sum = state_pair
        allowed = block_allowed(block_index)
        scores = jnp.where(
            allowed, head_scores(query_heads, block_rows(key_all, block_index), scale), MASKED
        )
        new_max = jnp.maximum(running_max, jnp.max(scores, axis=2))
        weights = jnp.where(allowed, jnp.exp(scores - new_max[:, :, None]), 0.0)
        return (new_max, running_sum * jnp.exp(running_max - new_max) + jnp.sum(weights, axis=2))

    start_max = jnp.full((HEADS, tok_rows), MASKED, jnp.float32)
    start_sum = jnp.zeros((HEADS, tok_rows), jnp.float32)
    running_max, running_sum = lax.fori_loop(0, block_count, stats_step, (start_max, start_sum))
    log_total = running_max + jnp.log(running_sum)

    def mix_step(block_index, mixed_sum):
        allowed = block_allowed(block_index)
        scores = head_scores(query_heads, block_rows(key_all, block_index), scale)
        probs = jnp.where(allowed, jnp.exp(scores - log_total[:, :, None]), 0.0).astype(
            jnp.bfloat16
        )
        return mixed_sum + jnp.einsum(
            "hqk,khd->qhd",
            probs,
            block_rows(value_all, block_index),
            preferred_element_type=jnp.float32,
        )

    mixed_heads = lax.fori_loop(
        0, block_count, mix_step, jnp.zeros((tok_rows, HEADS, HEAD_DIM), jnp.float32)
    )
    mixed = mixed_heads.reshape(tok_rows, feature_width)
    mixed_low = mixed.astype(jnp.bfloat16)
    second = (
        inputs
        + jnp.dot(mixed_low, w_output, preferred_element_type=jnp.float32)
        + b_output.astype(jnp.float32)
    )
    h_two = norm_rows(second, gain_second, shift_second)
    h_two_low = h_two.astype(jnp.bfloat16)
    up_value = jnp.dot(h_two_low, w_up, preferred_element_type=jnp.float32) + b_up.astype(
        jnp.float32
    )
    act_low = tanh_gelu(up_value).astype(jnp.bfloat16)
    result = (
        second
        + jnp.dot(act_low, w_down, preferred_element_type=jnp.float32)
        + b_down.astype(jnp.float32)
    )
    layer_output = result.astype(jnp.bfloat16)[None]
    valid_float = local_valid.astype(jnp.float32)
    mismatch = result - teacher[0].astype(jnp.float32)
    error_sum, valid_count = lax.psum(
        (jnp.sum(valid_float[:, None] * mismatch * mismatch), jnp.sum(valid_float)), ("ctx", "fsdp")
    )
    loss_value = error_sum / (feature_width * valid_count)
    d_result = (
        cotangent[0].astype(jnp.float32)
        + 2.0 / (feature_width * valid_count) * valid_float[:, None] * mismatch
    )
    d_down = d_result.astype(jnp.bfloat16)
    grad_down_bias = row_sum(d_down)
    grad_down_weight = left_product(act_low, d_down)
    d_act = right_product(d_down, w_down)
    gelu_value, gelu_pull = jax.vjp(tanh_gelu, up_value)
    d_up = gelu_pull(d_act)[0].astype(jnp.bfloat16)
    grad_up_bias = row_sum(d_up)
    grad_up_weight = left_product(h_two_low, d_up)
    d_h_two = right_product(d_up, w_up)
    norm_two_value, norm_two_pull = jax.vjp(norm_rows, second, gain_second, shift_second)
    d_second_norm, grad_second_gain, grad_second_shift = norm_two_pull(d_h_two)
    d_second = d_result + d_second_norm
    d_attn = d_second.astype(jnp.bfloat16)
    grad_output_bias = row_sum(d_attn)
    grad_output_weight = left_product(mixed_low, d_attn)
    d_mixed = right_product(d_attn, w_output).astype(jnp.bfloat16)
    d_heads = split_heads(d_mixed)
    delta = jnp.einsum("qhd,qhd->hq", d_heads.astype(jnp.float32), mixed_heads)
    key_back, value_back = (key_all, value_all)

    def score_grads(block_index):
        allowed = block_allowed(block_index)
        key_piece = block_rows(key_back, block_index)
        value_piece = block_rows(value_back, block_index)
        scores = head_scores(query_heads, key_piece, scale)
        probs = jnp.where(allowed, jnp.exp(scores - log_total[:, :, None]), 0.0)
        d_probs = jnp.einsum(
            "qhd,khd->hqk", d_heads, value_piece, preferred_element_type=jnp.float32
        )
        d_scores = (probs * (d_probs - delta[:, :, None])).astype(jnp.bfloat16)
        return (key_piece, probs, d_scores)

    zero_query = jnp.zeros((tok_rows, HEADS, HEAD_DIM), jnp.float32)

    def reduce_step(block_index, state_triple):
        d_query_sum, d_key_rows, d_value_rows = state_triple
        key_piece, probs, d_scores = score_grads(block_index)
        d_query_sum = d_query_sum + jnp.einsum(
            "hqk,khd->qhd", d_scores, key_piece, preferred_element_type=jnp.float32
        )
        d_key_piece = jnp.einsum(
            "hqk,qhd->khd", d_scores, query_heads, preferred_element_type=jnp.float32
        ).reshape(key_block, feature_width)
        d_value_piece = jnp.einsum(
            "hqk,qhd->khd", probs.astype(jnp.bfloat16), d_heads, preferred_element_type=jnp.float32
        ).reshape(key_block, feature_width)
        d_key_rows = lax.dynamic_update_slice_in_dim(
            d_key_rows, d_key_piece, block_index * key_block, 0
        )
        d_value_rows = lax.dynamic_update_slice_in_dim(
            d_value_rows, d_value_piece, block_index * key_block, 0
        )
        return (d_query_sum, d_key_rows, d_value_rows)

    zero_rows = jnp.zeros((key_block * block_count, feature_width), jnp.float32)
    d_query_sum, d_key_rows, d_value_rows = lax.fori_loop(
        0, block_count, reduce_step, (zero_query, zero_rows, zero_rows)
    )
    d_key_local, d_value_local = (
        lax.psum_scatter(d_key_rows, "ctx", scatter_dimension=0, tiled=True),
        lax.psum_scatter(d_value_rows, "ctx", scatter_dimension=0, tiled=True),
    )
    d_query = (d_query_sum.reshape(tok_rows, feature_width) * scale).astype(jnp.bfloat16)
    d_key = (d_key_local * scale).astype(jnp.bfloat16)
    d_value = d_value_local.astype(jnp.bfloat16)
    grad_query_bias = row_sum(d_query)
    grad_query_weight = left_product(h_one_low, d_query)
    grad_key_weight = left_product(h_one_low, d_key)
    grad_value_bias = row_sum(d_value)
    grad_value_weight = left_product(h_one_low, d_value)
    d_h_one = (
        right_product(d_query, w_query)
        + right_product(d_key, w_key)
        + right_product(d_value, w_value)
    )
    norm_one_value, norm_one_pull = jax.vjp(norm_rows, inputs, gain_first, shift_first)
    d_inputs_norm, grad_first_gain, grad_first_shift = norm_one_pull(d_h_one)
    grad_tokens = (d_second + d_inputs_norm).astype(jnp.bfloat16)[None]
    shares = (
        lax.psum_scatter(
            grad_first_gain.astype(jnp.bfloat16), "fsdp", scatter_dimension=0, tiled=True
        ).astype(jnp.float32),
        lax.psum_scatter(
            grad_first_shift.astype(jnp.bfloat16), "fsdp", scatter_dimension=0, tiled=True
        ).astype(jnp.float32),
        lax.psum_scatter(
            grad_query_weight.astype(jnp.bfloat16), "fsdp", scatter_dimension=0, tiled=True
        ).astype(jnp.float32),
        lax.psum_scatter(
            grad_query_bias.astype(jnp.bfloat16), "fsdp", scatter_dimension=0, tiled=True
        ).astype(jnp.float32),
        lax.psum_scatter(
            grad_key_weight.astype(jnp.bfloat16), "fsdp", scatter_dimension=0, tiled=True
        ).astype(jnp.float32),
        lax.psum_scatter(
            grad_value_weight.astype(jnp.bfloat16), "fsdp", scatter_dimension=0, tiled=True
        ).astype(jnp.float32),
        lax.psum_scatter(
            grad_value_bias.astype(jnp.bfloat16), "fsdp", scatter_dimension=0, tiled=True
        ).astype(jnp.float32),
        lax.psum_scatter(
            grad_output_weight.astype(jnp.bfloat16), "fsdp", scatter_dimension=0, tiled=True
        ).astype(jnp.float32),
        lax.psum_scatter(
            grad_output_bias.astype(jnp.bfloat16), "fsdp", scatter_dimension=0, tiled=True
        ).astype(jnp.float32),
        lax.psum_scatter(
            grad_second_gain.astype(jnp.bfloat16), "fsdp", scatter_dimension=0, tiled=True
        ).astype(jnp.float32),
        lax.psum_scatter(
            grad_second_shift.astype(jnp.bfloat16), "fsdp", scatter_dimension=0, tiled=True
        ).astype(jnp.float32),
        lax.psum_scatter(
            grad_up_weight.astype(jnp.bfloat16), "fsdp", scatter_dimension=0, tiled=True
        ).astype(jnp.float32),
        lax.psum_scatter(
            grad_up_bias.astype(jnp.bfloat16), "fsdp", scatter_dimension=0, tiled=True
        ).astype(jnp.float32),
        lax.psum_scatter(
            grad_down_weight.astype(jnp.bfloat16), "fsdp", scatter_dimension=0, tiled=True
        ).astype(jnp.float32),
        lax.psum_scatter(
            grad_down_bias.astype(jnp.bfloat16), "fsdp", scatter_dimension=0, tiled=True
        ).astype(jnp.float32),
    )
    totals = lax.psum(
        (
            shares[0],
            shares[1],
            shares[2],
            shares[3],
            shares[4],
            shares[5],
            shares[6],
            shares[7],
            shares[8],
            shares[9],
            shares[10],
            shares[11],
            shares[12],
            shares[13],
            shares[14],
        ),
        "ctx",
    )
    return (
        layer_output,
        loss_value,
        grad_tokens,
        totals[0],
        totals[1],
        totals[2],
        totals[3],
        totals[4],
        totals[5],
        totals[6],
        totals[7],
        totals[8],
        totals[9],
        totals[10],
        totals[11],
        totals[12],
        totals[13],
        totals[14],
    )


F32 = jnp.float32
BF16 = jnp.bfloat16
ANY = pl.BlockSpec(memory_space=pl.ANY)
HBM = pl.BlockSpec(memory_space=pltpu.HBM)
VMEM = pl.BlockSpec(memory_space=pltpu.VMEM)
SMEM = pl.BlockSpec(memory_space=pltpu.SMEM)
NT = (((1,), (1,)), ((), ()))
TN = (((0,), (0,)), ((), ()))
NN = (((1,), (0,)), ((), ()))


def swap_cores(value):
    size = lax.axis_size("ctx")
    return lax.ppermute(value, "ctx", [(i, i ^ 1) for i in range(size)])


def both_cores(value):
    pairs = [[i, i + 1] for i in range(0, lax.axis_size("ctx"), 2)]
    return lax.all_gather(value, "ctx", axis=0, tiled=True, axis_index_groups=pairs)


def swap_chips(value, step):
    size = lax.axis_size("ctx")
    return lax.ppermute(value, "ctx", [(i, i ^ (2 * step)) for i in range(size)])


def swap_planes(value, step):
    size = lax.axis_size("fsdp")
    return lax.ppermute(value, "fsdp", [(i, i ^ step) for i in range(size)])


def trade_chips(value):
    size = lax.axis_size("ctx")
    groups = [[i for i in range(size) if i % 2 == c] for c in (0, 1)]
    return lax.all_to_all(value, "ctx", 0, 0, axis_index_groups=groups, tiled=True)


def trade_planes(value):
    return lax.all_to_all(value, "fsdp", 0, 0, tiled=True)


def shaped(*shape, dtype=BF16):
    return jax.ShapeDtypeStruct(shape, dtype)


def wide(*shape):
    return jax.ShapeDtypeStruct(shape, F32)


def local_call(
    body,
    outs,
    where,
    args,
    far=(),
    far_outs=(),
    fetch=(),
    store=(),
    scalar=None,
    scratch=(),
    after=(),
    vmem=14,
    cost=0,
):
    fetch, store = list(fetch), list(store)
    args = [
        pltpu.with_memory_space_constraint(a, pltpu.HBM) if i in far or i in fetch else a
        for i, a in enumerate(args)
    ]
    after = list(after)
    many = isinstance(outs, tuple)
    outs = outs if many else (outs,)
    count, made, moved = len(args), len(outs), len(fetch) + len(store)
    held = [pltpu.VMEM(args[i].shape, args[i].dtype) for i in fetch]
    held += [pltpu.VMEM(outs[i].shape, outs[i].dtype) for i in store]
    if moved:
        held.append(pltpu.SemaphoreType.DMA((moved,)))

    def kernel(where_ref, *refs):
        start = count + len(after)
        given, results = list(refs[:count]), list(refs[start : start + made])
        token, extra = refs[start + made], refs[start + made + 1 :]
        extra, copied = extra[: len(extra) - len(held)], extra[len(extra) - len(held) :]
        token[...] = jnp.zeros(token.shape, token.dtype)
        into = [
            pltpu.make_async_copy(given[i], copied[n], copied[-1].at[n])
            for n, i in enumerate(fetch)
        ]
        out_of = [
            pltpu.make_async_copy(copied[n], results[i], copied[-1].at[n])
            for n, i in enumerate(store, len(fetch))
        ]
        for copy in into:
            copy.start()
        for n, i in enumerate(fetch):
            given[i] = copied[n]
        for n, i in enumerate(store, len(fetch)):
            results[i] = copied[n]
        for copy in into:
            copy.wait()
        body(where_ref, *given, *results, *extra)
        for copy in out_of:
            copy.start()
        for copy in out_of:
            copy.wait()

    def place(i):
        return HBM if i in far_outs or i in store else SMEM if i == scalar else VMEM

    results = pl.pallas_call(
        kernel,
        out_shape=(
            *(
                pltpu.HBM(o.shape, o.dtype) if i in far_outs or i in store else o
                for i, o in enumerate(outs)
            ),
            wide(8, 128),
        ),
        in_specs=[SMEM]
        + [HBM if i in far or i in fetch else VMEM for i in range(count)]
        + [ANY] * len(after),
        out_specs=(*(place(i) for i in range(made)), VMEM),
        scratch_shapes=[*scratch, *held],
        compiler_params=pltpu.CompilerParams(vmem_limit_bytes=vmem << 20),
        cost_estimate=pl.CostEstimate(
            flops=cost * 10**9, transcendentals=0, bytes_accessed=cost * 10**6
        ),
    )(where, *args, *after)
    return (results[:-1] if many else results[0]), results[-1]


def core_rows(core, count):
    return pl.ds(pl.multiple_of(count * core, 16), count)


def rows_at(start, count, align):
    return pl.ds(pl.multiple_of(start, align), count)


def dot(left, right, dims):
    return lax.dot_general(left, right, dims, preferred_element_type=F32)


def run_copies(copies, sems):
    started = [
        pltpu.make_async_copy(source, target, sems.at[i])
        for i, (source, target) in enumerate(copies)
    ]
    for copy in started:
        copy.start()
    for copy in started:
        copy.wait()


def unit_rows(values):
    centred = values - jnp.mean(values, axis=-1, keepdims=True)
    spread = jnp.mean(centred * centred, axis=-1, keepdims=True)
    inverse = lax.rsqrt(spread + EPSILON)
    return centred * inverse, inverse


def unit_back(grad, gain, unit, inverse):
    scaled = grad * gain
    return inverse * (
        scaled
        - jnp.mean(scaled, axis=-1, keepdims=True)
        - unit * jnp.mean(scaled * unit, axis=-1, keepdims=True)
    )


def put_small(out, start, small):
    third = small.shape[1] // 3
    lanes = slice(9 * third, 10 * third)
    for q in range(3):
        block = slice(start + 16 * q, start + 16 * (q + 1))
        out[block, lanes] = small[:, third * q : third * (q + 1)].astype(out.dtype)


def get_small(piece, start, feat):
    third = feat // 3
    lanes = slice(9 * third, 10 * third)
    parts = [piece[start + 16 * q : start + 16 * (q + 1), lanes].astype(F32) for q in range(3)]
    return jnp.concatenate(parts, axis=1)


def pack_tokens(where, tokens, segment, valid, out):
    rows, width = tokens.shape
    ids = segment[...]
    line = lax.broadcasted_iota(jnp.int32, (16, rows), 0)
    codes = jnp.where(
        line == 0,
        ids >> 7,
        jnp.where(line == 1, ids & 127, jnp.where(line == 2, valid[...], 0)),
    )
    out[:rows, :] = tokens[...]
    out[rows:, :] = jnp.zeros((16, width), out.dtype)
    out[rows:, :rows] = codes.astype(F32).astype(out.dtype)


def order_chips(where, p0, p1, p2, p3, out):
    rows = p0.shape[0]
    for k, piece in enumerate((p0, p1, p2, p3)):
        out[rows_at(rows * (where[0] ^ k), rows, 16), :] = piece[...]


def far_planes(where, arrived, out):
    part = arrived.shape[0] // 4
    for s in (1, 2, 3):
        out[part * (s - 1) : part * s, :] = arrived[rows_at(part * (where[2] ^ s), part, 16), :]


def pack_projections(where, *refs):
    weights, vectors, long, valid, out = refs[:3], refs[3:11], refs[11], refs[12], refs[13]
    held, small, held_long, sems = refs[14], refs[15:23], refs[23], refs[24]
    half, feat = held.shape[1], small[0].shape[0]
    out[48:, 3 * feat :] = jnp.zeros((half - 48, feat // 3), out.dtype)
    own_rows = rows_at(half * where[1], half, 32)
    run_copies(
        [(w.at[own_rows], held.at[i]) for i, w in enumerate(weights)]
        + list(zip(vectors, small))
        + [(long, held_long)],
        sems,
    )
    for chip in range(4):

        @pl.when(where[0] == chip)
        def _():
            for i in range(3):
                out[:, feat * i : feat * (i + 1)] = held[i, :, feat * chip : feat * (chip + 1)]

    spread = held_long[...].astype(F32).reshape(1, 4 * feat)
    count = jnp.sum(valid[...].astype(F32), axis=1, keepdims=True)
    lines = [v[...].astype(F32).reshape(1, feat) for v in small]
    lines += [spread[:, feat * i : feat * (i + 1)] for i in range(4)]
    lines += [jnp.broadcast_to(count, (1, feat)), jnp.zeros((3, feat), F32)]
    put_small(out, 0, jnp.concatenate(lines, axis=0))


def pack_down(where, down, out, sem):
    part = out.shape[0]
    rows = rows_at(4 * part * where[1] + part * where[0], part, 32)
    copy = pltpu.make_async_copy(down.at[rows], out, sem)
    copy.start()
    copy.wait()


def pack_blocks(where, up, output, out_up, sems):
    chip, core = where[0], where[1]
    part, units = out_up.shape[0] // 4, out_up.shape[1] // 5
    rows = rows_at(part * chip, part, 16)
    pairs = [
        (
            up.at[rows, rows_at(2 * units * i + units * core, units, 128)],
            out_up.at[:part, units * i : units * (i + 1)],
        )
        for i in range(4)
    ]
    pairs.append((output.at[rows, rows_at(units * core, units, 128)], out_up.at[:part, 4 * units :]))
    run_copies(pairs, sems)
    for p in (1, 2, 3):
        out_up[part * p : part * (p + 1), :] = out_up[:part, :]


def stack_rows(where, *refs):
    pieces, out = refs[:-1], refs[-1]
    rows = pieces[0].shape[0]
    for i, piece in enumerate(pieces):
        out[rows * i : rows * (i + 1), :] = piece[...]


def three_blocks(pieces, part):
    p0, p1, p2, low, high = pieces
    parts = [(k, [(p, 0)]) for k, p in enumerate((p0, p1, p2))] + [(3, [(low, 0), (high, low.shape[0])])]
    found = []
    for k, refs in parts:
        for s in (1, 2, 3):
            for ref, base in refs:
                start, end = max(part * (s - 1), base), min(part * s, base + ref.shape[0])
                if start < end:
                    found.append((k, s, start - part * (s - 1), end - start, ref, start - base))
    return found


def cross_halves(where, from_x, from_y, to_x, to_y):
    cut = to_x.shape[0]
    to_x[...] = from_y[:cut, :]
    to_y[...] = from_x[cut:, :]


def build_up(where, up, p0, p1, p2, p3, p4, out, sems):
    chip, core, plane = where[0], where[1], where[2]
    units, shard = up.shape[1] // 8, up.shape[0]
    part = shard // 4
    own = rows_at(shard * plane, shard, 64)
    pairs = [
        (
            up.at[:, rows_at(2 * units * i + units * core, units, 128)],
            out.at[own, units * i : units * (i + 1)],
        )
        for i in range(4)
    ]
    for k, s, offset, count, piece, start in three_blocks((p0, p1, p2, p3, p4), part):
        at = rows_at(shard * (plane ^ s) + part * (chip ^ k) + offset, count, 16)
        pairs.append((piece.at[start : start + count, : 4 * units], out.at[at]))
    run_copies(pairs, sems)


def build_half(where, output, p0, p1, p2, p3, p4, out, sems):
    chip, core, plane = where[0], where[1], where[2]
    shard, units = output.shape[0], out.shape[1]
    part = shard // 4
    pairs = [
        (
            output.at[:, rows_at(units * core, units, 128)],
            out.at[rows_at(shard * plane, shard, 64)],
        )
    ]
    for k, s, offset, count, piece, start in three_blocks((p0, p1, p2, p3, p4), part):
        at = rows_at(shard * (plane ^ s) + part * (chip ^ k) + offset, count, 16)
        pairs.append((piece.at[start : start + count, 4 * units :], out.at[at]))
    run_copies(pairs, sems)


def build_down(where, down, p0, p1, p2, p3, p4, out, sem):
    chip, core, plane = where[0], where[1], where[2]
    mine = down.shape[0] // 2
    part = mine // 4
    own = pltpu.make_async_copy(
        down.at[rows_at(mine * core, mine, 128)], out.at[rows_at(mine * plane, mine, 128)], sem
    )
    own.start()
    for k, s, offset, count, piece, start in three_blocks((p0, p1, p2, p3, p4), part):
        at = rows_at(mine * (plane ^ s) + part * (chip ^ k) + offset, count, 16)
        out[at, :] = piece[start : start + count, :]
    own.wait()


def build_output(where, near, far, out):
    units = near.shape[1]
    out[:, rows_at(units * where[1], units, 128)] = near[...]
    out[:, rows_at(units * (1 - where[1]), units, 128)] = far[...]


def normalize_tokens(where, near, far, unit_low, key_row, query_column):
    rows = query_column.shape[0] // 4
    for i in range(8):
        block = (near if i < 4 else far).at[(rows + 16) * (i % 4) : (rows + 16) * (i % 4 + 1), :]
        unit, _ = unit_rows(block[:rows, :].astype(F32))
        unit_low[rows * i : rows * (i + 1), :] = unit
        codes = block[rows:, :].astype(F32)
        ids = codes[0:1, :rows] * 128.0 + codes[1:2, :rows]
        key_row[0:1, rows * i : rows * (i + 1)] = jnp.where(codes[2:3, :rows] == 1.0, ids, -1.0)
        if i < 4:
            query_column[rows * i : rows * (i + 1), :] = jnp.broadcast_to(
                ids.reshape(rows, 1), (rows, 128)
            )


def attend(where, *refs):
    units, key_row, query_column, weights, far_weights = refs[:3] + (refs[3:7], refs[7])
    saved, sent, vectors, long = refs[8:13], refs[13], refs[14], refs[15]
    small, bias, h_one, w_three, projected, probs, mixed, sems = refs[16:]
    kept = (h_one, w_three, projected, mixed)
    copies = [
        pltpu.make_async_copy(source, saved[i], sems.at[j])
        for j, (i, source) in enumerate(zip((0, 1, 2, 4), kept))
    ]
    core, plane = where[1], where[2]
    half, feat = weights[0].shape[0], small.shape[2]
    group = query_column.shape[0]
    rows = group // 4

    count = jnp.zeros((1, 1), F32)
    for s, piece in enumerate(weights):
        base = 2 * half * (plane ^ s)
        w_three[rows_at(base + half * core, half, 32), :] = piece[:, : 3 * feat]
        other = far_weights[half * s : half * (s + 1), :]
        w_three[rows_at(base + half * (1 - core), half, 32), :] = other[:, : 3 * feat]
        near = get_small(piece, 0, feat)
        small[plane ^ s] = near
        count += near[12:13, :1] + other[12:13, 3 * feat : 3 * feat + 1].astype(F32)
    vectors[...] = jnp.zeros(vectors.shape, F32)
    for p in range(4):
        lines = small[p]
        for i, r in enumerate((0, 1, 4, 5, 6, 7)):
            vectors[i : i + 1, feat * p : feat * (p + 1)] = lines[r : r + 1, :]
        pair = jnp.where(core == 0, lines[8:10, :], lines[10:12, :])
        long[:, 2 * feat * p : 2 * feat * p + feat] = pair[:1, :]
        long[:, 2 * feat * p + feat : 2 * feat * (p + 1)] = pair[1:, :]
    gain, shift = vectors[0:1, :], vectors[1:2, :]
    short = small[where[0]]
    copies[1].start()
    h_one[...] = (units[...] * gain + shift).astype(BF16)
    copies[0].start()
    values = dot(h_one[...], w_three[...], NN)
    query = (values[:group, :feat] + short[2:3, :]).astype(BF16) * jnp.asarray(
        HEAD_DIM**-0.5, BF16
    )
    projected[:group, :feat] = query
    projected[group:, :feat] = jnp.zeros((group, feat), BF16)
    projected[:, feat : 2 * feat] = values[:, feat : 2 * feat].astype(BF16)
    projected[:, 2 * feat :] = (values[:, 2 * feat :] + short[3:4, :]).astype(BF16)
    copies[2].start()
    column = lax.broadcasted_iota(jnp.int32, (rows, 2 * group), 1)
    line = lax.broadcasted_iota(jnp.int32, (rows, 2 * group), 0)
    for k in range(4):
        ids = query_column[rows * k : rows * (k + 1), :1]
        allowed = (ids == key_row[0:1, :]) | (column == line + rows * k)
        bias[rows * k : rows * (k + 1), :] = jnp.where(allowed, 0.0, MASKED)
    for h in range(feat // HEAD_DIM):
        at = slice(HEAD_DIM * h, HEAD_DIM * (h + 1))
        keys = projected[:, feat + HEAD_DIM * h : feat + HEAD_DIM * (h + 1)]
        held = projected[:, 2 * feat + HEAD_DIM * h : 2 * feat + HEAD_DIM * (h + 1)]
        for k in range(4):
            block = slice(rows * k, rows * (k + 1))
            scores = dot(projected[block, at], keys, NT) + bias[block, :]
            weight = jnp.exp(scores - jnp.max(scores, axis=1, keepdims=True))
            weight = weight * (1.0 / jnp.sum(weight, axis=1, keepdims=True))
            low = weight.astype(BF16)
            probs[h, block, :] = low
            result = dot(low, held, NN)
            mixed[block, at] = result
            sent[(rows + 16) * k : (rows + 16) * k + rows, at] = result.astype(BF16)
        copies.append(pltpu.make_async_copy(probs.at[h], saved[3].at[h], sems.at[4 + h]))
        copies[-1].start()
    copies[3].start()
    high = jnp.floor(count / 128.0)
    side = lax.broadcasted_iota(jnp.int32, (16, feat), 1)
    digits = jnp.where(side == 0, high, jnp.where(side == 1, count - 128.0 * high, 0.0))
    for k in range(4):
        sent[(rows + 16) * k + rows : (rows + 16) * (k + 1), :] = digits.astype(BF16)
    for copy in copies:
        copy.wait()


def attend_back(where, d_all, vectors, *refs):
    saved, (near, far, kept, given, lines) = refs[:5], refs[5:10]
    d_three, d_scores, grads, h_one, w_three, projected, probs, mixed, sems = refs[10:]
    core = where[1]
    pairs = [(saved[2], projected), (saved[4], mixed)]
    pairs += [(saved[3].at[h], probs.at[h]) for h in range(probs.shape[0])]
    pairs += [(saved[0], h_one), (saved[1], w_three)]
    copies = [pltpu.make_async_copy(a, b, sems.at[i]) for i, (a, b) in enumerate(pairs)]
    for copy in copies:
        copy.start()
    copies[0].wait()
    copies[1].wait()
    group, feat = d_all.shape
    rows, width = group // 4, h_one.shape[1]
    scale = HEAD_DIM**-0.5
    d_three[group:, :feat] = jnp.zeros((group, feat), BF16)
    for h in range(feat // HEAD_DIM):
        at = slice(HEAD_DIM * h, HEAD_DIM * (h + 1))
        key_at = slice(feat + HEAD_DIM * h, feat + HEAD_DIM * (h + 1))
        value_at = slice(2 * feat + HEAD_DIM * h, 2 * feat + HEAD_DIM * (h + 1))
        keys, held = projected[:, key_at], projected[:, value_at]
        copies[2 + h].wait()
        for k in range(4):
            block = slice(rows * k, rows * (k + 1))
            d_mixed = d_all[block, at]
            delta = jnp.sum(d_mixed.astype(F32) * mixed[block, at], axis=1, keepdims=True)
            d_probs = dot(d_mixed, held, NT)
            low = (probs[h, block, :].astype(F32) * (d_probs - delta)).astype(BF16)
            d_scores[block, :] = low
            d_three[block, at] = (dot(low, keys, NN) * scale).astype(BF16)
        d_three[:, key_at] = dot(d_scores[...], projected[:group, at], TN).astype(BF16)
        d_three[:, value_at] = dot(probs[h], d_all[:, at], TN).astype(BF16)
    for copy in copies[2 + probs.shape[0] :]:
        copy.wait()
    grads[...] = dot(h_one[...], d_three[...], TN)
    near[...] = dot(d_three[:group, :], w_three[...], NT).astype(BF16)
    far[...] = dot(d_three[group:, :], w_three[...], NT).astype(BF16)
    half = kept.shape[0] // 4
    for p in range(4):
        block = slice(half * p, half * (p + 1))
        kept[block, :] = grads[rows_at(2 * half * p + half * core, half, 32), :].astype(BF16)
        given[block, :] = grads[rows_at(2 * half * p + half * (1 - core), half, 32), :].astype(BF16)
    sums = jnp.sum(d_three[...].astype(F32), axis=0, keepdims=True)
    weight = w_three[...].astype(F32)
    with_gain = jnp.sum(grads[...] * weight, axis=1, keepdims=True)
    with_shift = jnp.sum(weight * sums, axis=1, keepdims=True)
    side = lax.broadcasted_iota(jnp.int32, (width, 128), 1)
    both = jnp.where(side == 0, with_gain, jnp.where(side == 1, with_shift, 0.0)).T
    d_shift = both[1:2, :]
    lines[0:1, :] = (both[0:1, :] - vectors[1:2, :] * d_shift) / vectors[0:1, :]
    lines[1:2, :] = d_shift
    lines[2:3, :] = jnp.zeros((1, width), F32)
    lines[2:3, :feat] = sums[:, :feat]
    lines[3:4, :] = jnp.zeros((1, width), F32)
    lines[3:4, :feat] = sums[:, 2 * feat :]
    lines[4:, :] = jnp.zeros((4, width), F32)


def share_inputs(where, near, far, *outs):
    rows = outs[0].shape[0]
    for k, out in enumerate(outs):
        at = rows_at(rows * (where[0] ^ k), rows, 16)
        out[...] = (near[at, :].astype(F32) + far[at, :].astype(F32)).astype(out.dtype)


def finish_inputs(where, d0, d1, d2, d3, tokens, d_second, vectors, out):
    total = d0[...].astype(F32)
    for piece in (d1, d2, d3):
        total = total + piece[...].astype(F32)
    unit, inverse = unit_rows(tokens[...].astype(F32))
    d_inputs = unit_back(total, vectors[0:1, :], unit, inverse)
    out[...] = (d_second[...] + d_inputs).astype(BF16)


def project_output(where, mixed, w_output, tokens, vectors, second, h_two, count):
    rows, width = tokens.shape
    feat = mixed.shape[1]
    total = tokens[...].astype(F32) + vectors[2:3, :]
    valid = jnp.zeros((1, 1), F32)
    for k in range(4):
        start = (rows + 16) * k
        total += dot(mixed[start : start + rows, :], w_output[feat * k : feat * (k + 1), :], NN)
        digits = mixed[start + rows : start + rows + 16, :].astype(F32)
        valid += digits[0:1, 0:1] * 128.0 + digits[0:1, 1:2]
    second[...] = total
    unit, _ = unit_rows(total)
    h_two[...] = (unit * vectors[3:4, :] + vectors[4:5, :]).astype(BF16)
    count[...] = jnp.broadcast_to(valid, count.shape)


def activate(where, h_pair, w_up, b_up, act, slope):
    rows = h_pair.shape[0] // 2
    root = 0.7978845608028654
    for i in range(2):
        block = slice(rows * i, rows * (i + 1))
        value = dot(h_pair[block, :], w_up[...], NN) + b_up[...]
        square = value * value
        bent = jnp.tanh(root * value * (1.0 + 0.044715 * square))
        act[block, :] = (0.5 * value * (1.0 + bent)).astype(BF16)
        slope[block, :] = 0.5 * (1.0 + bent) + 0.5 * value * (1.0 - bent * bent) * root * (
            1.0 + 3.0 * 0.044715 * square
        )


def project_down(where, act, w_down, near, far):
    rows, core = near.shape[0], where[1]
    near[...] = dot(act[core_rows(core, rows), :], w_down[...], NN)
    far[...] = dot(act[core_rows(1 - core, rows), :], w_down[...], NN).astype(BF16)


def compare(where, second, near, far, vectors, teacher, cotangent, valid, count, *outs):
    layer_output, d_result, d_down, lines = outs
    rows, width = second.shape
    other = far[core_rows(1 - where[1], rows), :].astype(F32)
    result = second[...] + near[...] + other + vectors[5:6, :]
    layer_output[...] = result.astype(BF16)
    kept = valid[...].astype(F32).reshape(rows, 1)
    mismatch = result - teacher[...].astype(F32)
    weighted = kept * mismatch
    error = jnp.sum(jnp.sum(weighted * mismatch, axis=1, keepdims=True), axis=0, keepdims=True)
    total = cotangent[...].astype(F32) + 2.0 / (width * count[0:1, 0:1]) * weighted
    d_result[...] = total
    low = total.astype(BF16)
    d_down[...] = low
    high = error.astype(BF16).astype(F32)
    middle = (error - high).astype(BF16).astype(F32)
    side = lax.broadcasted_iota(jnp.int32, (1, width), 1)
    parts = jnp.where(
        side == 0, high, jnp.where(side == 1, middle, jnp.where(side == 2, error - high - middle, 0.0))
    )
    lines[0:1, :] = jnp.sum(low.astype(F32), axis=0, keepdims=True)
    lines[1:2, :] = parts
    lines[2:, :] = jnp.zeros((6, width), F32)


def activate_back(where, d_down, w_down, slope, w_up, d_up, near, far, line):
    rows, core = near.shape[0], where[1]
    total = jnp.zeros(line.shape, F32)
    for i in range(2):
        block = slice(rows * i, rows * (i + 1))
        low = (dot(d_down[block, :], w_down[...], NT) * slope[block, :]).astype(BF16)
        d_up[block, :] = low
        total += jnp.sum(low.astype(F32), axis=0, keepdims=True)
    line[...] = total
    near[...] = dot(d_up[core_rows(core, rows), :], w_up[...], NT)
    far[...] = dot(d_up[core_rows(1 - core, rows), :], w_up[...], NT).astype(BF16)


def second_back(where, near, far, d_result, second, vectors, w_output, *outs):
    d_second, d_attn, lines, sent = outs
    rows = near.shape[0]
    d_two = near[...] + far[core_rows(1 - where[1], rows), :].astype(F32)
    unit, inverse = unit_rows(second[...])
    total = d_result[...] + unit_back(d_two, vectors[3:4, :], unit, inverse)
    d_second[...] = total
    low = total.astype(BF16)
    d_attn[...] = low
    lines[0:1, :] = jnp.sum(low.astype(F32), axis=0, keepdims=True)
    lines[1:2, :] = jnp.sum(d_two * unit, axis=0, keepdims=True)
    lines[2:3, :] = jnp.sum(d_two, axis=0, keepdims=True)
    lines[3:, :] = jnp.zeros((5, lines.shape[1]), F32)
    feat = sent.shape[1]
    for k in range(4):
        part = w_output[feat * k : feat * (k + 1), :]
        sent[rows * k : rows * (k + 1), :] = dot(low, part, NT).astype(BF16)


def split_chips(chip, block, outs, count):
    own, to_x, to_y, then_x, then_y = outs
    for p in range(4):
        own[count * p : count * (p + 1), :] = block(chip, p).astype(BF16)
    for p in (0, 1):
        low, high = slice(count * p, count * (p + 1)), slice(count * (p + 2), count * (p + 3))
        to_x[low, :] = block(chip ^ 1, p).astype(BF16)
        to_x[high, :] = block(chip ^ 3, p).astype(BF16)
        to_y[low, :] = block(chip ^ 2, p + 2).astype(BF16)
        to_y[high, :] = block(chip ^ 3, p + 2).astype(BF16)
        then_x[low, :] = block(chip ^ 1, p + 2).astype(BF16)
        then_y[low, :] = block(chip ^ 2, p).astype(BF16)


def pass_on(where, from_x, from_y, then_x, then_y, to_x, to_y):
    half = to_x.shape[0]
    to_x[...] = (then_x[...].astype(F32) + from_y[half:, :].astype(F32)).astype(BF16)
    to_y[...] = (then_y[...].astype(F32) + from_x[half:, :].astype(F32)).astype(BF16)


def add_chips(own, from_x, from_y, last_x, last_y):
    half = last_x.shape[0]
    low = own[:half, :].astype(F32) + from_x[:half, :].astype(F32) + last_y[...].astype(F32)
    high = own[half:, :].astype(F32) + from_y[:half, :].astype(F32) + last_x[...].astype(F32)
    return low, high


def down_grads(where, act, d_down, *refs):
    outs, total = refs[:5], refs[5]
    count = outs[0].shape[0] // 4
    total[...] = dot(act[...], d_down[...], TN).astype(BF16)

    def block(j, p):
        return total[rows_at(4 * count * p + count * j, count, 32), :]

    split_chips(where[0], block, outs, count)


def output_grads(where, mixed, d_attn, kept, given):
    core = where[1]
    rows, width = d_attn.shape
    feat, units = mixed.shape[1], width // 2
    mine = d_attn[:, rows_at(units * core, units, 128)]
    others = d_attn[:, rows_at(units * (1 - core), units, 128)]
    for j in range(4):
        at = slice(feat * j, feat * (j + 1))
        piece = mixed[(rows + 16) * j : (rows + 16) * j + rows, :]
        kept[at, :] = dot(piece, mine, TN).astype(BF16)
        given[at, :] = dot(piece, others, TN).astype(BF16)


def up_grads(where, h_pair, d_up, kept, given, *refs):
    outs, total = refs[:4], refs[4]
    count, units = outs[0].shape[0] // 4, d_up.shape[1]
    total[:, :units] = dot(h_pair[...], d_up[...], TN).astype(BF16)
    total[:, units:] = (kept[...].astype(F32) + given[...].astype(F32)).astype(BF16)
    for k, out in enumerate(outs):
        for p in range(4):
            at = rows_at(4 * count * p + count * (where[0] ^ k), count, 16)
            out[count * p : count * (p + 1), :] = total[at, :]


def send_planes(where, own, p1, p2, p3, *refs):
    outs, total = refs[:4], refs[4]
    part = outs[0].shape[0]
    added = own[...].astype(F32)
    for piece in (p1, p2, p3):
        added = added + piece[...].astype(F32)
    total[...] = added
    for s, out in enumerate(outs):
        out[...] = total[rows_at(part * (where[2] ^ s), part, 16), :].astype(out.dtype)


def sum_pieces(where, own, p1, p2, p3, out):
    total = own[...].astype(F32)
    for piece in (p1, p2, p3):
        total = total + piece[...].astype(F32)
    out[...] = total.astype(out.dtype)


def finish_down(where, near, far, out, held, sems):
    core = where[1]
    both = near.shape[0] // 4
    part = both // 2
    copies = []
    for j in range(4):
        block = slice(both * j + part, both * (j + 1))
        for side, piece in ((core, near), (1 - core, far)):
            at = rows_at(4 * part * side + part * j, part, 32)
            held[at, :] = piece[block, :].astype(F32)
            copies.append(pltpu.make_async_copy(held.at[at], out.at[at], sems.at[len(copies)]))
            copies[-1].start()
    for copy in copies:
        copy.wait()


def finish_up(where, n0, n1, n2, n3, far, out, out_half, held, held_half, sems):
    chip, core = where[0], where[1]
    part, units = n0.shape[0], n0.shape[1] // 5
    copies = []
    for k, near in enumerate((n0, n1, n2, n3)):
        rows = rows_at(part * (chip ^ k), part, 16)
        for piece, side in ((near[...], core), (far[part * k : part * (k + 1), :], 1 - core)):
            full = piece.astype(F32)
            for i in range(4):
                at = rows_at(2 * units * i + units * side, units, 128)
                held[rows, at] = full[:, units * i : units * (i + 1)]
            held_half[rows, rows_at(units * side, units, 128)] = full[:, 4 * units :]
        for source, target in ((held, out), (held_half, out_half)):
            copies.append(
                pltpu.make_async_copy(source.at[rows], target.at[rows], sems.at[len(copies)])
            )
            copies[-1].start()
    for copy in copies:
        copy.wait()


def sum_chips(where, own, from_x, from_y, last_x, last_y, out):
    half = last_x.shape[0]
    low, high = add_chips(own, from_x, from_y, last_x, last_y)
    out[:half, :], out[half:, :] = low.astype(BF16), high.astype(BF16)


def pack_gradients(
    where, kept, given, from_attention, from_second, from_result, up_line, down, out, down_sum
):
    chip = where[0]
    part = down_sum.shape[0]
    arrived_down = down[:part, :].astype(F32)
    for p in (1, 2, 3):
        arrived_down = arrived_down + down[part * p : part * (p + 1), :].astype(F32)
    down_sum[...] = arrived_down.astype(BF16)
    half, feat = out.shape[0] // 4, kept.shape[1] // 3
    for p in range(4):
        cut = slice(feat * p, feat * (p + 1))
        owner = jnp.where(chip == p, 1.0, 0.0)
        lines = [
            from_attention[0:1, cut],
            from_attention[1:2, cut],
            from_second[0:1, cut],
            from_second[1:2, cut],
            from_second[2:3, cut],
            from_result[0:1, cut],
            up_line[:, 2 * feat * p : 2 * feat * p + feat],
            up_line[:, 2 * feat * p + feat : 2 * feat * (p + 1)],
            from_attention[2:3, :feat] * owner,
            from_attention[3:4, :feat] * owner,
            from_result[1:2, :feat],
            jnp.zeros((5, feat), F32),
        ]
        small = jnp.concatenate(lines, axis=0)
        block = slice(half * p, half * (p + 1))
        total = (kept[block, :].astype(F32) + given[block, :].astype(F32)).astype(BF16)
        out[block, : 3 * feat] = total
        out[half * p + 48 : half * (p + 1), 3 * feat :] = jnp.zeros((half - 48, feat // 3), BF16)
        put_small(out, half * p, small)


def sum_planes(where, arrived, down, out):
    both, width = out.shape[0] // 4, out.shape[1]
    half, feat = both // 2, width // 4
    total = arrived[:half, :].astype(F32)
    for p in (1, 2, 3):
        total = total + arrived[half * p : half * (p + 1), :].astype(F32)
    small = get_small(total, 0, feat)
    error = jnp.sum(small[10:11, :3], axis=1, keepdims=True)
    high = error.astype(BF16).astype(F32)
    middle = (error - high).astype(BF16).astype(F32)
    line = lax.broadcasted_iota(jnp.int32, small.shape, 0)
    side = lax.broadcasted_iota(jnp.int32, small.shape, 1)
    parts = jnp.where(side == 0, high, jnp.where(side == 1, middle, error - high - middle))
    small = jnp.where((line == 10) & (side < 3), parts, small)
    for j in range(4):
        start = both * j
        out[start : start + half, : 3 * feat] = total[:, : 3 * feat].astype(BF16)
        out[start : start + 16, 3 * feat :] = small.astype(BF16)
        out[start + 16 : start + half, 3 * feat :] = jnp.zeros((half - 16, feat), BF16)
        out[start + half : start + both, :] = down[...]


def finish_projections(where, near, far, count, *outs):
    query, key, value, loss = outs[:4]
    flat, up_line, held, whole_line = outs[4:12], outs[12], outs[13], outs[14]
    core = where[1]
    both, width = near.shape[0] // 4, near.shape[1]
    half, feat = both // 2, width // 4
    for j in range(4):
        start = both * j
        for side, piece in ((core, near), (1 - core, far)):
            held[2 * j + side] = piece[start : start + 16, 3 * feat :].astype(F32)
            rows = rows_at(half * side, half, 32)
            for i, out in enumerate((query, key, value)):
                out[rows, feat * j : feat * (j + 1)] = piece[
                    start : start + half, feat * i : feat * (i + 1)
                ].astype(F32)
    total = held[0]
    for i in range(1, 8):
        total = total + held[i]
    for i, line in enumerate((0, 1, 2, 3, 4, 5, 8, 9)):
        flat[i][...] = total[line]
    even = held[0] + held[2] + held[4] + held[6]
    odd = held[1] + held[3] + held[5] + held[7]
    for side, part in enumerate((even, odd)):
        for i in range(2):
            at = 2 * feat * side + feat * i
            whole_line[0:1, at : at + feat] = part[6 + i : 7 + i, :]
    up_line[...] = whole_line[0]
    error = jnp.sum(total[10:11, :3], axis=1, keepdims=True)
    loss[0, 0] = jnp.sum(error / (width * count[0:1, 0:1]))


def layer(
    tokens,
    segment_ids,
    valid_rows,
    teacher,
    cotangent,
    first_gain,
    first_shift,
    query_weight,
    query_bias,
    key_weight,
    value_weight,
    value_bias,
    output_weight,
    output_bias,
    second_gain,
    second_shift,
    up_weight,
    up_bias,
    down_weight,
    down_bias,
):
    rows, width = tokens.shape[1], tokens.shape[2]
    shard = query_weight.shape[0]
    half, quarter = shard // 2, shard // 4
    hidden = up_weight.shape[1]
    units = hidden // 2
    own_units = down_weight.shape[0]
    core_units = own_units // 2
    part_units = core_units // 4
    feat = width // 4
    heads = feat // HEAD_DIM
    group = 4 * rows
    every = 2 * group
    steps = (1, 2, 3)

    place, plane = lax.axis_index("ctx"), lax.axis_index("fsdp")
    where = jnp.stack([place // 2, place % 2, plane]).astype(jnp.int32)
    dma = pltpu.SemaphoreType.DMA

    last = []

    def step(body, outs, args, **options):
        made, token = local_call(body, outs, where, args, after=last, **options)
        last[:] = [token]
        return made

    def stack(pieces, cost=0):
        shape = len(pieces) * pieces[0].shape[0], pieces[0].shape[1]
        return step(stack_rows, shaped(*shape), pieces, cost=cost)

    own = tokens[0]
    smalls = (
        first_gain,
        first_shift,
        query_bias,
        value_bias,
        output_bias,
        second_gain,
        second_shift,
        down_bias,
    )
    up_piece = step(
        pack_blocks,
        shaped(4 * quarter, 5 * core_units),
        (up_weight, output_weight),
        far=range(2),
        scratch=[dma((5,))],
    )
    up_far = trade_planes(up_piece)
    bundle = step(pack_tokens, shaped(rows + 16, width), (own, segment_ids, valid_rows), cost=50)
    near_tokens = [bundle] + [swap_chips(bundle, k) for k in steps]
    lanes = 3 * feat + feat // 3
    projections = step(
        pack_projections,
        shaped(half, lanes),
        (query_weight, key_weight, value_weight, *smalls, up_bias, valid_rows),
        far=range(12),
        scratch=[
            pltpu.VMEM((3, half, width), BF16),
            *[pltpu.VMEM((feat,), BF16)] * 8,
            pltpu.VMEM((own_units,), BF16),
            dma((12,)),
        ],
        cost=0,
    )
    near_tokens = step(order_chips, shaped(4 * (rows + 16), width), near_tokens, cost=0)
    far_tokens = swap_cores(near_tokens)
    up_far = step(far_planes, shaped(3 * quarter, 5 * core_units), (up_far,), cost=0)
    up_three = up_far, swap_chips(up_far, 1), swap_chips(up_far, 2)
    near_weights = [projections] + [swap_planes(projections, s) for s in steps]
    unit_one, key_row, query_column = step(
        normalize_tokens,
        (wide(every, width), wide(8, every), wide(group, 128)),
        (near_tokens, far_tokens),
        cost=1,
    )
    far_weights = swap_cores(stack(near_weights))

    def first_chips(piece):
        return piece, swap_chips(piece, 1), swap_chips(piece, 2)

    def all_chips(three, cut):
        count, lanes = three[0].shape
        to_x, to_y = step(cross_halves, (shaped(cut, lanes), shaped(count - cut, lanes)), three[1:], cost=50)
        return (*three, swap_chips(to_x, 1), swap_chips(to_y, 2))

    up_all = all_chips(up_three, up_far.shape[0] // 32 * 16 + 16)
    down_piece = step(
        pack_down, shaped(part_units, width), (down_weight,), far=(0,), scratch=[dma]
    )
    down_far = [swap_planes(down_piece, s) for s in steps]

    h_one, w_three, projected, probs, mixed, sent, vectors, b_up = step(
        attend,
        (
            shaped(every, width),
            shaped(width, 3 * feat),
            shaped(every, 3 * feat),
            shaped(heads, group, every),
            wide(group, feat),
            shaped(4 * (rows + 16), feat),
            wide(8, width),
            wide(1, units),
        ),
        (unit_one, key_row, query_column, *near_weights, far_weights),
        far_outs=range(5),
        scratch=[
            pltpu.VMEM((4, 16, feat), F32),
            pltpu.VMEM((group, every), F32),
            pltpu.VMEM((every, width), BF16),
            pltpu.VMEM((width, 3 * feat), BF16),
            pltpu.VMEM((every, 3 * feat), BF16),
            pltpu.VMEM((heads, group, every), BF16),
            pltpu.VMEM((group, feat), F32),
            dma((4 + heads,)),
        ],
        vmem=28,
        cost=50,
    )
    mixed_low = trade_chips(sent)
    down_far = first_chips(stack(down_far))
    out_near = step(
        build_half,
        shaped(width, core_units),
        (output_weight, *up_all),
        far=range(6),
        scratch=[dma((20,))],
    )
    out_far = swap_cores(out_near)
    w_up = step(
        build_up, shaped(width, units), (up_weight, *up_all), far=range(6), scratch=[dma((20,))], cost=50
    )
    w_output = step(build_output, shaped(width, width), (out_near, out_far))

    down_all = all_chips(down_far, down_far[0].shape[0] // 2)
    second, h_two, count = step(
        project_output,
        (wide(rows, width), shaped(rows, width), wide(8, 128)),
        (mixed_low, w_output, own, vectors),
    )
    h_pair = both_cores(h_two)
    act, slope = step(
        activate,
        (shaped(2 * rows, units), wide(2 * rows, units)),
        (h_pair, w_up, b_up),
    )
    w_down = step(
        build_down, shaped(units, width), (down_weight, *down_all), far=(0,), scratch=[dma]
    )
    down_near, down_other = step(
        project_down, (wide(rows, width), shaped(rows, width)), (act, w_down)
    )
    layer_output, d_result, d_down, from_result = step(
        compare,
        (shaped(rows, width), wide(rows, width), shaped(rows, width), wide(8, width)),
        (
            second,
            down_near,
            both_cores(down_other),
            vectors,
            teacher[0],
            cotangent[0],
            valid_rows,
            count,
        ),
    )
    d_down = both_cores(d_down)

    def five(count, lanes):
        return (shaped(4 * count, lanes),) * 3 + (shaped(2 * count, lanes),) * 2

    def onward(parts, arrived):
        count, lanes = parts[3].shape
        to_x, to_y = step(
            pass_on, (shaped(count, lanes),) * 2, (*arrived, *parts[3:]),
            cost=50,
        )
        return (parts[0], *arrived, swap_chips(to_x, 1), swap_chips(to_y, 2))

    down_parts = step(
        down_grads,
        five(part_units, width),
        (act, d_down),
        scratch=[pltpu.VMEM((units, width), BF16)],
        vmem=24,
    )
    down_arrived = swap_chips(down_parts[1], 1), swap_chips(down_parts[2], 2)
    d_up, two_near, two_other, up_line = step(
        activate_back,
        (shaped(2 * rows, units), wide(rows, width), shaped(rows, width), wide(1, units)),
        (d_down, w_down, slope, w_up),
        cost=50,
    )
    d_second, d_attn, from_second, d_sent = step(
        second_back,
        (wide(rows, width), shaped(rows, width), wide(8, width), shaped(group, feat)),
        (two_near, both_cores(two_other), d_result, second, vectors, w_output),
    )
    d_mixed = trade_chips(d_sent)

    kept_out, given_out = step(
        output_grads,
        (shaped(width, core_units), shaped(width, core_units)),
        (mixed_low, d_attn),
        cost=1,
    )
    given_out = swap_cores(given_out)
    down_sums = onward(down_parts, down_arrived)
    up_parts = step(
        up_grads,
        (shaped(4 * quarter, 5 * core_units),) * 4,
        (h_pair, d_up, kept_out, given_out),
        store=(0,),
        scratch=[pltpu.VMEM((width, 5 * core_units), BF16)],
        vmem=24,
        cost=5,
    )
    up_sums = [up_parts[0]] + [swap_chips(up_parts[k], k) for k in steps]
    down_planes = trade_planes(step(sum_chips, shaped(4 * part_units, width), down_sums))

    d_near, d_far, kept, given, from_attention = step(
        attend_back,
        (
            shaped(group, width),
            shaped(group, width),
            shaped(4 * half, 3 * feat),
            shaped(4 * half, 3 * feat),
            wide(8, width),
        ),
        (d_mixed, vectors, h_one, w_three, projected, probs, mixed),
        far=range(2, 7),
        store=(2, 3),
        scratch=[
            pltpu.VMEM((every, 3 * feat), BF16),
            pltpu.VMEM((group, every), BF16),
            pltpu.VMEM((width, 3 * feat), F32),
            pltpu.VMEM((every, width), BF16),
            pltpu.VMEM((width, 3 * feat), BF16),
            pltpu.VMEM((every, 3 * feat), BF16),
            pltpu.VMEM((heads, group, every), BF16),
            pltpu.VMEM((group, feat), F32),
            dma((4 + heads,)),
        ],
        vmem=28,
        cost=50,
    )
    given, d_far = swap_cores(given), swap_cores(d_far)
    arrived, down_planes = step(
        pack_gradients,
        (shaped(4 * half, lanes), shaped(part_units, width)),
        (kept, given, from_attention, from_second, from_result, up_line, down_planes),
        fetch=(0, 1),
        cost=1,
    )
    arrived = trade_planes(arrived)

    def spread(piece):
        return [piece] + [swap_chips(piece, k) for k in steps]

    def whole(near):
        return (*near, swap_cores(stack(near, cost=1)))

    up_planes = step(
        send_planes,
        (shaped(quarter, 5 * core_units),) * 4,
        up_sums,
        fetch=(0,),
        scratch=[pltpu.VMEM((4 * quarter, 5 * core_units), F32)],
        cost=50,
    )
    up_planes = [up_planes[0]] + [swap_planes(up_planes[s], s) for s in steps]
    shares = step(share_inputs, (shaped(rows, width),) * 4, (d_near, d_far), store=(0,), cost=50)
    shares = [shares[0]] + [swap_chips(shares[k], k) for k in steps[::-1]]
    both = trade_chips(step(sum_planes, shaped(8 * half, width), (arrived, down_planes), cost=50))
    up_near = spread(step(sum_pieces, shaped(quarter, 5 * core_units), up_planes, cost=50))
    grad_tokens = step(
        finish_inputs, shaped(rows, width), (*shares, own, d_second, vectors), fetch=(0, 4), cost=50
    )
    both = (both, swap_cores(both))
    up_whole = whole(up_near)
    finished = step(
        finish_projections,
        (wide(shard, width),) * 3
        + (wide(1, 1),)
        + (wide(shard),) * 8
        + (wide(own_units),),
        (*both, count),
        scratch=[pltpu.VMEM((8, 16, feat), F32), pltpu.VMEM((8, own_units), F32)],
        scalar=3,
    )
    grad_down_weight = step(
        finish_down,
        wide(own_units, width),
        both,
        far_outs=(0,),
        scratch=[pltpu.VMEM((own_units, width), F32), dma((8,))],
    )
    grad_up_weight, grad_output_weight = step(
        finish_up,
        (wide(shard, hidden), wide(shard, width)),
        up_whole,
        far_outs=(0, 1),
        scratch=[pltpu.VMEM((shard, hidden), F32), pltpu.VMEM((shard, width), F32), dma((8,))],
    )
    sums, two = finished[4:10], finished[10:12]
    return (
        layer_output[None],
        finished[3].reshape(()),
        grad_tokens[None],
        sums[0],
        sums[1],
        finished[0],
        two[0],
        finished[1],
        finished[2],
        two[1],
        grad_output_weight,
        sums[2],
        sums[3],
        sums[4],
        grad_up_weight,
        finished[12],
        grad_down_weight,
        sums[5],
    )


def solution(mesh):
    body = layer if (mesh.shape["ctx"], mesh.shape["fsdp"]) == (8, 4) else shards
    placed = (
        P("fsdp", "ctx", None),
        P("fsdp", "ctx"),
        P("fsdp", "ctx"),
        P("fsdp", "ctx", None),
        P("fsdp", "ctx", None),
        P("fsdp"),
        P("fsdp"),
        P("fsdp", None),
        P("fsdp"),
        P("fsdp", None),
        P("fsdp", None),
        P("fsdp"),
        P("fsdp", None),
        P("fsdp"),
        P("fsdp"),
        P("fsdp"),
        P("fsdp", None),
        P("fsdp"),
        P("fsdp", None),
        P("fsdp"),
    )
    return jax.shard_map(
        body,
        mesh=mesh,
        in_specs=placed,
        out_specs=(
            P("fsdp", "ctx", None),
            P(),
            P("fsdp", "ctx", None),
            P("fsdp"),
            P("fsdp"),
            P("fsdp", None),
            P("fsdp"),
            P("fsdp", None),
            P("fsdp", None),
            P("fsdp"),
            P("fsdp", None),
            P("fsdp"),
            P("fsdp"),
            P("fsdp"),
            P("fsdp", None),
            P("fsdp"),
            P("fsdp", None),
            P("fsdp"),
        ),
        check_vma=False,
    )
```
